32 devices in a mesh: gx: 4 (over y, x), gy: 8 (over z, core).
Axes of the slice: x: 2, y: 2, z: 4, core: 2. Of those that a mesh axis runs over, the one named last changes fastest.
Arguments:
- grid_scalars: float32 [54, 8, 16, 128], P(None, 'gx', 'gy'), may hold values from -6 to 6
- axial_speed: float32 [8, 16, 128], P('gx', 'gy'), may hold values from 0.1 to 0.4
- particles: float32 [54, 32, 16384], P(None, None, ('gx', 'gy')), may hold values from -6 to 6
- cell_owner: int32 [8, 16, 128], P('gx', 'gy'), may hold values from 0 to 7, as said below
- cell_slot: int32 [8, 16, 128], P('gx', 'gy'), may hold values from 0 to 511, as said below
- mix_rate: float32 [16384], P(('gx', 'gy')), may hold values from 0.2 to 0.6
- partner: int32 [32, 16384], P(None, ('gx', 'gy')), may hold values from 0 to 31, as said below
- chem_input: bfloat16 [256, 54], replicated, may hold values from -0.875 to 0.875
- chem_hidden: bfloat16 [256, 256], replicated, may hold values from -0.375 to 0.375
- chem_output: bfloat16 [54, 256], replicated, may hold values from -0.375 to 0.375
- react_slots: int32 [32, 256], P(('gx', 'gy')), may hold values from 0 to 511, as said below
- react_count: int32 [32], P(('gx', 'gy')), may hold values from 1 to 256, as said below
- leave_slots: int32 [32, 64], P(('gx', 'gy')), may hold values from 0 to 512, as said below
- arrive_slots: int32 [32, 64], P(('gx', 'gy')), may hold values from 0 to 512, as said below
Outputs:
- grid_out: float32 [54, 8, 16, 128], P(None, 'gx', 'gy')
- particles_out: float32 [54, 32, 16384], P(None, None, ('gx', 'gy'))
The draws below stay inside these ranges and needn't reach their ends.
Inputs may be any that keep to these rules, and one draw needn't show every extreme that they name: `cell_owner`: within each gx index, each of the 8 owners holds exactly 512 cells of that gx index's grid boxes, each slot once; from one grid box to one owner go at most 96 cells, and exactly 96 for some pairs in every draw. `cell_slot`: slots as described for cell_owner. In each cell partner pairs the 32 particles: partner of partner is the particle itself, never itself. `react_slots`: distinct slots in each owner's row. `react_count`: some owner has 256 live entries in every draw. `leave_slots`: every device hands one or 2 cells to every device, 2 to some; the value 512 marks an empty place; the leaving slots of a device are distinct and are exactly the slots that arriving cells take there. `arrive_slots`: as for leave_slots.
All inputs are finite; a program needn't handle non-finite values.
Results may differ from the reference program's by a relative error of at most 0.0013.
Values sent between devices are 32-bit elements; how exact they have to be, the bound alone decides.
No kernel may reach another device: no remote copies, remote signals or barrier semaphores. Data moves between devices by JAX's collectives and lax.ppermute only.
A program may use at most 128 MiB of HBM per device.

```python
import jax
import jax.numpy as jnp
from jax import lax

NS = 54
HID = 256
NP = 32
BX = 2
BY = 2
BZ = 128
SUBSTEPS = 2
CAPM = 2
CDEV = 512
RMAX = 256
NX = 8
NY = 16
NZ = 128
PCELLS = 16384
N_GX = 4
N_GY = 8
DEVICES = 32


def shuffled(key, leading, length):
    scores = jax.random.randint(key, leading + (length,), 0, 1 << 20) * length + jnp.arange(length, dtype=jnp.int32)
    return jnp.argsort(scores, axis=-1).astype(jnp.int32)


def arrange(values):
    return values.reshape(N_GX, N_GY, BX, BY, BZ).transpose(0, 2, 1, 3, 4).reshape(NX, NY, NZ).astype(jnp.int32)


def partition_maps(key):
    base = jax.random.fold_in(key, 7)
    first_key, second_key, third_key = jax.random.split(base, 3)
    share = CDEV // N_GY
    ordering = shuffled(first_key, (N_GX,), N_GY)
    counts = jnp.where(ordering < N_GY // 2, 3 * share // 2, share // 2)
    ending = jnp.cumsum(counts, axis=1)
    within = jnp.arange(CDEV, dtype=jnp.int32)
    offset = jnp.sum((ending[:, None, :] <= within[None, :, None]).astype(jnp.int32), axis=2)
    boxes = jnp.arange(N_GY, dtype=jnp.int32)
    owner_of = (boxes[None, :, None] + offset[:, None, :]) % N_GY
    slot_perm = shuffled(second_key, (N_GX, N_GY), CDEV)
    row_index = jnp.arange(N_GX, dtype=jnp.int32)[:, None, None]
    slot_of = slot_perm.reshape(-1)[(row_index * N_GY + owner_of) * CDEV + within[None, None, :]]
    cell_perm = shuffled(third_key, (N_GX, N_GY), CDEV)
    inverse = jnp.argsort(cell_perm, axis=-1)
    owner_local = jnp.take_along_axis(owner_of, inverse, axis=-1)
    slot_local = jnp.take_along_axis(slot_of, inverse, axis=-1)
    return (arrange(owner_local), arrange(slot_local))


def draw_cell_owner(key, part):
    return partition_maps(key)[0]


def draw_cell_slot(key, part):
    return partition_maps(key)[1]


def migration_lists(key):
    base = jax.random.fold_in(key, 29)
    first_key, second_key, third_key = jax.random.split(base, 3)
    device_ids = jnp.arange(DEVICES, dtype=jnp.int32)
    extra = jax.random.randint(first_key, (DEVICES,), 0, 2)
    forced = jax.random.randint(second_key, (), 0, DEVICES)
    counts = 1 + jnp.maximum(extra, (device_ids == forced).astype(jnp.int32))
    starting = jnp.cumsum(counts) - counts
    leaving = shuffled(third_key, (DEVICES,), CDEV)
    offset = (device_ids[None, :] - device_ids[:, None]) % DEVICES
    send_parts = []
    place_parts = []
    for copy_index in range(CAPM):
        position = starting[offset] + copy_index
        valid = copy_index < counts[offset]
        sending = jnp.take_along_axis(leaving, jnp.clip(position, 0, CDEV - 1), axis=1)
        send_parts.append(jnp.where(valid, sending, CDEV))
        position_back = position.T
        valid_back = valid.T
        placing = jnp.take_along_axis(leaving, jnp.clip(position_back, 0, CDEV - 1), axis=1)
        place_parts.append(jnp.where(valid_back, placing, CDEV))
    send_table = jnp.stack(send_parts, axis=-1).reshape(DEVICES, DEVICES * CAPM).astype(jnp.int32)
    place_table = jnp.stack(place_parts, axis=-1).reshape(DEVICES, DEVICES * CAPM).astype(jnp.int32)
    return (send_table, place_table)


def draw_leave_slots(key, part):
    return migration_lists(key)[0]


def draw_arrive_slots(key, part):
    return migration_lists(key)[1]


def draw_react_slots(key, part):
    return shuffled(jax.random.fold_in(key, 41), (DEVICES,), CDEV)[:, :RMAX]


def draw_react_count(key, part):
    first_key, second_key = jax.random.split(jax.random.fold_in(key, 43))
    counts = jax.random.randint(first_key, (DEVICES,), RMAX // 8, RMAX // 2 + 1)
    forced = jax.random.randint(second_key, (), 0, DEVICES)
    return jnp.where(jnp.arange(DEVICES, dtype=jnp.int32) == forced, RMAX, counts).astype(jnp.int32)


def draw_partner(key, part):
    ordering = shuffled(jax.random.fold_in(key, 53), (PCELLS,), NP)
    inverse = jnp.argsort(ordering, axis=-1).astype(jnp.int32)
    mates = jnp.take_along_axis(ordering, jnp.bitwise_xor(inverse, 1), axis=-1)
    return mates.T.astype(jnp.int32)


def level_of(own_key, shape, shards, least, high):
    level = 1.0
    for dim, blocks in shards:
        steps = jax.random.uniform(jax.random.fold_in(jax.random.fold_in(own_key, 6), dim), (blocks,), jnp.float32, least / len(shards), high / len(shards))
        level = level * jnp.repeat(jnp.exp(steps), shape[dim] // blocks).reshape((-1,) + (1,) * (len(shape) - 1 - dim))
    return level


def scatter_about(stream_key, extent, spread, most, shards=(), kind=jnp.bfloat16):
    drawn = spread * jax.random.normal(stream_key, extent, jnp.float32)
    if shards:
        drawn = drawn * level_of(stream_key, extent, shards, -0.22, 0.18)
    return jnp.clip(drawn, -most, most).astype(kind)


def setup_inputs(seed: int = 0) -> dict:
    splits = jax.random.split(jax.random.key(seed), 15)
    grid_scalars = scatter_about(splits[0], (NS, NX, NY, NZ), 1.0, 6.0, ((1, 4), (2, 8)), jnp.float32)
    axial_speed = jnp.clip(0.1 + 0.3 * jax.random.uniform(splits[1], (NX, NY, NZ), jnp.float32) ** level_of(splits[1], (NX, NY, NZ), ((0, 4), (1, 8)), -0.2, 0.2), 0.1, 0.4)
    particles = scatter_about(splits[2], (NS, NP, PCELLS), 1.0, 6.0, ((2, 32),), jnp.float32)
    cell_owner = draw_cell_owner(jax.random.fold_in(splits[14], 71), 0)
    cell_slot = draw_cell_slot(jax.random.fold_in(splits[14], 71), 0)
    mix_rate = jnp.clip(0.2 + 0.400000021 * jax.random.uniform(splits[5], (PCELLS,), jnp.float32) ** level_of(splits[5], (PCELLS,), ((0, 32),), -0.2, 0.2), 0.2, 0.6)
    partner = draw_partner(jax.random.fold_in(splits[14], 71), 0)
    chem_input = scatter_about(splits[7], (HID, NS), NS ** -0.5, 0.875)
    chem_hidden = scatter_about(splits[8], (HID, HID), HID ** -0.5, 0.375)
    chem_output = scatter_about(splits[9], (NS, HID), HID ** -0.5, 0.375)
    react_slots = draw_react_slots(jax.random.fold_in(splits[14], 71), 0)
    react_count = draw_react_count(jax.random.fold_in(splits[14], 71), 0)
    leave_slots = draw_leave_slots(jax.random.fold_in(splits[14], 71), 0)
    arrive_slots = draw_arrive_slots(jax.random.fold_in(splits[14], 71), 0)
    return dict(grid_scalars=grid_scalars, axial_speed=axial_speed, particles=particles, cell_owner=cell_owner, cell_slot=cell_slot, mix_rate=mix_rate, partner=partner, chem_input=chem_input, chem_hidden=chem_hidden, chem_output=chem_output, react_slots=react_slots, react_count=react_count, leave_slots=leave_slots, arrive_slots=arrive_slots)


DIFFUSION = 0.1
PAIR_WEIGHT = 0.4


def advance(padded, axial_speed):
    center = padded[:, 1:-1, 1:-1, :]
    upstream = padded[:, :-2, 1:-1, :]
    beside = upstream + padded[:, 2:, 1:-1, :]
    beside = beside + padded[:, 1:-1, :-2, :] + padded[:, 1:-1, 2:, :]
    beside = beside + jnp.roll(center, 1, axis=3) + jnp.roll(center, -1, axis=3)
    return center + DIFFUSION * (beside - 6.0 * center) - axial_speed[None] * (center - upstream)


def particle_section(state, filtered, relaxation, partner, chem_input, chem_hidden, chem_output, chosen_slots, live_count):
    state = state + relaxation[None, None, :] * (filtered[:, None, :] - state)
    partner_state = jnp.take_along_axis(state, partner[None, :, :], axis=1)
    state = state + PAIR_WEIGHT * (partner_state - state)
    chosen = jnp.take(state, chosen_slots, axis=2)
    feed_rows = chosen.reshape(chosen.shape[0], -1).astype(jnp.bfloat16)
    layer_one = jax.nn.silu(jnp.dot(chem_input, feed_rows, preferred_element_type=jnp.float32)).astype(jnp.bfloat16)
    layer_two = jax.nn.silu(jnp.dot(chem_hidden, layer_one, preferred_element_type=jnp.float32)).astype(jnp.bfloat16)
    change = jnp.dot(chem_output, layer_two, preferred_element_type=jnp.float32).astype(jnp.bfloat16)
    change = change.reshape(chosen.shape).astype(jnp.float32)
    active = jnp.arange(chosen_slots.shape[0], dtype=jnp.int32) < live_count
    change = jnp.where(active[None, None, :], change, jnp.zeros_like(change))
    state = state.at[:, :, chosen_slots].add(change)
    source = jnp.zeros(filtered.shape, filtered.dtype).at[:, chosen_slots].set(jnp.mean(change, axis=1))
    return state, source


def reference(grid_scalars, axial_speed, particles, cell_owner, cell_slot, mix_rate, partner, chem_input, chem_hidden, chem_output, react_slots, react_count, leave_slots, arrive_slots):
    devices = N_GX * N_GY
    slab_cells = BX * BY * BZ
    row_index = jnp.arange(NX, dtype=jnp.int32)[:, None, None] // BX
    target = ((row_index * N_GY + cell_owner) * slab_cells + cell_slot).reshape(-1).astype(jnp.int32)
    state = particles.reshape(NS, NP, devices, slab_cells).transpose(2, 0, 1, 3)
    relaxation = mix_rate.reshape(devices, slab_cells)
    pairings = partner.reshape(NP, devices, slab_cells).transpose(1, 0, 2)
    grid = grid_scalars
    for substep in range(SUBSTEPS):
        padded = jnp.pad(grid, ((0, 0), (1, 1), (1, 1), (0, 0)))
        grid = advance(padded, axial_speed)
        flattened = grid.reshape(NS, -1)
        filtered = jnp.zeros((NS, devices * slab_cells), grid.dtype).at[:, target].set(flattened)
        filtered = filtered.reshape(NS, devices, slab_cells).transpose(1, 0, 2)

        def per_device(device_index, current=state, values=filtered):
            return particle_section(current[device_index], values[device_index], relaxation[device_index], pairings[device_index], chem_input, chem_hidden, chem_output, react_slots[device_index], react_count[device_index])

        state, source = lax.map(per_device, jnp.arange(devices, dtype=jnp.int32))
        returned = source.transpose(1, 0, 2).reshape(NS, -1)
        grid = grid + jnp.take(returned, target, axis=1).reshape(grid.shape)
    flat_parts = state.reshape(devices, NS * NP, slab_cells)

    def pick(bundle, indices):
        return jnp.take(bundle, indices, axis=1, mode="fill", fill_value=0.0)

    departing = jax.vmap(pick)(flat_parts, leave_slots)
    departing = departing.reshape(devices, NS * NP, devices, CAPM).transpose(2, 1, 0, 3).reshape(devices, NS * NP, devices * CAPM)

    def settle(bundle, arrived, indices):
        return bundle.at[:, indices].set(arrived, mode="drop")

    relocated = jax.vmap(settle)(flat_parts, departing, arrive_slots)
    relocated = relocated.reshape(devices, NS, NP, slab_cells).transpose(1, 2, 0, 3).reshape(NS, NP, devices * slab_cells)
    return grid, relocated
```

```python
import functools

import jax
import jax.numpy as jnp
from jax import lax
from jax.experimental import pallas as pl
from jax.experimental.pallas import tpu as pltpu
from jax.sharding import PartitionSpec as P

SUBSTEPS = 2
DIFFUSION = 0.1
PAIR_WEIGHT = 0.4
LANES = 128
SUB = 8
BF = jnp.bfloat16
F32 = jnp.float32
I32 = jnp.int32

NT = (((1,), (1,)), ((), ()))
NN = (((1,), (0,)), ((), ()))


def call(body, outs, ins, smem=(), scratch=(), limit=40, name=None):
    specs = [
        pl.BlockSpec(memory_space=pltpu.SMEM if i in smem else pltpu.VMEM) for i in range(len(ins))
    ]
    return pl.pallas_call(
        body,
        out_shape=[jax.ShapeDtypeStruct(s, d) for s, d in outs],
        in_specs=specs,
        out_specs=[pl.BlockSpec(memory_space=pltpu.VMEM)] * len(outs),
        scratch_shapes=list(scratch),
        compiler_params=pltpu.CompilerParams(vmem_limit_bytes=limit << 20),
        name=name,
    )(*ins)


def dot(a, b, dims):
    return lax.dot_general(a, b, dims, preferred_element_type=F32)


def dot_split(x, onehot, dims):
    high = x.astype(BF)
    low = (x - high.astype(F32)).astype(BF)
    return dot(high, onehot, dims) + dot(low, onehot, dims)


def divisor(n, most):
    return max(k for k in range(1, most + 1) if n % k == 0)


def mix_in_place(q_ref, partner_ref):
    scalars, particles, cells = q_ref.shape
    groups = particles // SUB
    for t in range(cells // LANES):
        lanes = pl.ds(t * LANES, LANES)
        rows, homes = [], []
        for j in range(groups):
            index = partner_ref[pl.ds(j * SUB, SUB), lanes]
            rows.append(index & (SUB - 1))
            homes.append(index >> 3)

        def step(s, carry):
            x = [q_ref[s, pl.ds(k * SUB, SUB), lanes] for k in range(groups)]
            for j in range(groups):
                mate = jnp.take_along_axis(x[0], rows[j], axis=0)
                for k in range(1, groups):
                    other = jnp.take_along_axis(x[k], rows[j], axis=0)
                    mate = jnp.where(homes[j] == k, other, mate)
                q_ref[s, pl.ds(j * SUB, SUB), lanes] = x[j] + PAIR_WEIGHT * (mate - x[j])
            return carry

        lax.fori_loop(0, scalars, step, 0, unroll=2)


def store_tiles(ref, first, count, stride, value):
    slab = ref.shape[0] * LANES // value.shape[1]
    for t in range(value.shape[1] // LANES):
        at = pl.ds(t * slab + first, count, stride=stride)
        ref[at, :] = value[:, t * LANES : (t + 1) * LANES]


def load_tiles(ref, tiles, first, count, stride=1):
    slab = ref.shape[0] // tiles
    parts = [ref[pl.ds(t * slab + first, count, stride=stride), :] for t in range(tiles)]
    return jnp.concatenate(parts, axis=1)


def list_cells(q_ref, onehot, keep, a_ref, rows):
    scalars, particles, cells = q_ref.shape
    block = divisor(scalars, 8)

    def step(b, carry):
        s0 = b * block
        x = q_ref[pl.ds(s0, block), :, :].reshape(block * particles, cells)
        y = dot_split(x, onehot, NT) * keep
        for i in range(block):
            store_tiles(a_ref, s0 + i, particles, rows, y[i * particles : (i + 1) * particles])
        return carry

    lax.fori_loop(0, scalars // block, step, 0)
    for s in range(scalars, rows):
        store_tiles(a_ref, s, particles, rows, jnp.zeros((particles, onehot.shape[0]), F32))


def open_body(rows, p_ref, partner_ref, rate_ref, rcol_ref, q_ref, a_ref, ot_ref, rsel_ref):
    scalars, particles, cells = p_ref.shape
    onehot = (rcol_ref[...] == lax.broadcasted_iota(I32, ot_ref.shape, 1)).astype(F32).astype(BF)
    ot_ref[...] = onehot
    rate = jnp.broadcast_to(rate_ref[...], (SUB, cells))
    rsel_ref[...] = dot_split(rate, onehot, NT)

    def step(s, carry):
        q_ref[s] = p_ref[s]
        return carry

    lax.fori_loop(0, scalars, step, 0)
    mix_in_place(q_ref, partner_ref)
    list_cells(q_ref, ot_ref[...], 1.0 - rsel_ref[0:1, :], a_ref, rows)


def settle_state(q_ref, f_ref, r_ref, ot_ref, rate_ref, out_ref, rows):
    scalars, particles, cells = q_ref.shape
    tiles = cells // LANES
    block = divisor(scalars, 8)
    listed_tiles = ot_ref.shape[0] // LANES
    rate = rate_ref[...]
    keep = 1.0 - rate

    def step(b, carry):
        s0 = b * block
        r = jnp.concatenate(
            [load_tiles(r_ref, listed_tiles, s0 + i, particles, rows) for i in range(block)],
            axis=0,
        )
        spread = dot(r.astype(BF), ot_ref[...], NN)
        for i in range(block):
            f = jnp.concatenate(
                [f_ref[pl.ds((s0 + i) * tiles + t, 1), :] for t in range(tiles)], axis=1
            )
            out_ref[s0 + i] = (
                keep * q_ref[s0 + i] + rate * f + spread[i * particles : (i + 1) * particles]
            )
        return carry

    lax.fori_loop(0, scalars // block, step, 0)


def middle_body(
    rows, q_ref, f_ref, r_ref, ot_ref, rate_ref, rsel_ref, partner_ref, out_ref, a_ref
):
    settle_state(q_ref, f_ref, r_ref, ot_ref, rate_ref, out_ref, rows)
    mix_in_place(out_ref, partner_ref)
    list_cells(out_ref, ot_ref[...], 1.0 - rsel_ref[0:1, :], a_ref, rows)


def half_silu(y):
    return y + y * jnp.tanh(y)


def chem_body(
    particles, count_ref, f_ref, a_ref, ot_ref, rsel_ref, w1_ref, w2_ref, w3_ref, r_ref, s_ref
):
    tiles = ot_ref.shape[1] // LANES
    rows = f_ref.shape[0] // tiles
    listed = ot_ref.shape[0]
    f = jnp.concatenate([f_ref[pl.ds(t, rows, stride=tiles), :] for t in range(tiles)], axis=1)
    pull = rsel_ref[0:1, :] * dot_split(f, ot_ref[...], NT)
    live = lax.broadcasted_iota(I32, (1, listed), 1) < count_ref[0]
    group = divisor(particles, 2)

    def step(b, total):
        feed = jnp.concatenate(
            [
                (load_tiles(a_ref, listed // LANES, (b * group + i) * rows, rows) + pull).astype(BF)
                for i in range(group)
            ],
            axis=1,
        )
        one = half_silu(dot(w1_ref[...], feed, NN)).astype(BF)
        two = half_silu(dot(w2_ref[...], one, NN)).astype(BF)
        change = dot(w3_ref[...], two, NN).astype(BF).astype(F32)
        for i in range(group):
            r = jnp.where(live, change[:, i * listed : (i + 1) * listed], 0.0)
            store_tiles(r_ref, (b * group + i) * rows, rows, 1, r)
            total = total + r
        return total

    total = lax.fori_loop(0, particles // group, step, jnp.zeros((rows, listed), F32))
    source = dot_split(total * (1.0 / particles), ot_ref[...], NN)
    for t in range(tiles):
        s_ref[pl.ds(t, rows, stride=tiles), :] = source[:, t * LANES : (t + 1) * LANES]


def close_body(
    rows, span, q_ref, f_ref, r_ref, ot_ref, rate_ref, lcol_ref, out_ref, leave_ref
):
    settle_state(q_ref, f_ref, r_ref, ot_ref, rate_ref, out_ref, rows)
    scalars, particles, cells = q_ref.shape
    places = lcol_ref.shape[0]
    onehot = (lcol_ref[...] == lax.broadcasted_iota(I32, (places, cells), 1)).astype(F32).astype(BF)
    per = LANES // particles

    def pick(s0, count):
        x = out_ref[pl.ds(s0, count), :, :].reshape(count * particles, cells)
        high = x.astype(BF)
        low = (x - high.astype(F32)).astype(BF)
        return dot(onehot, high, NT) + dot(onehot, low, NT)

    def step(b, carry):
        leave_ref[pl.ds(b, places, stride=span), :] = pick(b * per, per)
        return carry

    whole = scalars // per
    lax.fori_loop(0, whole, step, 0)
    left = scalars - whole * per
    zeros = jnp.zeros((places, LANES), F32)
    for b in range(whole, span):
        if b == whole and left:
            part = jnp.concatenate(
                [pick(b * per, left), zeros[:, left * particles :]], axis=1
            )
            leave_ref[pl.ds(b, places, stride=span), :] = part
        else:
            leave_ref[pl.ds(b, places, stride=span), :] = zeros


def arrive_body(span, p_ref, arr_ref, acol_ref, out_ref):
    scalars, particles, cells = p_ref.shape
    places = acol_ref.shape[0]
    hit = (acol_ref[...] == lax.broadcasted_iota(I32, (places, cells), 1)).astype(F32)
    taken = jnp.sum(hit, axis=0, keepdims=True) > 0.5
    onehot = hit.astype(BF)
    per = LANES // particles

    def place(b, count):
        x = arr_ref[pl.ds(b, places, stride=span), :].T
        y = dot_split(x, onehot, NN)
        for i in range(count):
            s = b * per + i
            out_ref[s] = jnp.where(taken, y[i * particles : (i + 1) * particles], p_ref[s])

    whole = scalars // per

    def step(b, carry):
        place(b, per)
        return carry

    lax.fori_loop(0, whole, step, 0)
    if scalars > whole * per:
        place(whole, scalars - whole * per)


def stencil(value, speed, bx, by, lanes_y):
    boxes = value[0].shape[0]
    row = lax.broadcasted_iota(I32, value[0].shape, 0) % lanes_y
    zero = jnp.zeros((lanes_y, LANES), F32)

    def x_low(v):
        return jnp.concatenate([zero, v[: boxes - lanes_y]], axis=0)

    def x_high(v):
        return jnp.concatenate([v[lanes_y:], zero], axis=0)

    def y_low(v):
        return jnp.where(row == 0, 0.0, pltpu.roll(v, 1, 0))

    def y_high(v):
        return jnp.where(row == lanes_y - 1, 0.0, pltpu.roll(v, boxes - 1, 0))

    out = []
    for i in range(bx):
        for j in range(by):
            c = value[i * by + j]
            up = value[(i - 1) * by + j] if i else x_low(value[(bx - 1) * by + j])
            down = value[(i + 1) * by + j] if i < bx - 1 else x_high(value[j])
            left = value[i * by + j - 1] if j else y_low(value[i * by + by - 1])
            right = value[i * by + j + 1] if j < by - 1 else y_high(value[i * by])
            beside = up + down + left + right + pltpu.roll(c, 1, 1) + pltpu.roll(c, LANES - 1, 1)
            out.append(c + DIFFUSION * (beside - 6.0 * c) - speed[i * by + j] * (c - up))
    return out


def route(src_ref, first_row, row_step, item_step, items, own, quads, lanes_y, rows, lanes):
    shape = (lanes_y, LANES)
    out = [[jnp.zeros(shape, F32) for _ in rows] for _ in range(own)]

    def step(y, out):
        out = [list(o) for o in out]
        for j in range(items):
            hits = [r == (j * lanes_y + y) for r in rows]
            for s in range(own):
                line = src_ref[pl.ds(first_row + y * row_step + s * quads + j * item_step, 1), :]
                line = jnp.broadcast_to(line, shape)
                for k in range(len(rows)):
                    out[s][k] = jnp.where(
                        hits[k], jnp.take_along_axis(line, lanes[k], axis=1), out[s][k]
                    )
        return tuple(tuple(o) for o in out)

    return lax.fori_loop(0, lanes_y, step, tuple(tuple(o) for o in out), unroll=2)


def load_rows(ref, offset, stride, count):
    return ref[pl.ds(offset, count, stride=stride), :]


def start_body(dims, arr_ref, g_ref, f_ref, inv_ref, lab_ref):
    nx, ny, own, bx, by = dims
    quads = bx * by
    boxes = nx * ny
    width = own * quads
    stride = width + 2 * quads
    turns = quads * ny
    speed = [load_rows(arr_ref, width + quads + j, stride, boxes) for j in range(quads)]
    for s in range(own):
        value = [load_rows(arr_ref, s * quads + j, stride, boxes) for j in range(quads)]
        for j, v in enumerate(stencil(value, speed, bx, by, ny)):
            g_ref[pl.ds(s * quads + j, boxes, stride=width), :] = v
    for j in range(quads):
        lab_ref[pl.ds(j * boxes, boxes), :] = load_rows(arr_ref, width + j, stride, boxes).astype(
            I32
        )
    lane_of = lax.broadcasted_iota(I32, (turns, LANES), 1).astype(F32)
    sub_of = lax.broadcasted_iota(I32, (turns, LANES), 0)
    sub_lane = lax.broadcasted_iota(I32, (LANES, LANES), 0)

    def group(x, carry):
        def gather(y, acc):
            left, right = [], []
            for j in range(quads):
                line = lab_ref[pl.ds(j * boxes + x * ny + y, 1), :]
                hit = jnp.broadcast_to(line >> 7, (turns, LANES)) == sub_of
                code = (j * ny + y).astype(F32)
                left.append(
                    jnp.concatenate(
                        [jnp.where(hit, code, 0.0), jnp.where(hit, lane_of, 0.0)], axis=0
                    ).astype(BF)
                )
                right.append(
                    (jnp.broadcast_to(line & (LANES - 1), (LANES, LANES)) == sub_lane)
                    .astype(F32)
                    .astype(BF)
                )
            return acc + dot(
                jnp.concatenate(left, axis=1), jnp.concatenate(right, axis=1), NT
            )

        code = lax.fori_loop(0, ny, gather, jnp.zeros((2 * turns, LANES), F32), unroll=2)
        code = code.astype(I32)
        inv_ref[pl.ds(x * 2 * turns, 2 * turns), :] = code
        return carry

    lax.fori_loop(0, nx, group, 0)
    send_filtered(dims, g_ref, inv_ref, f_ref)


def send_filtered(dims, g_ref, inv_ref, f_ref):
    nx, ny, own, bx, by = dims
    quads = bx * by
    width = own * quads
    turns = quads * ny

    def group(x, carry):
        base = x * 2 * turns
        rows = [inv_ref[pl.ds(base + k * ny, ny), :] for k in range(quads)]
        lanes = [inv_ref[pl.ds(base + turns + k * ny, ny), :] for k in range(quads)]
        out = route(g_ref, x * ny * width, width, 1, quads, own, quads, ny, rows, lanes)
        for s in range(own):
            for k in range(quads):
                f_ref[pl.ds(x * ny * width + s * quads + k, ny, stride=width), :] = out[s][k]
        return carry

    lax.fori_loop(0, nx, group, 0)


def add_source(dims, s_ref, g_ref, lab_ref, out_ref):
    nx, ny, own, bx, by = dims
    quads = bx * by
    boxes = nx * ny
    width = own * quads

    def group(x, carry):
        labels = [lab_ref[pl.ds(j * boxes + x * ny, ny), :] for j in range(quads)]
        rows = [v >> 7 for v in labels]
        lanes = [v & (LANES - 1) for v in labels]
        out = route(s_ref, x * ny * width, width, 1, quads, own, quads, ny, rows, lanes)
        for s in range(own):
            for k in range(quads):
                at = pl.ds(x * ny * width + s * quads + k, ny, stride=width)
                out_ref[at, :] = g_ref[at, :] + out[s][k]
        return carry

    lax.fori_loop(0, nx, group, 0)


def again_body(dims, s_ref, g_ref, arr_ref, inv_ref, lab_ref, out_ref, f_ref, mid_ref):
    nx, ny, own, bx, by = dims
    quads = bx * by
    boxes = nx * ny
    width = own * quads
    stride = width + 2 * quads
    add_source(dims, s_ref, g_ref, lab_ref, mid_ref)
    speed = [load_rows(arr_ref, width + quads + j, stride, boxes) for j in range(quads)]
    for s in range(own):
        value = [load_rows(mid_ref, s * quads + j, width, boxes) for j in range(quads)]
        for j, v in enumerate(stencil(value, speed, bx, by, ny)):
            out_ref[pl.ds(s * quads + j, boxes, stride=width), :] = v
    send_filtered(dims, out_ref, inv_ref, f_ref)


def last_body(dims, s_ref, g_ref, lab_ref, out_ref):
    add_source(dims, s_ref, g_ref, lab_ref, out_ref)


def per_device(
    grid_scalars,
    axial_speed,
    particles,
    cell_owner,
    cell_slot,
    mix_rate,
    partner,
    chem_input,
    chem_hidden,
    chem_output,
    react_slots,
    react_count,
    leave_slots,
    arrive_slots,
):
    both = ("gx", "gy")
    nx, ny = lax.axis_size("gx"), lax.axis_size("gy")
    devices = nx * ny
    scalars, bx, by, nz = grid_scalars.shape
    heads, cells = partner.shape
    listed = react_slots.shape[1]
    hidden = chem_hidden.shape[0]
    quads = bx * by
    own = -(-scalars // devices)
    rows = devices * own
    width = own * quads
    tiles = cells // LANES
    assert nz == LANES and tiles == quads and heads % SUB == 0 and LANES % heads == 0
    dims = (nx, ny, own, bx, by)
    flat = devices * width

    label = ((cell_slot // LANES) * ny + cell_owner) * LANES + cell_slot % LANES
    padded = jnp.pad(grid_scalars, ((0, rows - scalars), (0, 0), (0, 0), (0, 0)))
    first = jnp.concatenate(
        [
            padded.reshape(devices, width, LANES),
            jnp.broadcast_to(label.astype(F32).reshape(1, quads, LANES), (devices, quads, LANES)),
            jnp.broadcast_to(axial_speed.reshape(1, quads, LANES), (devices, quads, LANES)),
        ],
        axis=1,
    )

    def exchange(x):
        x = x.reshape(devices, -1, LANES)
        return lax.all_to_all(x, both, split_axis=0, concat_axis=0, tiled=True).reshape(-1, LANES)

    arrival = exchange(first)

    rate = mix_rate.reshape(1, cells)
    rcol = react_slots.reshape(listed, 1)
    lcol = leave_slots.reshape(-1, 1)
    acol = arrive_slots.reshape(-1, 1)
    w1 = jnp.pad(chem_input, ((0, 0), (0, rows - scalars))) * jnp.asarray(0.5, BF)
    w2 = chem_hidden * jnp.asarray(0.5, BF)
    w3 = jnp.pad(chem_output, ((0, rows - scalars), (0, 0)))

    state_shape = (scalars, heads, cells)
    q, a, ot, rsel = call(
        functools.partial(open_body, rows),
        [
            (state_shape, F32),
            ((listed // LANES * heads * rows, LANES), F32),
            ((listed, cells), BF),
            ((SUB, listed), F32),
        ],
        [particles, partner, rate, rcol],
        name="open",
    )
    grid, sent, inv, lab = call(
        functools.partial(start_body, dims),
        [
            ((flat, LANES), F32),
            ((flat, LANES), F32),
            ((nx * 2 * quads * ny, LANES), I32),
            ((quads * devices, LANES), I32),
        ],
        [arrival],
        name="start",
    )

    def chemistry(f, a):
        return call(
            functools.partial(chem_body, heads),
            [((listed // LANES * heads * rows, LANES), F32), ((flat, LANES), F32)],
            [react_count, f, a, ot, rsel, w1, w2, w3],
            smem=(0,),
            name="chem",
        )

    for substep in range(SUBSTEPS):
        f = exchange(sent)
        change, source = chemistry(f, a)
        home = exchange(source)
        if substep < SUBSTEPS - 1:
            q, a = call(
                functools.partial(middle_body, rows),
                [(state_shape, F32), ((listed // LANES * heads * rows, LANES), F32)],
                [q, f, change, ot, rate, rsel, partner],
                name="middle",
            )
            grid, sent = call(
                functools.partial(again_body, dims),
                [((flat, LANES), F32), ((flat, LANES), F32)],
                [home, grid, arrival, inv, lab],
                scratch=[pltpu.VMEM((flat, LANES), F32)],
                name="again",
            )
    per = LANES // heads
    span = SUB * (-(-scalars // (per * SUB)))
    places = leave_slots.shape[1]
    state, leaving = call(
        functools.partial(close_body, rows, span),
        [(state_shape, F32), ((places * span, LANES), F32)],
        [q, f, change, ot, rate, lcol],
        name="close",
    )
    (grid,) = call(
        functools.partial(last_body, dims), [((flat, LANES), F32)], [home, grid, lab], name="last"
    )
    moved = exchange(leaving)
    grid_out = exchange(grid).reshape(rows, bx, by, nz)[:scalars]
    (state,) = call(
        functools.partial(arrive_body, span), [(state_shape, F32)], [state, moved, acol], name="arrive"
    )
    return (grid_out, state)


def solution(mesh):
    placed = (
        P(None, "gx", "gy", None),
        P("gx", "gy", None),
        P(None, None, ("gx", "gy")),
        P("gx", "gy", None),
        P("gx", "gy", None),
        P(("gx", "gy")),
        P(None, ("gx", "gy")),
        P(),
        P(),
        P(),
        P(("gx", "gy"), None),
        P(("gx", "gy")),
        P(("gx", "gy"), None),
        P(("gx", "gy"), None),
    )
    return jax.shard_map(
        per_device,
        mesh=mesh,
        in_specs=placed,
        out_specs=(P(None, "gx", "gy", None), P(None, None, ("gx", "gy"))),
        check_vma=False,
    )
```

```python
import functools

import jax
import jax.numpy as jnp
from jax import lax
from jax.experimental import pallas as pl
from jax.experimental.pallas import tpu as pltpu
from jax.sharding import PartitionSpec as P

SUBSTEPS = 2
DIFFUSION = 0.1
PAIR_WEIGHT = 0.4
LANES = 128
SUB = 8
BF = jnp.bfloat16
F32 = jnp.float32
I32 = jnp.int32

NT = (((1,), (1,)), ((), ()))
NN = (((1,), (0,)), ((), ()))


def call(body, outs, ins, smem=(), scratch=(), limit=16, name=None, steps=None, blocks=None):
    blocks = blocks or {}

    def spec(i, shape):
        if i in smem:
            return pl.BlockSpec(memory_space=pltpu.SMEM)
        if steps is None:
            return pl.BlockSpec(memory_space=pltpu.VMEM)
        if i in blocks:
            return pl.BlockSpec(*blocks[i])
        return pl.BlockSpec(shape, lambda *_: (0,) * len(shape))

    grid = {} if steps is None else {"grid": (steps,)}
    return pl.pallas_call(
        body,
        out_shape=[
            pltpu.HBM(o[0], o[1]) if len(o) > 2 else jax.ShapeDtypeStruct(o[0], o[1]) for o in outs
        ],
        in_specs=[spec(i, x.shape) for i, x in enumerate(ins)],
        out_specs=[spec(len(ins) + i, o[0]) for i, o in enumerate(outs)],
        scratch_shapes=list(scratch),
        compiler_params=pltpu.CompilerParams(vmem_limit_bytes=limit << 20),
        name=name,
        **grid,
    )(*ins)


def far(x):
    return pltpu.with_memory_space_constraint(x, pltpu.HBM)


def dot(a, b, dims):
    return lax.dot_general(a, b, dims, preferred_element_type=F32)


def dot_split(x, onehot, dims):
    high = x.astype(BF)
    low = (x - high.astype(F32)).astype(BF)
    return dot(high, onehot, dims) + dot(low, onehot, dims)


def divisor(n, most):
    return max(k for k in range(1, most + 1) if n % k == 0)


def mix(p_ref, partner_ref, q_ref):
    scalars, particles, cells = p_ref.shape
    groups = particles // SUB
    for t in range(cells // LANES):
        lanes = pl.ds(t * LANES, LANES)
        rows, homes = [], []
        for j in range(groups):
            index = partner_ref[pl.ds(j * SUB, SUB), lanes]
            rows.append(index & (SUB - 1))
            homes.append(index >> 3)

        def step(s, carry):
            x = [p_ref[s, pl.ds(k * SUB, SUB), lanes] for k in range(groups)]
            for j in range(groups):
                mate = jnp.take_along_axis(x[0], rows[j], axis=0)
                for k in range(1, groups):
                    other = jnp.take_along_axis(x[k], rows[j], axis=0)
                    mate = jnp.where(homes[j] == k, other, mate)
                q_ref[s, pl.ds(j * SUB, SUB), lanes] = x[j] + PAIR_WEIGHT * (mate - x[j])
            return carry

        lax.fori_loop(0, scalars, step, 0, unroll=2)


def store_tiles(ref, at, value):
    for t in range(value.shape[1] // LANES):
        ref[t, at, :] = value[:, t * LANES : (t + 1) * LANES]


def load_tiles(ref, at):
    return jnp.concatenate([ref[t, at, :] for t in range(ref.shape[0])], axis=1)


def list_cells(s0, q_ref, onehot, keep, a_ref, rows):
    block, particles, cells = q_ref.shape
    y = dot_split(q_ref[...].reshape(block * particles, cells), onehot, NT) * keep
    for i in range(block):
        at = pl.ds(s0 + i, particles, stride=rows)
        store_tiles(a_ref, at, y[i * particles : (i + 1) * particles])


def clear_rest(scalars, rows, a_ref):
    particles = a_ref.shape[1] // rows
    zeros = jnp.zeros((particles, a_ref.shape[0] * LANES), F32)
    for s in range(scalars, rows):
        store_tiles(a_ref, pl.ds(s, particles, stride=rows), zeros)


def open_body(
    scalars, rows, p_ref, partner_ref, rate_ref, rcol_ref, q_ref, a_ref, ot_ref, rsel_ref
):
    block, particles, cells = p_ref.shape

    @pl.when(pl.program_id(0) == 0)
    def _():
        onehot = (rcol_ref[...] == lax.broadcasted_iota(I32, ot_ref.shape, 1)).astype(F32)
        ot_ref[...] = onehot.astype(BF)
        rate = jnp.broadcast_to(rate_ref[...], (SUB, cells))
        rsel_ref[...] = dot_split(rate, onehot.astype(BF), NT)
        clear_rest(scalars, rows, a_ref)

    mix(p_ref, partner_ref, q_ref)
    s0 = pl.program_id(0) * block
    list_cells(s0, q_ref, ot_ref[...], 1.0 - rsel_ref[0:1, :], a_ref, rows)


def settle_state(s0, q_ref, f_ref, r_ref, ot_ref, rate_ref, out_ref, rows):
    block, particles, cells = q_ref.shape
    tiles = cells // LANES
    rate = rate_ref[...]
    keep = 1.0 - rate
    r = jnp.concatenate(
        [load_tiles(r_ref, pl.ds(s0 + i, particles, stride=rows)) for i in range(block)], axis=0
    )
    spread = dot(r.astype(BF), ot_ref[...], NN)
    for i in range(block):
        f = jnp.concatenate(
            [f_ref[pl.ds((s0 + i) * tiles + t, 1), :] for t in range(tiles)], axis=1
        )
        out_ref[i] = keep * q_ref[i] + rate * f + spread[i * particles : (i + 1) * particles]


def middle_body(
    scalars,
    rows,
    q_ref,
    f_ref,
    r_ref,
    ot_ref,
    rate_ref,
    rsel_ref,
    partner_ref,
    out_ref,
    a_ref,
    token_ref,
    now_ref,
):
    @pl.when(pl.program_id(0) == 0)
    def _():
        clear_rest(scalars, rows, a_ref)
        token_ref[...] = rsel_ref[:, :LANES]

    s0 = pl.program_id(0) * q_ref.shape[0]
    settle_state(s0, q_ref, f_ref, r_ref, ot_ref, rate_ref, now_ref, rows)
    mix(now_ref, partner_ref, out_ref)
    list_cells(s0, out_ref, ot_ref[...], 1.0 - rsel_ref[0:1, :], a_ref, rows)


def half_silu(y):
    return y + y * jnp.tanh(y)


def chem_body(
    particles,
    count_ref,
    f_ref,
    a_ref,
    ot_ref,
    rsel_ref,
    w1_ref,
    w2_ref,
    w3_ref,
    token_ref,
    r_ref,
    s_ref,
    pull_ref,
    total_ref,
):
    tiles = ot_ref.shape[1] // LANES
    rows = f_ref.shape[0] // tiles
    listed = ot_ref.shape[0]

    @pl.when(pl.program_id(0) == 0)
    def _():
        f = jnp.concatenate([f_ref[pl.ds(t, rows, stride=tiles), :] for t in range(tiles)], axis=1)
        pull_ref[...] = rsel_ref[0:1, :] * dot_split(f, ot_ref[...], NT)
        total_ref[...] = jnp.zeros_like(total_ref)

    live = lax.broadcasted_iota(I32, (1, listed), 1) < count_ref[0]
    group = divisor(a_ref.shape[1] // rows, 2)

    def step(b, total):
        pull = pull_ref[...]
        at = [pl.ds((b * group + i) * rows, rows) for i in range(group)]
        feed = jnp.concatenate([(load_tiles(a_ref, k) + pull).astype(BF) for k in at], axis=1)
        one = half_silu(dot(w1_ref[...], feed, NN)).astype(BF)
        two = half_silu(dot(w2_ref[...], one, NN)).astype(BF)
        change = dot(w3_ref[...], two, NN).astype(BF).astype(F32)
        for i, k in enumerate(at):
            r = jnp.where(live, change[:, i * listed : (i + 1) * listed], 0.0)
            store_tiles(r_ref, k, r)
            total = total + r
        return total

    total = lax.fori_loop(0, a_ref.shape[1] // (rows * group), step, total_ref[...])
    total_ref[...] = total

    @pl.when(pl.program_id(0) == pl.num_programs(0) - 1)
    def _():
        source = dot_split(total * (1.0 / particles), ot_ref[...], NN)
        for t in range(tiles):
            s_ref[pl.ds(t, rows, stride=tiles), :] = source[:, t * LANES : (t + 1) * LANES]


def cell_onehot(col_ref, cells):
    shape = (col_ref.shape[0], cells)
    return (col_ref[...] == lax.broadcasted_iota(I32, shape, 1)).astype(F32).astype(BF)


def split_dot(onehot, x, dims):
    high = x.astype(BF)
    low = (x - high.astype(F32)).astype(BF)
    return dot(onehot, high, dims) + dot(onehot, low, dims)


def leave_blocks(scalars, particles, span, store, part):
    per = LANES // particles

    def step(b, carry):
        store(b, part(b * per, per))
        return carry

    whole = scalars // per
    lax.fori_loop(0, whole, step, 0)
    left = scalars - whole * per
    for b in range(whole, span):
        if b == whole and left:
            value = part(b * per, left)
            zeros = jnp.zeros((value.shape[0], LANES - left * particles), F32)
            store(b, jnp.concatenate([value, zeros], axis=1))
        else:
            store(b, None)


def base_body(span, q_ref, rate_ref, lcol_ref, out_ref, token_ref):
    scalars, particles, cells = q_ref.shape
    onehot = cell_onehot(lcol_ref, cells)
    keep = 1.0 - rate_ref[...]

    def part(s0, count):
        x = q_ref[pl.ds(s0, count), :, :].reshape(count * particles, cells) * keep
        return split_dot(onehot, x, NT)

    def store(b, value):
        if value is not None:
            out_ref[pl.ds(b, lcol_ref.shape[0], stride=span), :] = value

    leave_blocks(scalars, particles, span, store, part)
    token_ref[...] = keep[:, :LANES]


def leave_body(
    rows,
    span,
    scalars,
    particles,
    devices,
    base_ref,
    f_ref,
    r_ref,
    rate_ref,
    lcol_ref,
    rrow_ref,
    source_ref,
    out_ref,
):
    width = source_ref.shape[0] // devices
    stride = out_ref.shape[0] // devices
    for d in range(devices):
        out_ref[d * stride : d * stride + width] = source_ref[d * width : (d + 1) * width]
    cells = rate_ref.shape[1]
    tiles = cells // LANES
    places = lcol_ref.shape[0]
    f = jnp.concatenate([f_ref[pl.ds(t, rows, stride=tiles), :] for t in range(tiles)], axis=1)
    pull = split_dot(cell_onehot(lcol_ref, cells), f * rate_ref[...], NT)
    reacts = (lcol_ref[...] == rrow_ref[...]).astype(F32).astype(BF)

    def part(s0, count):
        wide = count * particles
        r = jnp.concatenate(
            [load_tiles(r_ref, pl.ds(s0 + i, particles, stride=rows)) for i in range(count)], axis=0
        )
        of = lax.broadcasted_iota(I32, (rows, wide), 1) // particles + s0
        mine = (of == lax.broadcasted_iota(I32, (rows, wide), 0)).astype(F32).astype(BF)
        at = pl.ds(s0 * particles // LANES, places, stride=span)
        return base_ref[at, :][:, :wide] + dot_split(pull, mine, NN) + dot(reacts, r.astype(BF), NT)

    def store(b, value):
        for c in range(places // devices):
            at = pl.ds(width + c * span + b, devices, stride=stride)
            if value is None:
                out_ref[at, :] = jnp.zeros((devices, LANES), F32)
            else:
                out_ref[at, :] = value[c * devices : (c + 1) * devices]

    leave_blocks(scalars, particles, span, store, part)


def settle_body(rows, q_ref, f_ref, r_ref, ot_ref, rate_ref, out_ref):
    s0 = pl.program_id(0) * q_ref.shape[0]
    settle_state(s0, q_ref, f_ref, r_ref, ot_ref, rate_ref, out_ref, rows)


def arrive_body(span, devices, p_ref, arr_ref, acol_ref, out_ref, hit_ref, taken_ref):
    per, particles, cells = p_ref.shape
    places = acol_ref.shape[0]
    b = pl.program_id(0)

    @pl.when(b == 0)
    def _():
        hit = (acol_ref[...] == lax.broadcasted_iota(I32, (places, cells), 1)).astype(F32)
        hit_ref[...] = hit.astype(BF)
        taken_ref[...] = jnp.broadcast_to(jnp.sum(hit, axis=0, keepdims=True), taken_ref.shape)

    stride = arr_ref.shape[0] // devices
    count = places // devices
    first = stride - count * span + b
    x = jnp.concatenate(
        [arr_ref[pl.ds(first + c * span, devices, stride=stride), :] for c in range(count)], axis=0
    ).T
    y = dot_split(x, hit_ref[...], NN)
    taken = taken_ref[0:1, :] > 0.5
    for i in range(per):
        out_ref[i] = jnp.where(taken, y[i * particles : (i + 1) * particles], p_ref[i])


def stencil(value, speed, bx, by, lanes_y):
    boxes = value[0].shape[0]
    row = lax.broadcasted_iota(I32, value[0].shape, 0) % lanes_y
    zero = jnp.zeros((lanes_y, LANES), F32)

    def x_low(v):
        return jnp.concatenate([zero, v[: boxes - lanes_y]], axis=0)

    def x_high(v):
        return jnp.concatenate([v[lanes_y:], zero], axis=0)

    def y_low(v):
        return jnp.where(row == 0, 0.0, pltpu.roll(v, 1, 0))

    def y_high(v):
        return jnp.where(row == lanes_y - 1, 0.0, pltpu.roll(v, boxes - 1, 0))

    out = []
    for i in range(bx):
        for j in range(by):
            c = value[i * by + j]
            up = value[(i - 1) * by + j] if i else x_low(value[(bx - 1) * by + j])
            down = value[(i + 1) * by + j] if i < bx - 1 else x_high(value[j])
            left = value[i * by + j - 1] if j else y_low(value[i * by + by - 1])
            right = value[i * by + j + 1] if j < by - 1 else y_high(value[i * by])
            beside = up + down + left + right + pltpu.roll(c, 1, 1) + pltpu.roll(c, LANES - 1, 1)
            out.append(c + DIFFUSION * (beside - 6.0 * c) - speed[i * by + j] * (c - up))
    return out


def route(src_ref, first_row, row_step, item_step, items, own, quads, lanes_y, rows, lanes):
    shape = (lanes_y, LANES)
    out = [[jnp.zeros(shape, F32) for _ in rows] for _ in range(own)]

    def step(y, out):
        out = [list(o) for o in out]
        for j in range(items):
            hits = [r == (j * lanes_y + y) for r in rows]
            for s in range(own):
                line = src_ref[pl.ds(first_row + y * row_step + s * quads + j * item_step, 1), :]
                line = jnp.broadcast_to(line, shape)
                for k in range(len(rows)):
                    out[s][k] = jnp.where(
                        hits[k], jnp.take_along_axis(line, lanes[k], axis=1), out[s][k]
                    )
        return tuple(tuple(o) for o in out)

    return lax.fori_loop(0, lanes_y, step, tuple(tuple(o) for o in out), unroll=2)


def load_rows(ref, offset, stride, count):
    return ref[pl.ds(offset, count, stride=stride), :]


def pack_body(width, grid_ref, owner_ref, slot_ref, speed_ref, lanes_y, out_ref):
    quads = owner_ref.shape[0]
    stride = width + 2 * quads
    total = grid_ref.shape[0]
    slot = slot_ref[...]
    label = ((slot >> 7) * lanes_y + owner_ref[...]) * LANES + (slot & (LANES - 1))
    tail = jnp.concatenate([label.astype(F32), speed_ref[...]], axis=0)
    for d in range(out_ref.shape[0] // stride):
        count = max(0, min(width, total - d * width))
        if count:
            out_ref[d * stride : d * stride + count] = grid_ref[d * width : d * width + count]
        if count < width:
            zeros = jnp.zeros((width - count, LANES), F32)
            out_ref[d * stride + count : d * stride + width] = zeros
        out_ref[d * stride + width : (d + 1) * stride] = tail


def start_body(dims, arr_ref, token_ref, g_ref, f_ref, inv_ref, lab_ref):
    nx, ny, own, bx, by = dims
    quads = bx * by
    boxes = nx * ny
    width = own * quads
    stride = width + 2 * quads
    turns = quads * ny
    speed = [load_rows(arr_ref, width + quads + j, stride, boxes) for j in range(quads)]
    for s in range(own):
        value = [load_rows(arr_ref, s * quads + j, stride, boxes) for j in range(quads)]
        for j, v in enumerate(stencil(value, speed, bx, by, ny)):
            g_ref[pl.ds(s * quads + j, boxes, stride=width), :] = v
    for j in range(quads):
        lab_ref[pl.ds(j * boxes, boxes), :] = load_rows(arr_ref, width + j, stride, boxes).astype(
            I32
        )
    lane_of = lax.broadcasted_iota(I32, (turns, LANES), 1).astype(F32)
    sub_of = lax.broadcasted_iota(I32, (turns, LANES), 0)
    sub_lane = lax.broadcasted_iota(I32, (LANES, LANES), 0)

    def group(x, carry):
        def gather(y, acc):
            left, right = [], []
            for j in range(quads):
                line = lab_ref[pl.ds(j * boxes + x * ny + y, 1), :]
                hit = jnp.broadcast_to(line >> 7, (turns, LANES)) == sub_of
                code = (j * ny + y).astype(F32)
                left.append(
                    jnp.concatenate(
                        [jnp.where(hit, code, 0.0), jnp.where(hit, lane_of, 0.0)], axis=0
                    ).astype(BF)
                )
                right.append(
                    (jnp.broadcast_to(line & (LANES - 1), (LANES, LANES)) == sub_lane)
                    .astype(F32)
                    .astype(BF)
                )
            return acc + dot(
                jnp.concatenate(left, axis=1), jnp.concatenate(right, axis=1), NT
            )

        code = lax.fori_loop(0, ny, gather, jnp.zeros((2 * turns, LANES), F32), unroll=2)
        code = code.astype(I32)
        inv_ref[pl.ds(x * 2 * turns, 2 * turns), :] = code
        return carry

    lax.fori_loop(0, nx, group, 0)
    send_filtered(dims, g_ref, inv_ref, f_ref)


def send_filtered(dims, g_ref, inv_ref, f_ref):
    nx, ny, own, bx, by = dims
    quads = bx * by
    width = own * quads
    turns = quads * ny

    def group(x, carry):
        base = x * 2 * turns
        rows = [inv_ref[pl.ds(base + k * ny, ny), :] for k in range(quads)]
        lanes = [inv_ref[pl.ds(base + turns + k * ny, ny), :] for k in range(quads)]
        out = route(g_ref, x * ny * width, width, 1, quads, own, quads, ny, rows, lanes)
        for s in range(own):
            for k in range(quads):
                f_ref[pl.ds(x * ny * width + s * quads + k, ny, stride=width), :] = out[s][k]
        return carry

    lax.fori_loop(0, nx, group, 0)


def add_source(dims, s_ref, g_ref, lab_ref, out_ref):
    nx, ny, own, bx, by = dims
    quads = bx * by
    boxes = nx * ny
    width = own * quads
    stride = s_ref.shape[0] // boxes

    def group(x, carry):
        labels = [lab_ref[pl.ds(j * boxes + x * ny, ny), :] for j in range(quads)]
        rows = [v >> 7 for v in labels]
        lanes = [v & (LANES - 1) for v in labels]
        out = route(s_ref, x * ny * stride, stride, 1, quads, own, quads, ny, rows, lanes)
        for s in range(own):
            for k in range(quads):
                at = pl.ds(x * ny * width + s * quads + k, ny, stride=width)
                out_ref[at, :] = g_ref[at, :] + out[s][k]
        return carry

    lax.fori_loop(0, nx, group, 0)


def again_body(dims, s_ref, g_ref, arr_ref, inv_ref, lab_ref, token_ref, out_ref, f_ref, mid_ref):
    nx, ny, own, bx, by = dims
    quads = bx * by
    boxes = nx * ny
    width = own * quads
    stride = width + 2 * quads
    add_source(dims, s_ref, g_ref, lab_ref, mid_ref)
    speed = [load_rows(arr_ref, width + quads + j, stride, boxes) for j in range(quads)]
    for s in range(own):
        value = [load_rows(mid_ref, s * quads + j, width, boxes) for j in range(quads)]
        for j, v in enumerate(stencil(value, speed, bx, by, ny)):
            out_ref[pl.ds(s * quads + j, boxes, stride=width), :] = v
    send_filtered(dims, out_ref, inv_ref, f_ref)


def last_body(dims, s_ref, g_ref, lab_ref, out_ref):
    add_source(dims, s_ref, g_ref, lab_ref, out_ref)


def per_device(
    grid_scalars,
    axial_speed,
    particles,
    cell_owner,
    cell_slot,
    mix_rate,
    partner,
    chem_input,
    chem_hidden,
    chem_output,
    react_slots,
    react_count,
    leave_slots,
    arrive_slots,
):
    both = ("gx", "gy")
    nx, ny = lax.axis_size("gx"), lax.axis_size("gy")
    devices = nx * ny
    scalars, bx, by, nz = grid_scalars.shape
    heads, cells = partner.shape
    listed = react_slots.shape[1]
    hidden = chem_hidden.shape[0]
    quads = bx * by
    own = -(-scalars // devices)
    rows = devices * own
    width = own * quads
    tiles = cells // LANES
    assert nz == LANES and tiles == quads and heads % SUB == 0 and LANES % heads == 0
    dims = (nx, ny, own, bx, by)
    flat = devices * width

    (first,) = call(
        lambda g, o, c, u, out: pack_body(width, g, o, c, u, ny, out),
        [((devices * (width + 2 * quads), LANES), F32)],
        [
            grid_scalars.reshape(-1, LANES),
            cell_owner.reshape(quads, LANES),
            cell_slot.reshape(quads, LANES),
            axial_speed.reshape(quads, LANES),
        ],
        name="pack",
    )

    def exchange(x):
        x = x.reshape(devices, -1, LANES)
        return lax.all_to_all(x, both, split_axis=0, concat_axis=0, tiled=True).reshape(-1, LANES)

    arrival = exchange(first)

    rate = mix_rate.reshape(1, cells)
    rcol = react_slots.reshape(listed, 1)
    lcol = leave_slots.reshape(devices, -1).T.reshape(-1, 1)
    acol = arrive_slots.reshape(devices, -1).T.reshape(-1, 1)
    w1 = jnp.pad(chem_input, ((0, 0), (0, rows - scalars))) * jnp.asarray(0.5, BF)
    w2 = chem_hidden * jnp.asarray(0.5, BF)
    w3 = jnp.pad(chem_output, ((0, rows - scalars), (0, 0)))

    state_shape = (scalars, heads, cells)
    listed_shape = (listed // LANES, heads * rows, LANES)
    block = divisor(scalars, 6)
    some = ((block, heads, cells), lambda i: (i, 0, 0))
    turn = divisor(heads, 8)
    part = ((listed // LANES, turn * rows, LANES), lambda i: (0, i, 0))
    q, a, ot, rsel = call(
        functools.partial(open_body, scalars, rows),
        [
            (state_shape, F32, True),
            (listed_shape, F32, True),
            ((listed, cells), BF),
            ((SUB, listed), F32),
        ],
        [far(particles), partner, rate, rcol],
        steps=scalars // block,
        blocks={0: some, 4: some},
        name="open",
    )
    grid, sent, inv, lab = call(
        functools.partial(start_body, dims),
        [
            ((flat, LANES), F32),
            ((flat, LANES), F32),
            ((nx * 2 * quads * ny, LANES), I32),
            ((quads * devices, LANES), I32),
        ],
        [arrival, rsel],
        name="start",
    )

    def chemistry(f, a, token):
        return call(
            functools.partial(chem_body, heads),
            [(listed_shape, F32, True), ((flat, LANES), F32)],
            [react_count, f, far(a), ot, rsel, w1, w2, w3, token],
            smem=(0,),
            scratch=[pltpu.VMEM((rows, listed), F32), pltpu.VMEM((rows, listed), F32)],
            steps=heads // turn,
            blocks={2: part, 9: part},
            name="chem",
        )

    per = LANES // heads
    span = SUB * (-(-scalars // (per * SUB)))
    places = leave_slots.shape[1]
    token = rsel
    for substep in range(SUBSTEPS):
        f = exchange(sent)
        change, source = chemistry(f, a, token)
        if substep < SUBSTEPS - 1:
            home = exchange(source)
            q, a, token = call(
                functools.partial(middle_body, scalars, rows),
                [(state_shape, F32, True), (listed_shape, F32, True), ((SUB, LANES), F32)],
                [far(q), f, far(change), ot, rate, rsel, partner],
                scratch=[pltpu.VMEM((block, heads, cells), F32)],
                steps=scalars // block,
                blocks={0: some, 7: some},
                name="middle",
            )
            grid, sent = call(
                functools.partial(again_body, dims),
                [((flat, LANES), F32), ((flat, LANES), F32)],
                [home, grid, arrival, inv, lab, token],
                scratch=[pltpu.VMEM((flat, LANES), F32)],
                name="again",
            )
        if substep == SUBSTEPS - 2:
            base, token = call(
                functools.partial(base_body, span),
                [((places * span, LANES), F32, True), ((1, LANES), F32)],
                [far(q), rate, lcol],
                name="base",
            )
    (leaving,) = call(
        functools.partial(leave_body, rows, span, scalars, heads, devices),
        [((flat + places * span, LANES), F32)],
        [far(base), f, far(change), rate, lcol, react_slots, source],
        name="leave",
    )
    moved = exchange(leaving)
    (grid,) = call(
        functools.partial(last_body, dims), [((flat, LANES), F32)], [moved, grid, lab], name="last"
    )
    grid_out = exchange(grid).reshape(rows, bx, by, nz)[:scalars]
    (state,) = call(
        functools.partial(settle_body, rows),
        [(state_shape, F32, True)],
        [far(q), f, far(change), ot, rate],
        steps=scalars // block,
        blocks={0: some, 5: some},
        name="settle",
    )
    four = ((per, heads, cells), lambda i: (i, 0, 0))
    (state,) = call(
        functools.partial(arrive_body, span, devices),
        [(state_shape, F32, True)],
        [far(state), moved, acol],
        scratch=[pltpu.VMEM((places, cells), BF), pltpu.VMEM((SUB, cells), F32)],
        steps=-(-scalars // per),
        blocks={0: four, 3: four},
        name="arrive",
    )
    return (grid_out, state)


def solution(mesh):
    placed = (
        P(None, "gx", "gy", None),
        P("gx", "gy", None),
        P(None, None, ("gx", "gy")),
        P("gx", "gy", None),
        P("gx", "gy", None),
        P(("gx", "gy")),
        P(None, ("gx", "gy")),
        P(),
        P(),
        P(),
        P(("gx", "gy"), None),
        P(("gx", "gy")),
        P(("gx", "gy"), None),
        P(("gx", "gy"), None),
    )
    return jax.shard_map(
        per_device,
        mesh=mesh,
        in_specs=placed,
        out_specs=(P(None, "gx", "gy", None), P(None, None, ("gx", "gy"))),
        check_vma=False,
    )
```

```python
import functools

import jax
import jax.numpy as jnp
from jax import lax
from jax.experimental import pallas as pl
from jax.experimental.pallas import tpu as pltpu
from jax.sharding import PartitionSpec as P

SUBSTEPS = 2
DIFFUSION = 0.1
PAIR_WEIGHT = 0.4
LANES = 128
SUB = 8
BF = jnp.bfloat16
F32 = jnp.float32
I32 = jnp.int32

NT = (((1,), (1,)), ((), ()))
NN = (((1,), (0,)), ((), ()))


def call(body, outs, ins, smem=(), hbm=(), scratch=(), limit=24, name=None):
    spaces = {**{i: pltpu.SMEM for i in smem}, **{i: pl.ANY for i in hbm}}
    ins = [pltpu.with_memory_space_constraint(x, pltpu.HBM) if i in hbm else x for i, x in enumerate(ins)]
    return pl.pallas_call(
        body,
        out_shape=[
            pltpu.HBM(o[0], o[1]) if len(o) > 2 else jax.ShapeDtypeStruct(o[0], o[1]) for o in outs
        ],
        in_specs=[
            pl.BlockSpec(memory_space=spaces.get(i, pltpu.VMEM)) for i in range(len(ins))
        ],
        out_specs=[
            pl.BlockSpec(memory_space=pl.ANY if len(o) > 2 else pltpu.VMEM) for o in outs
        ],
        scratch_shapes=list(scratch),
        compiler_params=pltpu.CompilerParams(vmem_limit_bytes=limit << 20),
        name=name,
    )(*ins)


class Stream:
    def __init__(self, src, dst, sem, size, dim=0):
        self.src, self.dst, self.sem, self.size, self.dim = src, dst, sem, size, dim
        self.count = -(-src.shape[dim] // size)

    def copy(self, i, size=None):
        at = (slice(None),) * self.dim + (pl.ds(i * self.size, size or self.size),)
        return pltpu.make_async_copy(self.src.at[at], self.dst.at[at], self.sem.at[i])

    def tail(self, i):
        return min(self.size, self.src.shape[self.dim] - i * self.size)

    def start_all(self):
        for i in range(self.count):
            self.copy(i, self.tail(i)).start()

    def wait_all(self, first=0):
        for i in range(first, self.count):
            self.copy(i, self.tail(i)).wait()


def dot(a, b, dims):
    return lax.dot_general(a, b, dims, preferred_element_type=F32)


def dot_split(x, onehot, dims):
    high = x.astype(BF)
    low = (x - high.astype(F32)).astype(BF)
    return dot(high, onehot, dims) + dot(low, onehot, dims)


def divisor(n, most):
    return max(k for k in range(1, most + 1) if n % k == 0)


def mix(s0, block, p_ref, partner_ref, q_ref):
    scalars, particles, cells = p_ref.shape
    groups = particles // SUB
    for t in range(cells // LANES):
        lanes = pl.ds(t * LANES, LANES)
        rows, homes = [], []
        for j in range(groups):
            index = partner_ref[pl.ds(j * SUB, SUB), lanes]
            rows.append(index & (SUB - 1))
            homes.append(index >> 3)

        def step(s, carry):
            x = [p_ref[s, pl.ds(k * SUB, SUB), lanes] for k in range(groups)]
            for j in range(groups):
                mate = jnp.take_along_axis(x[0], rows[j], axis=0)
                for k in range(1, groups):
                    other = jnp.take_along_axis(x[k], rows[j], axis=0)
                    mate = jnp.where(homes[j] == k, other, mate)
                q_ref[s, pl.ds(j * SUB, SUB), lanes] = x[j] + PAIR_WEIGHT * (mate - x[j])
            return carry

        lax.fori_loop(s0, s0 + block, step, 0)


def put_scalar(ref, s, value, rows):
    for o in range(value.shape[0] // SUB):
        for t in range(value.shape[1] // LANES):
            part = value[o * SUB : (o + 1) * SUB, t * LANES : (t + 1) * LANES]
            ref[t, pl.ds(o * rows * SUB + s * SUB, SUB), :] = part


def get_scalar(ref, s, rows):
    octets = ref.shape[1] // (rows * SUB)
    return jnp.concatenate(
        [
            jnp.concatenate(
                [ref[t, pl.ds(o * rows * SUB + s * SUB, SUB), :] for t in range(ref.shape[0])],
                axis=1,
            )
            for o in range(octets)
        ],
        axis=0,
    )


def particle_rows(p, rows):
    return pl.ds((p >> 3) * (rows * SUB) + (p & (SUB - 1)), rows, stride=SUB)


def list_cells(s0, block, q_ref, onehot, keep, a_ref, rows):
    scalars, particles, cells = q_ref.shape
    x = q_ref[pl.ds(s0, block)].reshape(block * particles, cells)
    y = dot_split(x, onehot, NT) * keep
    for i in range(block):
        put_scalar(a_ref, s0 + i, y[i * particles : (i + 1) * particles], rows)


def clear_rest(scalars, rows, a_ref):
    particles = a_ref.shape[1] // rows
    zeros = jnp.zeros((particles, a_ref.shape[0] * LANES), F32)
    for s in range(scalars, rows):
        put_scalar(a_ref, s, zeros, rows)


def open_body(
    rows,
    block,
    p_hbm,
    partner_ref,
    rate_ref,
    rcol_ref,
    q_hbm,
    a_hbm,
    ot_ref,
    rsel_ref,
    p_ref,
    q_ref,
    a_ref,
    in_sem,
    out_sem,
    a_sem,
):
    scalars, particles, cells = p_ref.shape
    into, out = Stream(p_hbm, p_ref, in_sem, block), Stream(q_ref, q_hbm, out_sem, block)
    into.start_all()
    onehot = (rcol_ref[...] == lax.broadcasted_iota(I32, ot_ref.shape, 1)).astype(F32)
    ot_ref[...] = onehot.astype(BF)
    rate = jnp.broadcast_to(rate_ref[...], (SUB, cells))
    rsel_ref[...] = dot_split(rate, onehot.astype(BF), NT)
    clear_rest(scalars, rows, a_ref)

    def step(b, carry):
        into.copy(b).wait()
        mix(b * block, block, p_ref, partner_ref, q_ref)
        out.copy(b).start()
        list_cells(b * block, block, q_ref, ot_ref[...], 1.0 - rsel_ref[0:1, :], a_ref, rows)
        return carry

    lax.fori_loop(0, scalars // block, step, 0)
    last = pltpu.make_async_copy(a_ref, a_hbm, a_sem)
    last.start()
    out.wait_all()
    last.wait()


def settle_block(s0, block, q_ref, f_ref, r_ref, ot_ref, rate_ref, out_ref, rows):
    scalars, particles, cells = q_ref.shape
    tiles = cells // LANES
    rate = rate_ref[...]
    keep = 1.0 - rate
    r = jnp.concatenate([get_scalar(r_ref, s0 + i, rows) for i in range(block)], axis=0)
    spread = dot(r.astype(BF), ot_ref[...], NN)
    for i in range(block):
        f = jnp.concatenate(
            [f_ref[pl.ds((s0 + i) * tiles + t, 1), :] for t in range(tiles)], axis=1
        )
        out_ref[s0 + i] = (
            keep * q_ref[s0 + i] + rate * f + spread[i * particles : (i + 1) * particles]
        )


def middle_body(
    rows,
    block,
    q_hbm,
    f_ref,
    r_hbm,
    ot_ref,
    rate_ref,
    rsel_ref,
    partner_ref,
    out_hbm,
    a_hbm,
    token_ref,
    q_ref,
    now_ref,
    r_ref,
    in_sem,
    out_sem,
    r_sem,
):
    scalars = q_ref.shape[0]
    into, out = Stream(q_hbm, q_ref, in_sem, block), Stream(q_ref, out_hbm, out_sem, block)
    first = pltpu.make_async_copy(r_hbm, r_ref, r_sem)
    first.start()
    into.start_all()
    token_ref[...] = rsel_ref[:, :LANES]
    first.wait()

    def step(b, carry):
        into.copy(b).wait()
        s0 = b * block
        settle_block(s0, block, q_ref, f_ref, r_ref, ot_ref, rate_ref, now_ref, rows)
        mix(s0, block, now_ref, partner_ref, q_ref)
        out.copy(b).start()
        list_cells(s0, block, q_ref, ot_ref[...], 1.0 - rsel_ref[0:1, :], r_ref, rows)
        return carry

    lax.fori_loop(0, scalars // block, step, 0)
    clear_rest(scalars, rows, r_ref)
    last = pltpu.make_async_copy(r_ref, a_hbm, r_sem)
    last.start()
    out.wait_all()
    last.wait()


def half_silu(y):
    return y + y * jnp.tanh(y)


def chem_body(
    count_ref,
    f_ref,
    a_hbm,
    ot_ref,
    rsel_ref,
    w1_ref,
    w2_ref,
    w3_ref,
    token_ref,
    r_hbm,
    s_ref,
    a_ref,
    r_ref,
    pull_ref,
    one_a,
    one_b,
    two_a,
    two_b,
    in_sem,
    out_sem,
):
    tiles = ot_ref.shape[1] // LANES
    rows = f_ref.shape[0] // tiles
    listed = ot_ref.shape[0]
    particles = a_ref.shape[1] // rows
    into = Stream(a_hbm, a_ref, in_sem, SUB * rows, 1)
    out = Stream(r_ref, r_hbm, out_sem, SUB * rows, 1)
    into.start_all()
    f = jnp.concatenate([f_ref[pl.ds(t, rows, stride=tiles), :] for t in range(tiles)], axis=1)
    pull_ref[...] = rsel_ref[0:1, :] * dot_split(f, ot_ref[...], NT)
    live = lax.broadcasted_iota(I32, (1, listed), 1) < count_ref[0]

    def first(g):
        parts = []
        for i in range(2):
            at = particle_rows(2 * g + i, rows)
            for t in range(listed // LANES):
                pull = pull_ref[:, t * LANES : (t + 1) * LANES]
                parts.append((a_ref[t, at, :] + pull).astype(BF))
        return half_silu(dot(w1_ref[...], jnp.concatenate(parts, axis=1), NN)).astype(BF)

    def second(one):
        return half_silu(dot(w2_ref[...], one, NN)).astype(BF)

    def third(g, two, total):
        change = dot(w3_ref[...], two, NN).astype(BF).astype(F32)
        for i in range(2):
            r = jnp.where(live, change[:, i * listed : (i + 1) * listed], 0.0)
            at = particle_rows(2 * g + i, rows)
            for t in range(listed // LANES):
                r_ref[t, at, :] = r[:, t * LANES : (t + 1) * LANES]
            total = total + r
        return total

    def step(g, total, old, new):
        total = third(g - 2, old[1][...], total)
        new[1][...] = second(old[0][...])
        new[0][...] = first(g)
        return total

    left, right = (one_a, two_a), (one_b, two_b)

    def pair(m, total):
        total = step(2 * m, total, right, left)
        return step(2 * m + 1, total, left, right)

    total = jnp.zeros((rows, listed), F32)
    each = SUB // 4
    for o in range(particles // SUB):
        into.copy(o).wait()
        if o == 0:
            one_a[...] = first(0)
            two_b[...] = second(one_a[...])
            one_b[...] = first(1)
        total = lax.fori_loop(max(1, o * each), (o + 1) * each, pair, total)
        if o:
            out.copy(o - 1).start()
    last = particles // 2 - 1
    total = third(last - 1, two_b[...], total)
    total = third(last, second(one_b[...]), total)
    out.copy(particles // SUB - 1).start()
    source = dot_split(total * (1.0 / particles), ot_ref[...], NN)
    for t in range(tiles):
        s_ref[pl.ds(t, rows, stride=tiles), :] = source[:, t * LANES : (t + 1) * LANES]
    out.wait_all()


def cell_onehot(col_ref, cells):
    shape = (col_ref.shape[0], cells)
    return (col_ref[...] == lax.broadcasted_iota(I32, shape, 1)).astype(F32).astype(BF)


def split_dot(onehot, x, dims):
    high = x.astype(BF)
    low = (x - high.astype(F32)).astype(BF)
    return dot(onehot, high, dims) + dot(onehot, low, dims)


def leave_blocks(scalars, particles, span, store, part):
    per = LANES // particles

    def step(b, carry):
        store(b, part(b * per, per))
        return carry

    whole = scalars // per
    lax.fori_loop(0, whole, step, 0)
    left = scalars - whole * per
    for b in range(whole, span):
        if b == whole and left:
            value = part(b * per, left)
            zeros = jnp.zeros((value.shape[0], LANES - left * particles), F32)
            store(b, jnp.concatenate([value, zeros], axis=1))
        else:
            store(b, None)


def base_body(span, q_hbm, rate_ref, lcol_ref, out_ref, token_ref, q_ref, sem):
    per = LANES // q_ref.shape[1]
    into = Stream(q_hbm, q_ref, sem, per)
    into.start_all()
    scalars, particles, cells = q_ref.shape
    onehot = cell_onehot(lcol_ref, cells)
    keep = 1.0 - rate_ref[...]

    def part(s0, count):
        into.copy(s0 // per, count).wait()
        x = q_ref[pl.ds(s0, count), :, :].reshape(count * particles, cells) * keep
        return split_dot(onehot, x, NT)

    def store(b, value):
        if value is not None:
            out_ref[pl.ds(b, lcol_ref.shape[0], stride=span), :] = value

    leave_blocks(scalars, particles, span, store, part)
    token_ref[...] = keep[:, :LANES]


def leave_body(
    rows,
    span,
    scalars,
    particles,
    devices,
    base_hbm,
    f_ref,
    r_hbm,
    rate_ref,
    lcol_ref,
    rrow_ref,
    source_ref,
    out_ref,
    base_ref,
    r_ref,
    sem,
):
    loads = [
        pltpu.make_async_copy(r_hbm, r_ref, sem.at[0]),
        pltpu.make_async_copy(base_hbm, base_ref, sem.at[1]),
    ]
    for c in loads:
        c.start()
    width = source_ref.shape[0] // devices
    stride = out_ref.shape[0] // devices
    for d in range(devices):
        out_ref[d * stride : d * stride + width] = source_ref[d * width : (d + 1) * width]
    cells = rate_ref.shape[1]
    tiles = cells // LANES
    places = lcol_ref.shape[0]
    f = jnp.concatenate([f_ref[pl.ds(t, rows, stride=tiles), :] for t in range(tiles)], axis=1)
    pull = split_dot(cell_onehot(lcol_ref, cells), f * rate_ref[...], NT)
    reacts = (lcol_ref[...] == rrow_ref[...]).astype(F32).astype(BF)
    for c in loads:
        c.wait()

    def part(s0, count):
        wide = count * particles
        r = jnp.concatenate([get_scalar(r_ref, s0 + i, rows) for i in range(count)], axis=0)
        of = lax.broadcasted_iota(I32, (rows, wide), 1) // particles + s0
        mine = (of == lax.broadcasted_iota(I32, (rows, wide), 0)).astype(F32).astype(BF)
        at = pl.ds(s0 * particles // LANES, places, stride=span)
        return base_ref[at, :][:, :wide] + dot_split(pull, mine, NN) + dot(reacts, r.astype(BF), NT)

    def store(b, value):
        for c in range(places // devices):
            at = pl.ds(width + c * span + b, devices, stride=stride)
            if value is None:
                out_ref[at, :] = jnp.zeros((devices, LANES), F32)
            else:
                out_ref[at, :] = value[c * devices : (c + 1) * devices]

    leave_blocks(scalars, particles, span, store, part)


def settle_body(
    rows,
    block,
    q_hbm,
    f_ref,
    r_hbm,
    ot_ref,
    rate_ref,
    out_hbm,
    token_ref,
    q_ref,
    out_ref,
    r_ref,
    in_sem,
    out_sem,
    r_sem,
):
    into, out = Stream(q_hbm, q_ref, in_sem, block), Stream(out_ref, out_hbm, out_sem, block)
    first = pltpu.make_async_copy(r_hbm, r_ref, r_sem)
    first.start()
    into.start_all()
    token_ref[...] = rate_ref[:, :LANES]
    first.wait()

    def step(b, carry):
        into.copy(b).wait()
        settle_block(b * block, block, q_ref, f_ref, r_ref, ot_ref, rate_ref, out_ref, rows)
        out.copy(b).start()
        return carry

    lax.fori_loop(0, q_ref.shape[0] // block, step, 0)
    out.wait_all()


def arrive_body(
    span, devices, p_hbm, arr_ref, acol_ref, out_hbm, p_ref, out_ref, hit_ref, in_sem, out_sem
):
    scalars, particles, cells = p_ref.shape
    places = acol_ref.shape[0]
    per = LANES // particles
    into, out = Stream(p_hbm, p_ref, in_sem, per), Stream(out_ref, out_hbm, out_sem, per)
    into.start_all()
    hit = (acol_ref[...] == lax.broadcasted_iota(I32, (places, cells), 1)).astype(F32)
    hit_ref[...] = hit.astype(BF)
    taken = jnp.sum(hit, axis=0, keepdims=True) > 0.5
    stride = arr_ref.shape[0] // devices
    count = places // devices

    def place(b, size):
        first = stride - count * span + b
        x = jnp.concatenate(
            [arr_ref[pl.ds(first + c * span, devices, stride=stride), :] for c in range(count)],
            axis=0,
        ).T
        y = dot_split(x, hit_ref[...], NN)
        into.copy(b, size).wait()
        for i in range(size):
            s = b * per + i
            out_ref[s] = jnp.where(taken, y[i * particles : (i + 1) * particles], p_ref[s])
        out.copy(b, size).start()

    def step(b, carry):
        place(b, per)
        return carry

    whole = scalars // per
    lax.fori_loop(0, whole, step, 0)
    if scalars > whole * per:
        place(whole, scalars - whole * per)
    out.wait_all()


def stencil(value, speed, bx, by, lanes_y):
    boxes = value[0].shape[0]
    row = lax.broadcasted_iota(I32, value[0].shape, 0) % lanes_y
    zero = jnp.zeros((lanes_y, LANES), F32)

    def x_low(v):
        return jnp.concatenate([zero, v[: boxes - lanes_y]], axis=0)

    def x_high(v):
        return jnp.concatenate([v[lanes_y:], zero], axis=0)

    def y_low(v):
        return jnp.where(row == 0, 0.0, pltpu.roll(v, 1, 0))

    def y_high(v):
        return jnp.where(row == lanes_y - 1, 0.0, pltpu.roll(v, boxes - 1, 0))

    out = []
    for i in range(bx):
        for j in range(by):
            c = value[i * by + j]
            up = value[(i - 1) * by + j] if i else x_low(value[(bx - 1) * by + j])
            down = value[(i + 1) * by + j] if i < bx - 1 else x_high(value[j])
            left = value[i * by + j - 1] if j else y_low(value[i * by + by - 1])
            right = value[i * by + j + 1] if j < by - 1 else y_high(value[i * by])
            beside = up + down + left + right + pltpu.roll(c, 1, 1) + pltpu.roll(c, LANES - 1, 1)
            out.append(c + DIFFUSION * (beside - 6.0 * c) - speed[i * by + j] * (c - up))
    return out


def route(src_ref, first_row, row_step, item_step, items, own, quads, lanes_y, rows, lanes):
    shape = (lanes_y, LANES)
    out = []
    for k in range(len(rows)):

        def step(y, acc):
            for j in range(items):
                hit = rows[k] == (j * lanes_y + y)
                at = first_row + y * row_step + j * item_step
                lines = [src_ref[pl.ds(at + s * quads, 1), :] for s in range(own)]
                acc = [
                    jnp.where(
                        hit,
                        jnp.take_along_axis(jnp.broadcast_to(v, shape), lanes[k], axis=1),
                        old,
                    )
                    for v, old in zip(lines, acc)
                ]
            return tuple(acc)

        zero = tuple(jnp.zeros(shape, F32) for _ in range(own))
        out.append(lax.fori_loop(0, lanes_y, step, zero, unroll=min(lanes_y, 8)))
    return [[out[k][s] for k in range(len(rows))] for s in range(own)]


def load_rows(ref, offset, stride, count):
    return ref[pl.ds(offset, count, stride=stride), :]


def pack_body(width, grid_ref, owner_ref, slot_ref, speed_ref, lanes_y, out_ref):
    quads = owner_ref.shape[0]
    stride = width + 2 * quads
    total = grid_ref.shape[0]
    slot = slot_ref[...]
    label = ((slot >> 7) * lanes_y + owner_ref[...]) * LANES + (slot & (LANES - 1))
    tail = jnp.concatenate([label.astype(F32), speed_ref[...]], axis=0)
    for d in range(out_ref.shape[0] // stride):
        count = max(0, min(width, total - d * width))
        if count:
            out_ref[d * stride : d * stride + count] = grid_ref[d * width : d * width + count]
        if count < width:
            zeros = jnp.zeros((width - count, LANES), F32)
            out_ref[d * stride + count : d * stride + width] = zeros
        out_ref[d * stride + width : (d + 1) * stride] = tail


def start_body(dims, arr_ref, token_ref, g_ref, f_ref, inv_ref, lab_ref):
    nx, ny, own, bx, by = dims
    quads = bx * by
    boxes = nx * ny
    width = own * quads
    stride = width + 2 * quads
    turns = quads * ny
    speed = [load_rows(arr_ref, width + quads + j, stride, boxes) for j in range(quads)]
    for s in range(own):
        value = [load_rows(arr_ref, s * quads + j, stride, boxes) for j in range(quads)]
        for j, v in enumerate(stencil(value, speed, bx, by, ny)):
            g_ref[pl.ds(s * quads + j, boxes, stride=width), :] = v
    for j in range(quads):
        lab_ref[pl.ds(j * boxes, boxes), :] = load_rows(arr_ref, width + j, stride, boxes).astype(
            I32
        )
    lane_of = lax.broadcasted_iota(I32, (turns, LANES), 1).astype(F32)
    sub_of = lax.broadcasted_iota(I32, (turns, LANES), 0)
    sub_lane = lax.broadcasted_iota(I32, (LANES, LANES), 0)

    def group(x, carry):
        def gather(y, acc):
            left, right = [], []
            for j in range(quads):
                line = lab_ref[pl.ds(j * boxes + x * ny + y, 1), :]
                hit = jnp.broadcast_to(line >> 7, (turns, LANES)) == sub_of
                code = (j * ny + y).astype(F32)
                left.append(
                    jnp.concatenate(
                        [jnp.where(hit, code, 0.0), jnp.where(hit, lane_of, 0.0)], axis=0
                    ).astype(BF)
                )
                right.append(
                    (jnp.broadcast_to(line & (LANES - 1), (LANES, LANES)) == sub_lane)
                    .astype(F32)
                    .astype(BF)
                )
            return acc + dot(
                jnp.concatenate(left, axis=1), jnp.concatenate(right, axis=1), NT
            )

        code = lax.fori_loop(0, ny, gather, jnp.zeros((2 * turns, LANES), F32), unroll=2)
        code = code.astype(I32)
        inv_ref[pl.ds(x * 2 * turns, 2 * turns), :] = code
        return carry

    lax.fori_loop(0, nx, group, 0)
    send_filtered(dims, g_ref, inv_ref, f_ref)


def send_filtered(dims, g_ref, inv_ref, f_ref):
    nx, ny, own, bx, by = dims
    quads = bx * by
    width = own * quads
    turns = quads * ny

    def group(x, carry):
        base = x * 2 * turns
        rows = [inv_ref[pl.ds(base + k * ny, ny), :] for k in range(quads)]
        lanes = [inv_ref[pl.ds(base + turns + k * ny, ny), :] for k in range(quads)]
        out = route(g_ref, x * ny * width, width, 1, quads, own, quads, ny, rows, lanes)
        for s in range(own):
            for k in range(quads):
                f_ref[pl.ds(x * ny * width + s * quads + k, ny, stride=width), :] = out[s][k]
        return carry

    lax.fori_loop(0, nx, group, 0)


def add_source(dims, s_ref, g_ref, lab_ref, out_ref):
    nx, ny, own, bx, by = dims
    quads = bx * by
    boxes = nx * ny
    width = own * quads
    stride = s_ref.shape[0] // boxes

    def group(x, carry):
        labels = [lab_ref[pl.ds(j * boxes + x * ny, ny), :] for j in range(quads)]
        rows = [v >> 7 for v in labels]
        lanes = [v & (LANES - 1) for v in labels]
        out = route(s_ref, x * ny * stride, stride, 1, quads, own, quads, ny, rows, lanes)
        for s in range(own):
            for k in range(quads):
                at = pl.ds(x * ny * width + s * quads + k, ny, stride=width)
                out_ref[at, :] = g_ref[at, :] + out[s][k]
        return carry

    lax.fori_loop(0, nx, group, 0)


def again_body(dims, s_ref, g_ref, arr_ref, inv_ref, lab_ref, token_ref, out_ref, f_ref, mid_ref):
    nx, ny, own, bx, by = dims
    quads = bx * by
    boxes = nx * ny
    width = own * quads
    stride = width + 2 * quads
    add_source(dims, s_ref, g_ref, lab_ref, mid_ref)
    speed = [load_rows(arr_ref, width + quads + j, stride, boxes) for j in range(quads)]
    for s in range(own):
        value = [load_rows(mid_ref, s * quads + j, width, boxes) for j in range(quads)]
        for j, v in enumerate(stencil(value, speed, bx, by, ny)):
            out_ref[pl.ds(s * quads + j, boxes, stride=width), :] = v
    send_filtered(dims, out_ref, inv_ref, f_ref)


def last_body(dims, s_ref, g_ref, lab_ref, token_ref, out_ref):
    add_source(dims, s_ref, g_ref, lab_ref, out_ref)


def per_device(
    grid_scalars,
    axial_speed,
    particles,
    cell_owner,
    cell_slot,
    mix_rate,
    partner,
    chem_input,
    chem_hidden,
    chem_output,
    react_slots,
    react_count,
    leave_slots,
    arrive_slots,
):
    both = ("gx", "gy")
    nx, ny = lax.axis_size("gx"), lax.axis_size("gy")
    devices = nx * ny
    scalars, bx, by, nz = grid_scalars.shape
    heads, cells = partner.shape
    listed = react_slots.shape[1]
    hidden = chem_hidden.shape[0]
    quads = bx * by
    own = -(-scalars // devices)
    rows = devices * own
    width = own * quads
    tiles = cells // LANES
    assert nz == LANES and tiles == quads and heads % SUB == 0 and LANES % heads == 0
    dims = (nx, ny, own, bx, by)
    flat = devices * width

    (first,) = call(
        lambda g, o, c, u, out: pack_body(width, g, o, c, u, ny, out),
        [((devices * (width + 2 * quads), LANES), F32)],
        [
            grid_scalars.reshape(-1, LANES),
            cell_owner.reshape(quads, LANES),
            cell_slot.reshape(quads, LANES),
            axial_speed.reshape(quads, LANES),
        ],
        name="pack",
    )

    def exchange(x):
        x = x.reshape(devices, -1, LANES)
        return lax.all_to_all(x, both, split_axis=0, concat_axis=0, tiled=True).reshape(-1, LANES)

    arrival = exchange(first)

    rate = mix_rate.reshape(1, cells)
    rcol = react_slots.reshape(listed, 1)
    lcol = leave_slots.reshape(devices, -1).T.reshape(-1, 1)
    acol = arrive_slots.reshape(devices, -1).T.reshape(-1, 1)
    w1 = jnp.pad(chem_input, ((0, 0), (0, rows - scalars))) * jnp.asarray(0.5, BF)
    w2 = chem_hidden * jnp.asarray(0.5, BF)
    w3 = jnp.pad(chem_output, ((0, rows - scalars), (0, 0)))

    state_shape = (scalars, heads, cells)
    listed_shape = (listed // LANES, heads * rows, LANES)
    block = divisor(scalars, 6)
    octets = heads // SUB
    state_vmem = pltpu.VMEM(state_shape, F32)
    listed_vmem = pltpu.VMEM(listed_shape, F32)
    dma = pltpu.SemaphoreType.DMA
    per_block = dma((scalars // block,))
    q, a, ot, rsel = call(
        functools.partial(open_body, rows, block),
        [
            (state_shape, F32, True),
            (listed_shape, F32, True),
            ((listed, cells), BF),
            ((SUB, listed), F32),
        ],
        [particles, partner, rate, rcol],
        hbm=(0,),
        scratch=[state_vmem, state_vmem, listed_vmem, per_block, per_block, dma],
        name="open",
    )
    grid, sent, inv, lab = call(
        functools.partial(start_body, dims),
        [
            ((flat, LANES), F32),
            ((flat, LANES), F32),
            ((nx * 2 * quads * ny, LANES), I32),
            ((quads * devices, LANES), I32),
        ],
        [arrival, rsel],
        name="start",
    )

    def chemistry(f, a, token):
        pair = pltpu.VMEM((hidden, 2 * listed), BF)
        return call(
            chem_body,
            [(listed_shape, F32, True), ((flat, LANES), F32)],
            [react_count, f, a, ot, rsel, w1, w2, w3, token],
            smem=(0,),
            hbm=(2,),
            scratch=[listed_vmem, listed_vmem, pltpu.VMEM((rows, listed), F32)]
            + [pair] * 4
            + [dma((octets,)), dma((octets,))],
            name="chem",
        )

    per = LANES // heads
    span = SUB * (-(-scalars // (per * SUB)))
    places = leave_slots.shape[1]
    token = rsel
    for substep in range(SUBSTEPS):
        f = exchange(sent)
        change, source = chemistry(f, a, token)
        if substep < SUBSTEPS - 1:
            home = exchange(source)
            q, a, token = call(
                functools.partial(middle_body, rows, block),
                [(state_shape, F32, True), (listed_shape, F32, True), ((SUB, LANES), F32)],
                [q, f, change, ot, rate, rsel, partner],
                hbm=(0, 2),
                scratch=[state_vmem, state_vmem, listed_vmem, per_block, per_block, dma],
                name="middle",
            )
            grid, sent = call(
                functools.partial(again_body, dims),
                [((flat, LANES), F32), ((flat, LANES), F32)],
                [home, grid, arrival, inv, lab, token],
                scratch=[pltpu.VMEM((flat, LANES), F32)],
                name="again",
            )
        if substep == SUBSTEPS - 2:
            base, token = call(
                functools.partial(base_body, span),
                [((places * span, LANES), F32), ((1, LANES), F32)],
                [q, rate, lcol],
                hbm=(0,),
                scratch=[state_vmem, dma((-(-scalars // per),))],
                name="base",
            )
    (leaving,) = call(
        functools.partial(leave_body, rows, span, scalars, heads, devices),
        [((flat + places * span, LANES), F32)],
        [base, f, change, rate, lcol, react_slots, source],
        hbm=(0, 2),
        scratch=[pltpu.VMEM((places * span, LANES), F32), listed_vmem, dma((2,))],
        name="leave",
    )
    moved = exchange(leaving)
    state, token = call(
        functools.partial(settle_body, rows, block),
        [(state_shape, F32, True), ((1, LANES), F32)],
        [q, f, change, ot, rate],
        hbm=(0, 2),
        scratch=[state_vmem, state_vmem, listed_vmem, per_block, per_block, dma],
        name="settle",
    )
    (grid,) = call(
        functools.partial(last_body, dims),
        [((flat, LANES), F32)],
        [moved, grid, lab, token],
        name="last",
    )
    grid_out = exchange(grid).reshape(rows, bx, by, nz)[:scalars]
    steps = -(-scalars // per)
    (state,) = call(
        functools.partial(arrive_body, span, devices),
        [(state_shape, F32, True)],
        [state, moved, acol],
        hbm=(0,),
        scratch=[
            state_vmem,
            state_vmem,
            pltpu.VMEM((places, cells), BF),
            dma((steps,)),
            dma((steps,)),
        ],
        name="arrive",
    )
    return (grid_out, state)


def solution(mesh):
    placed = (
        P(None, "gx", "gy", None),
        P("gx", "gy", None),
        P(None, None, ("gx", "gy")),
        P("gx", "gy", None),
        P("gx", "gy", None),
        P(("gx", "gy")),
        P(None, ("gx", "gy")),
        P(),
        P(),
        P(),
        P(("gx", "gy"), None),
        P(("gx", "gy")),
        P(("gx", "gy"), None),
        P(("gx", "gy"), None),
    )
    return jax.shard_map(
        per_device,
        mesh=mesh,
        in_specs=placed,
        out_specs=(P(None, "gx", "gy", None), P(None, None, ("gx", "gy"))),
        check_vma=False,
    )
```

```python
import functools

import jax
import jax.numpy as jnp
from jax import lax
from jax.experimental import pallas as pl
from jax.experimental.pallas import tpu as pltpu
from jax.sharding import PartitionSpec as P

SUBSTEPS = 2
DIFFUSION = 0.1
PAIR_WEIGHT = 0.4
LANES = 128
SUB = 8
BF = jnp.bfloat16
F32 = jnp.float32
I32 = jnp.int32

NT = (((1,), (1,)), ((), ()))
NN = (((1,), (0,)), ((), ()))


def call(body, outs, ins, smem=(), hbm=(), scratch=(), limit=24, name=None):
    spaces = {**{i: pltpu.SMEM for i in smem}, **{i: pl.ANY for i in hbm}}
    ins = [pltpu.with_memory_space_constraint(x, pltpu.HBM) if i in hbm else x for i, x in enumerate(ins)]
    return pl.pallas_call(
        body,
        out_shape=[
            pltpu.HBM(o[0], o[1]) if len(o) > 2 else jax.ShapeDtypeStruct(o[0], o[1]) for o in outs
        ],
        in_specs=[
            pl.BlockSpec(memory_space=spaces.get(i, pltpu.VMEM)) for i in range(len(ins))
        ],
        out_specs=[
            pl.BlockSpec(memory_space=pl.ANY if len(o) > 2 else pltpu.VMEM) for o in outs
        ],
        scratch_shapes=list(scratch),
        compiler_params=pltpu.CompilerParams(vmem_limit_bytes=limit << 20),
        name=name,
    )(*ins)


class Stream:
    def __init__(self, src, dst, sem, size, dim=0):
        self.src, self.dst, self.sem, self.size, self.dim = src, dst, sem, size, dim
        self.count = -(-src.shape[dim] // size)

    def copy(self, i, size=None):
        at = (slice(None),) * self.dim + (pl.ds(i * self.size, size or self.size),)
        return pltpu.make_async_copy(self.src.at[at], self.dst.at[at], self.sem.at[i])

    def tail(self, i):
        return min(self.size, self.src.shape[self.dim] - i * self.size)

    def start_all(self):
        for i in range(self.count):
            self.copy(i, self.tail(i)).start()

    def wait_all(self, first=0):
        for i in range(first, self.count):
            self.copy(i, self.tail(i)).wait()


def dot(a, b, dims):
    return lax.dot_general(a, b, dims, preferred_element_type=F32)


def halves(x):
    high = x.astype(BF)
    return high, (x - high.astype(F32)).astype(BF)


def dot_split(x, onehot, dims):
    high, low = halves(x)
    y = dot(jnp.concatenate([high, low], axis=0), onehot, dims)
    return y[: x.shape[0]] + y[x.shape[0] :]


def divisor(n, most):
    return max(k for k in range(1, most + 1) if n % k == 0)


def mix(s0, block, p_ref, partner_ref, q_ref):
    scalars, particles, cells = p_ref.shape
    groups = particles // SUB
    for t in range(cells // LANES):
        lanes = pl.ds(t * LANES, LANES)
        rows, homes = [], []
        for j in range(groups):
            index = partner_ref[pl.ds(j * SUB, SUB), lanes]
            rows.append(index & (SUB - 1))
            homes.append(index >> 3)

        def step(s, carry):
            x = [p_ref[s, pl.ds(k * SUB, SUB), lanes] for k in range(groups)]
            for j in range(groups):
                mate = jnp.take_along_axis(x[0], rows[j], axis=0)
                for k in range(1, groups):
                    other = jnp.take_along_axis(x[k], rows[j], axis=0)
                    mate = jnp.where(homes[j] == k, other, mate)
                q_ref[s, pl.ds(j * SUB, SUB), lanes] = x[j] + PAIR_WEIGHT * (mate - x[j])
            return carry

        lax.fori_loop(s0, s0 + block, step, 0)


def put_scalar(ref, s, value, rows):
    for o in range(value.shape[0] // SUB):
        for t in range(value.shape[1] // LANES):
            part = value[o * SUB : (o + 1) * SUB, t * LANES : (t + 1) * LANES]
            ref[t, pl.ds(o * rows * SUB + s * SUB, SUB), :] = part


def get_scalar(ref, s, rows):
    octets = ref.shape[1] // (rows * SUB)
    return jnp.concatenate(
        [
            jnp.concatenate(
                [ref[t, pl.ds(o * rows * SUB + s * SUB, SUB), :] for t in range(ref.shape[0])],
                axis=1,
            )
            for o in range(octets)
        ],
        axis=0,
    )


def particle_rows(p, rows):
    return pl.ds((p >> 3) * (rows * SUB) + (p & (SUB - 1)), rows, stride=SUB)


def list_cells(s0, block, q_ref, onehot, keep, a_ref, rows):
    scalars, particles, cells = q_ref.shape
    x = q_ref[pl.ds(s0, block)].reshape(block * particles, cells)
    y = dot_split(x, onehot, NT) * keep
    for i in range(block):
        put_scalar(a_ref, s0 + i, y[i * particles : (i + 1) * particles], rows)


def list_body(
    rows,
    span,
    q_hbm,
    rate_ref,
    rsel_ref,
    ot_ref,
    lcol_ref,
    a_hbm,
    base_hbm,
    token_ref,
    q_ref,
    a_ref,
    base_ref,
    in_sem,
    out_sem,
):
    scalars, particles, cells = q_ref.shape
    per = LANES // particles
    into = Stream(q_hbm, q_ref, in_sem, per)
    into.start_all()
    token_ref[...] = rate_ref[:, :LANES]
    leaves = cell_onehot(lcol_ref, cells)
    places = lcol_ref.shape[0]
    keep = 1.0 - rate_ref[...]

    def part(b, count):
        into.copy(b, count).wait()
        x = q_ref[pl.ds(b * per, count)].reshape(count * particles, cells) * keep
        high, low = halves(x)
        y = dot(jnp.concatenate([high, low], axis=0), ot_ref[...], NT)
        half = count * particles
        y = y[:half] + y[half:]
        for i in range(count):
            put_scalar(a_ref, b * per + i, y[i * particles : (i + 1) * particles], rows)
        base_ref[pl.ds(b, places, stride=span), :half] = dot(leaves, high, NT) + dot(
            leaves, low, NT
        )

    def step(b, carry):
        part(b, per)
        return carry

    whole = scalars // per
    lax.fori_loop(0, whole, step, 0)
    zeros = jnp.zeros((places, LANES), F32)
    for b in range(whole, span):
        base_ref[pl.ds(b, places, stride=span), :] = zeros
    if scalars > whole * per:
        part(whole, scalars - whole * per)
    clear_rest(scalars, rows, a_ref)
    copies = [
        pltpu.make_async_copy(a_ref, a_hbm, out_sem.at[0]),
        pltpu.make_async_copy(base_ref, base_hbm, out_sem.at[1]),
    ]
    for c in copies:
        c.start()
    for c in copies:
        c.wait()


def clear_rest(scalars, rows, a_ref):
    particles = a_ref.shape[1] // rows
    zeros = jnp.zeros((particles, a_ref.shape[0] * LANES), F32)
    for s in range(scalars, rows):
        put_scalar(a_ref, s, zeros, rows)


def open_body(
    rows,
    block,
    p_hbm,
    partner_hbm,
    rate_hbm,
    list_hbm,
    q_hbm,
    a_hbm,
    ot_ref,
    rsel_ref,
    p_ref,
    q_ref,
    a_ref,
    partner_ref,
    rate_ref,
    list_ref,
    in_sem,
    out_sem,
    a_sem,
    few_sem,
):
    scalars, particles, cells = p_ref.shape
    into, out = Stream(p_hbm, p_ref, in_sem, block), Stream(q_ref, q_hbm, out_sem, block)
    few = [
        pltpu.make_async_copy(src, dst, few_sem.at[i])
        for i, (src, dst) in enumerate(
            [(list_hbm, list_ref), (rate_hbm, rate_ref), (partner_hbm, partner_ref)]
        )
    ]
    for c in few:
        c.start()
    into.start_all()
    for c in few:
        c.wait()
    column = jnp.broadcast_to(list_ref[...].astype(F32), (SUB, list_ref.shape[1])).T[:, :1]
    cell = lax.broadcasted_iota(I32, ot_ref.shape, 1).astype(F32)
    onehot = (column == cell).astype(F32)
    ot_ref[...] = onehot.astype(BF)
    rate = jnp.broadcast_to(rate_ref[...], (SUB, cells))
    rsel_ref[...] = dot_split(rate, onehot.astype(BF), NT)
    clear_rest(scalars, rows, a_ref)

    def step(b, carry):
        into.copy(b).wait()
        mix(b * block, block, p_ref, partner_ref, q_ref)
        out.copy(b).start()
        list_cells(b * block, block, q_ref, ot_ref[...], 1.0 - rsel_ref[0:1, :], a_ref, rows)
        return carry

    lax.fori_loop(0, scalars // block, step, 0)
    last = pltpu.make_async_copy(a_ref, a_hbm, a_sem)
    last.start()
    out.wait_all()
    last.wait()


def settle_block(s0, block, q_ref, f_ref, r_ref, ot_ref, rate_ref, out_ref, rows):
    scalars, particles, cells = q_ref.shape
    tiles = cells // LANES
    rate = rate_ref[...]
    keep = 1.0 - rate
    r = jnp.concatenate([get_scalar(r_ref, s0 + i, rows) for i in range(block)], axis=0)
    spread = dot(r.astype(BF), ot_ref[...], NN)
    for i in range(block):
        f = jnp.concatenate(
            [f_ref[pl.ds((s0 + i) * tiles + t, 1), :] for t in range(tiles)], axis=1
        )
        out_ref[s0 + i] = (
            keep * q_ref[s0 + i] + rate * f + spread[i * particles : (i + 1) * particles]
        )


def middle_body(
    rows,
    block,
    q_hbm,
    f_ref,
    r_hbm,
    ot_ref,
    rate_ref,
    partner_ref,
    out_hbm,
    token_ref,
    q_ref,
    now_ref,
    r_ref,
    in_sem,
    out_sem,
    r_sem,
):
    scalars = q_ref.shape[0]
    into, out = Stream(q_hbm, q_ref, in_sem, block), Stream(q_ref, out_hbm, out_sem, block)
    first = pltpu.make_async_copy(r_hbm, r_ref, r_sem)
    first.start()
    into.start_all()
    token_ref[...] = rate_ref[:, :LANES]
    first.wait()

    def step(b, carry):
        into.copy(b).wait()
        s0 = b * block
        settle_block(s0, block, q_ref, f_ref, r_ref, ot_ref, rate_ref, now_ref, rows)
        mix(s0, block, now_ref, partner_ref, q_ref)
        out.copy(b).start()
        return carry

    lax.fori_loop(0, scalars // block, step, 0)
    out.wait_all()


def half_silu(y):
    y = y.astype(BF)
    return y + y * jnp.tanh(y)


def chem_body(
    leave,
    count_ref,
    f_ref,
    a_hbm,
    ot_ref,
    rsel_ref,
    w1_ref,
    w2_ref,
    w3_ref,
    token_ref,
    *refs,
):
    leave_refs, refs = (refs[:4], refs[4:]) if leave else (None, refs)
    r_hbm, s_ref, a_ref, r_ref, pull_ref, one_a, one_b, two_a, two_b, in_sem, out_sem, *more = refs
    tiles = ot_ref.shape[1] // LANES
    rows = f_ref.shape[0] // tiles
    listed = ot_ref.shape[0]
    particles = a_ref.shape[1] // rows
    into = Stream(a_hbm, a_ref, in_sem, SUB * rows, 1)
    out = Stream(r_ref, r_hbm, out_sem, SUB * rows, 1)
    into.start_all()
    if leave:
        base = pltpu.make_async_copy(leave_refs[0], more[0], more[1])
        base.start()
    f = jnp.concatenate([f_ref[pl.ds(t, rows, stride=tiles), :] for t in range(tiles)], axis=1)
    pull_ref[...] = rsel_ref[0:1, :] * dot_split(f, ot_ref[...], NT)
    live = lax.broadcasted_iota(I32, (1, listed), 1) < count_ref[0]

    def first(g):
        parts = []
        for i in range(2):
            at = particle_rows(2 * g + i, rows)
            for t in range(listed // LANES):
                pull = pull_ref[:, t * LANES : (t + 1) * LANES]
                parts.append((a_ref[t, at, :] + pull).astype(BF))
        return half_silu(dot(w1_ref[...], jnp.concatenate(parts, axis=1), NN))

    def second(one):
        return half_silu(dot(w2_ref[...], one, NN))

    def third(g, two, total):
        change = dot(w3_ref[...], two, NN).astype(BF).astype(F32)
        for i in range(2):
            r = jnp.where(live, change[:, i * listed : (i + 1) * listed], 0.0)
            at = particle_rows(2 * g + i, rows)
            for t in range(listed // LANES):
                r_ref[t, at, :] = r[:, t * LANES : (t + 1) * LANES]
            total = total + r
        return total

    def step(g, total, old, new):
        total = third(g - 2, old[1][...], total)
        new[1][...] = second(old[0][...])
        new[0][...] = first(g)
        return total

    left, right = (one_a, two_a), (one_b, two_b)

    def pair(m, total):
        total = step(2 * m, total, right, left)
        return step(2 * m + 1, total, left, right)

    total = jnp.zeros((rows, listed), F32)
    each = SUB // 4
    for o in range(particles // SUB):
        into.copy(o).wait()
        if o == 0:
            one_a[...] = first(0)
            two_b[...] = second(one_a[...])
            one_b[...] = first(1)
        total = lax.fori_loop(max(1, o * each), (o + 1) * each, pair, total)
        if o:
            out.copy(o - 1).start()
    last = particles // 2 - 1
    total = third(last - 1, two_b[...], total)
    total = third(last, second(one_b[...]), total)
    out.copy(particles // SUB - 1).start()
    source = dot_split(total * (1.0 / particles), ot_ref[...], NN)
    if leave:
        base.wait()
        source_rows(source, rows, tiles, leave, s_ref)
        leave_rows(leave, f, r_ref, more[0], *leave_refs[1:], s_ref)
    else:
        for t in range(tiles):
            s_ref[pl.ds(t, rows, stride=tiles), :] = source[:, t * LANES : (t + 1) * LANES]
    out.wait_all()


def cell_onehot(col_ref, cells):
    shape = (col_ref.shape[0], cells)
    return (col_ref[...] == lax.broadcasted_iota(I32, shape, 1)).astype(F32).astype(BF)


def split_dot(onehot, x, dims):
    high = x.astype(BF)
    low = (x - high.astype(F32)).astype(BF)
    return dot(onehot, high, dims) + dot(onehot, low, dims)


def source_rows(source, rows, tiles, leave, out_ref):
    devices, own = leave["devices"], rows // leave["devices"]
    stride = out_ref.shape[0] // devices
    for i in range(own):
        mine = source.reshape(devices, own, source.shape[1])[:, i] if own > 1 else source
        for t in range(tiles):
            at = pl.ds(i * tiles + t, devices, stride=stride)
            out_ref[at, :] = mine[:, t * LANES : (t + 1) * LANES]


def leave_rows(leave, f, r_ref, base_ref, rate_ref, lcol_ref, rrow_ref, out_ref):
    devices, span, scalars = leave["devices"], leave["span"], leave["scalars"]
    rows, cells = f.shape
    particles = r_ref.shape[1] // rows
    per = LANES // particles
    places = lcol_ref.shape[0]
    stride = out_ref.shape[0] // devices
    width = stride - places // devices * span
    leaves = cell_onehot(lcol_ref, cells)
    high, low = halves(f * rate_ref[...])
    pull = dot(leaves, high, NT) + dot(leaves, low, NT)
    reacts = (lcol_ref[...] == rrow_ref[...]).astype(F32).astype(BF)
    pull = jnp.concatenate([*halves(pull), reacts], axis=1)

    def part(b, count):
        wide = count * particles
        r = jnp.concatenate([get_scalar(r_ref, b * per + i, rows) for i in range(count)], axis=0)
        of = lax.broadcasted_iota(I32, (wide, rows), 0) // particles + b * per
        mine = (of == lax.broadcasted_iota(I32, (wide, rows), 1)).astype(F32).astype(BF)
        value = dot(pull, jnp.concatenate([mine, mine, r.astype(BF)], axis=1), NT)
        value = base_ref[pl.ds(b, places, stride=span), :][:, :wide] + value
        for c in range(places // devices):
            at = pl.ds(width + c * span + b, devices, stride=stride)
            out_ref[at, :wide] = value[c * devices : (c + 1) * devices]

    def step(b, carry):
        part(b, per)
        return carry

    whole = scalars // per
    lax.fori_loop(0, whole, step, 0, unroll=2)
    zeros = jnp.zeros((devices, LANES), F32)
    for c in range(places // devices):
        for b in range(whole, span):
            out_ref[pl.ds(width + c * span + b, devices, stride=stride), :] = zeros
    if scalars > whole * per:
        part(whole, scalars - whole * per)


def settle_body(
    rows,
    block,
    q_hbm,
    f_ref,
    r_hbm,
    ot_ref,
    rate_ref,
    out_hbm,
    token_ref,
    q_ref,
    out_ref,
    r_ref,
    in_sem,
    out_sem,
    r_sem,
):
    into, out = Stream(q_hbm, q_ref, in_sem, block), Stream(out_ref, out_hbm, out_sem, block)
    first = pltpu.make_async_copy(r_hbm, r_ref, r_sem)
    first.start()
    into.start_all()
    token_ref[...] = rate_ref[:, :LANES]
    first.wait()

    def step(b, carry):
        into.copy(b).wait()
        settle_block(b * block, block, q_ref, f_ref, r_ref, ot_ref, rate_ref, out_ref, rows)
        out.copy(b).start()
        return carry

    lax.fori_loop(0, q_ref.shape[0] // block, step, 0)
    out.wait_all()


def arrive_body(
    span, devices, p_hbm, arr_ref, acol_ref, out_hbm, p_ref, out_ref, hit_ref, in_sem, out_sem
):
    scalars, particles, cells = p_ref.shape
    places = acol_ref.shape[0]
    per = LANES // particles
    into, out = Stream(p_hbm, p_ref, in_sem, per), Stream(out_ref, out_hbm, out_sem, per)
    into.start_all()
    hit = (acol_ref[...] == lax.broadcasted_iota(I32, (places, cells), 1)).astype(F32)
    hit_ref[...] = hit.astype(BF)
    taken = jnp.sum(hit, axis=0, keepdims=True) > 0.5
    stride = arr_ref.shape[0] // devices
    count = places // devices

    def place(b, size):
        first = stride - count * span + b
        x = jnp.concatenate(
            [arr_ref[pl.ds(first + c * span, devices, stride=stride), :] for c in range(count)],
            axis=0,
        ).T
        y = dot_split(x, hit_ref[...], NN)
        into.copy(b, size).wait()
        for i in range(size):
            s = b * per + i
            out_ref[s] = jnp.where(taken, y[i * particles : (i + 1) * particles], p_ref[s])
        out.copy(b, size).start()

    def step(b, carry):
        place(b, per)
        return carry

    whole = scalars // per
    lax.fori_loop(0, whole, step, 0)
    if scalars > whole * per:
        place(whole, scalars - whole * per)
    out.wait_all()


def stencil(value, speed, bx, by, lanes_y):
    boxes = value[0].shape[0]
    row = lax.broadcasted_iota(I32, value[0].shape, 0) % lanes_y
    zero = jnp.zeros((lanes_y, LANES), F32)

    def x_low(v):
        return jnp.concatenate([zero, v[: boxes - lanes_y]], axis=0)

    def x_high(v):
        return jnp.concatenate([v[lanes_y:], zero], axis=0)

    def y_low(v):
        return jnp.where(row == 0, 0.0, pltpu.roll(v, 1, 0))

    def y_high(v):
        return jnp.where(row == lanes_y - 1, 0.0, pltpu.roll(v, boxes - 1, 0))

    out = []
    for i in range(bx):
        for j in range(by):
            c = value[i * by + j]
            up = value[(i - 1) * by + j] if i else x_low(value[(bx - 1) * by + j])
            down = value[(i + 1) * by + j] if i < bx - 1 else x_high(value[j])
            left = value[i * by + j - 1] if j else y_low(value[i * by + by - 1])
            right = value[i * by + j + 1] if j < by - 1 else y_high(value[i * by])
            beside = up + down + left + right + pltpu.roll(c, 1, 1) + pltpu.roll(c, LANES - 1, 1)
            out.append(c + DIFFUSION * (beside - 6.0 * c) - speed[i * by + j] * (c - up))
    return out


def route(src_ref, first_row, row_step, item_step, items, own, quads, lanes_y, rows, lanes):
    shape = (lanes_y, LANES)
    out = []
    for k in range(len(rows)):

        def step(y, acc):
            for j in range(items):
                hit = rows[k] == (j * lanes_y + y)
                at = first_row + y * row_step + j * item_step
                lines = [src_ref[pl.ds(at + s * quads, 1), :] for s in range(own)]
                acc = [
                    jnp.where(
                        hit,
                        jnp.take_along_axis(jnp.broadcast_to(v, shape), lanes[k], axis=1),
                        old,
                    )
                    for v, old in zip(lines, acc)
                ]
            return tuple(acc)

        zero = tuple(jnp.zeros(shape, F32) for _ in range(own))
        out.append(lax.fori_loop(0, lanes_y, step, zero, unroll=min(lanes_y, 8)))
    return [[out[k][s] for k in range(len(rows))] for s in range(own)]


def load_rows(ref, offset, stride, count):
    return ref[pl.ds(offset, count, stride=stride), :]


def pack_body(
    width,
    lanes_y,
    grid_hbm,
    owner_hbm,
    slot_hbm,
    speed_hbm,
    out_ref,
    grid_ref,
    owner_ref,
    slot_ref,
    speed_ref,
    sem,
):
    pairs = [
        (grid_hbm, grid_ref),
        (owner_hbm, owner_ref),
        (slot_hbm, slot_ref),
        (speed_hbm, speed_ref),
    ]
    copies = [pltpu.make_async_copy(a, b, sem.at[i]) for i, (a, b) in enumerate(pairs)]
    for c in copies:
        c.start()
    for c in copies:
        c.wait()
    quads = owner_ref.shape[0]
    stride = width + 2 * quads
    total = grid_ref.shape[0]
    slot = slot_ref[...]
    label = ((slot >> 7) * lanes_y + owner_ref[...]) * LANES + (slot & (LANES - 1))
    tail = jnp.concatenate([label.astype(F32), speed_ref[...]], axis=0)
    for d in range(out_ref.shape[0] // stride):
        count = max(0, min(width, total - d * width))
        if count:
            out_ref[d * stride : d * stride + count] = grid_ref[d * width : d * width + count]
        if count < width:
            zeros = jnp.zeros((width - count, LANES), F32)
            out_ref[d * stride + count : d * stride + width] = zeros
        out_ref[d * stride + width : (d + 1) * stride] = tail


def weights_body(w1_ref, w2_ref, w3_ref, token_ref, a_ref, b_ref, c_ref):
    scalars, hidden = w1_ref.shape
    rest = jnp.zeros((a_ref.shape[1] - scalars, hidden), F32)
    a_ref[...] = jnp.concatenate([w1_ref[...].astype(F32) * 0.5, rest], axis=0).T.astype(BF)
    b_ref[...] = (w2_ref[...].astype(F32) * 0.5).astype(BF)
    c_ref[...] = jnp.concatenate([w3_ref[...].astype(F32), rest], axis=0).astype(BF)


def start_body(dims, arr_ref, token_ref, g_ref, f_ref, inv_ref, lab_ref):
    nx, ny, own, bx, by = dims
    quads = bx * by
    boxes = nx * ny
    width = own * quads
    stride = width + 2 * quads
    turns = quads * ny
    speed = [load_rows(arr_ref, width + quads + j, stride, boxes) for j in range(quads)]
    for s in range(own):
        value = [load_rows(arr_ref, s * quads + j, stride, boxes) for j in range(quads)]
        for j, v in enumerate(stencil(value, speed, bx, by, ny)):
            g_ref[pl.ds(s * quads + j, boxes, stride=width), :] = v
    for j in range(quads):
        lab_ref[pl.ds(j * boxes, boxes), :] = load_rows(arr_ref, width + j, stride, boxes).astype(
            I32
        )
    lane_of = lax.broadcasted_iota(I32, (turns, LANES), 1).astype(F32)
    sub_of = lax.broadcasted_iota(I32, (turns, LANES), 0)
    sub_lane = lax.broadcasted_iota(I32, (LANES, LANES), 0)

    def group(x, carry):
        def gather(y, acc):
            left, right = [], []
            for j in range(quads):
                line = lab_ref[pl.ds(j * boxes + x * ny + y, 1), :]
                hit = jnp.broadcast_to(line >> 7, (turns, LANES)) == sub_of
                code = (j * ny + y).astype(F32)
                left.append(
                    jnp.concatenate(
                        [jnp.where(hit, code, 0.0), jnp.where(hit, lane_of, 0.0)], axis=0
                    ).astype(BF)
                )
                right.append(
                    (jnp.broadcast_to(line & (LANES - 1), (LANES, LANES)) == sub_lane)
                    .astype(F32)
                    .astype(BF)
                )
            return acc + dot(
                jnp.concatenate(left, axis=1), jnp.concatenate(right, axis=1), NT
            )

        code = lax.fori_loop(0, ny, gather, jnp.zeros((2 * turns, LANES), F32), unroll=2)
        code = code.astype(I32)
        inv_ref[pl.ds(x * 2 * turns, 2 * turns), :] = code
        return carry

    lax.fori_loop(0, nx, group, 0)
    send_filtered(dims, g_ref, inv_ref, f_ref)


def send_filtered(dims, g_ref, inv_ref, f_ref):
    nx, ny, own, bx, by = dims
    quads = bx * by
    width = own * quads
    turns = quads * ny

    def group(x, carry):
        base = x * 2 * turns
        rows = [inv_ref[pl.ds(base + k * ny, ny), :] for k in range(quads)]
        lanes = [inv_ref[pl.ds(base + turns + k * ny, ny), :] for k in range(quads)]
        out = route(g_ref, x * ny * width, width, 1, quads, own, quads, ny, rows, lanes)
        for s in range(own):
            for k in range(quads):
                f_ref[pl.ds(x * ny * width + s * quads + k, ny, stride=width), :] = out[s][k]
        return carry

    lax.fori_loop(0, nx, group, 0)


def add_source(dims, s_ref, g_ref, lab_ref, out_ref):
    nx, ny, own, bx, by = dims
    quads = bx * by
    boxes = nx * ny
    width = own * quads
    stride = s_ref.shape[0] // boxes

    def group(x, carry):
        labels = [lab_ref[pl.ds(j * boxes + x * ny, ny), :] for j in range(quads)]
        rows = [v >> 7 for v in labels]
        lanes = [v & (LANES - 1) for v in labels]
        out = route(s_ref, x * ny * stride, stride, 1, quads, own, quads, ny, rows, lanes)
        for s in range(own):
            for k in range(quads):
                at = pl.ds(x * ny * width + s * quads + k, ny, stride=width)
                out_ref[at, :] = g_ref[at, :] + out[s][k]
        return carry

    lax.fori_loop(0, nx, group, 0)


def again_body(dims, s_ref, g_ref, arr_ref, inv_ref, lab_ref, token_ref, out_ref, f_ref, mid_ref):
    nx, ny, own, bx, by = dims
    quads = bx * by
    boxes = nx * ny
    width = own * quads
    stride = width + 2 * quads
    add_source(dims, s_ref, g_ref, lab_ref, mid_ref)
    speed = [load_rows(arr_ref, width + quads + j, stride, boxes) for j in range(quads)]
    for s in range(own):
        value = [load_rows(mid_ref, s * quads + j, width, boxes) for j in range(quads)]
        for j, v in enumerate(stencil(value, speed, bx, by, ny)):
            out_ref[pl.ds(s * quads + j, boxes, stride=width), :] = v
    send_filtered(dims, out_ref, inv_ref, f_ref)


def last_body(dims, s_ref, g_ref, lab_ref, token_ref, out_ref):
    add_source(dims, s_ref, g_ref, lab_ref, out_ref)


def per_device(
    grid_scalars,
    axial_speed,
    particles,
    cell_owner,
    cell_slot,
    mix_rate,
    partner,
    chem_input,
    chem_hidden,
    chem_output,
    react_slots,
    react_count,
    leave_slots,
    arrive_slots,
):
    both = ("gx", "gy")
    nx, ny = lax.axis_size("gx"), lax.axis_size("gy")
    devices = nx * ny
    scalars, bx, by, nz = grid_scalars.shape
    heads, cells = partner.shape
    listed = react_slots.shape[1]
    hidden = chem_hidden.shape[0]
    quads = bx * by
    own = -(-scalars // devices)
    rows = devices * own
    width = own * quads
    tiles = cells // LANES
    assert nz == LANES and tiles == quads and heads % SUB == 0 and LANES % heads == 0
    dims = (nx, ny, own, bx, by)
    flat = devices * width

    box = [
        grid_scalars.reshape(-1, LANES),
        cell_owner.reshape(quads, LANES),
        cell_slot.reshape(quads, LANES),
        axial_speed.reshape(quads, LANES),
    ]
    (first,) = call(
        functools.partial(pack_body, width, ny),
        [((devices * (width + 2 * quads), LANES), F32)],
        box,
        hbm=(0, 1, 2, 3),
        scratch=[pltpu.VMEM(x.shape, x.dtype) for x in box] + [pltpu.SemaphoreType.DMA((4,))],
        name="pack",
    )

    def exchange(x):
        x = x.reshape(devices, -1, LANES)
        return lax.all_to_all(x, both, split_axis=0, concat_axis=0, tiled=True).reshape(-1, LANES)

    arrival = exchange(first)

    rate = mix_rate.reshape(1, cells)
    lcol = leave_slots.reshape(devices, -1).T.reshape(-1, 1)
    acol = arrive_slots.reshape(devices, -1).T.reshape(-1, 1)
    state_shape = (scalars, heads, cells)
    listed_shape = (listed // LANES, heads * rows, LANES)
    block = divisor(scalars, 6)
    octets = heads // SUB
    state_vmem = pltpu.VMEM(state_shape, F32)
    listed_vmem = pltpu.VMEM(listed_shape, F32)
    dma = pltpu.SemaphoreType.DMA
    per_block = dma((scalars // block,))
    q, a, ot, rsel = call(
        functools.partial(open_body, rows, block),
        [
            (state_shape, F32, True),
            (listed_shape, F32, True),
            ((listed, cells), BF),
            ((SUB, listed), F32),
        ],
        [particles, partner, rate, react_slots],
        hbm=(0, 1, 2, 3),
        scratch=[
            state_vmem,
            state_vmem,
            listed_vmem,
            pltpu.VMEM(partner.shape, I32),
            pltpu.VMEM(rate.shape, F32),
            pltpu.VMEM(react_slots.shape, I32),
            per_block,
            per_block,
            dma,
            dma((3,)),
        ],
        name="open",
    )
    grid, sent, inv, lab = call(
        functools.partial(start_body, dims),
        [
            ((flat, LANES), F32),
            ((flat, LANES), F32),
            ((nx * 2 * quads * ny, LANES), I32),
            ((quads * devices, LANES), I32),
        ],
        [arrival, rsel],
        name="start",
    )

    w1, w2, w3 = call(
        weights_body,
        [((hidden, rows), BF), ((hidden, hidden), BF), ((rows, hidden), BF)],
        [chem_input.T, chem_hidden, chem_output, lab],
        name="weights",
    )

    per = LANES // heads
    span = SUB * (-(-scalars // (per * SUB)))
    places = leave_slots.shape[1]
    pair = pltpu.VMEM((hidden, 2 * listed), BF)

    def chemistry(f, a, token, leave=None, more=()):
        out = (flat + places * span, LANES) if leave else (flat, LANES)
        extra = [pltpu.VMEM((places * span, LANES), F32), dma] if leave else []
        return call(
            functools.partial(chem_body, leave),
            [(listed_shape, F32, True), (out, F32)],
            [react_count, f, a, ot, rsel, w1, w2, w3, token, *more],
            smem=(0,),
            hbm=(2, 9) if leave else (2,),
            scratch=[listed_vmem, listed_vmem, pltpu.VMEM((rows, listed), F32)]
            + [pair] * 4
            + [dma((octets,)), dma((octets,))]
            + extra,
            name="chem",
        )

    token = rsel
    for substep in range(SUBSTEPS - 1):
        f = exchange(sent)
        change, source = chemistry(f, a, token)
        home = exchange(source)
        q, token = call(
            functools.partial(middle_body, rows, block),
            [(state_shape, F32, True), ((1, LANES), F32)],
            [q, f, change, ot, rate, partner],
            hbm=(0, 2),
            scratch=[state_vmem, state_vmem, listed_vmem, per_block, per_block, dma],
            name="middle",
        )
        grid, sent = call(
            functools.partial(again_body, dims),
            [((flat, LANES), F32), ((flat, LANES), F32)],
            [home, grid, arrival, inv, lab, token],
            scratch=[pltpu.VMEM((flat, LANES), F32)],
            name="again",
        )
        a, base, token = call(
            functools.partial(list_body, rows, span),
            [(listed_shape, F32, True), ((places * span, LANES), F32, True), ((1, LANES), F32)],
            [q, rate, rsel, ot, lcol],
            hbm=(0,),
            scratch=[
                state_vmem,
                listed_vmem,
                pltpu.VMEM((places * span, LANES), F32),
                dma((-(-scalars // per),)),
                dma((2,)),
            ],
            name="list",
        )
    f = exchange(sent)
    leave = dict(devices=devices, span=span, scalars=scalars)
    change, leaving = chemistry(f, a, token, leave, [base, rate, lcol, react_slots])
    moved = exchange(leaving)
    state, token = call(
        functools.partial(settle_body, rows, block),
        [(state_shape, F32, True), ((1, LANES), F32)],
        [q, f, change, ot, rate],
        hbm=(0, 2),
        scratch=[state_vmem, state_vmem, listed_vmem, per_block, per_block, dma],
        name="settle",
    )
    (grid,) = call(
        functools.partial(last_body, dims),
        [((flat, LANES), F32)],
        [moved, grid, lab, token],
        name="last",
    )
    grid_out = exchange(grid).reshape(rows, bx, by, nz)[:scalars]
    steps = -(-scalars // per)
    (state,) = call(
        functools.partial(arrive_body, span, devices),
        [(state_shape, F32, True)],
        [state, moved, acol],
        hbm=(0,),
        scratch=[
            state_vmem,
            state_vmem,
            pltpu.VMEM((places, cells), BF),
            dma((steps,)),
            dma((steps,)),
        ],
        name="arrive",
    )
    return (grid_out, state)


def solution(mesh):
    placed = (
        P(None, "gx", "gy", None),
        P("gx", "gy", None),
        P(None, None, ("gx", "gy")),
        P("gx", "gy", None),
        P("gx", "gy", None),
        P(("gx", "gy")),
        P(None, ("gx", "gy")),
        P(),
        P(),
        P(),
        P(("gx", "gy"), None),
        P(("gx", "gy")),
        P(("gx", "gy"), None),
        P(("gx", "gy"), None),
    )
    return jax.shard_map(
        per_device,
        mesh=mesh,
        in_specs=placed,
        out_specs=(P(None, "gx", "gy", None), P(None, None, ("gx", "gy"))),
        check_vma=False,
    )
```

```python
import functools

import jax
import jax.numpy as jnp
from jax import lax
from jax.experimental import pallas as pl
from jax.experimental.pallas import tpu as pltpu
from jax.sharding import PartitionSpec as P

DIFFUSION = 0.1
PAIR_WEIGHT = 0.4
LANES = 128
SUB = 8
BF = jnp.bfloat16
F32 = jnp.float32
I32 = jnp.int32

NT = (((1,), (1,)), ((), ()))
NN = (((1,), (0,)), ((), ()))


def call(body, outs, ins, smem=(), hbm=(), scratch=(), limit=24, name=None):
    spaces = {**{i: pltpu.SMEM for i in smem}, **{i: pl.ANY for i in hbm}}
    ins = [pltpu.with_memory_space_constraint(x, pltpu.HBM) if i in hbm else x for i, x in enumerate(ins)]
    return pl.pallas_call(
        body,
        out_shape=[
            pltpu.HBM(o[0], o[1]) if len(o) > 2 else jax.ShapeDtypeStruct(o[0], o[1]) for o in outs
        ],
        in_specs=[
            pl.BlockSpec(memory_space=spaces.get(i, pltpu.VMEM)) for i in range(len(ins))
        ],
        out_specs=[
            pl.BlockSpec(memory_space=pl.ANY if len(o) > 2 else pltpu.VMEM) for o in outs
        ],
        scratch_shapes=list(scratch),
        compiler_params=pltpu.CompilerParams(vmem_limit_bytes=limit << 20),
        name=name,
    )(*ins)


class Stream:
    def __init__(self, src, dst, sem, size, dim=0):
        self.src, self.dst, self.sem, self.size, self.dim = src, dst, sem, size, dim
        self.count = -(-src.shape[dim] // size)

    def copy(self, i, size=None):
        at = (slice(None),) * self.dim + (pl.ds(i * self.size, size or self.size),)
        return pltpu.make_async_copy(self.src.at[at], self.dst.at[at], self.sem.at[i])

    def tail(self, i):
        return min(self.size, self.src.shape[self.dim] - i * self.size)

    def start_all(self):
        for i in range(self.count):
            self.copy(i, self.tail(i)).start()

    def wait_all(self, first=0):
        for i in range(first, self.count):
            self.copy(i, self.tail(i)).wait()


def dot(a, b, dims):
    return lax.dot_general(a, b, dims, preferred_element_type=F32)


def halves(x):
    high = x.astype(BF)
    return high, (x - high.astype(F32)).astype(BF)


def dot_split(x, onehot, dims):
    high, low = halves(x)
    y = dot(jnp.concatenate([high, low], axis=0), onehot, dims)
    return y[: x.shape[0]] + y[x.shape[0] :]


def load_filtered(f_ref, devices, rows, tiles):
    stride = f_ref.shape[0] // devices
    return jnp.concatenate(
        [
            jnp.concatenate(
                [
                    f_ref[pl.ds(i * tiles + t, devices, stride=stride), :]
                    for i in range(rows // devices)
                ],
                axis=0,
            )
            for t in range(tiles)
        ],
        axis=1,
    )


def divisor(n, most):
    return max(k for k in range(1, most + 1) if n % k == 0)


def mix(s0, block, p_ref, partner_ref, q_ref):
    scalars, particles, cells = p_ref.shape
    groups = particles // SUB
    for t in range(cells // LANES):
        lanes = pl.ds(t * LANES, LANES)
        rows, homes = [], []
        for j in range(groups):
            index = partner_ref[pl.ds(j * SUB, SUB), lanes]
            rows.append(index & (SUB - 1))
            homes.append(index >> 3)

        def step(s, carry):
            x = [p_ref[s, pl.ds(k * SUB, SUB), lanes] for k in range(groups)]
            for j in range(groups):
                mate = jnp.take_along_axis(x[0], rows[j], axis=0)
                for k in range(1, groups):
                    other = jnp.take_along_axis(x[k], rows[j], axis=0)
                    mate = jnp.where(homes[j] == k, other, mate)
                q_ref[s, pl.ds(j * SUB, SUB), lanes] = x[j] + PAIR_WEIGHT * (mate - x[j])
            return carry

        lax.fori_loop(s0, s0 + block, step, 0)


def put_scalar(ref, s, value, rows):
    for o in range(value.shape[0] // SUB):
        for t in range(value.shape[1] // LANES):
            part = value[o * SUB : (o + 1) * SUB, t * LANES : (t + 1) * LANES]
            ref[t, pl.ds(o * rows * SUB + s * SUB, SUB), :] = part


def get_scalar(ref, s, rows):
    octets = ref.shape[1] // (rows * SUB)
    return jnp.concatenate(
        [
            jnp.concatenate(
                [ref[t, pl.ds(o * rows * SUB + s * SUB, SUB), :] for t in range(ref.shape[0])],
                axis=1,
            )
            for o in range(octets)
        ],
        axis=0,
    )


def particle_rows(p, rows):
    return pl.ds((p >> 3) * (rows * SUB) + (p & (SUB - 1)), rows, stride=SUB)


def list_cells(s0, block, q_ref, onehot, keep, a_ref, rows):
    scalars, particles, cells = q_ref.shape
    x = q_ref[pl.ds(s0, block)].reshape(block * particles, cells)
    y = dot_split(x, onehot, NT) * keep
    for i in range(block):
        put_scalar(a_ref, s0 + i, y[i * particles : (i + 1) * particles], rows)


def list_body(
    rows,
    q_hbm,
    rate_ref,
    rsel_ref,
    ot_ref,
    lcol_ref,
    a_hbm,
    base_hbm,
    token_ref,
    q_ref,
    a_ref,
    base_ref,
    in_sem,
    out_sem,
):
    scalars, particles, cells = q_ref.shape
    per = LANES // particles
    into = Stream(q_hbm, q_ref, in_sem, per)
    into.start_all()
    token_ref[...] = rate_ref[:, :LANES]
    leaves = cell_onehot(lcol_ref, cells)
    places = lcol_ref.shape[0]
    side = max(1, LANES // places)
    keep = 1.0 - rate_ref[...]

    def part(b, count):
        into.copy(b, count).wait()
        x = q_ref[pl.ds(b * per, count)].reshape(count * particles, cells) * keep
        high, low = halves(x)
        both = jnp.concatenate([high, low], axis=0)
        half = count * particles
        y = dot(both, ot_ref[...], NT)
        y = y[:half] + y[half:]
        z = dot(both, leaves, NT)
        z = z[:half] + z[half:]
        for i in range(count):
            put_scalar(a_ref, b * per + i, y[i * particles : (i + 1) * particles], rows)
            for o in range(0, particles // SUB, side):
                first = i * particles + o * SUB
                octets = [z[first + u * SUB : first + (u + 1) * SUB] for u in range(side)]
                at = pl.ds(o // side * rows * SUB + (b * per + i) * SUB, SUB)
                wide = jnp.concatenate(octets, axis=1)
                for t in range(base_ref.shape[0]):
                    base_ref[t, at, :] = wide[:, t * LANES : (t + 1) * LANES]

    def step(b, carry):
        part(b, per)
        return carry

    whole = scalars // per
    lax.fori_loop(0, whole, step, 0)
    if scalars > whole * per:
        part(whole, scalars - whole * per)
    clear_rest(scalars, rows, a_ref)
    for o in range(particles // SUB // side):
        rest = (rows - scalars) * SUB
        at = pl.ds(o * rows * SUB + scalars * SUB, rest)
        base_ref[:, at, :] = jnp.zeros((base_ref.shape[0], rest, LANES), F32)
    copies = [
        pltpu.make_async_copy(a_ref, a_hbm, out_sem.at[0]),
        pltpu.make_async_copy(base_ref, base_hbm, out_sem.at[1]),
    ]
    for c in copies:
        c.start()
    for c in copies:
        c.wait()


def clear_rest(scalars, rows, a_ref):
    particles = a_ref.shape[1] // rows
    zeros = jnp.zeros((particles, a_ref.shape[0] * LANES), F32)
    for s in range(scalars, rows):
        put_scalar(a_ref, s, zeros, rows)


def open_body(
    rows,
    block,
    p_hbm,
    partner_hbm,
    rate_hbm,
    list_hbm,
    q_hbm,
    a_hbm,
    ot_ref,
    rsel_ref,
    p_ref,
    q_ref,
    a_ref,
    partner_ref,
    rate_ref,
    list_ref,
    in_sem,
    out_sem,
    a_sem,
    few_sem,
):
    scalars, particles, cells = p_ref.shape
    into, out = Stream(p_hbm, p_ref, in_sem, block), Stream(q_ref, q_hbm, out_sem, block)
    few = [
        pltpu.make_async_copy(src, dst, few_sem.at[i])
        for i, (src, dst) in enumerate(
            [(list_hbm, list_ref), (rate_hbm, rate_ref), (partner_hbm, partner_ref)]
        )
    ]
    for c in few:
        c.start()
    into.start_all()
    for c in few:
        c.wait()
    column = jnp.broadcast_to(list_ref[...].astype(F32), (SUB, list_ref.shape[1])).T[:, :1]
    cell = lax.broadcasted_iota(I32, ot_ref.shape, 1).astype(F32)
    onehot = (column == cell).astype(F32)
    ot_ref[...] = onehot.astype(BF)
    rate = jnp.broadcast_to(rate_ref[...], (SUB, cells))
    rsel_ref[...] = dot_split(rate, onehot.astype(BF), NT)
    clear_rest(scalars, rows, a_ref)

    def step(b, carry):
        into.copy(b).wait()
        mix(b * block, block, p_ref, partner_ref, q_ref)
        out.copy(b).start()
        list_cells(b * block, block, q_ref, ot_ref[...], 1.0 - rsel_ref[0:1, :], a_ref, rows)
        return carry

    lax.fori_loop(0, scalars // block, step, 0)
    last = pltpu.make_async_copy(a_ref, a_hbm, a_sem)
    last.start()
    out.wait_all()
    last.wait()


def settle_block(s0, block, q_ref, f_ref, r_ref, ot_ref, rate_ref, out_ref, rows, devices):
    scalars, particles, cells = q_ref.shape
    tiles = cells // LANES
    rate = rate_ref[...]
    keep = 1.0 - rate
    r = jnp.concatenate([get_scalar(r_ref, s0 + i, rows) for i in range(block)], axis=0)
    spread = dot(r.astype(BF), ot_ref[...], NN)
    for i in range(block):
        s = s0 + i
        at = lax.rem(s, devices) * (f_ref.shape[0] // devices) + lax.div(s, devices) * tiles
        f = jnp.concatenate([f_ref[pl.ds(at + t, 1), :] for t in range(tiles)], axis=1)
        out_ref[s0 + i] = (
            keep * q_ref[s0 + i] + rate * f + spread[i * particles : (i + 1) * particles]
        )


def middle_body(
    rows,
    block,
    devices,
    q_hbm,
    f_ref,
    r_hbm,
    ot_ref,
    rate_ref,
    partner_ref,
    out_hbm,
    token_ref,
    q_ref,
    now_ref,
    r_ref,
    in_sem,
    out_sem,
    r_sem,
):
    scalars = q_ref.shape[0]
    into, out = Stream(q_hbm, q_ref, in_sem, block), Stream(q_ref, out_hbm, out_sem, block)
    first = pltpu.make_async_copy(r_hbm, r_ref, r_sem)
    first.start()
    into.start_all()
    token_ref[...] = rate_ref[:, :LANES]
    first.wait()

    def step(b, carry):
        into.copy(b).wait()
        s0 = b * block
        settle_block(s0, block, q_ref, f_ref, r_ref, ot_ref, rate_ref, now_ref, rows, devices)
        mix(s0, block, now_ref, partner_ref, q_ref)
        out.copy(b).start()
        return carry

    lax.fori_loop(0, scalars // block, step, 0)
    out.wait_all()


def half_silu(y):
    return (y + y * jnp.tanh(y)).astype(BF)


def chem_body(
    devices,
    rows,
    count_ref,
    f_ref,
    a_hbm,
    ot_ref,
    rsel_ref,
    w1_ref,
    w2_ref,
    w3_ref,
    token_ref,
    *refs,
):
    pos_refs, refs = refs[:-11], refs[-11:]
    r_hbm, s_ref, a_ref, r_ref, pull_ref, one_a, one_b, two_a, two_b, in_sem, out_sem = refs
    tiles = ot_ref.shape[1] // LANES
    listed = ot_ref.shape[0]
    particles = a_ref.shape[1] // rows
    into = Stream(a_hbm, a_ref, in_sem, SUB * rows, 1)
    out = Stream(r_ref, r_hbm, out_sem, SUB * rows, 1)
    into.start_all()
    f = load_filtered(f_ref, devices, rows, tiles)
    pull_ref[...] = rsel_ref[0:1, :] * dot_split(f, ot_ref[...], NT)
    live = lax.broadcasted_iota(I32, (1, listed), 1) < count_ref[0]

    def first(g):
        parts = []
        for i in range(2):
            at = particle_rows(2 * g + i, rows)
            for t in range(listed // LANES):
                pull = pull_ref[:, t * LANES : (t + 1) * LANES]
                parts.append((a_ref[t, at, :] + pull).astype(BF))
        return half_silu(dot(w1_ref[...], jnp.concatenate(parts, axis=1), NN))

    def second(one):
        return half_silu(dot(w2_ref[...], one, NN))

    def third(g, two, total):
        change = dot(w3_ref[...], two, NN).astype(BF).astype(F32)
        for i in range(2):
            r = jnp.where(live, change[:, i * listed : (i + 1) * listed], 0.0)
            at = particle_rows(2 * g + i, rows)
            for t in range(listed // LANES):
                r_ref[t, at, :] = r[:, t * LANES : (t + 1) * LANES]
            total = total + r
        return total

    def step(g, total, old, new):
        total = third(g - 2, old[1][...], total)
        new[1][...] = second(old[0][...])
        new[0][...] = first(g)
        return total

    left, right = (one_a, two_a), (one_b, two_b)

    def pair(m, total):
        total = step(2 * m, total, right, left)
        return step(2 * m + 1, total, left, right)

    total = jnp.zeros((rows, listed), F32)
    each = SUB // 4
    for o in range(particles // SUB):
        into.copy(o).wait()
        if o == 0:
            one_a[...] = first(0)
            two_b[...] = second(one_a[...])
            one_b[...] = first(1)
        total = lax.fori_loop(max(1, o * each), (o + 1) * each, pair, total)
        if o:
            out.copy(o - 1).start()
    last = particles // 2 - 1
    total = third(last - 1, two_b[...], total)
    total = third(last, second(one_b[...]), total)
    out.copy(particles // SUB - 1).start()
    source = total * (1.0 / particles)
    if pos_refs:
        boxes_source(source, *pos_refs, s_ref)
    else:
        source = dot_split(source, ot_ref[...], NN)
        stride = s_ref.shape[0] // devices
        for i in range(rows // devices):
            for t in range(tiles):
                part = source[i * devices : (i + 1) * devices, t * LANES : (t + 1) * LANES]
                s_ref[pl.ds(i * tiles + t, devices, stride=stride), :] = part
    out.wait_all()


def boxes_source(source, pos_ref, s_ref):
    listed = source.shape[1]
    boxes = s_ref.shape[0]
    put = lax.broadcasted_iota(I32, (listed, boxes * LANES), 1).astype(F32) == pos_ref[:, :1]
    sent = dot_split(source, put.astype(F32).astype(BF), NN)
    for b in range(boxes):
        s_ref[b] = sent[: s_ref.shape[1], b * LANES : (b + 1) * LANES]


def early_body(
    devices,
    rows,
    span,
    scalars,
    particles,
    count_ref,
    f_ref,
    base_ref,
    ot_ref,
    rate_ref,
    lcol_ref,
    w1_ref,
    w2_ref,
    w3_ref,
    token_ref,
    out_ref,
    end_ref,
    v_ref,
):
    listed, cells = ot_ref.shape
    tiles = cells // LANES
    places = lcol_ref.shape[0]
    side = max(1, LANES // places)
    wide = base_ref.shape[0]
    end_ref[...] = rate_ref[:, :LANES]
    f = load_filtered(f_ref, devices, rows, tiles)
    leaves = cell_onehot(lcol_ref, cells)
    rate = dot_split(jnp.broadcast_to(rate_ref[...], (SUB, cells)), leaves, NT)[:1]
    pull = rate * dot_split(f, leaves, NT)
    live = (lax.broadcasted_iota(I32, (SUB, listed), 1) < count_ref[0]).astype(F32).astype(BF)
    live = dot(dot(live, ot_ref[...], NN).astype(BF), leaves, NT)[:1]
    pull = jnp.concatenate([pull] * side, axis=1)
    live = jnp.concatenate([live] * side, axis=1) > 0.5
    count = 4 // wide

    for o in range(particles // SUB // side):
        for i in range(0, SUB, count):
            ats = [pl.ds(o * rows * SUB + i + u, rows, stride=SUB) for u in range(count)]
            x = jnp.concatenate(
                [base_ref[t, at, :] + pull[:, t * LANES : (t + 1) * LANES] for at in ats for t in range(wide)],
                axis=1,
            )
            one = half_silu(dot(w1_ref[...], x.astype(BF), NN))
            two = half_silu(dot(w2_ref[...], one, NN))
            change = dot(w3_ref[...], two, NN).astype(BF).astype(F32)
            for n, (at, t) in enumerate((at, t) for at in ats for t in range(wide)):
                cols = slice(n * LANES, (n + 1) * LANES)
                mask = live[:, t * LANES : (t + 1) * LANES]
                v_ref[t, at, :] = x[:, cols] + jnp.where(mask, change[:, cols], 0.0)

    per = LANES // particles
    stride = out_ref.shape[0] // devices

    def scalar(s):
        parts = []
        for o in range(particles // SUB // side):
            at = pl.ds(o * rows * SUB + s * SUB, SUB)
            row = jnp.concatenate([v_ref[t, at, :] for t in range(wide)], axis=1)
            parts += [row[:, u * places : (u + 1) * places] for u in range(side)]
        return jnp.concatenate(parts, axis=0)

    def part(b, count):
        value = jnp.concatenate([scalar(b * per + i) for i in range(count)], axis=0)
        if count < per:
            rest = jnp.zeros(((per - count) * particles, places), F32)
            value = jnp.concatenate([value, rest], axis=0)
        value = value.T
        for c in range(places // devices):
            at = pl.ds(c * span + b, devices, stride=stride)
            out_ref[at, :] = value[c * devices : (c + 1) * devices]

    def step(b, carry):
        part(b, per)
        return carry

    whole = scalars // per
    lax.fori_loop(0, whole, step, 0, unroll=2)
    zeros = jnp.zeros((devices, LANES), F32)
    for c in range(places // devices):
        for b in range(whole, span):
            out_ref[pl.ds(c * span + b, devices, stride=stride), :] = zeros
    if scalars > whole * per:
        part(whole, scalars - whole * per)


def maps_body(dims, me_ref, inv_ref, ot_ref, owner_ref, slot_ref, pos_ref, put_ref):
    nx, ny, own, bx, by = dims
    quads = bx * by
    turns = quads * ny
    listed, cells = ot_ref.shape
    at = me_ref[0] * 2 * turns + me_ref[1]
    code = jnp.concatenate([inv_ref[pl.ds(at + k * ny, 1), :] for k in range(quads)], axis=1)
    box = lax.rem(code, ny).astype(F32)
    boxes = lax.broadcasted_iota(I32, (ny, cells), 0).astype(F32)
    mine = (jnp.broadcast_to(box, (ny, cells)) == boxes).astype(F32)
    before = lax.broadcasted_iota(I32, (cells, cells), 0) < lax.broadcasted_iota(
        I32, (cells, cells), 1
    )
    count = dot(mine.astype(BF), before.astype(F32).astype(BF), NN)
    rank = jnp.sum(mine * count, axis=0, keepdims=True)
    rest = jnp.zeros((SUB - 2, cells), F32)
    found = dot(ot_ref[...], jnp.concatenate([box, rank, rest], axis=0).astype(BF), NT)
    pos = found[:, :1] * LANES + found[:, 1:2]
    pos_ref[...] = jnp.broadcast_to(pos, pos_ref.shape)
    flat = lambda ref: jnp.concatenate([ref[j : j + 1, :] for j in range(quads)], axis=1)
    owner, slot = flat(owner_ref).astype(F32), flat(slot_ref).astype(F32)
    first = owner * cells
    key = first + slot
    column = jnp.broadcast_to(key, (SUB, cells)).T[:, :1]
    ahead = (column < key) & (column >= first)
    place = owner * LANES + jnp.sum(ahead.astype(F32), axis=0, keepdims=True)
    step = min(cells, put_ref.shape[0])
    for b in range(put_ref.shape[0] // step):
        row = lax.broadcasted_iota(I32, (step, cells), 0).astype(F32) + b * step
        put_ref[b * step : (b + 1) * step] = (row == place).astype(F32).astype(BF)


def unpack_body(devices, own, s_ref, arr_ref, put_ref, out_ref):
    boxes, rows = s_ref.shape[:2]
    cells = put_ref.shape[1]
    quads = cells // LANES
    scalars = out_ref.shape[0] // quads
    stride = arr_ref.shape[0] // devices
    got = jnp.concatenate([s_ref[b] for b in range(boxes)], axis=1)
    source = dot_split(got, put_ref[...], NN)
    for j in range(quads):
        for i in range(own):
            n = min(devices, scalars - i * devices)
            if n > 0:
                grid = arr_ref[pl.ds(stride - own * quads + i * quads + j, n, stride=stride), :]
                part = source[i * devices : i * devices + n, j * LANES : (j + 1) * LANES]
                out_ref[pl.ds(i * devices * quads + j, n, stride=quads), :] = grid + part


def cell_onehot(col_ref, cells):
    shape = (col_ref.shape[0], cells)
    return (col_ref[...] == lax.broadcasted_iota(I32, shape, 1)).astype(F32).astype(BF)


def settle_body(
    rows,
    block,
    devices,
    q_hbm,
    f_ref,
    r_hbm,
    ot_ref,
    rate_ref,
    out_hbm,
    token_ref,
    q_ref,
    out_ref,
    r_ref,
    in_sem,
    out_sem,
    r_sem,
):
    into, out = Stream(q_hbm, q_ref, in_sem, block), Stream(out_ref, out_hbm, out_sem, block)
    first = pltpu.make_async_copy(r_hbm, r_ref, r_sem)
    first.start()
    into.start_all()
    token_ref[...] = rate_ref[:, :LANES]
    first.wait()

    def step(b, carry):
        into.copy(b).wait()
        settle_block(b * block, block, q_ref, f_ref, r_ref, ot_ref, rate_ref, out_ref, rows, devices)
        out.copy(b).start()
        return carry

    lax.fori_loop(0, q_ref.shape[0] // block, step, 0)
    out.wait_all()


def arrive_body(
    span, devices, p_hbm, arr_ref, acol_ref, out_hbm, p_ref, out_ref, hit_ref, in_sem, out_sem
):
    scalars, particles, cells = p_ref.shape
    places = acol_ref.shape[0]
    per = LANES // particles
    into, out = Stream(p_hbm, p_ref, in_sem, per), Stream(out_ref, out_hbm, out_sem, per)
    into.start_all()
    hit = (acol_ref[...] == lax.broadcasted_iota(I32, (places, cells), 1)).astype(F32)
    hit_ref[...] = hit.astype(BF)
    taken = jnp.sum(hit, axis=0, keepdims=True) > 0.5
    stride = arr_ref.shape[0] // devices
    count = places // devices

    def place(b, size):
        first = stride - count * span + b
        x = jnp.concatenate(
            [arr_ref[pl.ds(first + c * span, devices, stride=stride), :] for c in range(count)],
            axis=0,
        ).T
        y = dot_split(x, hit_ref[...], NN)
        into.copy(b, size).wait()
        for i in range(size):
            s = b * per + i
            out_ref[s] = jnp.where(taken, y[i * particles : (i + 1) * particles], p_ref[s])
        out.copy(b, size).start()

    def step(b, carry):
        place(b, per)
        return carry

    whole = scalars // per
    lax.fori_loop(0, whole, step, 0)
    if scalars > whole * per:
        place(whole, scalars - whole * per)
    out.wait_all()


def stencil(value, speed, bx, by, lanes_y):
    boxes = value[0].shape[0]
    row = lax.broadcasted_iota(I32, value[0].shape, 0) % lanes_y
    zero = jnp.zeros((lanes_y, LANES), F32)

    def x_low(v):
        return jnp.concatenate([zero, v[: boxes - lanes_y]], axis=0)

    def x_high(v):
        return jnp.concatenate([v[lanes_y:], zero], axis=0)

    def y_low(v):
        return jnp.where(row == 0, 0.0, pltpu.roll(v, 1, 0))

    def y_high(v):
        return jnp.where(row == lanes_y - 1, 0.0, pltpu.roll(v, boxes - 1, 0))

    out = []
    for i in range(bx):
        for j in range(by):
            c = value[i * by + j]
            up = value[(i - 1) * by + j] if i else x_low(value[(bx - 1) * by + j])
            down = value[(i + 1) * by + j] if i < bx - 1 else x_high(value[j])
            left = value[i * by + j - 1] if j else y_low(value[i * by + by - 1])
            right = value[i * by + j + 1] if j < by - 1 else y_high(value[i * by])
            beside = up + down + left + right + pltpu.roll(c, 1, 1) + pltpu.roll(c, LANES - 1, 1)
            out.append(c + DIFFUSION * (beside - 6.0 * c) - speed[i * by + j] * (c - up))
    return out


def route(src_ref, first_row, row_step, item_step, items, own, quads, lanes_y, rows, lanes):
    shape = (lanes_y, LANES)
    out = []
    for k in range(len(rows)):

        def step(y, acc):
            for j in range(items):
                hit = rows[k] == (j * lanes_y + y)
                at = first_row + y * row_step + j * item_step
                lines = [src_ref[pl.ds(at + s * quads, 1), :] for s in range(own)]
                acc = [
                    jnp.where(
                        hit,
                        jnp.take_along_axis(jnp.broadcast_to(v, shape), lanes[k], axis=1),
                        old,
                    )
                    for v, old in zip(lines, acc)
                ]
            return tuple(acc)

        zero = tuple(jnp.zeros(shape, F32) for _ in range(own))
        out.append(lax.fori_loop(0, lanes_y, step, zero, unroll=min(lanes_y, 8)))
    return [[out[k][s] for k in range(len(rows))] for s in range(own)]


def load_rows(ref, offset, stride, count):
    return ref[pl.ds(offset, count, stride=stride), :]


def pack_body(
    width,
    lanes_y,
    grid_hbm,
    owner_hbm,
    slot_hbm,
    speed_hbm,
    out_ref,
    grid_ref,
    owner_ref,
    slot_ref,
    speed_ref,
    sem,
):
    pairs = [
        (grid_hbm, grid_ref),
        (owner_hbm, owner_ref),
        (slot_hbm, slot_ref),
        (speed_hbm, speed_ref),
    ]
    copies = [pltpu.make_async_copy(a, b, sem.at[i]) for i, (a, b) in enumerate(pairs)]
    for c in copies:
        c.start()
    for c in copies:
        c.wait()
    quads = owner_ref.shape[0]
    stride = width + 2 * quads
    total = grid_ref.shape[0]
    slot = slot_ref[...]
    label = ((slot >> 7) * lanes_y + owner_ref[...]) * LANES + (slot & (LANES - 1))
    tail = jnp.concatenate([label.astype(F32), speed_ref[...]], axis=0)
    devices = out_ref.shape[0] // stride
    for d in range(devices):
        for i in range(width // quads):
            at = d * stride + i * quads
            src = (i * devices + d) * quads
            if src < total:
                out_ref[at : at + quads] = grid_ref[src : src + quads]
            else:
                out_ref[at : at + quads] = jnp.zeros((quads, LANES), F32)
        out_ref[d * stride + width : (d + 1) * stride] = tail


def weights_body(w1_ref, w2_ref, w3_ref, token_ref, a_ref, b_ref, c_ref):
    scalars, hidden = w1_ref.shape
    rest = jnp.zeros((a_ref.shape[1] - scalars, hidden), F32)
    a_ref[...] = jnp.concatenate([w1_ref[...].astype(F32) * 0.5, rest], axis=0).T.astype(BF)
    b_ref[...] = (w2_ref[...].astype(F32) * 0.5).astype(BF)
    c_ref[...] = jnp.concatenate([w3_ref[...].astype(F32), rest], axis=0).astype(BF)


def start_body(dims, arr_ref, token_ref, g_ref, f_ref, inv_ref, lab_ref):
    nx, ny, own, bx, by = dims
    quads = bx * by
    boxes = nx * ny
    width = own * quads
    stride = width + 2 * quads
    turns = quads * ny
    speed = [load_rows(arr_ref, width + quads + j, stride, boxes) for j in range(quads)]
    for s in range(own):
        value = [load_rows(arr_ref, s * quads + j, stride, boxes) for j in range(quads)]
        for j, v in enumerate(stencil(value, speed, bx, by, ny)):
            g_ref[pl.ds(s * quads + j, boxes, stride=width), :] = v
    for j in range(quads):
        lab_ref[pl.ds(j * boxes, boxes), :] = load_rows(arr_ref, width + j, stride, boxes).astype(
            I32
        )
    lane_of = lax.broadcasted_iota(I32, (turns, LANES), 1).astype(F32)
    sub_of = lax.broadcasted_iota(I32, (turns, LANES), 0)
    sub_lane = lax.broadcasted_iota(I32, (LANES, LANES), 0)

    def group(x, carry):
        def gather(y, acc):
            left, right = [], []
            for j in range(quads):
                line = lab_ref[pl.ds(j * boxes + x * ny + y, 1), :]
                hit = jnp.broadcast_to(line >> 7, (turns, LANES)) == sub_of
                code = (j * ny + y).astype(F32)
                left.append(
                    jnp.concatenate(
                        [jnp.where(hit, code, 0.0), jnp.where(hit, lane_of, 0.0)], axis=0
                    ).astype(BF)
                )
                right.append(
                    (jnp.broadcast_to(line & (LANES - 1), (LANES, LANES)) == sub_lane)
                    .astype(F32)
                    .astype(BF)
                )
            return acc + dot(
                jnp.concatenate(left, axis=1), jnp.concatenate(right, axis=1), NT
            )

        code = lax.fori_loop(0, ny, gather, jnp.zeros((2 * turns, LANES), F32), unroll=2)
        code = code.astype(I32)
        inv_ref[pl.ds(x * 2 * turns, 2 * turns), :] = code
        return carry

    lax.fori_loop(0, nx, group, 0)
    send_filtered(dims, g_ref, width, 0, inv_ref, f_ref)


def send_filtered(dims, g_ref, g_stride, g_first, inv_ref, f_ref):
    nx, ny, own, bx, by = dims
    quads = bx * by
    width = own * quads
    turns = quads * ny
    f_stride = f_ref.shape[0] // (nx * ny)

    def group(x, carry):
        base = x * 2 * turns
        rows = [inv_ref[pl.ds(base + k * ny, ny), :] for k in range(quads)]
        lanes = [inv_ref[pl.ds(base + turns + k * ny, ny), :] for k in range(quads)]
        first = x * ny * g_stride + g_first
        out = route(g_ref, first, g_stride, 1, quads, own, quads, ny, rows, lanes)
        for s in range(own):
            for k in range(quads):
                at = pl.ds(x * ny * f_stride + s * quads + k, ny, stride=f_stride)
                f_ref[at, :] = out[s][k]
        return carry

    lax.fori_loop(0, nx, group, 0)


def add_source(dims, s_ref, g_ref, lab_ref, out_ref):
    nx, ny, own, bx, by = dims
    quads = bx * by
    boxes = nx * ny
    width = own * quads
    stride = s_ref.shape[0] // boxes

    def group(x, carry):
        labels = [lab_ref[pl.ds(j * boxes + x * ny, ny), :] for j in range(quads)]
        rows = [v >> 7 for v in labels]
        lanes = [v & (LANES - 1) for v in labels]
        out = route(s_ref, x * ny * stride, stride, 1, quads, own, quads, ny, rows, lanes)
        for s in range(own):
            for k in range(quads):
                at = pl.ds(x * ny * width + s * quads + k, ny, stride=width)
                out_ref[at, :] = g_ref[at, :] + out[s][k]
        return carry

    lax.fori_loop(0, nx, group, 0)


def again_body(dims, s_ref, g_ref, arr_ref, inv_ref, lab_ref, token_ref, f_ref, mid_ref):
    nx, ny, own, bx, by = dims
    quads = bx * by
    boxes = nx * ny
    width = own * quads
    stride = width + 2 * quads
    add_source(dims, s_ref, g_ref, lab_ref, mid_ref)
    speed = [load_rows(arr_ref, width + quads + j, stride, boxes) for j in range(quads)]
    for s in range(own):
        value = [load_rows(mid_ref, s * quads + j, width, boxes) for j in range(quads)]
        for j, v in enumerate(stencil(value, speed, bx, by, ny)):
            f_ref[pl.ds(width + s * quads + j, boxes, stride=2 * width), :] = v
    send_filtered(dims, f_ref, 2 * width, width, inv_ref, f_ref)


def per_device(
    grid_scalars,
    axial_speed,
    particles,
    cell_owner,
    cell_slot,
    mix_rate,
    partner,
    chem_input,
    chem_hidden,
    chem_output,
    react_slots,
    react_count,
    leave_slots,
    arrive_slots,
):
    both = ("gx", "gy")
    nx, ny = lax.axis_size("gx"), lax.axis_size("gy")
    devices = nx * ny
    scalars, bx, by, nz = grid_scalars.shape
    heads, cells = partner.shape
    listed = react_slots.shape[1]
    hidden = chem_hidden.shape[0]
    quads = bx * by
    own = -(-scalars // devices)
    rows = devices * own
    width = own * quads
    tiles = cells // LANES
    assert nz == LANES and tiles == quads and heads % SUB == 0 and LANES % heads == 0
    dims = (nx, ny, own, bx, by)
    flat = devices * width

    box = [
        grid_scalars.reshape(-1, LANES),
        cell_owner.reshape(quads, LANES),
        cell_slot.reshape(quads, LANES),
        axial_speed.reshape(quads, LANES),
    ]
    (first,) = call(
        functools.partial(pack_body, width, ny),
        [((devices * (width + 2 * quads), LANES), F32)],
        box,
        hbm=(0, 1, 2, 3),
        scratch=[pltpu.VMEM(x.shape, x.dtype) for x in box] + [pltpu.SemaphoreType.DMA((4,))],
        name="pack",
    )

    def exchange(x):
        x = x.reshape(devices, -1, LANES)
        return lax.all_to_all(x, both, split_axis=0, concat_axis=0, tiled=True).reshape(-1, LANES)

    arrival = exchange(first)

    rate = mix_rate.reshape(1, cells)
    lcol = leave_slots.reshape(devices, -1).T.reshape(-1, 1)
    acol = arrive_slots.reshape(devices, -1).T.reshape(-1, 1)
    state_shape = (scalars, heads, cells)
    listed_shape = (listed // LANES, heads * rows, LANES)
    block = divisor(scalars, 6)
    octets = heads // SUB
    state_vmem = pltpu.VMEM(state_shape, F32)
    listed_vmem = pltpu.VMEM(listed_shape, F32)
    dma = pltpu.SemaphoreType.DMA
    per_block = dma((scalars // block,))
    q, a, ot, rsel = call(
        functools.partial(open_body, rows, block),
        [
            (state_shape, F32, True),
            (listed_shape, F32, True),
            ((listed, cells), BF),
            ((SUB, listed), F32),
        ],
        [particles, partner, rate, react_slots],
        hbm=(0, 1, 2, 3),
        scratch=[
            state_vmem,
            state_vmem,
            listed_vmem,
            pltpu.VMEM(partner.shape, I32),
            pltpu.VMEM(rate.shape, F32),
            pltpu.VMEM(react_slots.shape, I32),
            per_block,
            per_block,
            dma,
            dma((3,)),
        ],
        name="open",
    )
    grid, sent, inv, lab = call(
        functools.partial(start_body, dims),
        [
            ((flat, LANES), F32),
            ((flat, LANES), F32),
            ((nx * 2 * quads * ny, LANES), I32),
            ((quads * devices, LANES), I32),
        ],
        [arrival, rsel],
        name="start",
    )

    w1, w2, w3 = call(
        weights_body,
        [((hidden, rows), BF), ((hidden, hidden), BF), ((rows, hidden), BF)],
        [chem_input.T, chem_hidden, chem_output, lab],
        name="weights",
    )

    per = LANES // heads
    span = SUB * (-(-scalars // (per * SUB)))
    places = leave_slots.shape[1]
    side = max(1, LANES // places)
    base_shape = (max(1, places // LANES), octets // side * rows * SUB, LANES)
    kept = SUB * (-(-scalars // SUB))
    pair = pltpu.VMEM((hidden, 2 * listed), BF)
    me = jnp.stack([lax.axis_index("gx"), lax.axis_index("gy")]).astype(I32)
    pos, put = call(
        functools.partial(maps_body, dims),
        [((listed, LANES), F32), ((ny * LANES, cells), BF)],
        [me, inv, ot, box[1], box[2]],
        smem=(0,),
        name="maps",
    )

    def chemistry(f, a, token, out, more=()):
        return call(
            functools.partial(chem_body, devices, rows),
            [(listed_shape, F32, True), (out, F32)],
            [react_count, f, a, ot, rsel, w1, w2, w3, token, *more],
            smem=(0,),
            hbm=(2,),
            scratch=[listed_vmem, listed_vmem, pltpu.VMEM((rows, listed), F32)]
            + [pair] * 4
            + [dma((octets,)), dma((octets,))],
            name="chem",
        )

    f = exchange(sent)
    change, source = chemistry(f, a, pos, (flat, LANES))
    home = exchange(source)
    q, token = call(
        functools.partial(middle_body, rows, block, devices),
        [(state_shape, F32, True), ((1, LANES), F32)],
        [q, f, change, ot, rate, partner],
        hbm=(0, 2),
        scratch=[state_vmem, state_vmem, listed_vmem, per_block, per_block, dma],
        name="middle",
    )
    (sent,) = call(
        functools.partial(again_body, dims),
        [((2 * flat, LANES), F32)],
        [home, grid, arrival, inv, lab, token],
        scratch=[pltpu.VMEM((flat, LANES), F32)],
        name="again",
    )
    a, base, token = call(
        functools.partial(list_body, rows),
        [(listed_shape, F32, True), (base_shape, F32, True), ((1, LANES), F32)],
        [q, rate, rsel, ot, lcol],
        hbm=(0,),
        scratch=[
            state_vmem,
            listed_vmem,
            pltpu.VMEM(base_shape, F32),
            dma((-(-scalars // per),)),
            dma((2,)),
        ],
        name="list",
    )
    f = exchange(sent)
    leaving, token = call(
        functools.partial(early_body, devices, rows, span, scalars, heads),
        [((places * span, LANES), F32), ((1, LANES), F32)],
        [react_count, f, base, ot, rate, lcol, w1, w2, w3, token],
        smem=(0,),
        scratch=[pltpu.VMEM(base_shape, F32)],
        name="early",
    )
    change, source = chemistry(f, a, token, (ny, kept, LANES), [pos])
    moved = exchange(leaving)
    state, token = call(
        functools.partial(settle_body, rows, block, devices),
        [(state_shape, F32, True), ((1, LANES), F32)],
        [q, f, change, ot, rate],
        hbm=(0, 2),
        scratch=[state_vmem, state_vmem, listed_vmem, per_block, per_block, dma],
        name="settle",
    )
    source = lax.all_to_all(source, "gy", split_axis=0, concat_axis=0, tiled=True)
    (grid,) = call(
        functools.partial(unpack_body, devices, own),
        [((scalars * quads, LANES), F32)],
        [source, f, put],
        name="unpack",
    )
    grid_out = grid.reshape(grid_scalars.shape)
    steps = -(-scalars // per)
    (state,) = call(
        functools.partial(arrive_body, span, devices),
        [(state_shape, F32, True)],
        [state, moved, acol],
        hbm=(0,),
        scratch=[
            state_vmem,
            state_vmem,
            pltpu.VMEM((places, cells), BF),
            dma((steps,)),
            dma((steps,)),
        ],
        name="arrive",
    )
    return (grid_out, state)


def solution(mesh):
    placed = (
        P(None, "gx", "gy", None),
        P("gx", "gy", None),
        P(None, None, ("gx", "gy")),
        P("gx", "gy", None),
        P("gx", "gy", None),
        P(("gx", "gy")),
        P(None, ("gx", "gy")),
        P(),
        P(),
        P(),
        P(("gx", "gy"), None),
        P(("gx", "gy")),
        P(("gx", "gy"), None),
        P(("gx", "gy"), None),
    )
    return jax.shard_map(
        per_device,
        mesh=mesh,
        in_specs=placed,
        out_specs=(P(None, "gx", "gy", None), P(None, None, ("gx", "gy"))),
        check_vma=False,
    )
```

```python
import functools

import jax
import jax.numpy as jnp
from jax import lax
from jax.experimental import pallas as pl
from jax.experimental.pallas import tpu as pltpu
from jax.sharding import PartitionSpec as P


DIFFUSION = 0.1
PAIR_WEIGHT = 0.4
LANES = 128
SUB = 8
BF = jnp.bfloat16
F32 = jnp.float32
I32 = jnp.int32

NT = (((1,), (1,)), ((), ()))
NN = (((1,), (0,)), ((), ()))


def call(body, outs, ins, smem=(), hbm=(), scratch=(), limit=24):
    spaces = {**{i: pltpu.SMEM for i in smem}, **{i: pl.ANY for i in hbm}}
    ins = [pltpu.with_memory_space_constraint(x, pltpu.HBM) if i in hbm else x for i, x in enumerate(ins)]
    return pl.pallas_call(
        body,
        out_shape=[
            pltpu.HBM(o[0], o[1]) if len(o) > 2 else jax.ShapeDtypeStruct(o[0], o[1]) for o in outs
        ],
        in_specs=[
            pl.BlockSpec(memory_space=spaces.get(i, pltpu.VMEM)) for i in range(len(ins))
        ],
        out_specs=[
            pl.BlockSpec(memory_space=pl.ANY if len(o) > 2 else pltpu.VMEM) for o in outs
        ],
        scratch_shapes=list(scratch),
        compiler_params=pltpu.CompilerParams(vmem_limit_bytes=limit << 20),
    )(*ins)


class Stream:
    def __init__(self, src, dst, sem, size, dim=0):
        self.src, self.dst, self.sem, self.size, self.dim = src, dst, sem, size, dim
        self.count = -(-src.shape[dim] // size)

    def copy(self, i, size=None):
        at = (slice(None),) * self.dim + (pl.ds(i * self.size, size or self.size),)
        return pltpu.make_async_copy(self.src.at[at], self.dst.at[at], self.sem.at[i])

    def tail(self, i):
        return min(self.size, self.src.shape[self.dim] - i * self.size)

    def start_all(self):
        for i in range(self.count):
            self.copy(i, self.tail(i)).start()

    def wait_all(self, first=0):
        for i in range(first, self.count):
            self.copy(i, self.tail(i)).wait()


def dot(a, b, dims):
    return lax.dot_general(a, b, dims, preferred_element_type=F32)


def halves(x):
    high = x.astype(BF)
    return high, (x - high.astype(F32)).astype(BF)


def dot_split(x, onehot, dims):
    high, low = halves(x)
    y = dot(jnp.concatenate([high, low], axis=0), onehot, dims)
    return y[: x.shape[0]] + y[x.shape[0] :]


def load_filtered(f_ref, devices, rows, tiles):
    stride = f_ref.shape[0] // devices
    return jnp.concatenate(
        [
            jnp.concatenate(
                [
                    f_ref[pl.ds(i * tiles + t, devices, stride=stride), :]
                    for i in range(rows // devices)
                ],
                axis=0,
            )
            for t in range(tiles)
        ],
        axis=1,
    )


def divisor(n, most):
    return max(k for k in range(1, most + 1) if n % k == 0)


def mix(s0, block, p_ref, partner_ref, q_ref):
    _, particles, cells = p_ref.shape
    groups = particles // SUB
    for t in range(cells // LANES):
        lanes = pl.ds(t * LANES, LANES)
        rows, homes = [], []
        for j in range(groups):
            index = partner_ref[pl.ds(j * SUB, SUB), lanes]
            rows.append(index & (SUB - 1))
            homes.append(index >> 3)

        def step(s, carry):
            x = [p_ref[s, pl.ds(k * SUB, SUB), lanes] for k in range(groups)]
            for j in range(groups):
                mate = jnp.take_along_axis(x[0], rows[j], axis=0)
                for k in range(1, groups):
                    other = jnp.take_along_axis(x[k], rows[j], axis=0)
                    mate = jnp.where(homes[j] == k, other, mate)
                q_ref[s, pl.ds(j * SUB, SUB), lanes] = x[j] + PAIR_WEIGHT * (mate - x[j])
            return carry

        lax.fori_loop(s0, s0 + block, step, 0)


def put_scalar(ref, s, value, rows):
    for o in range(value.shape[0] // SUB):
        for t in range(value.shape[1] // LANES):
            part = value[o * SUB : (o + 1) * SUB, t * LANES : (t + 1) * LANES]
            ref[t, pl.ds(o * rows * SUB + s * SUB, SUB), :] = part


def get_scalar(ref, s, rows):
    octets = ref.shape[1] // (rows * SUB)
    return jnp.concatenate(
        [
            jnp.concatenate(
                [ref[t, pl.ds(o * rows * SUB + s * SUB, SUB), :] for t in range(ref.shape[0])],
                axis=1,
            )
            for o in range(octets)
        ],
        axis=0,
    )


def particle_rows(p, rows):
    return pl.ds((p >> 3) * (rows * SUB) + (p & (SUB - 1)), rows, stride=SUB)


def list_cells(s0, block, q_ref, onehot, keep, a_ref, rows):
    _, particles, cells = q_ref.shape
    x = q_ref[pl.ds(s0, block)].reshape(block * particles, cells)
    y = dot_split(x, onehot, NT) * keep
    for i in range(block):
        put_scalar(a_ref, s0 + i, y[i * particles : (i + 1) * particles], rows)


def list_body(
    rows,
    q_hbm,
    rate_ref,
    rsel_ref,
    ot_ref,
    lcol_ref,
    a_hbm,
    base_hbm,
    token_ref,
    q_ref,
    a_ref,
    base_ref,
    in_sem,
    out_sem,
):
    scalars, particles, cells = q_ref.shape
    per = LANES // particles
    into = Stream(q_hbm, q_ref, in_sem, per)
    into.start_all()
    token_ref[...] = rate_ref[:, :LANES]
    leaves = cell_onehot(lcol_ref, cells)
    places = lcol_ref.shape[0]
    side = max(1, LANES // places)
    keep = 1.0 - rate_ref[...]

    def part(b, count):
        into.copy(b, count).wait()
        x = q_ref[pl.ds(b * per, count)].reshape(count * particles, cells) * keep
        high, low = halves(x)
        both = jnp.concatenate([high, low], axis=0)
        half = count * particles
        y = dot(both, ot_ref[...], NT)
        y = y[:half] + y[half:]
        z = dot(both, leaves, NT)
        z = z[:half] + z[half:]
        for i in range(count):
            put_scalar(a_ref, b * per + i, y[i * particles : (i + 1) * particles], rows)
            for o in range(0, particles // SUB, side):
                first = i * particles + o * SUB
                octets = [z[first + u * SUB : first + (u + 1) * SUB] for u in range(side)]
                at = pl.ds(o // side * rows * SUB + (b * per + i) * SUB, SUB)
                wide = jnp.concatenate(octets, axis=1)
                for t in range(base_ref.shape[0]):
                    base_ref[t, at, :] = wide[:, t * LANES : (t + 1) * LANES]

    def step(b, carry):
        part(b, per)
        return carry

    whole = scalars // per
    lax.fori_loop(0, whole, step, 0)
    if scalars > whole * per:
        part(whole, scalars - whole * per)
    clear_rest(scalars, rows, a_ref)
    for o in range(particles // SUB // side):
        rest = (rows - scalars) * SUB
        at = pl.ds(o * rows * SUB + scalars * SUB, rest)
        base_ref[:, at, :] = jnp.zeros((base_ref.shape[0], rest, LANES), F32)
    copies = [
        pltpu.make_async_copy(a_ref, a_hbm, out_sem.at[0]),
        pltpu.make_async_copy(base_ref, base_hbm, out_sem.at[1]),
    ]
    for c in copies:
        c.start()
    for c in copies:
        c.wait()


def clear_rest(scalars, rows, a_ref):
    particles = a_ref.shape[1] // rows
    zeros = jnp.zeros((particles, a_ref.shape[0] * LANES), F32)
    for s in range(scalars, rows):
        put_scalar(a_ref, s, zeros, rows)


def open_body(
    rows,
    block,
    p_hbm,
    partner_hbm,
    rate_hbm,
    list_hbm,
    q_hbm,
    a_hbm,
    ot_ref,
    rsel_ref,
    p_ref,
    q_ref,
    a_ref,
    partner_ref,
    rate_ref,
    list_ref,
    in_sem,
    out_sem,
    a_sem,
    few_sem,
):
    scalars, _, cells = p_ref.shape
    into, out = Stream(p_hbm, p_ref, in_sem, block), Stream(q_ref, q_hbm, out_sem, block)
    few = [
        pltpu.make_async_copy(src, dst, few_sem.at[i])
        for i, (src, dst) in enumerate(
            [(list_hbm, list_ref), (rate_hbm, rate_ref), (partner_hbm, partner_ref)]
        )
    ]
    for c in few:
        c.start()
    into.start_all()
    for c in few:
        c.wait()
    column = jnp.broadcast_to(list_ref[...].astype(F32), (SUB, list_ref.shape[1])).T[:, :1]
    cell = lax.broadcasted_iota(I32, ot_ref.shape, 1).astype(F32)
    onehot = (column == cell).astype(F32)
    ot_ref[...] = onehot.astype(BF)
    rate = jnp.broadcast_to(rate_ref[...], (SUB, cells))
    rsel_ref[...] = dot_split(rate, onehot.astype(BF), NT)
    clear_rest(scalars, rows, a_ref)

    def step(b, carry):
        into.copy(b).wait()
        mix(b * block, block, p_ref, partner_ref, q_ref)
        out.copy(b).start()
        list_cells(b * block, block, q_ref, ot_ref[...], 1.0 - rsel_ref[0:1, :], a_ref, rows)
        return carry

    lax.fori_loop(0, scalars // block, step, 0)
    last = pltpu.make_async_copy(a_ref, a_hbm, a_sem)
    last.start()
    out.wait_all()
    last.wait()


def settle_block(s0, block, q_ref, f_ref, r_ref, ot_ref, rate_ref, out_ref, rows, devices):
    _, particles, cells = q_ref.shape
    tiles = cells // LANES
    rate = rate_ref[...]
    keep = 1.0 - rate
    r = jnp.concatenate([get_scalar(r_ref, s0 + i, rows) for i in range(block)], axis=0)
    spread = dot(r.astype(BF), ot_ref[...], NN)
    for i in range(block):
        s = s0 + i
        at = lax.rem(s, devices) * (f_ref.shape[0] // devices) + lax.div(s, devices) * tiles
        f = jnp.concatenate([f_ref[pl.ds(at + t, 1), :] for t in range(tiles)], axis=1)
        out_ref[s0 + i] = (
            keep * q_ref[s0 + i] + rate * f + spread[i * particles : (i + 1) * particles]
        )


def middle_body(
    rows,
    block,
    devices,
    q_hbm,
    f_ref,
    r_hbm,
    ot_ref,
    rate_ref,
    partner_ref,
    out_hbm,
    token_ref,
    q_ref,
    now_ref,
    r_ref,
    in_sem,
    out_sem,
    r_sem,
):
    scalars = q_ref.shape[0]
    into, out = Stream(q_hbm, q_ref, in_sem, block), Stream(q_ref, out_hbm, out_sem, block)
    first = pltpu.make_async_copy(r_hbm, r_ref, r_sem)
    first.start()
    into.start_all()
    token_ref[...] = rate_ref[:, :LANES]
    first.wait()

    def step(b, carry):
        into.copy(b).wait()
        s0 = b * block
        settle_block(s0, block, q_ref, f_ref, r_ref, ot_ref, rate_ref, now_ref, rows, devices)
        mix(s0, block, now_ref, partner_ref, q_ref)
        out.copy(b).start()
        return carry

    lax.fori_loop(0, scalars // block, step, 0)
    out.wait_all()


def half_silu(y):
    return (y + y * jnp.tanh(y)).astype(BF)


def chem_body(
    devices,
    rows,
    count_ref,
    f_ref,
    a_hbm,
    ot_ref,
    rsel_ref,
    w1_ref,
    w2_ref,
    w3_ref,
    token_ref,
    *refs,
):
    pos_refs, refs = refs[:-11], refs[-11:]
    r_hbm, s_ref, a_ref, r_ref, pull_ref, one_a, one_b, two_a, two_b, in_sem, out_sem = refs
    tiles = ot_ref.shape[1] // LANES
    listed = ot_ref.shape[0]
    particles = a_ref.shape[1] // rows
    into = Stream(a_hbm, a_ref, in_sem, SUB * rows, 1)
    out = Stream(r_ref, r_hbm, out_sem, SUB * rows, 1)
    into.start_all()
    f = load_filtered(f_ref, devices, rows, tiles)
    pull_ref[...] = rsel_ref[0:1, :] * dot_split(f, ot_ref[...], NT)
    live = lax.broadcasted_iota(I32, (1, listed), 1) < count_ref[0]

    def first(g):
        parts = []
        for i in range(2):
            at = particle_rows(2 * g + i, rows)
            for t in range(listed // LANES):
                pull = pull_ref[:, t * LANES : (t + 1) * LANES]
                parts.append((a_ref[t, at, :] + pull).astype(BF))
        return half_silu(dot(w1_ref[...], jnp.concatenate(parts, axis=1), NN))

    def second(one):
        return half_silu(dot(w2_ref[...], one, NN))

    def third(g, two, total):
        change = dot(w3_ref[...], two, NN).astype(BF).astype(F32)
        for i in range(2):
            r = jnp.where(live, change[:, i * listed : (i + 1) * listed], 0.0)
            at = particle_rows(2 * g + i, rows)
            for t in range(listed // LANES):
                r_ref[t, at, :] = r[:, t * LANES : (t + 1) * LANES]
            total = total + r
        return total

    def step(g, total, old, new):
        total = third(g - 2, old[1][...], total)
        new[1][...] = second(old[0][...])
        new[0][...] = first(g)
        return total

    left, right = (one_a, two_a), (one_b, two_b)

    def pair(m, total):
        total = step(2 * m, total, right, left)
        return step(2 * m + 1, total, left, right)

    total = jnp.zeros((rows, listed), F32)
    each = SUB // 4
    for o in range(particles // SUB):
        into.copy(o).wait()
        if o == 0:
            one_a[...] = first(0)
            two_b[...] = second(one_a[...])
            one_b[...] = first(1)
        total = lax.fori_loop(max(1, o * each), (o + 1) * each, pair, total)
        if o:
            out.copy(o - 1).start()
    last = particles // 2 - 1
    total = third(last - 1, two_b[...], total)
    total = third(last, second(one_b[...]), total)
    out.copy(particles // SUB - 1).start()
    source = total * (1.0 / particles)
    if pos_refs:
        boxes_source(source, *pos_refs, s_ref)
    else:
        source = dot_split(source, ot_ref[...], NN)
        stride = s_ref.shape[0] // devices
        for i in range(rows // devices):
            for t in range(tiles):
                part = source[i * devices : (i + 1) * devices, t * LANES : (t + 1) * LANES]
                s_ref[pl.ds(i * tiles + t, devices, stride=stride), :] = part
    out.wait_all()


def boxes_source(source, pos_ref, s_ref):
    listed = source.shape[1]
    boxes = s_ref.shape[0]
    put = lax.broadcasted_iota(I32, (listed, boxes * LANES), 1).astype(F32) == pos_ref[:, :1]
    sent = dot_split(source, put.astype(F32).astype(BF), NN)
    for b in range(boxes):
        s_ref[b] = sent[: s_ref.shape[1], b * LANES : (b + 1) * LANES]


def early_body(
    devices,
    rows,
    span,
    scalars,
    particles,
    count_ref,
    f_ref,
    base_hbm,
    ot_ref,
    rate_ref,
    lcol_ref,
    w1_ref,
    w2_ref,
    w3_ref,
    token_ref,
    out_ref,
    end_ref,
    v_ref,
    base_ref,
    sem,
):
    load = pltpu.make_async_copy(base_hbm, base_ref, sem)
    load.start()
    listed, cells = ot_ref.shape
    tiles = cells // LANES
    places = lcol_ref.shape[0]
    side = max(1, LANES // places)
    wide = base_ref.shape[0]
    end_ref[...] = rate_ref[:, :LANES]
    f = load_filtered(f_ref, devices, rows, tiles)
    leaves = cell_onehot(lcol_ref, cells)
    rate = dot_split(jnp.broadcast_to(rate_ref[...], (SUB, cells)), leaves, NT)[:1]
    pull = rate * dot_split(f, leaves, NT)
    live = (lax.broadcasted_iota(I32, (SUB, listed), 1) < count_ref[0]).astype(F32).astype(BF)
    live = dot(dot(live, ot_ref[...], NN).astype(BF), leaves, NT)[:1]
    pull = jnp.concatenate([pull] * side, axis=1)
    live = jnp.concatenate([live] * side, axis=1) > 0.5
    count = 4 // wide
    load.wait()

    for o in range(particles // SUB // side):
        for i in range(0, SUB, count):
            ats = [pl.ds(o * rows * SUB + i + u, rows, stride=SUB) for u in range(count)]
            x = jnp.concatenate(
                [base_ref[t, at, :] + pull[:, t * LANES : (t + 1) * LANES] for at in ats for t in range(wide)],
                axis=1,
            )
            one = half_silu(dot(w1_ref[...], x.astype(BF), NN))
            two = half_silu(dot(w2_ref[...], one, NN))
            change = dot(w3_ref[...], two, NN).astype(BF).astype(F32)
            for n, (at, t) in enumerate((at, t) for at in ats for t in range(wide)):
                cols = slice(n * LANES, (n + 1) * LANES)
                mask = live[:, t * LANES : (t + 1) * LANES]
                v_ref[t, at, :] = x[:, cols] + jnp.where(mask, change[:, cols], 0.0)

    per = LANES // particles
    stride = out_ref.shape[0] // devices

    def scalar(s):
        parts = []
        for o in range(particles // SUB // side):
            at = pl.ds(o * rows * SUB + s * SUB, SUB)
            row = jnp.concatenate([v_ref[t, at, :] for t in range(wide)], axis=1)
            parts += [row[:, u * places : (u + 1) * places] for u in range(side)]
        return jnp.concatenate(parts, axis=0)

    def part(b, count):
        value = jnp.concatenate([scalar(b * per + i) for i in range(count)], axis=0)
        if count < per:
            rest = jnp.zeros(((per - count) * particles, places), F32)
            value = jnp.concatenate([value, rest], axis=0)
        value = value.T
        for c in range(places // devices):
            at = pl.ds(c * span + b, devices, stride=stride)
            out_ref[at, :] = value[c * devices : (c + 1) * devices]

    def step(b, carry):
        part(b, per)
        return carry

    whole = scalars // per
    lax.fori_loop(0, whole, step, 0, unroll=2)
    zeros = jnp.zeros((devices, LANES), F32)
    for c in range(places // devices):
        for b in range(whole, span):
            out_ref[pl.ds(c * span + b, devices, stride=stride), :] = zeros
    if scalars > whole * per:
        part(whole, scalars - whole * per)


def columns(row_ref, devices, out_ref, turn_ref):
    places = row_ref.shape[1]
    count = places // devices
    column = jnp.broadcast_to(row_ref[...].astype(F32), (SUB, places)).T[:, :1]
    turn_ref[...] = jnp.broadcast_to(column, turn_ref.shape)
    for c in range(count):
        part = turn_ref[pl.ds(c, devices, stride=count), :]
        out_ref[c * devices : (c + 1) * devices] = part.astype(I32)


def maps_body(
    dims,
    me_ref,
    inv_ref,
    ot_ref,
    owner_ref,
    slot_ref,
    leave_ref,
    arrive_ref,
    pos_ref,
    put_ref,
    lcol_ref,
    acol_ref,
    turn_ref,
):
    nx, ny, _, bx, by = dims
    columns(leave_ref, nx * ny, lcol_ref, turn_ref)
    columns(arrive_ref, nx * ny, acol_ref, turn_ref)
    quads = bx * by
    turns = quads * ny
    _, cells = ot_ref.shape
    at = me_ref[0] * 2 * turns + me_ref[1]
    code = jnp.concatenate([inv_ref[pl.ds(at + k * ny, 1), :] for k in range(quads)], axis=1)
    box = lax.rem(code, ny).astype(F32)
    boxes = lax.broadcasted_iota(I32, (ny, cells), 0).astype(F32)
    mine = (jnp.broadcast_to(box, (ny, cells)) == boxes).astype(F32)
    before = lax.broadcasted_iota(I32, (cells, cells), 0) < lax.broadcasted_iota(
        I32, (cells, cells), 1
    )
    count = dot(mine.astype(BF), before.astype(F32).astype(BF), NN)
    rank = jnp.sum(mine * count, axis=0, keepdims=True)
    rest = jnp.zeros((SUB - 2, cells), F32)
    found = dot(ot_ref[...], jnp.concatenate([box, rank, rest], axis=0).astype(BF), NT)
    pos = found[:, :1] * LANES + found[:, 1:2]
    pos_ref[...] = jnp.broadcast_to(pos, pos_ref.shape)
    flat = lambda ref: jnp.concatenate([ref[j : j + 1, :] for j in range(quads)], axis=1)
    owner, slot = flat(owner_ref).astype(F32), flat(slot_ref).astype(F32)
    first = owner * cells
    key = first + slot
    column = jnp.broadcast_to(key, (SUB, cells)).T[:, :1]
    ahead = (column < key) & (column >= first)
    place = owner * LANES + jnp.sum(ahead.astype(F32), axis=0, keepdims=True)
    step = min(cells, put_ref.shape[0])
    for b in range(put_ref.shape[0] // step):
        row = lax.broadcasted_iota(I32, (step, cells), 0).astype(F32) + b * step
        put_ref[b * step : (b + 1) * step] = (row == place).astype(F32).astype(BF)


def unpack_body(devices, own, s_ref, arr_ref, put_ref, out_ref):
    boxes, _ = s_ref.shape[:2]
    cells = put_ref.shape[1]
    quads = cells // LANES
    scalars = out_ref.shape[0] // quads
    stride = arr_ref.shape[0] // devices
    got = jnp.concatenate([s_ref[b] for b in range(boxes)], axis=1)
    source = dot_split(got, put_ref[...], NN)
    for j in range(quads):
        for i in range(own):
            n = min(devices, scalars - i * devices)
            if n > 0:
                grid = arr_ref[pl.ds(stride - own * quads + i * quads + j, n, stride=stride), :]
                part = source[i * devices : i * devices + n, j * LANES : (j + 1) * LANES]
                out_ref[pl.ds(i * devices * quads + j, n, stride=quads), :] = grid + part


def cell_onehot(col_ref, cells):
    shape = (col_ref.shape[0], cells)
    return (col_ref[:, :1] == lax.broadcasted_iota(I32, shape, 1)).astype(F32).astype(BF)


def settle_body(
    rows,
    block,
    devices,
    q_hbm,
    f_ref,
    r_hbm,
    ot_ref,
    rate_ref,
    out_hbm,
    token_ref,
    q_ref,
    out_ref,
    r_ref,
    in_sem,
    out_sem,
    r_sem,
):
    into, out = Stream(q_hbm, q_ref, in_sem, block), Stream(out_ref, out_hbm, out_sem, block)
    first = pltpu.make_async_copy(r_hbm, r_ref, r_sem)
    first.start()
    into.start_all()
    token_ref[...] = rate_ref[:, :LANES]
    first.wait()

    def step(b, carry):
        into.copy(b).wait()
        settle_block(b * block, block, q_ref, f_ref, r_ref, ot_ref, rate_ref, out_ref, rows, devices)
        out.copy(b).start()
        return carry

    lax.fori_loop(0, q_ref.shape[0] // block, step, 0)
    out.wait_all()


def arrive_body(
    span, devices, p_hbm, arr_ref, acol_ref, out_hbm, p_ref, out_ref, hit_ref, in_sem, out_sem
):
    scalars, particles, cells = p_ref.shape
    places = acol_ref.shape[0]
    per = LANES // particles
    into, out = Stream(p_hbm, p_ref, in_sem, per), Stream(out_ref, out_hbm, out_sem, per)
    into.start_all()
    hit = (acol_ref[:, :1] == lax.broadcasted_iota(I32, (places, cells), 1)).astype(F32)
    hit_ref[...] = hit.astype(BF)
    taken = jnp.sum(hit, axis=0, keepdims=True) > 0.5
    stride = arr_ref.shape[0] // devices
    count = places // devices

    def place(b, size):
        first = stride - count * span + b
        x = jnp.concatenate(
            [arr_ref[pl.ds(first + c * span, devices, stride=stride), :] for c in range(count)],
            axis=0,
        ).T
        y = dot_split(x, hit_ref[...], NN)
        into.copy(b, size).wait()
        for i in range(size):
            s = b * per + i
            out_ref[s] = jnp.where(taken, y[i * particles : (i + 1) * particles], p_ref[s])
        out.copy(b, size).start()

    def step(b, carry):
        place(b, per)
        return carry

    whole = scalars // per
    lax.fori_loop(0, whole, step, 0)
    if scalars > whole * per:
        place(whole, scalars - whole * per)
    out.wait_all()


def stencil(value, speed, bx, by, lanes_y):
    boxes = value[0].shape[0]
    row = lax.broadcasted_iota(I32, value[0].shape, 0) % lanes_y
    zero = jnp.zeros((lanes_y, LANES), F32)

    def x_low(v):
        return jnp.concatenate([zero, v[: boxes - lanes_y]], axis=0)

    def x_high(v):
        return jnp.concatenate([v[lanes_y:], zero], axis=0)

    def y_low(v):
        return jnp.where(row == 0, 0.0, pltpu.roll(v, 1, 0))

    def y_high(v):
        return jnp.where(row == lanes_y - 1, 0.0, pltpu.roll(v, boxes - 1, 0))

    out = []
    for i in range(bx):
        for j in range(by):
            c = value[i * by + j]
            up = value[(i - 1) * by + j] if i else x_low(value[(bx - 1) * by + j])
            down = value[(i + 1) * by + j] if i < bx - 1 else x_high(value[j])
            left = value[i * by + j - 1] if j else y_low(value[i * by + by - 1])
            right = value[i * by + j + 1] if j < by - 1 else y_high(value[i * by])
            beside = up + down + left + right + pltpu.roll(c, 1, 1) + pltpu.roll(c, LANES - 1, 1)
            out.append(c + DIFFUSION * (beside - 6.0 * c) - speed[i * by + j] * (c - up))
    return out


def route(src_ref, first_row, row_step, item_step, items, own, quads, lanes_y, rows, lanes):
    shape = (lanes_y, LANES)
    out = []
    for k in range(len(rows)):

        def step(y, acc):
            for j in range(items):
                hit = rows[k] == (j * lanes_y + y)
                at = first_row + y * row_step + j * item_step
                lines = [src_ref[pl.ds(at + s * quads, 1), :] for s in range(own)]
                acc = [
                    jnp.where(
                        hit,
                        jnp.take_along_axis(jnp.broadcast_to(v, shape), lanes[k], axis=1),
                        old,
                    )
                    for v, old in zip(lines, acc)
                ]
            return tuple(acc)

        zero = tuple(jnp.zeros(shape, F32) for _ in range(own))
        out.append(lax.fori_loop(0, lanes_y, step, zero, unroll=min(lanes_y, 8)))
    return [[out[k][s] for k in range(len(rows))] for s in range(own)]


def load_rows(ref, offset, stride, count):
    return ref[pl.ds(offset, count, stride=stride), :]


def pack_body(
    width,
    lanes_y,
    grid_hbm,
    owner_hbm,
    slot_hbm,
    speed_hbm,
    out_ref,
    grid_ref,
    owner_ref,
    slot_ref,
    speed_ref,
    sem,
):
    pairs = [
        (grid_hbm, grid_ref),
        (owner_hbm, owner_ref),
        (slot_hbm, slot_ref),
        (speed_hbm, speed_ref),
    ]
    copies = [pltpu.make_async_copy(a, b, sem.at[i]) for i, (a, b) in enumerate(pairs)]
    for c in copies:
        c.start()
    for c in copies:
        c.wait()
    quads = owner_ref.shape[0]
    stride = width + 2 * quads
    total = grid_ref.shape[0]
    slot = slot_ref[...]
    label = ((slot >> 7) * lanes_y + owner_ref[...]) * LANES + (slot & (LANES - 1))
    tail = jnp.concatenate([label.astype(F32), speed_ref[...]], axis=0)
    devices = out_ref.shape[0] // stride
    for d in range(devices):
        for i in range(width // quads):
            at = d * stride + i * quads
            src = (i * devices + d) * quads
            if src < total:
                out_ref[at : at + quads] = grid_ref[src : src + quads]
            else:
                out_ref[at : at + quads] = jnp.zeros((quads, LANES), F32)
        out_ref[d * stride + width : (d + 1) * stride] = tail


def weights_body(w1_ref, w2_ref, w3_ref, token_ref, a_ref, b_ref, c_ref):
    scalars, hidden = w1_ref.shape
    rest = jnp.zeros((a_ref.shape[1] - scalars, hidden), F32)
    a_ref[...] = jnp.concatenate([w1_ref[...].astype(F32) * 0.5, rest], axis=0).T.astype(BF)
    b_ref[...] = (w2_ref[...].astype(F32) * 0.5).astype(BF)
    c_ref[...] = jnp.concatenate([w3_ref[...].astype(F32), rest], axis=0).astype(BF)


def start_body(dims, arr_ref, token_ref, g_ref, f_ref, inv_ref, lab_ref):
    nx, ny, own, bx, by = dims
    quads = bx * by
    boxes = nx * ny
    width = own * quads
    stride = width + 2 * quads
    turns = quads * ny
    speed = [load_rows(arr_ref, width + quads + j, stride, boxes) for j in range(quads)]
    for s in range(own):
        value = [load_rows(arr_ref, s * quads + j, stride, boxes) for j in range(quads)]
        for j, v in enumerate(stencil(value, speed, bx, by, ny)):
            g_ref[pl.ds(s * quads + j, boxes, stride=width), :] = v
    for j in range(quads):
        lab_ref[pl.ds(j * boxes, boxes), :] = load_rows(arr_ref, width + j, stride, boxes).astype(
            I32
        )
    lane_of = lax.broadcasted_iota(I32, (turns, LANES), 1).astype(F32)
    sub_of = lax.broadcasted_iota(I32, (turns, LANES), 0)
    sub_lane = lax.broadcasted_iota(I32, (LANES, LANES), 0)

    def group(x, carry):
        def gather(y, acc):
            left, right = [], []
            for j in range(quads):
                line = lab_ref[pl.ds(j * boxes + x * ny + y, 1), :]
                hit = jnp.broadcast_to(line >> 7, (turns, LANES)) == sub_of
                code = (j * ny + y).astype(F32)
                left.append(
                    jnp.concatenate(
                        [jnp.where(hit, code, 0.0), jnp.where(hit, lane_of, 0.0)], axis=0
                    ).astype(BF)
                )
                right.append(
                    (jnp.broadcast_to(line & (LANES - 1), (LANES, LANES)) == sub_lane)
                    .astype(F32)
                    .astype(BF)
                )
            return acc + dot(
                jnp.concatenate(left, axis=1), jnp.concatenate(right, axis=1), NT
            )

        code = lax.fori_loop(0, ny, gather, jnp.zeros((2 * turns, LANES), F32), unroll=2)
        code = code.astype(I32)
        inv_ref[pl.ds(x * 2 * turns, 2 * turns), :] = code
        return carry

    lax.fori_loop(0, nx, group, 0)
    send_filtered(dims, g_ref, width, 0, inv_ref, f_ref)


def send_filtered(dims, g_ref, g_stride, g_first, inv_ref, f_ref):
    nx, ny, own, bx, by = dims
    quads = bx * by
    turns = quads * ny
    f_stride = f_ref.shape[0] // (nx * ny)

    def group(x, carry):
        base = x * 2 * turns
        rows = [inv_ref[pl.ds(base + k * ny, ny), :] for k in range(quads)]
        lanes = [inv_ref[pl.ds(base + turns + k * ny, ny), :] for k in range(quads)]
        first = x * ny * g_stride + g_first
        out = route(g_ref, first, g_stride, 1, quads, own, quads, ny, rows, lanes)
        for s in range(own):
            for k in range(quads):
                at = pl.ds(x * ny * f_stride + s * quads + k, ny, stride=f_stride)
                f_ref[at, :] = out[s][k]
        return carry

    lax.fori_loop(0, nx, group, 0)


def add_source(dims, s_ref, g_ref, lab_ref, out_ref):
    nx, ny, own, bx, by = dims
    quads = bx * by
    boxes = nx * ny
    width = own * quads
    stride = s_ref.shape[0] // boxes

    def group(x, carry):
        labels = [lab_ref[pl.ds(j * boxes + x * ny, ny), :] for j in range(quads)]
        rows = [v >> 7 for v in labels]
        lanes = [v & (LANES - 1) for v in labels]
        out = route(s_ref, x * ny * stride, stride, 1, quads, own, quads, ny, rows, lanes)
        for s in range(own):
            for k in range(quads):
                at = pl.ds(x * ny * width + s * quads + k, ny, stride=width)
                out_ref[at, :] = g_ref[at, :] + out[s][k]
        return carry

    lax.fori_loop(0, nx, group, 0)


def again_body(dims, s_ref, g_ref, arr_ref, inv_ref, lab_ref, token_ref, f_ref, mid_ref):
    nx, ny, own, bx, by = dims
    quads = bx * by
    boxes = nx * ny
    width = own * quads
    stride = width + 2 * quads
    add_source(dims, s_ref, g_ref, lab_ref, mid_ref)
    speed = [load_rows(arr_ref, width + quads + j, stride, boxes) for j in range(quads)]
    for s in range(own):
        value = [load_rows(mid_ref, s * quads + j, width, boxes) for j in range(quads)]
        for j, v in enumerate(stencil(value, speed, bx, by, ny)):
            f_ref[pl.ds(width + s * quads + j, boxes, stride=2 * width), :] = v
    send_filtered(dims, f_ref, 2 * width, width, inv_ref, f_ref)


def per_device(
    grid_scalars,
    axial_speed,
    particles,
    cell_owner,
    cell_slot,
    mix_rate,
    partner,
    chem_input,
    chem_hidden,
    chem_output,
    react_slots,
    react_count,
    leave_slots,
    arrive_slots,
):
    both = ("gx", "gy")
    nx, ny = lax.axis_size("gx"), lax.axis_size("gy")
    devices = nx * ny
    scalars, bx, by, nz = grid_scalars.shape
    heads, cells = partner.shape
    listed = react_slots.shape[1]
    hidden = chem_hidden.shape[0]
    quads = bx * by
    own = -(-scalars // devices)
    rows = devices * own
    width = own * quads
    tiles = cells // LANES
    assert nz == LANES and tiles == quads and heads % SUB == 0 and LANES % heads == 0
    dims = (nx, ny, own, bx, by)
    flat = devices * width

    box = [
        grid_scalars.reshape(-1, LANES),
        cell_owner.reshape(quads, LANES),
        cell_slot.reshape(quads, LANES),
        axial_speed.reshape(quads, LANES),
    ]
    (first,) = call(
        functools.partial(pack_body, width, ny),
        [((devices * (width + 2 * quads), LANES), F32)],
        box,
        hbm=(0, 1, 2, 3),
        scratch=[pltpu.VMEM(x.shape, x.dtype) for x in box] + [pltpu.SemaphoreType.DMA((4,))],
    )

    def exchange(x):
        x = x.reshape(devices, -1, LANES)
        return lax.all_to_all(x, both, split_axis=0, concat_axis=0, tiled=True).reshape(-1, LANES)

    arrival = exchange(first)

    rate = mix_rate.reshape(1, cells)
    state_shape = (scalars, heads, cells)
    listed_shape = (listed // LANES, heads * rows, LANES)
    block = divisor(scalars, 6)
    octets = heads // SUB
    state_vmem = pltpu.VMEM(state_shape, F32)
    listed_vmem = pltpu.VMEM(listed_shape, F32)
    dma = pltpu.SemaphoreType.DMA
    per_block = dma((scalars // block,))
    q, a, ot, rsel = call(
        functools.partial(open_body, rows, block),
        [
            (state_shape, F32, True),
            (listed_shape, F32, True),
            ((listed, cells), BF),
            ((SUB, listed), F32),
        ],
        [particles, partner, rate, react_slots],
        hbm=(0, 1, 2, 3),
        scratch=[
            state_vmem,
            state_vmem,
            listed_vmem,
            pltpu.VMEM(partner.shape, I32),
            pltpu.VMEM(rate.shape, F32),
            pltpu.VMEM(react_slots.shape, I32),
            per_block,
            per_block,
            dma,
            dma((3,)),
        ],
    )
    grid, sent, inv, lab = call(
        functools.partial(start_body, dims),
        [
            ((flat, LANES), F32),
            ((flat, LANES), F32),
            ((nx * 2 * quads * ny, LANES), I32),
            ((quads * devices, LANES), I32),
        ],
        [arrival, rsel],
    )

    w1, w2, w3 = call(
        weights_body,
        [((hidden, rows), BF), ((hidden, hidden), BF), ((rows, hidden), BF)],
        [chem_input.T, chem_hidden, chem_output, lab],
    )

    per = LANES // heads
    span = SUB * (-(-scalars // (per * SUB)))
    places = leave_slots.shape[1]
    side = max(1, LANES // places)
    base_shape = (max(1, places // LANES), octets // side * rows * SUB, LANES)
    kept = SUB * (-(-scalars // SUB))
    pair = pltpu.VMEM((hidden, 2 * listed), BF)
    me = jnp.stack([lax.axis_index("gx"), lax.axis_index("gy")]).astype(I32)
    pos, put, lcol, acol = call(
        functools.partial(maps_body, dims),
        [
            ((listed, LANES), F32),
            ((ny * LANES, cells), BF),
            ((places, LANES), I32),
            ((places, LANES), I32),
        ],
        [me, inv, ot, box[1], box[2], leave_slots, arrive_slots],
        smem=(0,),
        scratch=[pltpu.VMEM((places, LANES), F32)],
    )

    def chemistry(f, a, token, out, more=()):
        return call(
            functools.partial(chem_body, devices, rows),
            [(listed_shape, F32, True), (out, F32)],
            [react_count, f, a, ot, rsel, w1, w2, w3, token, *more],
            smem=(0,),
            hbm=(2,),
            scratch=[listed_vmem, listed_vmem, pltpu.VMEM((rows, listed), F32)]
            + [pair] * 4
            + [dma((octets,)), dma((octets,))],
        )

    f = exchange(sent)
    change, source = chemistry(f, a, pos, (flat, LANES))
    home = exchange(source)
    q, token = call(
        functools.partial(middle_body, rows, block, devices),
        [(state_shape, F32, True), ((1, LANES), F32)],
        [q, f, change, ot, rate, partner],
        hbm=(0, 2),
        scratch=[state_vmem, state_vmem, listed_vmem, per_block, per_block, dma],
    )
    (sent,) = call(
        functools.partial(again_body, dims),
        [((2 * flat, LANES), F32)],
        [home, grid, arrival, inv, lab, token],
        scratch=[pltpu.VMEM((flat, LANES), F32)],
    )
    a, base, token = call(
        functools.partial(list_body, rows),
        [(listed_shape, F32, True), (base_shape, F32, True), ((1, LANES), F32)],
        [q, rate, rsel, ot, lcol],
        hbm=(0,),
        scratch=[
            state_vmem,
            listed_vmem,
            pltpu.VMEM(base_shape, F32),
            dma((-(-scalars // per),)),
            dma((2,)),
        ],
    )
    f = exchange(sent)
    leaving, token = call(
        functools.partial(early_body, devices, rows, span, scalars, heads),
        [((places * span, LANES), F32), ((1, LANES), F32)],
        [react_count, f, base, ot, rate, lcol, w1, w2, w3, token],
        smem=(0,),
        hbm=(2,),
        scratch=[pltpu.VMEM(base_shape, F32), pltpu.VMEM(base_shape, F32), dma],
    )
    change, source = chemistry(f, a, token, (ny, kept, LANES), [pos])
    moved = exchange(leaving)
    state, token = call(
        functools.partial(settle_body, rows, block, devices),
        [(state_shape, F32, True), ((1, LANES), F32)],
        [q, f, change, ot, rate],
        hbm=(0, 2),
        scratch=[state_vmem, state_vmem, listed_vmem, per_block, per_block, dma],
    )
    source = lax.all_to_all(source, "gy", split_axis=0, concat_axis=0, tiled=True)
    (grid,) = call(
        functools.partial(unpack_body, devices, own),
        [((scalars * quads, LANES), F32)],
        [source, f, put],
    )
    grid_out = grid.reshape(grid_scalars.shape)
    steps = -(-scalars // per)
    (state,) = call(
        functools.partial(arrive_body, span, devices),
        [(state_shape, F32, True)],
        [state, moved, acol],
        hbm=(0,),
        scratch=[
            state_vmem,
            state_vmem,
            pltpu.VMEM((places, cells), BF),
            dma((steps,)),
            dma((steps,)),
        ],
    )
    return (grid_out, state)


def solution(mesh):
    placed = (
        P(None, "gx", "gy", None),
        P("gx", "gy", None),
        P(None, None, ("gx", "gy")),
        P("gx", "gy", None),
        P("gx", "gy", None),
        P(("gx", "gy")),
        P(None, ("gx", "gy")),
        P(),
        P(),
        P(),
        P(("gx", "gy"), None),
        P(("gx", "gy")),
        P(("gx", "gy"), None),
        P(("gx", "gy"), None),
    )

    return jax.shard_map(
        per_device,
        mesh=mesh,
        in_specs=placed,
        out_specs=(P(None, "gx", "gy", None), P(None, None, ("gx", "gy"))),
        check_vma=False,
    )
```

```python
import functools

import jax
import jax.numpy as jnp
from jax import lax
from jax.experimental import pallas as pl
from jax.experimental.pallas import tpu as pltpu
from jax.sharding import PartitionSpec as P


DIFFUSION = 0.1
PAIR_WEIGHT = 0.4
LANES = 128
SUB = 8
BF = jnp.bfloat16
F32 = jnp.float32
I32 = jnp.int32

NT = (((1,), (1,)), ((), ()))
NN = (((1,), (0,)), ((), ()))


def call(body, outs, ins, smem=(), hbm=(), scratch=(), limit=24):
    spaces = {**{i: pltpu.SMEM for i in smem}, **{i: pl.ANY for i in hbm}}
    ins = [pltpu.with_memory_space_constraint(x, pltpu.HBM) if i in hbm else x for i, x in enumerate(ins)]
    return pl.pallas_call(
        body,
        out_shape=[
            pltpu.HBM(o[0], o[1]) if len(o) > 2 else jax.ShapeDtypeStruct(o[0], o[1]) for o in outs
        ],
        in_specs=[
            pl.BlockSpec(memory_space=spaces.get(i, pltpu.VMEM)) for i in range(len(ins))
        ],
        out_specs=[
            pl.BlockSpec(memory_space=pl.ANY if len(o) > 2 else pltpu.VMEM) for o in outs
        ],
        scratch_shapes=list(scratch),
        compiler_params=pltpu.CompilerParams(vmem_limit_bytes=limit << 20),
    )(*ins)


class Stream:
    def __init__(self, src, dst, sem, size, dim=0):
        self.src, self.dst, self.sem, self.size, self.dim = src, dst, sem, size, dim
        self.count = -(-src.shape[dim] // size)

    def copy(self, i, size=None):
        at = (slice(None),) * self.dim + (pl.ds(i * self.size, size or self.size),)
        return pltpu.make_async_copy(self.src.at[at], self.dst.at[at], self.sem.at[i])

    def tail(self, i):
        return min(self.size, self.src.shape[self.dim] - i * self.size)

    def start_all(self):
        for i in range(self.count):
            self.copy(i, self.tail(i)).start()

    def wait_all(self, first=0):
        for i in range(first, self.count):
            self.copy(i, self.tail(i)).wait()


def dot(a, b, dims):
    return lax.dot_general(a, b, dims, preferred_element_type=F32)


def halves(x):
    high = x.astype(BF)
    return high, (x - high.astype(F32)).astype(BF)


def dot_split(x, onehot, dims):
    high, low = halves(x)
    y = dot(jnp.concatenate([high, low], axis=0), onehot, dims)
    return y[: x.shape[0]] + y[x.shape[0] :]


def load_filtered(f_ref, devices, rows, tiles):
    stride = f_ref.shape[0] // devices
    return jnp.concatenate(
        [
            jnp.concatenate(
                [
                    f_ref[pl.ds(i * tiles + t, devices, stride=stride), :]
                    for i in range(rows // devices)
                ],
                axis=0,
            )
            for t in range(tiles)
        ],
        axis=1,
    )


def divisor(n, most):
    return max(k for k in range(1, most + 1) if n % k == 0)


def mix(s0, block, p_ref, partner_ref, q_ref):
    _, particles, cells = p_ref.shape
    groups = particles // SUB
    for t in range(cells // LANES):
        lanes = pl.ds(t * LANES, LANES)
        rows, homes = [], []
        for j in range(groups):
            index = partner_ref[pl.ds(j * SUB, SUB), lanes]
            rows.append(index & (SUB - 1))
            homes.append(index >> 3)

        def step(s, carry):
            x = [p_ref[s, pl.ds(k * SUB, SUB), lanes] for k in range(groups)]
            for j in range(groups):
                mate = jnp.take_along_axis(x[0], rows[j], axis=0)
                for k in range(1, groups):
                    other = jnp.take_along_axis(x[k], rows[j], axis=0)
                    mate = jnp.where(homes[j] == k, other, mate)
                q_ref[s, pl.ds(j * SUB, SUB), lanes] = x[j] + PAIR_WEIGHT * (mate - x[j])
            return carry

        lax.fori_loop(s0, s0 + block, step, 0)


def put_scalar(ref, s, value):
    for o in range(ref.shape[1]):
        for t in range(ref.shape[0]):
            part = value[o * SUB : (o + 1) * SUB, t * LANES : (t + 1) * LANES]
            ref[t, o, pl.ds(s * SUB, SUB), :] = part


def get_scalar(ref, s):
    return jnp.concatenate(
        [
            jnp.concatenate(
                [ref[t, o, pl.ds(s * SUB, SUB), :] for t in range(ref.shape[0])], axis=1
            )
            for o in range(ref.shape[1])
        ],
        axis=0,
    )


def list_cells(s0, block, q_ref, onehot, keep, a_ref):
    _, particles, cells = q_ref.shape
    x = q_ref[pl.ds(s0, block)].reshape(block * particles, cells)
    y = dot_split(x, onehot, NT) * keep
    for i in range(block):
        put_scalar(a_ref, s0 + i, y[i * particles : (i + 1) * particles])


def list_body(
    block,
    q_hbm,
    rate_ref,
    rsel_ref,
    ot_ref,
    lcol_ref,
    a_hbm,
    base_hbm,
    token_ref,
    q_ref,
    a_ref,
    base_ref,
    in_sem,
    a_sem,
    base_sem,
):
    scalars, particles, cells = q_ref.shape
    into = Stream(q_hbm, q_ref, in_sem, block)
    out_a = Stream(a_ref, a_hbm, a_sem, block * SUB, 2)
    out_base = Stream(base_ref, base_hbm, base_sem, block * SUB, 2)
    into.start_all()
    token_ref[...] = rate_ref[:, :LANES]
    leaves = cell_onehot(lcol_ref, cells)
    places = lcol_ref.shape[0]
    side = max(1, LANES // places)
    keep = 1.0 - rate_ref[...]
    half = block * particles

    def step(b, carry):
        into.copy(b).wait()
        x = q_ref[pl.ds(b * block, block)].reshape(half, cells) * keep
        both = jnp.concatenate(halves(x), axis=0)
        y = dot(both, ot_ref[...], NT)
        y = y[:half] + y[half:]
        z = dot(both, leaves, NT)
        z = z[:half] + z[half:]
        for i in range(block):
            put_scalar(a_ref, b * block + i, y[i * particles : (i + 1) * particles])
            mine = z[i * particles : (i + 1) * particles]
            for o in range(base_ref.shape[1]):
                octets = [
                    mine[(o * side + u) * SUB : (o * side + u + 1) * SUB] for u in range(side)
                ]
                wide = jnp.concatenate(octets, axis=1)
                for t in range(base_ref.shape[0]):
                    at = pl.ds((b * block + i) * SUB, SUB)
                    base_ref[t, o, at, :] = wide[:, t * LANES : (t + 1) * LANES]
        out_a.copy(b).start()
        out_base.copy(b).start()
        return carry

    lax.fori_loop(0, scalars // block, step, 0)
    for ref, out in ((a_ref, out_a), (base_ref, out_base)):
        clear_rest(scalars, ref)
        for b in range(scalars // block, out.count):
            out.copy(b, out.tail(b)).start()
    out_a.wait_all()
    out_base.wait_all()


def clear_rest(scalars, ref):
    rest = ref.shape[2] - scalars * SUB
    for t in range(ref.shape[0]):
        for o in range(ref.shape[1]):
            ref[t, o, pl.ds(scalars * SUB, rest), :] = jnp.zeros((rest, LANES), F32)


def open_body(
    block,
    p_hbm,
    partner_hbm,
    rate_hbm,
    list_hbm,
    q_hbm,
    a_hbm,
    ot_ref,
    rsel_ref,
    p_ref,
    q_ref,
    a_ref,
    partner_ref,
    rate_ref,
    list_ref,
    in_sem,
    out_sem,
    a_sem,
    few_sem,
):
    scalars, _, cells = p_ref.shape
    into, out = Stream(p_hbm, p_ref, in_sem, block), Stream(q_ref, q_hbm, out_sem, block)
    few = [
        pltpu.make_async_copy(src, dst, few_sem.at[i])
        for i, (src, dst) in enumerate(
            [(list_hbm, list_ref), (rate_hbm, rate_ref), (partner_hbm, partner_ref)]
        )
    ]
    for c in few:
        c.start()
    into.start_all()
    for c in few:
        c.wait()
    column = jnp.broadcast_to(list_ref[...].astype(F32), (SUB, list_ref.shape[1])).T[:, :1]
    cell = lax.broadcasted_iota(I32, ot_ref.shape, 1).astype(F32)
    onehot = (column == cell).astype(F32)
    ot_ref[...] = onehot.astype(BF)
    rate = jnp.broadcast_to(rate_ref[...], (SUB, cells))
    rsel_ref[...] = dot_split(rate, onehot.astype(BF), NT)
    clear_rest(scalars, a_ref)

    def step(b, carry):
        into.copy(b).wait()
        mix(b * block, block, p_ref, partner_ref, q_ref)
        out.copy(b).start()
        list_cells(b * block, block, q_ref, ot_ref[...], 1.0 - rsel_ref[0:1, :], a_ref)
        return carry

    lax.fori_loop(0, scalars // block, step, 0)
    last = pltpu.make_async_copy(a_ref, a_hbm, a_sem)
    last.start()
    out.wait_all()
    last.wait()


def settle_block(s0, block, q_ref, f_ref, r_ref, ot_ref, rate_ref, out_ref, devices):
    _, particles, cells = q_ref.shape
    tiles = cells // LANES
    rate = rate_ref[...]
    keep = 1.0 - rate
    r = jnp.concatenate([get_scalar(r_ref, s0 + i) for i in range(block)], axis=0)
    spread = dot(r.astype(BF), ot_ref[...], NN)
    for i in range(block):
        s = s0 + i
        at = lax.rem(s, devices) * (f_ref.shape[0] // devices) + lax.div(s, devices) * tiles
        f = jnp.concatenate([f_ref[pl.ds(at + t, 1), :] for t in range(tiles)], axis=1)
        out_ref[s0 + i] = (
            keep * q_ref[s0 + i] + rate * f + spread[i * particles : (i + 1) * particles]
        )


def middle_body(
    block,
    devices,
    q_hbm,
    f_ref,
    r_hbm,
    ot_ref,
    rate_ref,
    partner_ref,
    out_hbm,
    token_ref,
    q_ref,
    now_ref,
    r_ref,
    in_sem,
    out_sem,
    r_sem,
):
    scalars = q_ref.shape[0]
    into, out = Stream(q_hbm, q_ref, in_sem, block), Stream(q_ref, out_hbm, out_sem, block)
    changes = Stream(r_hbm, r_ref, r_sem, block * SUB, 2)
    for b in range(q_ref.shape[0] // block):
        changes.copy(b).start()
        into.copy(b).start()
    token_ref[...] = rate_ref[:, :LANES]

    def step(b, carry):
        changes.copy(b).wait()
        into.copy(b).wait()
        s0 = b * block
        settle_block(s0, block, q_ref, f_ref, r_ref, ot_ref, rate_ref, now_ref, devices)
        mix(s0, block, now_ref, partner_ref, q_ref)
        out.copy(b).start()
        return carry

    lax.fori_loop(0, scalars // block, step, 0)
    out.wait_all()


def half_silu(y):
    return (y + y * jnp.tanh(y)).astype(BF)


def chem_body(
    devices,
    rows,
    count_ref,
    f_ref,
    a_hbm,
    ot_ref,
    rsel_ref,
    w1_ref,
    w2_ref,
    w3_ref,
    token_ref,
    *refs,
):
    pos_refs, refs = refs[:-11], refs[-11:]
    r_hbm, s_ref, a_ref, r_ref, pull_ref, one_a, one_b, two_a, two_b, in_sem, out_sem = refs
    tiles = ot_ref.shape[1] // LANES
    listed = ot_ref.shape[0]
    particles = a_ref.shape[1] * SUB
    into, out = Stream(a_hbm, a_ref, in_sem, 1, 1), Stream(r_ref, r_hbm, out_sem, 1, 1)
    into.start_all()
    f = load_filtered(f_ref, devices, rows, tiles)
    pull_ref[...] = rsel_ref[0:1, :] * dot_split(f, ot_ref[...], NT)
    live = lax.broadcasted_iota(I32, (1, listed), 1) < count_ref[0]

    def first(g):
        parts = []
        for i in range(2):
            p = 2 * g + i
            at = pl.ds(p & (SUB - 1), rows, stride=SUB)
            for t in range(listed // LANES):
                pull = pull_ref[:, t * LANES : (t + 1) * LANES]
                parts.append((a_ref[t, p >> 3, at, :] + pull).astype(BF))
        return half_silu(dot(w1_ref[...], jnp.concatenate(parts, axis=1), NN))

    def second(one):
        return half_silu(dot(w2_ref[...], one, NN))

    def third(g, two, total):
        change = dot(w3_ref[...], two, NN).astype(BF).astype(F32)
        for i in range(2):
            r = jnp.where(live, change[:, i * listed : (i + 1) * listed], 0.0)
            p = 2 * g + i
            at = pl.ds(p & (SUB - 1), rows, stride=SUB)
            for t in range(listed // LANES):
                r_ref[t, p >> 3, at, :] = r[:, t * LANES : (t + 1) * LANES]
            total = total + r
        return total

    def step(g, total, old, new):
        new[0][...] = first(g)
        new[1][...] = second(old[0][...])
        return third(g - 2, old[1][...], total)

    left, right = (one_a, two_a), (one_b, two_b)

    def pair(m, total):
        total = step(2 * m, total, right, left)
        return step(2 * m + 1, total, left, right)

    total = jnp.zeros((rows, listed), F32)
    each = SUB // 4
    for o in range(particles // SUB):
        into.copy(o).wait()
        if o == 0:
            one_a[...] = first(0)
            two_b[...] = second(one_a[...])
            one_b[...] = first(1)
        total = lax.fori_loop(max(1, o * each), (o + 1) * each, pair, total)
        if o:
            out.copy(o - 1).start()
    last = particles // 2 - 1
    total = third(last - 1, two_b[...], total)
    total = third(last, second(one_b[...]), total)
    out.copy(particles // SUB - 1).start()
    source = total * (1.0 / particles)
    if pos_refs:
        boxes_source(source, *pos_refs, s_ref)
    else:
        source = dot_split(source, ot_ref[...], NN)
        stride = s_ref.shape[0] // devices
        for i in range(rows // devices):
            for t in range(tiles):
                part = source[i * devices : (i + 1) * devices, t * LANES : (t + 1) * LANES]
                s_ref[pl.ds(i * tiles + t, devices, stride=stride), :] = part
    out.wait_all()


def boxes_source(source, pos_ref, s_ref):
    listed = source.shape[1]
    boxes = s_ref.shape[0]
    put = lax.broadcasted_iota(I32, (listed, boxes * LANES), 1).astype(F32) == pos_ref[:, :1]
    sent = dot_split(source, put.astype(F32).astype(BF), NN)
    for b in range(boxes):
        s_ref[b] = sent[: s_ref.shape[1], b * LANES : (b + 1) * LANES]


def early_body(
    devices,
    rows,
    span,
    scalars,
    particles,
    count_ref,
    f_ref,
    base_hbm,
    ot_ref,
    rate_ref,
    lcol_ref,
    w1_ref,
    w2_ref,
    w3_ref,
    token_ref,
    out_ref,
    end_ref,
    v_ref,
    base_ref,
    sem,
):
    load = pltpu.make_async_copy(base_hbm, base_ref, sem)
    load.start()
    listed, cells = ot_ref.shape
    tiles = cells // LANES
    places = lcol_ref.shape[0]
    side = max(1, LANES // places)
    wide = base_ref.shape[0]
    end_ref[...] = rate_ref[:, :LANES]
    f = load_filtered(f_ref, devices, rows, tiles)
    leaves = cell_onehot(lcol_ref, cells)
    rate = dot_split(jnp.broadcast_to(rate_ref[...], (SUB, cells)), leaves, NT)[:1]
    pull = rate * dot_split(f, leaves, NT)
    live = (lax.broadcasted_iota(I32, (SUB, listed), 1) < count_ref[0]).astype(F32).astype(BF)
    live = dot(dot(live, ot_ref[...], NN).astype(BF), leaves, NT)[:1]
    pull = jnp.concatenate([pull] * side, axis=1)
    live = jnp.concatenate([live] * side, axis=1) > 0.5
    count = 4 // wide
    load.wait()

    for o in range(particles // SUB // side):
        for i in range(0, SUB, count):
            ats = [pl.ds(i + u, rows, stride=SUB) for u in range(count)]
            x = jnp.concatenate(
                [
                    base_ref[t, o, at, :] + pull[:, t * LANES : (t + 1) * LANES]
                    for at in ats
                    for t in range(wide)
                ],
                axis=1,
            )
            one = half_silu(dot(w1_ref[...], x.astype(BF), NN))
            two = half_silu(dot(w2_ref[...], one, NN))
            change = dot(w3_ref[...], two, NN).astype(BF).astype(F32)
            for n, (at, t) in enumerate((at, t) for at in ats for t in range(wide)):
                cols = slice(n * LANES, (n + 1) * LANES)
                mask = live[:, t * LANES : (t + 1) * LANES]
                v_ref[t, o, at, :] = x[:, cols] + jnp.where(mask, change[:, cols], 0.0)

    per = LANES // particles
    stride = out_ref.shape[0] // devices

    def scalar(s):
        parts = []
        for o in range(particles // SUB // side):
            at = pl.ds(s * SUB, SUB)
            row = jnp.concatenate([v_ref[t, o, at, :] for t in range(wide)], axis=1)
            parts += [row[:, u * places : (u + 1) * places] for u in range(side)]
        return jnp.concatenate(parts, axis=0)

    def part(b, count):
        value = jnp.concatenate([scalar(b * per + i) for i in range(count)], axis=0)
        if count < per:
            rest = jnp.zeros(((per - count) * particles, places), F32)
            value = jnp.concatenate([value, rest], axis=0)
        value = value.T
        for c in range(places // devices):
            at = pl.ds(c * span + b, devices, stride=stride)
            out_ref[at, :] = value[c * devices : (c + 1) * devices]

    def step(b, carry):
        part(b, per)
        return carry

    whole = scalars // per
    lax.fori_loop(0, whole, step, 0, unroll=2)
    zeros = jnp.zeros((devices, LANES), F32)
    for c in range(places // devices):
        for b in range(whole, span):
            out_ref[pl.ds(c * span + b, devices, stride=stride), :] = zeros
    if scalars > whole * per:
        part(whole, scalars - whole * per)


def columns(row_ref, devices, out_ref, turn_ref):
    places = row_ref.shape[1]
    count = places // devices
    column = jnp.broadcast_to(row_ref[...].astype(F32), (SUB, places)).T[:, :1]
    turn_ref[...] = jnp.broadcast_to(column, turn_ref.shape)
    for c in range(count):
        part = turn_ref[pl.ds(c, devices, stride=count), :]
        out_ref[c * devices : (c + 1) * devices] = part.astype(I32)


def maps_body(
    dims,
    me_ref,
    inv_ref,
    ot_ref,
    owner_ref,
    slot_ref,
    leave_ref,
    arrive_ref,
    pos_ref,
    put_ref,
    lcol_ref,
    acol_ref,
    turn_ref,
):
    nx, ny, _, bx, by = dims
    columns(leave_ref, nx * ny, lcol_ref, turn_ref)
    columns(arrive_ref, nx * ny, acol_ref, turn_ref)
    quads = bx * by
    turns = quads * ny
    _, cells = ot_ref.shape
    at = me_ref[0] * 2 * turns + me_ref[1]
    code = jnp.concatenate([inv_ref[pl.ds(at + k * ny, 1), :] for k in range(quads)], axis=1)
    box = lax.rem(code, ny).astype(F32)
    boxes = lax.broadcasted_iota(I32, (ny, cells), 0).astype(F32)
    mine = (jnp.broadcast_to(box, (ny, cells)) == boxes).astype(F32)
    before = lax.broadcasted_iota(I32, (cells, cells), 0) < lax.broadcasted_iota(
        I32, (cells, cells), 1
    )
    count = dot(mine.astype(BF), before.astype(F32).astype(BF), NN)
    rank = jnp.sum(mine * count, axis=0, keepdims=True)
    rest = jnp.zeros((SUB - 2, cells), F32)
    found = dot(ot_ref[...], jnp.concatenate([box, rank, rest], axis=0).astype(BF), NT)
    pos = found[:, :1] * LANES + found[:, 1:2]
    pos_ref[...] = jnp.broadcast_to(pos, pos_ref.shape)
    flat = lambda ref: jnp.concatenate([ref[j : j + 1, :] for j in range(quads)], axis=1)
    owner, slot = flat(owner_ref).astype(F32), flat(slot_ref).astype(F32)
    first = owner * cells
    key = first + slot
    column = jnp.broadcast_to(key, (SUB, cells)).T[:, :1]
    ahead = (column < key) & (column >= first)
    place = owner * LANES + jnp.sum(ahead.astype(F32), axis=0, keepdims=True)
    step = min(cells, put_ref.shape[0])
    for b in range(put_ref.shape[0] // step):
        row = lax.broadcasted_iota(I32, (step, cells), 0).astype(F32) + b * step
        put_ref[b * step : (b + 1) * step] = (row == place).astype(F32).astype(BF)


def unpack_body(devices, own, s_ref, arr_ref, put_ref, out_ref):
    boxes, _ = s_ref.shape[:2]
    cells = put_ref.shape[1]
    quads = cells // LANES
    scalars = out_ref.shape[0] // quads
    stride = arr_ref.shape[0] // devices
    got = jnp.concatenate([s_ref[b] for b in range(boxes)], axis=1)
    source = dot_split(got, put_ref[...], NN)
    for j in range(quads):
        for i in range(own):
            n = min(devices, scalars - i * devices)
            if n > 0:
                grid = arr_ref[pl.ds(stride - own * quads + i * quads + j, n, stride=stride), :]
                part = source[i * devices : i * devices + n, j * LANES : (j + 1) * LANES]
                out_ref[pl.ds(i * devices * quads + j, n, stride=quads), :] = grid + part


def cell_onehot(col_ref, cells):
    shape = (col_ref.shape[0], cells)
    return (col_ref[:, :1] == lax.broadcasted_iota(I32, shape, 1)).astype(F32).astype(BF)


def settle_body(
    block,
    devices,
    q_hbm,
    f_ref,
    r_hbm,
    ot_ref,
    rate_ref,
    out_hbm,
    token_ref,
    q_ref,
    out_ref,
    r_ref,
    in_sem,
    out_sem,
    r_sem,
):
    into, out = Stream(q_hbm, q_ref, in_sem, block), Stream(out_ref, out_hbm, out_sem, block)
    changes = Stream(r_hbm, r_ref, r_sem, block * SUB, 2)
    for b in range(q_ref.shape[0] // block):
        changes.copy(b).start()
        into.copy(b).start()
    token_ref[...] = rate_ref[:, :LANES]

    def step(b, carry):
        changes.copy(b).wait()
        into.copy(b).wait()
        settle_block(b * block, block, q_ref, f_ref, r_ref, ot_ref, rate_ref, out_ref, devices)
        out.copy(b).start()
        return carry

    lax.fori_loop(0, q_ref.shape[0] // block, step, 0)
    out.wait_all()


def arrive_body(
    span, devices, p_hbm, arr_ref, acol_ref, out_hbm, p_ref, out_ref, hit_ref, in_sem, out_sem
):
    scalars, particles, cells = p_ref.shape
    places = acol_ref.shape[0]
    per = LANES // particles
    into, out = Stream(p_hbm, p_ref, in_sem, per), Stream(out_ref, out_hbm, out_sem, per)
    into.start_all()
    hit = (acol_ref[:, :1] == lax.broadcasted_iota(I32, (places, cells), 1)).astype(F32)
    hit_ref[...] = hit.astype(BF)
    taken = jnp.sum(hit, axis=0, keepdims=True) > 0.5
    stride = arr_ref.shape[0] // devices
    count = places // devices

    def place(b, size):
        first = stride - count * span + b
        x = jnp.concatenate(
            [arr_ref[pl.ds(first + c * span, devices, stride=stride), :] for c in range(count)],
            axis=0,
        ).T
        y = dot_split(x, hit_ref[...], NN)
        into.copy(b, size).wait()
        for i in range(size):
            s = b * per + i
            out_ref[s] = jnp.where(taken, y[i * particles : (i + 1) * particles], p_ref[s])
        out.copy(b, size).start()

    def step(b, carry):
        place(b, per)
        return carry

    whole = scalars // per
    lax.fori_loop(0, whole, step, 0)
    if scalars > whole * per:
        place(whole, scalars - whole * per)
    out.wait_all()


def stencil(value, speed, bx, by, lanes_y):
    boxes = value[0].shape[0]
    row = lax.broadcasted_iota(I32, value[0].shape, 0) % lanes_y
    zero = jnp.zeros((lanes_y, LANES), F32)

    def x_low(v):
        return jnp.concatenate([zero, v[: boxes - lanes_y]], axis=0)

    def x_high(v):
        return jnp.concatenate([v[lanes_y:], zero], axis=0)

    def y_low(v):
        return jnp.where(row == 0, 0.0, pltpu.roll(v, 1, 0))

    def y_high(v):
        return jnp.where(row == lanes_y - 1, 0.0, pltpu.roll(v, boxes - 1, 0))

    out = []
    for i in range(bx):
        for j in range(by):
            c = value[i * by + j]
            up = value[(i - 1) * by + j] if i else x_low(value[(bx - 1) * by + j])
            down = value[(i + 1) * by + j] if i < bx - 1 else x_high(value[j])
            left = value[i * by + j - 1] if j else y_low(value[i * by + by - 1])
            right = value[i * by + j + 1] if j < by - 1 else y_high(value[i * by])
            beside = up + down + left + right + pltpu.roll(c, 1, 1) + pltpu.roll(c, LANES - 1, 1)
            out.append(c + DIFFUSION * (beside - 6.0 * c) - speed[i * by + j] * (c - up))
    return out


def route(src_ref, first_row, row_step, item_step, items, own, quads, lanes_y, rows, lanes):
    shape = (lanes_y, LANES)
    out = []
    for k in range(len(rows)):

        def step(y, acc):
            for j in range(items):
                hit = rows[k] == (j * lanes_y + y)
                at = first_row + y * row_step + j * item_step
                lines = [src_ref[pl.ds(at + s * quads, 1), :] for s in range(own)]
                acc = [
                    jnp.where(
                        hit,
                        jnp.take_along_axis(jnp.broadcast_to(v, shape), lanes[k], axis=1),
                        old,
                    )
                    for v, old in zip(lines, acc)
                ]
            return tuple(acc)

        zero = tuple(jnp.zeros(shape, F32) for _ in range(own))
        out.append(lax.fori_loop(0, lanes_y, step, zero, unroll=min(lanes_y, 8)))
    return [[out[k][s] for k in range(len(rows))] for s in range(own)]


def load_rows(ref, offset, stride, count):
    return ref[pl.ds(offset, count, stride=stride), :]


def pack_body(
    width,
    lanes_y,
    grid_hbm,
    owner_hbm,
    slot_hbm,
    speed_hbm,
    out_ref,
    grid_ref,
    owner_ref,
    slot_ref,
    speed_ref,
    sem,
):
    pairs = [
        (grid_hbm, grid_ref),
        (owner_hbm, owner_ref),
        (slot_hbm, slot_ref),
        (speed_hbm, speed_ref),
    ]
    copies = [pltpu.make_async_copy(a, b, sem.at[i]) for i, (a, b) in enumerate(pairs)]
    for c in copies:
        c.start()
    for c in copies:
        c.wait()
    quads = owner_ref.shape[0]
    stride = width + 2 * quads
    total = grid_ref.shape[0]
    slot = slot_ref[...]
    label = ((slot >> 7) * lanes_y + owner_ref[...]) * LANES + (slot & (LANES - 1))
    tail = jnp.concatenate([label.astype(F32), speed_ref[...]], axis=0)
    devices = out_ref.shape[0] // stride
    for d in range(devices):
        for i in range(width // quads):
            at = d * stride + i * quads
            src = (i * devices + d) * quads
            if src < total:
                out_ref[at : at + quads] = grid_ref[src : src + quads]
            else:
                out_ref[at : at + quads] = jnp.zeros((quads, LANES), F32)
        out_ref[d * stride + width : (d + 1) * stride] = tail


def weights_body(w1_ref, w2_ref, w3_ref, token_ref, a_ref, b_ref, c_ref):
    scalars, hidden = w1_ref.shape
    rest = jnp.zeros((a_ref.shape[1] - scalars, hidden), F32)
    a_ref[...] = jnp.concatenate([w1_ref[...].astype(F32) * 0.5, rest], axis=0).T.astype(BF)
    b_ref[...] = (w2_ref[...].astype(F32) * 0.5).astype(BF)
    c_ref[...] = jnp.concatenate([w3_ref[...].astype(F32), rest], axis=0).astype(BF)


def start_body(dims, arr_ref, token_ref, g_ref, f_ref, inv_ref, lab_ref):
    nx, ny, own, bx, by = dims
    quads = bx * by
    boxes = nx * ny
    width = own * quads
    stride = width + 2 * quads
    turns = quads * ny
    speed = [load_rows(arr_ref, width + quads + j, stride, boxes) for j in range(quads)]
    for s in range(own):
        value = [load_rows(arr_ref, s * quads + j, stride, boxes) for j in range(quads)]
        for j, v in enumerate(stencil(value, speed, bx, by, ny)):
            g_ref[pl.ds(s * quads + j, boxes, stride=width), :] = v
    for j in range(quads):
        lab_ref[pl.ds(j * boxes, boxes), :] = load_rows(arr_ref, width + j, stride, boxes).astype(
            I32
        )
    lane_of = lax.broadcasted_iota(I32, (turns, LANES), 1).astype(F32).astype(BF)
    sub_of = lax.broadcasted_iota(I32, (turns, LANES), 0).astype(F32).astype(BF)
    sub_lane = lax.broadcasted_iota(I32, (LANES, LANES), 0).astype(F32).astype(BF)
    none = jnp.zeros((turns, LANES), BF)
    unit = jnp.ones((LANES, LANES), BF)

    def group(x, carry):
        def gather(y, acc):
            left, right = [], []
            for j in range(quads):
                line = lab_ref[pl.ds(j * boxes + x * ny + y, 1), :]
                hit = jnp.broadcast_to((line >> 7).astype(F32).astype(BF), (turns, LANES)) == sub_of
                code = jnp.full((turns, LANES), j * ny + y).astype(F32).astype(BF)
                left.append(
                    jnp.concatenate([jnp.where(hit, code, none), jnp.where(hit, lane_of, none)], axis=0)
                )
                lane = jnp.broadcast_to((line & (LANES - 1)).astype(F32).astype(BF), (LANES, LANES))
                right.append(jnp.where(lane == sub_lane, unit, jnp.zeros_like(unit)))
            return acc + dot(
                jnp.concatenate(left, axis=1), jnp.concatenate(right, axis=1), NT
            )

        code = lax.fori_loop(0, ny, gather, jnp.zeros((2 * turns, LANES), F32), unroll=8)
        code = code.astype(I32)
        inv_ref[pl.ds(x * 2 * turns, 2 * turns), :] = code
        return carry

    lax.fori_loop(0, nx, group, 0)
    send_filtered(dims, g_ref, width, 0, inv_ref, f_ref)


def send_filtered(dims, g_ref, g_stride, g_first, inv_ref, f_ref):
    nx, ny, own, bx, by = dims
    quads = bx * by
    turns = quads * ny
    f_stride = f_ref.shape[0] // (nx * ny)

    def group(x, carry):
        base = x * 2 * turns
        rows = [inv_ref[pl.ds(base + k * ny, ny), :] for k in range(quads)]
        lanes = [inv_ref[pl.ds(base + turns + k * ny, ny), :] for k in range(quads)]
        first = x * ny * g_stride + g_first
        out = route(g_ref, first, g_stride, 1, quads, own, quads, ny, rows, lanes)
        for s in range(own):
            for k in range(quads):
                at = pl.ds(x * ny * f_stride + s * quads + k, ny, stride=f_stride)
                f_ref[at, :] = out[s][k]
        return carry

    lax.fori_loop(0, nx, group, 0)


def add_source(dims, s_ref, g_ref, lab_ref, out_ref):
    nx, ny, own, bx, by = dims
    quads = bx * by
    boxes = nx * ny
    width = own * quads
    stride = s_ref.shape[0] // boxes

    def group(x, carry):
        labels = [lab_ref[pl.ds(j * boxes + x * ny, ny), :] for j in range(quads)]
        rows = [v >> 7 for v in labels]
        lanes = [v & (LANES - 1) for v in labels]
        out = route(s_ref, x * ny * stride, stride, 1, quads, own, quads, ny, rows, lanes)
        for s in range(own):
            for k in range(quads):
                at = pl.ds(x * ny * width + s * quads + k, ny, stride=width)
                out_ref[at, :] = g_ref[at, :] + out[s][k]
        return carry

    lax.fori_loop(0, nx, group, 0)


def again_body(dims, s_ref, g_ref, arr_ref, inv_ref, lab_ref, token_ref, f_ref, mid_ref):
    nx, ny, own, bx, by = dims
    quads = bx * by
    boxes = nx * ny
    width = own * quads
    stride = width + 2 * quads
    add_source(dims, s_ref, g_ref, lab_ref, mid_ref)
    speed = [load_rows(arr_ref, width + quads + j, stride, boxes) for j in range(quads)]
    for s in range(own):
        value = [load_rows(mid_ref, s * quads + j, width, boxes) for j in range(quads)]
        for j, v in enumerate(stencil(value, speed, bx, by, ny)):
            f_ref[pl.ds(width + s * quads + j, boxes, stride=2 * width), :] = v
    send_filtered(dims, f_ref, 2 * width, width, inv_ref, f_ref)


def per_device(
    grid_scalars,
    axial_speed,
    particles,
    cell_owner,
    cell_slot,
    mix_rate,
    partner,
    chem_input,
    chem_hidden,
    chem_output,
    react_slots,
    react_count,
    leave_slots,
    arrive_slots,
):
    both = ("gx", "gy")
    nx, ny = lax.axis_size("gx"), lax.axis_size("gy")
    devices = nx * ny
    scalars, bx, by, nz = grid_scalars.shape
    heads, cells = partner.shape
    listed = react_slots.shape[1]
    hidden = chem_hidden.shape[0]
    quads = bx * by
    own = -(-scalars // devices)
    rows = devices * own
    width = own * quads
    tiles = cells // LANES
    assert nz == LANES and tiles == quads and heads % SUB == 0 and LANES % heads == 0
    dims = (nx, ny, own, bx, by)
    flat = devices * width

    box = [
        grid_scalars.reshape(-1, LANES),
        cell_owner.reshape(quads, LANES),
        cell_slot.reshape(quads, LANES),
        axial_speed.reshape(quads, LANES),
    ]
    (first,) = call(
        functools.partial(pack_body, width, ny),
        [((devices * (width + 2 * quads), LANES), F32)],
        box,
        hbm=(0, 1, 2, 3),
        scratch=[pltpu.VMEM(x.shape, x.dtype) for x in box] + [pltpu.SemaphoreType.DMA((4,))],
    )

    def exchange(x):
        x = x.reshape(devices, -1, LANES)
        return lax.all_to_all(x, both, split_axis=0, concat_axis=0, tiled=True).reshape(-1, LANES)

    arrival = exchange(first)

    rate = mix_rate.reshape(1, cells)
    state_shape = (scalars, heads, cells)
    listed_shape = (listed // LANES, heads // SUB, rows * SUB, LANES)
    block = divisor(scalars, 6)
    octets = heads // SUB
    state_vmem = pltpu.VMEM(state_shape, F32)
    listed_vmem = pltpu.VMEM(listed_shape, F32)
    dma = pltpu.SemaphoreType.DMA
    per_block = dma((scalars // block,))
    per_listed = dma((-(-rows // block),))
    q, a, ot, rsel = call(
        functools.partial(open_body, block),
        [
            (state_shape, F32, True),
            (listed_shape, F32, True),
            ((listed, cells), BF),
            ((SUB, listed), F32),
        ],
        [particles, partner, rate, react_slots],
        hbm=(0, 1, 2, 3),
        scratch=[
            state_vmem,
            state_vmem,
            listed_vmem,
            pltpu.VMEM(partner.shape, I32),
            pltpu.VMEM(rate.shape, F32),
            pltpu.VMEM(react_slots.shape, I32),
            per_block,
            per_block,
            dma,
            dma((3,)),
        ],
    )
    grid, sent, inv, lab = call(
        functools.partial(start_body, dims),
        [
            ((flat, LANES), F32),
            ((flat, LANES), F32),
            ((nx * 2 * quads * ny, LANES), I32),
            ((quads * devices, LANES), I32),
        ],
        [arrival, rsel],
    )

    w1, w2, w3 = call(
        weights_body,
        [((hidden, rows), BF), ((hidden, hidden), BF), ((rows, hidden), BF)],
        [chem_input.T, chem_hidden, chem_output, lab],
    )

    per = LANES // heads
    span = SUB * (-(-scalars // (per * SUB)))
    places = leave_slots.shape[1]
    side = max(1, LANES // places)
    base_shape = (max(1, places // LANES), octets // side, rows * SUB, LANES)
    kept = SUB * (-(-scalars // SUB))
    pair = pltpu.VMEM((hidden, 2 * listed), BF)
    me = jnp.stack([lax.axis_index("gx"), lax.axis_index("gy")]).astype(I32)
    pos, put, lcol, acol = call(
        functools.partial(maps_body, dims),
        [
            ((listed, LANES), F32),
            ((ny * LANES, cells), BF),
            ((places, LANES), I32),
            ((places, LANES), I32),
        ],
        [me, inv, ot, box[1], box[2], leave_slots, arrive_slots],
        smem=(0,),
        scratch=[pltpu.VMEM((places, LANES), F32)],
    )

    def chemistry(f, a, token, out, more=()):
        return call(
            functools.partial(chem_body, devices, rows),
            [(listed_shape, F32, True), (out, F32)],
            [react_count, f, a, ot, rsel, w1, w2, w3, token, *more],
            smem=(0,),
            hbm=(2,),
            scratch=[listed_vmem, listed_vmem, pltpu.VMEM((rows, listed), F32)]
            + [pair] * 4
            + [dma((octets,)), dma((octets,))],
        )

    f = exchange(sent)
    change, source = chemistry(f, a, pos, (flat, LANES))
    home = exchange(source)
    q, token = call(
        functools.partial(middle_body, block, devices),
        [(state_shape, F32, True), ((1, LANES), F32)],
        [q, f, change, ot, rate, partner],
        hbm=(0, 2),
        scratch=[state_vmem, state_vmem, listed_vmem, per_block, per_block, per_listed],
    )
    (sent,) = call(
        functools.partial(again_body, dims),
        [((2 * flat, LANES), F32)],
        [home, grid, arrival, inv, lab, token],
        scratch=[pltpu.VMEM((flat, LANES), F32)],
    )
    a, base, token = call(
        functools.partial(list_body, block),
        [(listed_shape, F32, True), (base_shape, F32, True), ((1, LANES), F32)],
        [q, rate, rsel, ot, lcol],
        hbm=(0,),
        scratch=[
            state_vmem,
            listed_vmem,
            pltpu.VMEM(base_shape, F32),
            per_block,
            per_listed,
            per_listed,
        ],
    )
    f = exchange(sent)
    leaving, token = call(
        functools.partial(early_body, devices, rows, span, scalars, heads),
        [((places * span, LANES), F32), ((1, LANES), F32)],
        [react_count, f, base, ot, rate, lcol, w1, w2, w3, token],
        smem=(0,),
        hbm=(2,),
        scratch=[pltpu.VMEM(base_shape, F32), pltpu.VMEM(base_shape, F32), dma],
    )
    change, source = chemistry(f, a, token, (ny, kept, LANES), [pos])
    moved = exchange(leaving)
    state, token = call(
        functools.partial(settle_body, block, devices),
        [(state_shape, F32, True), ((1, LANES), F32)],
        [q, f, change, ot, rate],
        hbm=(0, 2),
        scratch=[state_vmem, state_vmem, listed_vmem, per_block, per_block, per_listed],
    )
    source = lax.all_to_all(source, "gy", split_axis=0, concat_axis=0, tiled=True)
    (grid,) = call(
        functools.partial(unpack_body, devices, own),
        [((scalars * quads, LANES), F32)],
        [source, f, put],
    )
    grid_out = grid.reshape(grid_scalars.shape)
    steps = -(-scalars // per)
    (state,) = call(
        functools.partial(arrive_body, span, devices),
        [(state_shape, F32, True)],
        [state, moved, acol],
        hbm=(0,),
        scratch=[
            state_vmem,
            state_vmem,
            pltpu.VMEM((places, cells), BF),
            dma((steps,)),
            dma((steps,)),
        ],
    )
    return (grid_out, state)


def solution(mesh):
    placed = (
        P(None, "gx", "gy", None),
        P("gx", "gy", None),
        P(None, None, ("gx", "gy")),
        P("gx", "gy", None),
        P("gx", "gy", None),
        P(("gx", "gy")),
        P(None, ("gx", "gy")),
        P(),
        P(),
        P(),
        P(("gx", "gy"), None),
        P(("gx", "gy")),
        P(("gx", "gy"), None),
        P(("gx", "gy"), None),
    )

    return jax.shard_map(
        per_device,
        mesh=mesh,
        in_specs=placed,
        out_specs=(P(None, "gx", "gy", None), P(None, None, ("gx", "gy"))),
        check_vma=False,
    )
```

```python
import functools

import jax
import jax.numpy as jnp
from jax import lax
from jax.experimental import pallas as pl
from jax.experimental.pallas import tpu as pltpu
from jax.sharding import PartitionSpec as P


DIFFUSION = 0.1
PAIR_WEIGHT = 0.4
LANES = 128
SUB = 8
BF = jnp.bfloat16
F32 = jnp.float32
I32 = jnp.int32

NT = (((1,), (1,)), ((), ()))
NN = (((1,), (0,)), ((), ()))


def call(body, outs, ins, smem=(), hbm=(), scratch=(), limit=24):
    spaces = {**{i: pltpu.SMEM for i in smem}, **{i: pl.ANY for i in hbm}}
    ins = [pltpu.with_memory_space_constraint(x, pltpu.HBM) if i in hbm else x for i, x in enumerate(ins)]
    return pl.pallas_call(
        body,
        out_shape=[
            pltpu.HBM(o[0], o[1]) if len(o) > 2 else jax.ShapeDtypeStruct(o[0], o[1]) for o in outs
        ],
        in_specs=[
            pl.BlockSpec(memory_space=spaces.get(i, pltpu.VMEM)) for i in range(len(ins))
        ],
        out_specs=[
            pl.BlockSpec(memory_space=pl.ANY if len(o) > 2 else pltpu.VMEM) for o in outs
        ],
        scratch_shapes=list(scratch),
        compiler_params=pltpu.CompilerParams(vmem_limit_bytes=limit << 20),
    )(*ins)


class Stream:
    def __init__(self, src, dst, sem, size, dim=0):
        self.src, self.dst, self.sem, self.size, self.dim = src, dst, sem, size, dim
        self.count = -(-src.shape[dim] // size)

    def copy(self, i, size=None):
        at = (slice(None),) * self.dim + (pl.ds(i * self.size, size or self.size),)
        return pltpu.make_async_copy(self.src.at[at], self.dst.at[at], self.sem.at[i])

    def tail(self, i):
        return min(self.size, self.src.shape[self.dim] - i * self.size)

    def start_all(self):
        for i in range(self.count):
            self.copy(i, self.tail(i)).start()

    def wait_all(self, first=0):
        for i in range(first, self.count):
            self.copy(i, self.tail(i)).wait()


def dot(a, b, dims):
    return lax.dot_general(a, b, dims, preferred_element_type=F32)


def halves(x):
    high = x.astype(BF)
    return high, (x - high.astype(F32)).astype(BF)


def dot_split(x, onehot, dims):
    high, low = halves(x)
    y = dot(jnp.concatenate([high, low], axis=0), onehot, dims)
    return y[: x.shape[0]] + y[x.shape[0] :]


def load_filtered(f_ref, devices, rows, tiles):
    stride = f_ref.shape[0] // devices
    return jnp.concatenate(
        [
            jnp.concatenate(
                [
                    f_ref[pl.ds(i * tiles + t, devices, stride=stride), :]
                    for i in range(rows // devices)
                ],
                axis=0,
            )
            for t in range(tiles)
        ],
        axis=1,
    )


def divisor(n, most):
    return max(k for k in range(1, most + 1) if n % k == 0)


def mix(s0, block, p_ref, partner_ref, q_ref):
    _, particles, cells = p_ref.shape
    groups = particles // SUB
    for t in range(cells // LANES):
        lanes = pl.ds(t * LANES, LANES)
        rows, homes = [], []
        for j in range(groups):
            index = partner_ref[pl.ds(j * SUB, SUB), lanes]
            rows.append(index & (SUB - 1))
            homes.append(index >> 3)

        def step(i, carry):
            s = s0 + i
            x = [p_ref[s, pl.ds(k * SUB, SUB), lanes] for k in range(groups)]
            for j in range(groups):
                mate = jnp.take_along_axis(x[0], rows[j], axis=0)
                for k in range(1, groups):
                    other = jnp.take_along_axis(x[k], rows[j], axis=0)
                    mate = jnp.where(homes[j] == k, other, mate)
                q_ref[s, pl.ds(j * SUB, SUB), lanes] = x[j] + PAIR_WEIGHT * (mate - x[j])
            return carry

        lax.fori_loop(0, block, step, 0, unroll=True)


def put_scalar(ref, s, value):
    for o in range(ref.shape[1]):
        for t in range(ref.shape[0]):
            part = value[o * SUB : (o + 1) * SUB, t * LANES : (t + 1) * LANES]
            ref[t, o, pl.ds(s * SUB, SUB), :] = part


def get_scalar(ref, s):
    return jnp.concatenate(
        [
            jnp.concatenate(
                [ref[t, o, pl.ds(s * SUB, SUB), :] for t in range(ref.shape[0])], axis=1
            )
            for o in range(ref.shape[1])
        ],
        axis=0,
    )


def list_cells(s0, block, q_ref, onehot, keep, a_ref):
    _, particles, cells = q_ref.shape
    x = q_ref[pl.ds(s0, block)].reshape(block * particles, cells)
    y = dot_split(x, onehot, NT) * keep
    for i in range(block):
        put_scalar(a_ref, s0 + i, y[i * particles : (i + 1) * particles])


def list_body(
    block,
    q_hbm,
    rate_ref,
    rsel_ref,
    ot_ref,
    lcol_ref,
    a_hbm,
    base_ref,
    token_ref,
    q_ref,
    a_ref,
    in_sem,
    a_sem,
):
    scalars, particles, cells = q_ref.shape
    into = Stream(q_hbm, q_ref, in_sem, block)
    out_a = Stream(a_ref, a_hbm, a_sem, block * SUB, 2)
    into.start_all()
    token_ref[...] = rate_ref[:, :LANES]
    leaves = cell_onehot(lcol_ref, cells)
    places = lcol_ref.shape[0]
    side = max(1, LANES // places)
    keep = 1.0 - rate_ref[...]
    half = block * particles

    def step(b, carry):
        into.copy(b).wait()
        x = q_ref[pl.ds(b * block, block)].reshape(half, cells) * keep
        both = jnp.concatenate(halves(x), axis=0)
        y = dot(both, ot_ref[...], NT)
        y = y[:half] + y[half:]
        z = dot(both, leaves, NT)
        z = z[:half] + z[half:]
        for i in range(block):
            put_scalar(a_ref, b * block + i, y[i * particles : (i + 1) * particles])
            mine = z[i * particles : (i + 1) * particles]
            for o in range(base_ref.shape[1]):
                octets = [
                    mine[(o * side + u) * SUB : (o * side + u + 1) * SUB] for u in range(side)
                ]
                wide = jnp.concatenate(octets, axis=1)
                for t in range(base_ref.shape[0]):
                    at = pl.ds((b * block + i) * SUB, SUB)
                    base_ref[t, o, at, :] = wide[:, t * LANES : (t + 1) * LANES]
        out_a.copy(b).start()
        return carry

    lax.fori_loop(0, scalars // block, step, 0)
    clear_rest(scalars, base_ref)
    clear_rest(scalars, a_ref)
    for b in range(scalars // block, out_a.count):
        out_a.copy(b, out_a.tail(b)).start()
    out_a.wait_all()


def clear_rest(scalars, ref):
    rest = ref.shape[2] - scalars * SUB
    for t in range(ref.shape[0]):
        for o in range(ref.shape[1]):
            ref[t, o, pl.ds(scalars * SUB, rest), :] = jnp.zeros((rest, LANES), F32)


def open_body(
    block,
    p_hbm,
    partner_hbm,
    rate_hbm,
    list_hbm,
    q_hbm,
    a_hbm,
    ot_ref,
    rsel_ref,
    p_ref,
    q_ref,
    a_ref,
    partner_ref,
    rate_ref,
    list_ref,
    in_sem,
    out_sem,
    a_sem,
    few_sem,
):
    scalars, _, cells = p_ref.shape
    into, out = Stream(p_hbm, p_ref, in_sem, block), Stream(q_ref, q_hbm, out_sem, block)
    out_a = Stream(a_ref, a_hbm, a_sem, block * SUB, 2)
    few = [
        pltpu.make_async_copy(src, dst, few_sem.at[i])
        for i, (src, dst) in enumerate(
            [(list_hbm, list_ref), (rate_hbm, rate_ref), (partner_hbm, partner_ref)]
        )
    ]
    for c in few:
        c.start()
    into.start_all()
    for c in few:
        c.wait()
    column = jnp.broadcast_to(list_ref[...].astype(F32), (SUB, list_ref.shape[1])).T[:, :1]
    cell = lax.broadcasted_iota(I32, ot_ref.shape, 1).astype(F32)
    onehot = (column == cell).astype(F32)
    ot_ref[...] = onehot.astype(BF)
    rate = jnp.broadcast_to(rate_ref[...], (SUB, cells))
    rsel_ref[...] = dot_split(rate, onehot.astype(BF), NT)
    clear_rest(scalars, a_ref)

    def step(b, carry):
        into.copy(b).wait()
        mix(b * block, block, p_ref, partner_ref, q_ref)
        out.copy(b).start()
        list_cells(b * block, block, q_ref, ot_ref[...], 1.0 - rsel_ref[0:1, :], a_ref)
        out_a.copy(b).start()
        return carry

    whole = scalars // block
    for b in range(whole, out_a.count):
        out_a.copy(b, out_a.tail(b)).start()
    lax.fori_loop(0, whole, step, 0)
    out.wait_all()
    out_a.wait_all()


def settle_block(s0, block, q_ref, f_ref, r_ref, ot_ref, rate_ref, out_ref, devices):
    _, particles, cells = q_ref.shape
    tiles = cells // LANES
    rate = rate_ref[...]
    keep = 1.0 - rate
    r = jnp.concatenate([get_scalar(r_ref, s0 + i) for i in range(block)], axis=0)
    spread = dot(r.astype(BF), ot_ref[...], NN)
    for i in range(block):
        s = s0 + i
        at = lax.rem(s, devices) * (f_ref.shape[0] // devices) + lax.div(s, devices) * tiles
        f = jnp.concatenate([f_ref[pl.ds(at + t, 1), :] for t in range(tiles)], axis=1)
        out_ref[s0 + i] = (
            keep * q_ref[s0 + i] + rate * f + spread[i * particles : (i + 1) * particles]
        )


def middle_body(
    block,
    devices,
    q_hbm,
    f_ref,
    r_hbm,
    ot_ref,
    rate_ref,
    partner_ref,
    out_hbm,
    token_ref,
    q_ref,
    now_ref,
    r_ref,
    in_sem,
    out_sem,
    r_sem,
):
    scalars = q_ref.shape[0]
    into, out = Stream(q_hbm, q_ref, in_sem, block), Stream(q_ref, out_hbm, out_sem, block)
    changes = Stream(r_hbm, r_ref, r_sem, block * SUB, 2)
    for b in range(q_ref.shape[0] // block):
        changes.copy(b).start()
        into.copy(b).start()
    token_ref[...] = rate_ref[:, :LANES]

    def step(b, carry):
        changes.copy(b).wait()
        into.copy(b).wait()
        s0 = b * block
        settle_block(s0, block, q_ref, f_ref, r_ref, ot_ref, rate_ref, now_ref, devices)
        mix(s0, block, now_ref, partner_ref, q_ref)
        out.copy(b).start()
        return carry

    lax.fori_loop(0, scalars // block, step, 0)
    out.wait_all()


def half_silu(y):
    return (y + y * jnp.tanh(y)).astype(BF)


def chem_body(
    devices,
    rows,
    count_ref,
    f_ref,
    a_hbm,
    ot_ref,
    rsel_ref,
    w1_ref,
    w2_ref,
    w3_ref,
    token_ref,
    *refs,
):
    pos_refs, refs = refs[:-11], refs[-11:]
    r_hbm, s_ref, a_ref, r_ref, pull_ref, one_a, one_b, two_a, two_b, in_sem, out_sem = refs
    tiles = ot_ref.shape[1] // LANES
    listed = ot_ref.shape[0]
    particles = a_ref.shape[1] * SUB
    into, out = Stream(a_hbm, a_ref, in_sem, 1, 1), Stream(r_ref, r_hbm, out_sem, 1, 1)
    into.start_all()
    f = load_filtered(f_ref, devices, rows, tiles)
    pull_ref[...] = rsel_ref[0:1, :] * dot_split(f, ot_ref[...], NT)
    live = lax.broadcasted_iota(I32, (1, listed), 1) < count_ref[0]

    def first(g):
        parts = []
        for i in range(2):
            p = 2 * g + i
            at = pl.ds(p & (SUB - 1), rows, stride=SUB)
            for t in range(listed // LANES):
                pull = pull_ref[:, t * LANES : (t + 1) * LANES]
                parts.append((a_ref[t, p >> 3, at, :] + pull).astype(BF))
        return half_silu(dot(w1_ref[...], jnp.concatenate(parts, axis=1), NN))

    def second(one):
        return half_silu(dot(w2_ref[...], one, NN))

    def third(g, two, total):
        change = dot(w3_ref[...], two, NN).astype(BF).astype(F32)
        for i in range(2):
            r = jnp.where(live, change[:, i * listed : (i + 1) * listed], 0.0)
            p = 2 * g + i
            at = pl.ds(p & (SUB - 1), rows, stride=SUB)
            for t in range(listed // LANES):
                r_ref[t, p >> 3, at, :] = r[:, t * LANES : (t + 1) * LANES]
            total = total + r
        return total

    def step(g, total, old, new):
        new[0][...] = first(g)
        new[1][...] = second(old[0][...])
        return third(g - 2, old[1][...], total)

    left, right = (one_a, two_a), (one_b, two_b)

    def pair(m, total):
        total = step(2 * m, total, right, left)
        return step(2 * m + 1, total, left, right)

    total = jnp.zeros((rows, listed), F32)
    each = SUB // 4
    for o in range(particles // SUB):
        into.copy(o).wait()
        if o == 0:
            one_a[...] = first(0)
            two_b[...] = second(one_a[...])
            one_b[...] = first(1)
        total = lax.fori_loop(max(1, o * each), (o + 1) * each, pair, total)
        if o:
            out.copy(o - 1).start()
    last = particles // 2 - 1
    total = third(last - 1, two_b[...], total)
    total = third(last, second(one_b[...]), total)
    out.copy(particles // SUB - 1).start()
    source = total * (1.0 / particles)
    if pos_refs:
        boxes_source(source, *pos_refs, s_ref)
    else:
        source = dot_split(source, ot_ref[...], NN)
        stride = s_ref.shape[0] // devices
        for i in range(rows // devices):
            for t in range(tiles):
                part = source[i * devices : (i + 1) * devices, t * LANES : (t + 1) * LANES]
                s_ref[pl.ds(i * tiles + t, devices, stride=stride), :] = part
    out.wait_all()


def boxes_source(source, pos_ref, s_ref):
    listed = source.shape[1]
    boxes = s_ref.shape[0]
    put = lax.broadcasted_iota(I32, (listed, boxes * LANES), 1).astype(F32) == pos_ref[:, :1]
    sent = dot_split(source, put.astype(F32).astype(BF), NN)
    for b in range(boxes):
        s_ref[b] = sent[: s_ref.shape[1], b * LANES : (b + 1) * LANES]


def early_body(
    devices,
    rows,
    span,
    scalars,
    particles,
    count_ref,
    f_ref,
    base_ref,
    ot_ref,
    rate_ref,
    lcol_ref,
    w1_ref,
    w2_ref,
    w3_ref,
    token_ref,
    out_ref,
    end_ref,
    v_ref,
):
    listed, cells = ot_ref.shape
    tiles = cells // LANES
    places = lcol_ref.shape[0]
    side = max(1, LANES // places)
    wide = base_ref.shape[0]
    end_ref[...] = rate_ref[:, :LANES]
    f = load_filtered(f_ref, devices, rows, tiles)
    leaves = cell_onehot(lcol_ref, cells)
    rate = dot_split(jnp.broadcast_to(rate_ref[...], (SUB, cells)), leaves, NT)[:1]
    pull = rate * dot_split(f, leaves, NT)
    live = (lax.broadcasted_iota(I32, (SUB, listed), 1) < count_ref[0]).astype(F32).astype(BF)
    live = dot(dot(live, ot_ref[...], NN).astype(BF), leaves, NT)[:1]
    pull = jnp.concatenate([pull] * side, axis=1)
    live = jnp.concatenate([live] * side, axis=1) > 0.5
    count = 4 // wide

    for o in range(particles // SUB // side):
        for i in range(0, SUB, count):
            ats = [pl.ds(i + u, rows, stride=SUB) for u in range(count)]
            x = jnp.concatenate(
                [
                    base_ref[t, o, at, :] + pull[:, t * LANES : (t + 1) * LANES]
                    for at in ats
                    for t in range(wide)
                ],
                axis=1,
            )
            one = half_silu(dot(w1_ref[...], x.astype(BF), NN))
            two = half_silu(dot(w2_ref[...], one, NN))
            change = dot(w3_ref[...], two, NN).astype(BF).astype(F32)
            for n, (at, t) in enumerate((at, t) for at in ats for t in range(wide)):
                cols = slice(n * LANES, (n + 1) * LANES)
                mask = live[:, t * LANES : (t + 1) * LANES]
                v_ref[t, o, at, :] = x[:, cols] + jnp.where(mask, change[:, cols], 0.0)

    per = LANES // particles
    stride = out_ref.shape[0] // devices

    def scalar(s):
        parts = []
        for o in range(particles // SUB // side):
            at = pl.ds(s * SUB, SUB)
            row = jnp.concatenate([v_ref[t, o, at, :] for t in range(wide)], axis=1)
            parts += [row[:, u * places : (u + 1) * places] for u in range(side)]
        return jnp.concatenate(parts, axis=0)

    def part(b, count):
        value = jnp.concatenate([scalar(b * per + i) for i in range(count)], axis=0)
        if count < per:
            rest = jnp.zeros(((per - count) * particles, places), F32)
            value = jnp.concatenate([value, rest], axis=0)
        value = value.T
        for c in range(places // devices):
            at = pl.ds(c * span + b, devices, stride=stride)
            out_ref[at, :] = value[c * devices : (c + 1) * devices]

    def step(b, carry):
        part(b, per)
        return carry

    whole = scalars // per
    lax.fori_loop(0, whole, step, 0, unroll=2)
    zeros = jnp.zeros((devices, LANES), F32)
    for c in range(places // devices):
        for b in range(whole, span):
            out_ref[pl.ds(c * span + b, devices, stride=stride), :] = zeros
    if scalars > whole * per:
        part(whole, scalars - whole * per)


def columns(row_ref, devices, out_ref, turn_ref):
    places = row_ref.shape[1]
    count = places // devices
    column = jnp.broadcast_to(row_ref[...].astype(F32), (SUB, places)).T[:, :1]
    turn_ref[...] = jnp.broadcast_to(column, turn_ref.shape)
    for c in range(count):
        part = turn_ref[pl.ds(c, devices, stride=count), :]
        out_ref[c * devices : (c + 1) * devices] = part.astype(I32)


def maps_body(
    dims,
    me_ref,
    inv_ref,
    ot_ref,
    owner_ref,
    slot_ref,
    leave_ref,
    arrive_ref,
    pos_ref,
    put_ref,
    lcol_ref,
    acol_ref,
    turn_ref,
):
    nx, ny, _, bx, by = dims
    columns(leave_ref, nx * ny, lcol_ref, turn_ref)
    columns(arrive_ref, nx * ny, acol_ref, turn_ref)
    quads = bx * by
    turns = quads * ny
    _, cells = ot_ref.shape
    at = me_ref[0] * 2 * turns + me_ref[1]
    code = jnp.concatenate([inv_ref[pl.ds(at + k * ny, 1), :] for k in range(quads)], axis=1)
    box = lax.rem(code, ny).astype(F32)
    boxes = lax.broadcasted_iota(I32, (ny, cells), 0).astype(F32)
    mine = (jnp.broadcast_to(box, (ny, cells)) == boxes).astype(F32)
    before = lax.broadcasted_iota(I32, (cells, cells), 0) < lax.broadcasted_iota(
        I32, (cells, cells), 1
    )
    count = dot(mine.astype(BF), before.astype(F32).astype(BF), NN)
    rank = jnp.sum(mine * count, axis=0, keepdims=True)
    rest = jnp.zeros((SUB - 2, cells), F32)
    found = dot(ot_ref[...], jnp.concatenate([box, rank, rest], axis=0).astype(BF), NT)
    pos = found[:, :1] * LANES + found[:, 1:2]
    pos_ref[...] = jnp.broadcast_to(pos, pos_ref.shape)
    flat = lambda ref: jnp.concatenate([ref[j : j + 1, :] for j in range(quads)], axis=1)
    owner, slot = flat(owner_ref).astype(F32), flat(slot_ref).astype(F32)
    first = owner * cells
    key = first + slot
    column = jnp.broadcast_to(key, (SUB, cells)).T[:, :1]
    ahead = (column < key) & (column >= first)
    place = owner * LANES + jnp.sum(ahead.astype(F32), axis=0, keepdims=True)
    step = min(cells, put_ref.shape[0])
    for b in range(put_ref.shape[0] // step):
        row = lax.broadcasted_iota(I32, (step, cells), 0).astype(F32) + b * step
        put_ref[b * step : (b + 1) * step] = (row == place).astype(F32).astype(BF)


def unpack_body(devices, own, s_ref, arr_ref, put_ref, out_ref):
    boxes, _ = s_ref.shape[:2]
    cells = put_ref.shape[1]
    quads = cells // LANES
    scalars = out_ref.shape[0] // quads
    stride = arr_ref.shape[0] // devices
    got = jnp.concatenate([s_ref[b] for b in range(boxes)], axis=1)
    source = dot_split(got, put_ref[...], NN)
    for j in range(quads):
        for i in range(own):
            n = min(devices, scalars - i * devices)
            if n > 0:
                grid = arr_ref[pl.ds(stride - own * quads + i * quads + j, n, stride=stride), :]
                part = source[i * devices : i * devices + n, j * LANES : (j + 1) * LANES]
                out_ref[pl.ds(i * devices * quads + j, n, stride=quads), :] = grid + part


def cell_onehot(col_ref, cells):
    shape = (col_ref.shape[0], cells)
    return (col_ref[:, :1] == lax.broadcasted_iota(I32, shape, 1)).astype(F32).astype(BF)


def settle_body(
    block,
    devices,
    q_hbm,
    f_ref,
    r_hbm,
    ot_ref,
    rate_ref,
    out_hbm,
    token_ref,
    q_ref,
    out_ref,
    r_ref,
    in_sem,
    out_sem,
    r_sem,
):
    into, out = Stream(q_hbm, q_ref, in_sem, block), Stream(out_ref, out_hbm, out_sem, block)
    changes = Stream(r_hbm, r_ref, r_sem, block * SUB, 2)
    for b in range(q_ref.shape[0] // block):
        changes.copy(b).start()
        into.copy(b).start()
    token_ref[...] = rate_ref[:, :LANES]

    def step(b, carry):
        changes.copy(b).wait()
        into.copy(b).wait()
        settle_block(b * block, block, q_ref, f_ref, r_ref, ot_ref, rate_ref, out_ref, devices)
        out.copy(b).start()
        return carry

    lax.fori_loop(0, q_ref.shape[0] // block, step, 0)
    out.wait_all()


def arrive_body(
    span, devices, p_hbm, arr_ref, acol_ref, out_hbm, p_ref, out_ref, hit_ref, in_sem, out_sem
):
    scalars, particles, cells = p_ref.shape
    places = acol_ref.shape[0]
    per = LANES // particles
    into, out = Stream(p_hbm, p_ref, in_sem, per), Stream(out_ref, out_hbm, out_sem, per)
    into.start_all()
    hit = (acol_ref[:, :1] == lax.broadcasted_iota(I32, (places, cells), 1)).astype(F32)
    hit_ref[...] = hit.astype(BF)
    taken = jnp.sum(hit, axis=0, keepdims=True) > 0.5
    stride = arr_ref.shape[0] // devices
    count = places // devices

    def place(b, size):
        first = stride - count * span + b
        x = jnp.concatenate(
            [arr_ref[pl.ds(first + c * span, devices, stride=stride), :] for c in range(count)],
            axis=0,
        ).T
        y = dot_split(x, hit_ref[...], NN)
        into.copy(b, size).wait()
        for i in range(size):
            s = b * per + i
            out_ref[s] = jnp.where(taken, y[i * particles : (i + 1) * particles], p_ref[s])
        out.copy(b, size).start()

    def step(b, carry):
        place(b, per)
        return carry

    whole = scalars // per
    lax.fori_loop(0, whole, step, 0)
    if scalars > whole * per:
        place(whole, scalars - whole * per)
    out.wait_all()


def stencil(value, speed, bx, by, lanes_y):
    boxes = value[0].shape[0]
    row = lax.broadcasted_iota(I32, value[0].shape, 0) % lanes_y
    zero = jnp.zeros((lanes_y, LANES), F32)

    def x_low(v):
        return jnp.concatenate([zero, v[: boxes - lanes_y]], axis=0)

    def x_high(v):
        return jnp.concatenate([v[lanes_y:], zero], axis=0)

    def y_low(v):
        return jnp.where(row == 0, 0.0, pltpu.roll(v, 1, 0))

    def y_high(v):
        return jnp.where(row == lanes_y - 1, 0.0, pltpu.roll(v, boxes - 1, 0))

    out = []
    for i in range(bx):
        for j in range(by):
            c = value[i * by + j]
            up = value[(i - 1) * by + j] if i else x_low(value[(bx - 1) * by + j])
            down = value[(i + 1) * by + j] if i < bx - 1 else x_high(value[j])
            left = value[i * by + j - 1] if j else y_low(value[i * by + by - 1])
            right = value[i * by + j + 1] if j < by - 1 else y_high(value[i * by])
            beside = up + down + left + right + pltpu.roll(c, 1, 1) + pltpu.roll(c, LANES - 1, 1)
            out.append(c + DIFFUSION * (beside - 6.0 * c) - speed[i * by + j] * (c - up))
    return out


def route(src_ref, first_row, row_step, item_step, items, own, quads, lanes_y, rows, lanes):
    shape = (lanes_y, LANES)
    out = []
    for k in range(len(rows)):

        def step(y, acc):
            for j in range(items):
                hit = rows[k] == (j * lanes_y + y)
                at = first_row + y * row_step + j * item_step
                lines = [src_ref[pl.ds(at + s * quads, 1), :] for s in range(own)]
                acc = [
                    jnp.where(
                        hit,
                        jnp.take_along_axis(jnp.broadcast_to(v, shape), lanes[k], axis=1),
                        old,
                    )
                    for v, old in zip(lines, acc)
                ]
            return tuple(acc)

        zero = tuple(jnp.zeros(shape, F32) for _ in range(own))
        out.append(lax.fori_loop(0, lanes_y, step, zero, unroll=min(lanes_y, 8)))
    return [[out[k][s] for k in range(len(rows))] for s in range(own)]


def load_rows(ref, offset, stride, count):
    return ref[pl.ds(offset, count, stride=stride), :]


def pack_body(
    width,
    lanes_y,
    grid_hbm,
    owner_hbm,
    slot_hbm,
    speed_hbm,
    out_ref,
    grid_ref,
    owner_ref,
    slot_ref,
    speed_ref,
    sem,
):
    pairs = [
        (grid_hbm, grid_ref),
        (owner_hbm, owner_ref),
        (slot_hbm, slot_ref),
        (speed_hbm, speed_ref),
    ]
    copies = [pltpu.make_async_copy(a, b, sem.at[i]) for i, (a, b) in enumerate(pairs)]
    for c in copies:
        c.start()
    for c in copies:
        c.wait()
    quads = owner_ref.shape[0]
    stride = width + 2 * quads
    total = grid_ref.shape[0]
    slot = slot_ref[...]
    label = ((slot >> 7) * lanes_y + owner_ref[...]) * LANES + (slot & (LANES - 1))
    tail = jnp.concatenate([label.astype(F32), speed_ref[...]], axis=0)
    devices = out_ref.shape[0] // stride
    for d in range(devices):
        for i in range(width // quads):
            at = d * stride + i * quads
            src = (i * devices + d) * quads
            if src < total:
                out_ref[at : at + quads] = grid_ref[src : src + quads]
            else:
                out_ref[at : at + quads] = jnp.zeros((quads, LANES), F32)
        out_ref[d * stride + width : (d + 1) * stride] = tail


def weights_body(w1_ref, w2_ref, w3_ref, token_ref, a_ref, b_ref, c_ref):
    scalars, hidden = w1_ref.shape
    rest = jnp.zeros((a_ref.shape[1] - scalars, hidden), F32)
    a_ref[...] = jnp.concatenate([w1_ref[...].astype(F32) * 0.5, rest], axis=0).T.astype(BF)
    b_ref[...] = (w2_ref[...].astype(F32) * 0.5).astype(BF)
    c_ref[...] = jnp.concatenate([w3_ref[...].astype(F32), rest], axis=0).astype(BF)


def start_body(dims, arr_ref, token_ref, g_ref, f_ref, inv_ref, lab_ref):
    nx, ny, own, bx, by = dims
    quads = bx * by
    boxes = nx * ny
    width = own * quads
    stride = width + 2 * quads
    turns = quads * ny
    speed = [load_rows(arr_ref, width + quads + j, stride, boxes) for j in range(quads)]
    for s in range(own):
        value = [load_rows(arr_ref, s * quads + j, stride, boxes) for j in range(quads)]
        for j, v in enumerate(stencil(value, speed, bx, by, ny)):
            g_ref[pl.ds(s * quads + j, boxes, stride=width), :] = v
    for j in range(quads):
        lab_ref[pl.ds(j * boxes, boxes), :] = load_rows(arr_ref, width + j, stride, boxes).astype(
            I32
        )
    lane_of = lax.broadcasted_iota(I32, (turns, LANES), 1).astype(F32).astype(BF)
    sub_of = lax.broadcasted_iota(I32, (turns, LANES), 0).astype(F32).astype(BF)
    sub_lane = lax.broadcasted_iota(I32, (LANES, LANES), 0).astype(F32).astype(BF)
    none = jnp.zeros((turns, LANES), BF)
    unit = jnp.ones((LANES, LANES), BF)

    def group(x, carry):
        def gather(y, acc):
            left, right = [], []
            for j in range(quads):
                line = lab_ref[pl.ds(j * boxes + x * ny + y, 1), :]
                hit = jnp.broadcast_to((line >> 7).astype(F32).astype(BF), (turns, LANES)) == sub_of
                code = jnp.full((turns, LANES), j * ny + y).astype(F32).astype(BF)
                left.append(
                    jnp.concatenate([jnp.where(hit, code, none), jnp.where(hit, lane_of, none)], axis=0)
                )
                lane = jnp.broadcast_to((line & (LANES - 1)).astype(F32).astype(BF), (LANES, LANES))
                right.append(jnp.where(lane == sub_lane, unit, jnp.zeros_like(unit)))
            return acc + dot(
                jnp.concatenate(left, axis=1), jnp.concatenate(right, axis=1), NT
            )

        code = lax.fori_loop(0, ny, gather, jnp.zeros((2 * turns, LANES), F32), unroll=8)
        code = code.astype(I32)
        inv_ref[pl.ds(x * 2 * turns, 2 * turns), :] = code
        return carry

    lax.fori_loop(0, nx, group, 0)
    send_filtered(dims, g_ref, width, 0, inv_ref, f_ref)


def send_filtered(dims, g_ref, g_stride, g_first, inv_ref, f_ref):
    nx, ny, own, bx, by = dims
    quads = bx * by
    turns = quads * ny
    f_stride = f_ref.shape[0] // (nx * ny)

    def group(x, carry):
        base = x * 2 * turns
        rows = [inv_ref[pl.ds(base + k * ny, ny), :] for k in range(quads)]
        lanes = [inv_ref[pl.ds(base + turns + k * ny, ny), :] for k in range(quads)]
        first = x * ny * g_stride + g_first
        out = route(g_ref, first, g_stride, 1, quads, own, quads, ny, rows, lanes)
        for s in range(own):
            for k in range(quads):
                at = pl.ds(x * ny * f_stride + s * quads + k, ny, stride=f_stride)
                f_ref[at, :] = out[s][k]
        return carry

    lax.fori_loop(0, nx, group, 0)


def add_source(dims, s_ref, g_ref, lab_ref, out_ref):
    nx, ny, own, bx, by = dims
    quads = bx * by
    boxes = nx * ny
    width = own * quads
    stride = s_ref.shape[0] // boxes

    def group(x, carry):
        labels = [lab_ref[pl.ds(j * boxes + x * ny, ny), :] for j in range(quads)]
        rows = [v >> 7 for v in labels]
        lanes = [v & (LANES - 1) for v in labels]
        out = route(s_ref, x * ny * stride, stride, 1, quads, own, quads, ny, rows, lanes)
        for s in range(own):
            for k in range(quads):
                at = pl.ds(x * ny * width + s * quads + k, ny, stride=width)
                out_ref[at, :] = g_ref[at, :] + out[s][k]
        return carry

    lax.fori_loop(0, nx, group, 0)


def again_body(dims, s_ref, g_ref, arr_ref, inv_ref, lab_ref, token_ref, f_ref, mid_ref):
    nx, ny, own, bx, by = dims
    quads = bx * by
    boxes = nx * ny
    width = own * quads
    stride = width + 2 * quads
    add_source(dims, s_ref, g_ref, lab_ref, mid_ref)
    speed = [load_rows(arr_ref, width + quads + j, stride, boxes) for j in range(quads)]
    for s in range(own):
        value = [load_rows(mid_ref, s * quads + j, width, boxes) for j in range(quads)]
        for j, v in enumerate(stencil(value, speed, bx, by, ny)):
            f_ref[pl.ds(width + s * quads + j, boxes, stride=2 * width), :] = v
    send_filtered(dims, f_ref, 2 * width, width, inv_ref, f_ref)


def per_device(
    grid_scalars,
    axial_speed,
    particles,
    cell_owner,
    cell_slot,
    mix_rate,
    partner,
    chem_input,
    chem_hidden,
    chem_output,
    react_slots,
    react_count,
    leave_slots,
    arrive_slots,
):
    both = ("gx", "gy")
    nx, ny = lax.axis_size("gx"), lax.axis_size("gy")
    devices = nx * ny
    scalars, bx, by, nz = grid_scalars.shape
    heads, cells = partner.shape
    listed = react_slots.shape[1]
    hidden = chem_hidden.shape[0]
    quads = bx * by
    own = -(-scalars // devices)
    rows = devices * own
    width = own * quads
    tiles = cells // LANES
    assert nz == LANES and tiles == quads and heads % SUB == 0 and LANES % heads == 0
    dims = (nx, ny, own, bx, by)
    flat = devices * width

    box = [
        grid_scalars.reshape(-1, LANES),
        cell_owner.reshape(quads, LANES),
        cell_slot.reshape(quads, LANES),
        axial_speed.reshape(quads, LANES),
    ]
    (first,) = call(
        functools.partial(pack_body, width, ny),
        [((devices * (width + 2 * quads), LANES), F32)],
        box,
        hbm=(0, 1, 2, 3),
        scratch=[pltpu.VMEM(x.shape, x.dtype) for x in box] + [pltpu.SemaphoreType.DMA((4,))],
    )

    def exchange(x):
        count = x.shape[0] // devices
        tile = SUB if count % SUB == 0 else SUB // 2
        x = x.reshape(devices, count // tile, tile, LANES)
        return lax.all_to_all(x, both, split_axis=0, concat_axis=0, tiled=True).reshape(-1, LANES)

    arrival = exchange(first)

    rate = mix_rate.reshape(1, cells)
    state_shape = (scalars, heads, cells)
    listed_shape = (listed // LANES, heads // SUB, rows * SUB, LANES)
    block = divisor(scalars, 6)
    octets = heads // SUB
    state_vmem = pltpu.VMEM(state_shape, F32)
    listed_vmem = pltpu.VMEM(listed_shape, F32)
    dma = pltpu.SemaphoreType.DMA
    per_block = dma((scalars // block,))
    per_listed = dma((-(-rows // block),))
    q, a, ot, rsel = call(
        functools.partial(open_body, block),
        [
            (state_shape, F32, True),
            (listed_shape, F32, True),
            ((listed, cells), BF),
            ((SUB, listed), F32),
        ],
        [particles, partner, rate, react_slots],
        hbm=(0, 1, 2, 3),
        scratch=[
            state_vmem,
            state_vmem,
            listed_vmem,
            pltpu.VMEM(partner.shape, I32),
            pltpu.VMEM(rate.shape, F32),
            pltpu.VMEM(react_slots.shape, I32),
            per_block,
            per_block,
            per_listed,
            dma((3,)),
        ],
    )
    grid, sent, inv, lab = call(
        functools.partial(start_body, dims),
        [
            ((flat, LANES), F32),
            ((flat, LANES), F32),
            ((nx * 2 * quads * ny, LANES), I32),
            ((quads * devices, LANES), I32),
        ],
        [arrival, rsel],
    )

    w1, w2, w3 = call(
        weights_body,
        [((hidden, rows), BF), ((hidden, hidden), BF), ((rows, hidden), BF)],
        [chem_input.T, chem_hidden, chem_output, lab],
    )

    per = LANES // heads
    span = 2 * (-(-scalars // (per * 2)))
    places = leave_slots.shape[1]
    side = max(1, LANES // places)
    base_shape = (max(1, places // LANES), octets // side, rows * SUB, LANES)
    kept = SUB * (-(-scalars // SUB))
    pair = pltpu.VMEM((hidden, 2 * listed), BF)
    me = jnp.stack([lax.axis_index("gx"), lax.axis_index("gy")]).astype(I32)
    pos, put, lcol, acol = call(
        functools.partial(maps_body, dims),
        [
            ((listed, LANES), F32),
            ((ny * LANES, cells), BF),
            ((places, LANES), I32),
            ((places, LANES), I32),
        ],
        [me, inv, ot, box[1], box[2], leave_slots, arrive_slots],
        smem=(0,),
        scratch=[pltpu.VMEM((places, LANES), F32)],
    )

    def chemistry(f, a, token, out, more=()):
        return call(
            functools.partial(chem_body, devices, rows),
            [(listed_shape, F32, True), (out, F32)],
            [react_count, f, a, ot, rsel, w1, w2, w3, token, *more],
            smem=(0,),
            hbm=(2,),
            scratch=[listed_vmem, listed_vmem, pltpu.VMEM((rows, listed), F32)]
            + [pair] * 4
            + [dma((octets,)), dma((octets,))],
        )

    f = exchange(sent)
    change, source = chemistry(f, a, pos, (flat, LANES))
    home = exchange(source)
    q, token = call(
        functools.partial(middle_body, block, devices),
        [(state_shape, F32, True), ((1, LANES), F32)],
        [q, f, change, ot, rate, partner],
        hbm=(0, 2),
        scratch=[state_vmem, state_vmem, listed_vmem, per_block, per_block, per_listed],
    )
    (sent,) = call(
        functools.partial(again_body, dims),
        [((2 * flat, LANES), F32)],
        [home, grid, arrival, inv, lab, token],
        scratch=[pltpu.VMEM((flat, LANES), F32)],
    )
    a, base, token = call(
        functools.partial(list_body, block),
        [(listed_shape, F32, True), (base_shape, F32), ((1, LANES), F32)],
        [q, rate, rsel, ot, lcol],
        hbm=(0,),
        scratch=[
            state_vmem,
            listed_vmem,
            per_block,
            per_listed,
        ],
    )
    f = exchange(sent)
    leaving, token = call(
        functools.partial(early_body, devices, rows, span, scalars, heads),
        [((places * span, LANES), F32), ((1, LANES), F32)],
        [react_count, f, base, ot, rate, lcol, w1, w2, w3, token],
        smem=(0,),
        scratch=[pltpu.VMEM(base_shape, F32)],
    )
    change, source = chemistry(f, a, token, (ny, kept, LANES), [pos])
    moved = exchange(leaving)
    state, token = call(
        functools.partial(settle_body, block, devices),
        [(state_shape, F32, True), ((1, LANES), F32)],
        [q, f, change, ot, rate],
        hbm=(0, 2),
        scratch=[state_vmem, state_vmem, listed_vmem, per_block, per_block, per_listed],
    )
    source = lax.all_to_all(source, "gy", split_axis=0, concat_axis=0, tiled=True)
    (grid,) = call(
        functools.partial(unpack_body, devices, own),
        [((scalars * quads, LANES), F32)],
        [source, f, put],
    )
    grid_out = grid.reshape(grid_scalars.shape)
    steps = -(-scalars // per)
    (state,) = call(
        functools.partial(arrive_body, span, devices),
        [(state_shape, F32, True)],
        [state, moved, acol],
        hbm=(0,),
        scratch=[
            state_vmem,
            state_vmem,
            pltpu.VMEM((places, cells), BF),
            dma((steps,)),
            dma((steps,)),
        ],
    )
    return (grid_out, state)


def solution(mesh):
    placed = (
        P(None, "gx", "gy", None),
        P("gx", "gy", None),
        P(None, None, ("gx", "gy")),
        P("gx", "gy", None),
        P("gx", "gy", None),
        P(("gx", "gy")),
        P(None, ("gx", "gy")),
        P(),
        P(),
        P(),
        P(("gx", "gy"), None),
        P(("gx", "gy")),
        P(("gx", "gy"), None),
        P(("gx", "gy"), None),
    )

    return jax.shard_map(
        per_device,
        mesh=mesh,
        in_specs=placed,
        out_specs=(P(None, "gx", "gy", None), P(None, None, ("gx", "gy"))),
        check_vma=False,
    )
```

```python
import functools

import jax
import jax.numpy as jnp
from jax import lax
from jax.experimental import pallas as pl
from jax.experimental.pallas import tpu as pltpu
from jax.sharding import PartitionSpec as P


DIFFUSION = 0.1
PAIR_WEIGHT = 0.4
LANES = 128
SUB = 8
BF = jnp.bfloat16
F32 = jnp.float32
I32 = jnp.int32

NT = (((1,), (1,)), ((), ()))
NN = (((1,), (0,)), ((), ()))


def call(body, outs, ins, smem=(), hbm=(), scratch=(), limit=24):
    spaces = {**{i: pltpu.SMEM for i in smem}, **{i: pl.ANY for i in hbm}}
    ins = [pltpu.with_memory_space_constraint(x, pltpu.HBM) if i in hbm else x for i, x in enumerate(ins)]
    return pl.pallas_call(
        body,
        out_shape=[
            pltpu.HBM(o[0], o[1]) if len(o) > 2 else jax.ShapeDtypeStruct(o[0], o[1]) for o in outs
        ],
        in_specs=[
            pl.BlockSpec(memory_space=spaces.get(i, pltpu.VMEM)) for i in range(len(ins))
        ],
        out_specs=[
            pl.BlockSpec(memory_space=pl.ANY if len(o) > 2 else pltpu.VMEM) for o in outs
        ],
        scratch_shapes=list(scratch),
        compiler_params=pltpu.CompilerParams(vmem_limit_bytes=limit << 20),
    )(*ins)


class Stream:
    def __init__(self, src, dst, sem, size, dim=0):
        self.src, self.dst, self.sem, self.size, self.dim = src, dst, sem, size, dim
        self.count = -(-src.shape[dim] // size)

    def copy(self, i, size=None):
        at = (slice(None),) * self.dim + (pl.ds(i * self.size, size or self.size),)
        return pltpu.make_async_copy(self.src.at[at], self.dst.at[at], self.sem.at[i])

    def tail(self, i):
        return min(self.size, self.src.shape[self.dim] - i * self.size)

    def start_all(self):
        for i in range(self.count):
            self.copy(i, self.tail(i)).start()

    def wait_all(self, first=0):
        for i in range(first, self.count):
            self.copy(i, self.tail(i)).wait()


def dot(a, b, dims):
    return lax.dot_general(a, b, dims, preferred_element_type=F32)


def halves(x):
    high = x.astype(BF)
    return high, (x - high.astype(F32)).astype(BF)


def dot_split(x, onehot, dims):
    high, low = halves(x)
    y = dot(jnp.concatenate([high, low], axis=0), onehot, dims)
    return y[: x.shape[0]] + y[x.shape[0] :]


def load_filtered(f_ref, devices, rows, tiles):
    stride = f_ref.shape[0] // devices
    return jnp.concatenate(
        [
            jnp.concatenate(
                [
                    f_ref[pl.ds(i * tiles + t, devices, stride=stride), :]
                    for i in range(rows // devices)
                ],
                axis=0,
            )
            for t in range(tiles)
        ],
        axis=1,
    )


def divisor(n, most):
    return max(k for k in range(1, most + 1) if n % k == 0)


def mix(s0, block, p_ref, partner_ref, q_ref):
    _, particles, cells = p_ref.shape
    groups = particles // SUB
    for t in range(cells // LANES):
        lanes = pl.ds(t * LANES, LANES)
        rows, homes = [], []
        for j in range(groups):
            index = partner_ref[pl.ds(j * SUB, SUB), lanes]
            rows.append(index & (SUB - 1))
            homes.append(index >> 3)

        def step(i, carry):
            s = s0 + i
            x = [p_ref[s, pl.ds(k * SUB, SUB), lanes] for k in range(groups)]
            for j in range(groups):
                mate = jnp.take_along_axis(x[0], rows[j], axis=0)
                for k in range(1, groups):
                    other = jnp.take_along_axis(x[k], rows[j], axis=0)
                    mate = jnp.where(homes[j] == k, other, mate)
                q_ref[s, pl.ds(j * SUB, SUB), lanes] = x[j] + PAIR_WEIGHT * (mate - x[j])
            return carry

        lax.fori_loop(0, block, step, 0, unroll=True)


def put_scalar(ref, s, value):
    for o in range(ref.shape[1]):
        for t in range(ref.shape[0]):
            part = value[o * SUB : (o + 1) * SUB, t * LANES : (t + 1) * LANES]
            ref[t, o, pl.ds(s * SUB, SUB), :] = part


def get_scalar(ref, s):
    return jnp.concatenate(
        [
            jnp.concatenate(
                [ref[t, o, pl.ds(s * SUB, SUB), :] for t in range(ref.shape[0])], axis=1
            )
            for o in range(ref.shape[1])
        ],
        axis=0,
    )


def list_cells(s0, block, q_ref, onehot, keep, a_ref):
    _, particles, cells = q_ref.shape
    x = q_ref[pl.ds(s0, block)].reshape(block * particles, cells)
    y = dot_split(x, onehot, NT) * keep
    for i in range(block):
        put_scalar(a_ref, s0 + i, y[i * particles : (i + 1) * particles])


def list_body(
    block,
    q_hbm,
    rate_ref,
    rsel_ref,
    ot_ref,
    lcol_ref,
    a_hbm,
    base_ref,
    token_ref,
    q_ref,
    a_ref,
    in_sem,
    a_sem,
):
    scalars, particles, cells = q_ref.shape
    into = Stream(q_hbm, q_ref, in_sem, block)
    out_a = Stream(a_ref, a_hbm, a_sem, block * SUB, 2)
    into.start_all()
    token_ref[...] = rate_ref[:, :LANES]
    leaves = cell_onehot(lcol_ref, cells)
    places = lcol_ref.shape[0]
    side = max(1, LANES // places)
    keep = 1.0 - rate_ref[...]
    half = block * particles

    def step(b, carry):
        into.copy(b).wait()
        x = q_ref[pl.ds(b * block, block)].reshape(half, cells) * keep
        both = jnp.concatenate(halves(x), axis=0)
        y = dot(both, ot_ref[...], NT)
        y = y[:half] + y[half:]
        z = dot(both, leaves, NT)
        z = z[:half] + z[half:]
        for i in range(block):
            put_scalar(a_ref, b * block + i, y[i * particles : (i + 1) * particles])
            mine = z[i * particles : (i + 1) * particles]
            for o in range(base_ref.shape[1]):
                octets = [
                    mine[(o * side + u) * SUB : (o * side + u + 1) * SUB] for u in range(side)
                ]
                wide = jnp.concatenate(octets, axis=1)
                for t in range(base_ref.shape[0]):
                    at = pl.ds((b * block + i) * SUB, SUB)
                    base_ref[t, o, at, :] = wide[:, t * LANES : (t + 1) * LANES]
        out_a.copy(b).start()
        return carry

    lax.fori_loop(0, scalars // block, step, 0)
    clear_rest(scalars, base_ref)
    clear_rest(scalars, a_ref)
    for b in range(scalars // block, out_a.count):
        out_a.copy(b, out_a.tail(b)).start()
    out_a.wait_all()


def clear_rest(scalars, ref):
    rest = ref.shape[2] - scalars * SUB
    for t in range(ref.shape[0]):
        for o in range(ref.shape[1]):
            ref[t, o, pl.ds(scalars * SUB, rest), :] = jnp.zeros((rest, LANES), F32)


def open_body(
    block,
    p_hbm,
    partner_hbm,
    rate_hbm,
    list_hbm,
    q_hbm,
    a_hbm,
    ot_ref,
    rsel_ref,
    p_ref,
    q_ref,
    a_ref,
    partner_ref,
    rate_ref,
    list_ref,
    in_sem,
    out_sem,
    a_sem,
    few_sem,
):
    scalars, _, cells = p_ref.shape
    into, out = Stream(p_hbm, p_ref, in_sem, block), Stream(q_ref, q_hbm, out_sem, block)
    out_a = Stream(a_ref, a_hbm, a_sem, block * SUB, 2)
    few = [
        pltpu.make_async_copy(src, dst, few_sem.at[i])
        for i, (src, dst) in enumerate(
            [(list_hbm, list_ref), (rate_hbm, rate_ref), (partner_hbm, partner_ref)]
        )
    ]
    for c in few:
        c.start()
    into.start_all()
    for c in few:
        c.wait()
    column = jnp.broadcast_to(list_ref[...].astype(F32), (SUB, list_ref.shape[1])).T[:, :1]
    cell = lax.broadcasted_iota(I32, ot_ref.shape, 1).astype(F32)
    onehot = (column == cell).astype(F32)
    ot_ref[...] = onehot.astype(BF)
    rate = jnp.broadcast_to(rate_ref[...], (SUB, cells))
    rsel_ref[...] = dot_split(rate, onehot.astype(BF), NT)
    clear_rest(scalars, a_ref)

    def step(b, carry):
        into.copy(b).wait()
        mix(b * block, block, p_ref, partner_ref, q_ref)
        out.copy(b).start()
        list_cells(b * block, block, q_ref, ot_ref[...], 1.0 - rsel_ref[0:1, :], a_ref)
        out_a.copy(b).start()
        return carry

    whole = scalars // block
    for b in range(whole, out_a.count):
        out_a.copy(b, out_a.tail(b)).start()
    lax.fori_loop(0, whole, step, 0)
    out.wait_all()
    out_a.wait_all()


def settle_block(s0, block, q_ref, f_ref, r_ref, ot_ref, rate_ref, out_ref, devices):
    _, particles, cells = q_ref.shape
    tiles = cells // LANES
    rate = rate_ref[...]
    keep = 1.0 - rate
    r = jnp.concatenate([get_scalar(r_ref, s0 + i) for i in range(block)], axis=0)
    spread = dot(r.astype(BF), ot_ref[...], NN)
    for i in range(block):
        s = s0 + i
        at = lax.rem(s, devices) * (f_ref.shape[0] // devices) + lax.div(s, devices) * tiles
        f = jnp.concatenate([f_ref[pl.ds(at + t, 1), :] for t in range(tiles)], axis=1)
        out_ref[s0 + i] = (
            keep * q_ref[s0 + i] + rate * f + spread[i * particles : (i + 1) * particles]
        )


def middle_body(
    block,
    devices,
    q_hbm,
    f_ref,
    r_hbm,
    ot_ref,
    rate_ref,
    partner_ref,
    out_hbm,
    token_ref,
    q_ref,
    now_ref,
    r_ref,
    in_sem,
    out_sem,
    r_sem,
):
    scalars = q_ref.shape[0]
    into, out = Stream(q_hbm, q_ref, in_sem, block), Stream(q_ref, out_hbm, out_sem, block)
    changes = Stream(r_hbm, r_ref, r_sem, block * SUB, 2)
    for b in range(q_ref.shape[0] // block):
        changes.copy(b).start()
        into.copy(b).start()
    token_ref[...] = rate_ref[:, :LANES]

    def step(b, carry):
        changes.copy(b).wait()
        into.copy(b).wait()
        s0 = b * block
        settle_block(s0, block, q_ref, f_ref, r_ref, ot_ref, rate_ref, now_ref, devices)
        mix(s0, block, now_ref, partner_ref, q_ref)
        out.copy(b).start()
        return carry

    lax.fori_loop(0, scalars // block, step, 0)
    out.wait_all()


def half_silu(y):
    return (y + y * jnp.tanh(y)).astype(BF)


def chem_body(
    devices,
    rows,
    count_ref,
    f_ref,
    a_hbm,
    ot_ref,
    rsel_ref,
    w1_ref,
    w2_ref,
    w3_ref,
    token_ref,
    *refs,
):
    pos_refs, refs = refs[:-7], refs[-7:]
    r_hbm, s_ref, a_ref, r_ref, pull_ref, in_sem, out_sem = refs
    tiles = ot_ref.shape[1] // LANES
    listed = ot_ref.shape[0]
    particles = a_ref.shape[1] * SUB
    into, out = Stream(a_hbm, a_ref, in_sem, 1, 1), Stream(r_ref, r_hbm, out_sem, 1, 1)
    into.start_all()
    f = load_filtered(f_ref, devices, rows, tiles)
    pull_ref[...] = rsel_ref[0:1, :] * dot_split(f, ot_ref[...], NT)
    live = lax.broadcasted_iota(I32, (1, listed), 1) < count_ref[0]

    def first(g):
        parts = []
        for i in range(2):
            p = 2 * g + i
            at = pl.ds(p & (SUB - 1), rows, stride=SUB)
            for t in range(listed // LANES):
                pull = pull_ref[:, t * LANES : (t + 1) * LANES]
                parts.append((a_ref[t, p >> 3, at, :] + pull).astype(BF))
        return half_silu(dot(w1_ref[...], jnp.concatenate(parts, axis=1), NN))

    def second(one):
        return half_silu(dot(w2_ref[...], one, NN))

    def third(g, two, total):
        change = dot(w3_ref[...], two, NN).astype(BF).astype(F32)
        for i in range(2):
            r = jnp.where(live, change[:, i * listed : (i + 1) * listed], 0.0)
            p = 2 * g + i
            at = pl.ds(p & (SUB - 1), rows, stride=SUB)
            for t in range(listed // LANES):
                r_ref[t, p >> 3, at, :] = r[:, t * LANES : (t + 1) * LANES]
            total = total + r
        return total

    total = jnp.zeros((rows, listed), F32)
    groups, each = particles // 2, SUB // 2
    ones, twos = {}, {}
    for n in range(groups + 2):
        if n < groups:
            if n % each == 0:
                into.copy(n // each).wait()
            ones[n] = first(n)
        if 0 < n <= groups:
            twos[n - 1] = second(ones.pop(n - 1))
        if n > 1:
            total = third(n - 2, twos.pop(n - 2), total)
            if (n - 1) % each == 0 and n - 1 < groups:
                out.copy((n - 1) // each - 1).start()
    out.copy(particles // SUB - 1).start()
    source = total * (1.0 / particles)
    if pos_refs:
        boxes_source(source, *pos_refs, s_ref)
    else:
        source = dot_split(source, ot_ref[...], NN)
        stride = s_ref.shape[0] // devices
        for i in range(rows // devices):
            for t in range(tiles):
                part = source[i * devices : (i + 1) * devices, t * LANES : (t + 1) * LANES]
                s_ref[pl.ds(i * tiles + t, devices, stride=stride), :] = part
    out.wait_all()


def boxes_source(source, pos_ref, s_ref):
    listed = source.shape[1]
    boxes = s_ref.shape[0]
    put = lax.broadcasted_iota(I32, (listed, boxes * LANES), 1).astype(F32) == pos_ref[:, :1]
    sent = dot_split(source, put.astype(F32).astype(BF), NN)
    for b in range(boxes):
        s_ref[b] = sent[: s_ref.shape[1], b * LANES : (b + 1) * LANES]


def early_body(
    devices,
    rows,
    span,
    scalars,
    particles,
    count_ref,
    f_ref,
    base_ref,
    ot_ref,
    rate_ref,
    lcol_ref,
    w1_ref,
    w2_ref,
    w3_ref,
    grid_ref,
    token_ref,
    out_ref,
    end_ref,
    v_ref,
):
    listed, cells = ot_ref.shape
    tiles = cells // LANES
    places = lcol_ref.shape[0]
    side = max(1, LANES // places)
    wide = base_ref.shape[0]
    end_ref[...] = rate_ref[:, :LANES]
    f = load_filtered(f_ref, devices, rows, tiles)
    leaves = cell_onehot(lcol_ref, cells)
    rate = dot_split(jnp.broadcast_to(rate_ref[...], (SUB, cells)), leaves, NT)[:1]
    pull = rate * dot_split(f, leaves, NT)
    live = (lax.broadcasted_iota(I32, (SUB, listed), 1) < count_ref[0]).astype(F32).astype(BF)
    live = dot(dot(live, ot_ref[...], NN).astype(BF), leaves, NT)[:1]
    pull = jnp.concatenate([pull] * side, axis=1)
    live = jnp.concatenate([live] * side, axis=1) > 0.5
    count = 4 // wide

    todo = [(o, i) for o in range(particles // SUB // side) for i in range(0, SUB, count)]
    tile = [(u, t) for u in range(count) for t in range(wide)]
    ones, twos, fed = {}, {}, {}
    for n in range(len(todo) + 2):
        if n < len(todo):
            o, i = todo[n]
            fed[n] = jnp.concatenate(
                [
                    base_ref[t, o, pl.ds(i + u, rows, stride=SUB), :]
                    + pull[:, t * LANES : (t + 1) * LANES]
                    for u, t in tile
                ],
                axis=1,
            )
            ones[n] = half_silu(dot(w1_ref[...], fed[n].astype(BF), NN))
        if 0 < n <= len(todo):
            twos[n - 1] = half_silu(dot(w2_ref[...], ones[n - 1], NN))
        if n > 1:
            o, i = todo[n - 2]
            change = dot(w3_ref[...], twos[n - 2], NN).astype(BF).astype(F32)
            for c, (u, t) in enumerate(tile):
                cols = slice(c * LANES, (c + 1) * LANES)
                mask = live[:, t * LANES : (t + 1) * LANES]
                v_ref[t, o, pl.ds(i + u, rows, stride=SUB), :] = fed[n - 2][:, cols] + jnp.where(
                    mask, change[:, cols], 0.0
                )

    per = LANES // particles
    stride = out_ref.shape[0] // devices
    width = grid_ref.shape[0] // devices
    for d in range(devices):
        out_ref[(d + 1) * stride - width : (d + 1) * stride] = grid_ref[d * width : (d + 1) * width]

    def scalar(s):
        parts = []
        for o in range(particles // SUB // side):
            at = pl.ds(s * SUB, SUB)
            row = jnp.concatenate([v_ref[t, o, at, :] for t in range(wide)], axis=1)
            parts += [row[:, u * places : (u + 1) * places] for u in range(side)]
        return jnp.concatenate(parts, axis=0)

    def part(b, count):
        value = jnp.concatenate([scalar(b * per + i) for i in range(count)], axis=0)
        if count < per:
            rest = jnp.zeros(((per - count) * particles, places), F32)
            value = jnp.concatenate([value, rest], axis=0)
        value = value.T
        for c in range(places // devices):
            at = pl.ds(c * span + b, devices, stride=stride)
            out_ref[at, :] = value[c * devices : (c + 1) * devices]

    def step(b, carry):
        part(b, per)
        return carry

    whole = scalars // per
    lax.fori_loop(0, whole, step, 0, unroll=2)
    zeros = jnp.zeros((devices, LANES), F32)
    for c in range(places // devices):
        for b in range(whole, span):
            out_ref[pl.ds(c * span + b, devices, stride=stride), :] = zeros
    if scalars > whole * per:
        part(whole, scalars - whole * per)


def columns(row_ref, devices, out_ref, turn_ref):
    places = row_ref.shape[1]
    count = places // devices
    column = jnp.broadcast_to(row_ref[...].astype(F32), (SUB, places)).T[:, :1]
    turn_ref[...] = jnp.broadcast_to(column, turn_ref.shape)
    for c in range(count):
        part = turn_ref[pl.ds(c, devices, stride=count), :]
        out_ref[c * devices : (c + 1) * devices] = part.astype(I32)


def maps_body(
    dims,
    me_ref,
    inv_ref,
    ot_ref,
    owner_ref,
    slot_ref,
    leave_ref,
    arrive_ref,
    pos_ref,
    put_ref,
    lcol_ref,
    acol_ref,
    turn_ref,
):
    nx, ny, _, bx, by = dims
    columns(leave_ref, nx * ny, lcol_ref, turn_ref)
    columns(arrive_ref, nx * ny, acol_ref, turn_ref)
    quads = bx * by
    turns = quads * ny
    _, cells = ot_ref.shape
    at = me_ref[0] * 2 * turns + me_ref[1]
    code = jnp.concatenate([inv_ref[pl.ds(at + k * ny, 1), :] for k in range(quads)], axis=1)
    box = lax.rem(code, ny).astype(F32)
    boxes = lax.broadcasted_iota(I32, (ny, cells), 0).astype(F32)
    mine = (jnp.broadcast_to(box, (ny, cells)) == boxes).astype(F32)
    before = lax.broadcasted_iota(I32, (cells, cells), 0) < lax.broadcasted_iota(
        I32, (cells, cells), 1
    )
    count = dot(mine.astype(BF), before.astype(F32).astype(BF), NN)
    rank = jnp.sum(mine * count, axis=0, keepdims=True)
    rest = jnp.zeros((SUB - 2, cells), F32)
    found = dot(ot_ref[...], jnp.concatenate([box, rank, rest], axis=0).astype(BF), NT)
    pos = found[:, :1] * LANES + found[:, 1:2]
    pos_ref[...] = jnp.broadcast_to(pos, pos_ref.shape)
    flat = lambda ref: jnp.concatenate([ref[j : j + 1, :] for j in range(quads)], axis=1)
    owner, slot = flat(owner_ref).astype(F32), flat(slot_ref).astype(F32)
    first = owner * cells
    key = first + slot
    column = jnp.broadcast_to(key, (SUB, cells)).T[:, :1]
    ahead = (column < key) & (column >= first)
    place = owner * LANES + jnp.sum(ahead.astype(F32), axis=0, keepdims=True)
    step = min(cells, put_ref.shape[0])
    for b in range(put_ref.shape[0] // step):
        row = lax.broadcasted_iota(I32, (step, cells), 0).astype(F32) + b * step
        put_ref[b * step : (b + 1) * step] = (row == place).astype(F32).astype(BF)


def unpack_body(devices, own, s_ref, arr_ref, put_ref, out_ref):
    boxes, _ = s_ref.shape[:2]
    cells = put_ref.shape[1]
    quads = cells // LANES
    scalars = out_ref.shape[0] // quads
    stride = arr_ref.shape[0] // devices
    got = jnp.concatenate([s_ref[b] for b in range(boxes)], axis=1)
    source = dot_split(got, put_ref[...], NN)
    for j in range(quads):
        for i in range(own):
            n = min(devices, scalars - i * devices)
            if n > 0:
                grid = arr_ref[pl.ds(stride - own * quads + i * quads + j, n, stride=stride), :]
                part = source[i * devices : i * devices + n, j * LANES : (j + 1) * LANES]
                out_ref[pl.ds(i * devices * quads + j, n, stride=quads), :] = grid + part


def cell_onehot(col_ref, cells):
    shape = (col_ref.shape[0], cells)
    return (col_ref[:, :1] == lax.broadcasted_iota(I32, shape, 1)).astype(F32).astype(BF)


def settle_body(
    block,
    devices,
    q_hbm,
    f_ref,
    r_hbm,
    ot_ref,
    rate_ref,
    out_hbm,
    token_ref,
    q_ref,
    out_ref,
    r_ref,
    in_sem,
    out_sem,
    r_sem,
):
    into, out = Stream(q_hbm, q_ref, in_sem, block), Stream(out_ref, out_hbm, out_sem, block)
    changes = Stream(r_hbm, r_ref, r_sem, block * SUB, 2)
    for b in range(q_ref.shape[0] // block):
        changes.copy(b).start()
        into.copy(b).start()
    token_ref[...] = rate_ref[:, :LANES]

    def step(b, carry):
        changes.copy(b).wait()
        into.copy(b).wait()
        settle_block(b * block, block, q_ref, f_ref, r_ref, ot_ref, rate_ref, out_ref, devices)
        out.copy(b).start()
        return carry

    lax.fori_loop(0, q_ref.shape[0] // block, step, 0)
    out.wait_all()


def arrive_body(
    span, devices, p_hbm, arr_ref, acol_ref, out_hbm, p_ref, out_ref, hit_ref, in_sem, out_sem
):
    scalars, particles, cells = p_ref.shape
    places = acol_ref.shape[0]
    per = LANES // particles
    into, out = Stream(p_hbm, p_ref, in_sem, per), Stream(out_ref, out_hbm, out_sem, per)
    into.start_all()
    hit = (acol_ref[:, :1] == lax.broadcasted_iota(I32, (places, cells), 1)).astype(F32)
    hit_ref[...] = hit.astype(BF)
    taken = jnp.sum(hit, axis=0, keepdims=True) > 0.5
    stride = arr_ref.shape[0] // devices
    count = places // devices

    def place(b, size):
        first = b
        x = jnp.concatenate(
            [arr_ref[pl.ds(first + c * span, devices, stride=stride), :] for c in range(count)],
            axis=0,
        ).T
        y = dot_split(x, hit_ref[...], NN)
        into.copy(b, size).wait()
        for i in range(size):
            s = b * per + i
            out_ref[s] = jnp.where(taken, y[i * particles : (i + 1) * particles], p_ref[s])
        out.copy(b, size).start()

    def step(b, carry):
        place(b, per)
        return carry

    whole = scalars // per
    lax.fori_loop(0, whole, step, 0)
    if scalars > whole * per:
        place(whole, scalars - whole * per)
    out.wait_all()


def stencil(value, speed, bx, by, lanes_y):
    boxes = value[0].shape[0]
    row = lax.broadcasted_iota(I32, value[0].shape, 0) % lanes_y
    zero = jnp.zeros((lanes_y, LANES), F32)

    def x_low(v):
        return jnp.concatenate([zero, v[: boxes - lanes_y]], axis=0)

    def x_high(v):
        return jnp.concatenate([v[lanes_y:], zero], axis=0)

    def y_low(v):
        return jnp.where(row == 0, 0.0, pltpu.roll(v, 1, 0))

    def y_high(v):
        return jnp.where(row == lanes_y - 1, 0.0, pltpu.roll(v, boxes - 1, 0))

    out = []
    for i in range(bx):
        for j in range(by):
            c = value[i * by + j]
            up = value[(i - 1) * by + j] if i else x_low(value[(bx - 1) * by + j])
            down = value[(i + 1) * by + j] if i < bx - 1 else x_high(value[j])
            left = value[i * by + j - 1] if j else y_low(value[i * by + by - 1])
            right = value[i * by + j + 1] if j < by - 1 else y_high(value[i * by])
            beside = up + down + left + right + pltpu.roll(c, 1, 1) + pltpu.roll(c, LANES - 1, 1)
            out.append(c + DIFFUSION * (beside - 6.0 * c) - speed[i * by + j] * (c - up))
    return out


def route(src_ref, first_row, row_step, item_step, items, own, quads, lanes_y, rows, lanes):
    shape = (lanes_y, LANES)
    out = []
    for k in range(len(rows)):

        def step(y, acc):
            for j in range(items):
                hit = rows[k] == (j * lanes_y + y)
                at = first_row + y * row_step + j * item_step
                lines = [src_ref[pl.ds(at + s * quads, 1), :] for s in range(own)]
                acc = [
                    jnp.where(
                        hit,
                        jnp.take_along_axis(jnp.broadcast_to(v, shape), lanes[k], axis=1),
                        old,
                    )
                    for v, old in zip(lines, acc)
                ]
            return tuple(acc)

        zero = tuple(jnp.zeros(shape, F32) for _ in range(own))
        out.append(lax.fori_loop(0, lanes_y, step, zero, unroll=min(lanes_y, 8)))
    return [[out[k][s] for k in range(len(rows))] for s in range(own)]


def load_rows(ref, offset, stride, count):
    return ref[pl.ds(offset, count, stride=stride), :]


def pack_body(
    width,
    lanes_y,
    grid_hbm,
    owner_hbm,
    slot_hbm,
    speed_hbm,
    out_ref,
    grid_ref,
    owner_ref,
    slot_ref,
    speed_ref,
    sem,
):
    pairs = [
        (grid_hbm, grid_ref),
        (owner_hbm, owner_ref),
        (slot_hbm, slot_ref),
        (speed_hbm, speed_ref),
    ]
    copies = [pltpu.make_async_copy(a, b, sem.at[i]) for i, (a, b) in enumerate(pairs)]
    for c in copies:
        c.start()
    for c in copies:
        c.wait()
    quads = owner_ref.shape[0]
    stride = width + 2 * quads
    total = grid_ref.shape[0]
    slot = slot_ref[...]
    label = ((slot >> 7) * lanes_y + owner_ref[...]) * LANES + (slot & (LANES - 1))
    tail = jnp.concatenate([label.astype(F32), speed_ref[...]], axis=0)
    devices = out_ref.shape[0] // stride
    for d in range(devices):
        for i in range(width // quads):
            at = d * stride + i * quads
            src = (i * devices + d) * quads
            if src < total:
                out_ref[at : at + quads] = grid_ref[src : src + quads]
            else:
                out_ref[at : at + quads] = jnp.zeros((quads, LANES), F32)
        out_ref[d * stride + width : (d + 1) * stride] = tail


def weights_body(w1_ref, w2_ref, w3_ref, token_ref, a_ref, b_ref, c_ref):
    scalars, hidden = w1_ref.shape
    rest = jnp.zeros((a_ref.shape[1] - scalars, hidden), F32)
    a_ref[...] = jnp.concatenate([w1_ref[...].astype(F32) * 0.5, rest], axis=0).T.astype(BF)
    b_ref[...] = (w2_ref[...].astype(F32) * 0.5).astype(BF)
    c_ref[...] = jnp.concatenate([w3_ref[...].astype(F32), rest], axis=0).astype(BF)


def start_body(dims, arr_ref, token_ref, g_ref, f_ref, inv_ref, lab_ref):
    nx, ny, own, bx, by = dims
    quads = bx * by
    boxes = nx * ny
    width = own * quads
    stride = width + 2 * quads
    turns = quads * ny
    speed = [load_rows(arr_ref, width + quads + j, stride, boxes) for j in range(quads)]
    for s in range(own):
        value = [load_rows(arr_ref, s * quads + j, stride, boxes) for j in range(quads)]
        for j, v in enumerate(stencil(value, speed, bx, by, ny)):
            g_ref[pl.ds(s * quads + j, boxes, stride=width), :] = v
    for j in range(quads):
        lab_ref[pl.ds(j * boxes, boxes), :] = load_rows(arr_ref, width + j, stride, boxes).astype(
            I32
        )
    lane_of = lax.broadcasted_iota(I32, (turns, LANES), 1).astype(F32).astype(BF)
    sub_of = lax.broadcasted_iota(I32, (turns, LANES), 0).astype(F32).astype(BF)
    sub_lane = lax.broadcasted_iota(I32, (LANES, LANES), 0).astype(F32).astype(BF)
    none = jnp.zeros((turns, LANES), BF)
    unit = jnp.ones((LANES, LANES), BF)

    def group(x, carry):
        def gather(y, acc):
            left, right = [], []
            for j in range(quads):
                line = lab_ref[pl.ds(j * boxes + x * ny + y, 1), :]
                hit = jnp.broadcast_to((line >> 7).astype(F32).astype(BF), (turns, LANES)) == sub_of
                code = jnp.full((turns, LANES), j * ny + y).astype(F32).astype(BF)
                left.append(
                    jnp.concatenate([jnp.where(hit, code, none), jnp.where(hit, lane_of, none)], axis=0)
                )
                lane = jnp.broadcast_to((line & (LANES - 1)).astype(F32).astype(BF), (LANES, LANES))
                right.append(jnp.where(lane == sub_lane, unit, jnp.zeros_like(unit)))
            return acc + dot(
                jnp.concatenate(left, axis=1), jnp.concatenate(right, axis=1), NT
            )

        code = lax.fori_loop(0, ny, gather, jnp.zeros((2 * turns, LANES), F32), unroll=8)
        code = code.astype(I32)
        inv_ref[pl.ds(x * 2 * turns, 2 * turns), :] = code
        return carry

    lax.fori_loop(0, nx, group, 0)
    send_filtered(dims, g_ref, inv_ref, f_ref)


def send_filtered(dims, g_ref, inv_ref, f_ref):
    nx, ny, own, bx, by = dims
    quads = bx * by
    width = own * quads
    turns = quads * ny

    def group(x, carry):
        base = x * 2 * turns
        rows = [inv_ref[pl.ds(base + k * ny, ny), :] for k in range(quads)]
        lanes = [inv_ref[pl.ds(base + turns + k * ny, ny), :] for k in range(quads)]
        out = route(g_ref, x * ny * width, width, 1, quads, own, quads, ny, rows, lanes)
        for s in range(own):
            for k in range(quads):
                f_ref[pl.ds(x * ny * width + s * quads + k, ny, stride=width), :] = out[s][k]
        return carry

    lax.fori_loop(0, nx, group, 0)


def add_source(dims, s_ref, g_ref, lab_ref, out_ref):
    nx, ny, own, bx, by = dims
    quads = bx * by
    boxes = nx * ny
    width = own * quads
    stride = s_ref.shape[0] // boxes

    def group(x, carry):
        labels = [lab_ref[pl.ds(j * boxes + x * ny, ny), :] for j in range(quads)]
        rows = [v >> 7 for v in labels]
        lanes = [v & (LANES - 1) for v in labels]
        out = route(s_ref, x * ny * stride, stride, 1, quads, own, quads, ny, rows, lanes)
        for s in range(own):
            for k in range(quads):
                at = pl.ds(x * ny * width + s * quads + k, ny, stride=width)
                out_ref[at, :] = g_ref[at, :] + out[s][k]
        return carry

    lax.fori_loop(0, nx, group, 0)


def again_body(
    dims, s_ref, g_ref, arr_ref, inv_ref, lab_ref, token_ref, f_ref, out_ref, mid_ref
):
    nx, ny, own, bx, by = dims
    quads = bx * by
    boxes = nx * ny
    width = own * quads
    stride = width + 2 * quads
    add_source(dims, s_ref, g_ref, lab_ref, mid_ref)
    speed = [load_rows(arr_ref, width + quads + j, stride, boxes) for j in range(quads)]
    for s in range(own):
        value = [load_rows(mid_ref, s * quads + j, width, boxes) for j in range(quads)]
        for j, v in enumerate(stencil(value, speed, bx, by, ny)):
            out_ref[pl.ds(s * quads + j, boxes, stride=width), :] = v
    send_filtered(dims, out_ref, inv_ref, f_ref)


def per_device(
    grid_scalars,
    axial_speed,
    particles,
    cell_owner,
    cell_slot,
    mix_rate,
    partner,
    chem_input,
    chem_hidden,
    chem_output,
    react_slots,
    react_count,
    leave_slots,
    arrive_slots,
):
    both = ("gx", "gy")
    nx, ny = lax.axis_size("gx"), lax.axis_size("gy")
    devices = nx * ny
    scalars, bx, by, nz = grid_scalars.shape
    heads, cells = partner.shape
    listed = react_slots.shape[1]
    hidden = chem_hidden.shape[0]
    quads = bx * by
    own = -(-scalars // devices)
    rows = devices * own
    width = own * quads
    tiles = cells // LANES
    assert nz == LANES and tiles == quads and heads % SUB == 0 and LANES % heads == 0
    dims = (nx, ny, own, bx, by)
    flat = devices * width

    box = [
        grid_scalars.reshape(-1, LANES),
        cell_owner.reshape(quads, LANES),
        cell_slot.reshape(quads, LANES),
        axial_speed.reshape(quads, LANES),
    ]
    (first,) = call(
        functools.partial(pack_body, width, ny),
        [((devices * (width + 2 * quads), LANES), F32)],
        box,
        hbm=(0, 1, 2, 3),
        scratch=[pltpu.VMEM(x.shape, x.dtype) for x in box] + [pltpu.SemaphoreType.DMA((4,))],
    )

    def exchange(x):
        count = x.shape[0] // devices
        tile = SUB if count % SUB == 0 else SUB // 2
        x = x.reshape(devices, count // tile, tile, LANES)
        return lax.all_to_all(x, both, split_axis=0, concat_axis=0, tiled=True).reshape(-1, LANES)

    arrival = exchange(first)

    rate = mix_rate.reshape(1, cells)
    state_shape = (scalars, heads, cells)
    listed_shape = (listed // LANES, heads // SUB, rows * SUB, LANES)
    block = divisor(scalars, 6)
    octets = heads // SUB
    state_vmem = pltpu.VMEM(state_shape, F32)
    listed_vmem = pltpu.VMEM(listed_shape, F32)
    dma = pltpu.SemaphoreType.DMA
    per_block = dma((scalars // block,))
    per_listed = dma((-(-rows // block),))
    q, a, ot, rsel = call(
        functools.partial(open_body, block),
        [
            (state_shape, F32, True),
            (listed_shape, F32, True),
            ((listed, cells), BF),
            ((SUB, listed), F32),
        ],
        [particles, partner, rate, react_slots],
        hbm=(0, 1, 2, 3),
        scratch=[
            state_vmem,
            state_vmem,
            listed_vmem,
            pltpu.VMEM(partner.shape, I32),
            pltpu.VMEM(rate.shape, F32),
            pltpu.VMEM(react_slots.shape, I32),
            per_block,
            per_block,
            per_listed,
            dma((3,)),
        ],
    )
    grid, sent, inv, lab = call(
        functools.partial(start_body, dims),
        [
            ((flat, LANES), F32),
            ((flat, LANES), F32),
            ((nx * 2 * quads * ny, LANES), I32),
            ((quads * devices, LANES), I32),
        ],
        [arrival, rsel],
    )

    w1, w2, w3 = call(
        weights_body,
        [((hidden, rows), BF), ((hidden, hidden), BF), ((rows, hidden), BF)],
        [chem_input.T, chem_hidden, chem_output, lab],
    )

    per = LANES // heads
    span = 2 * (-(-scalars // (per * 2)))
    places = leave_slots.shape[1]
    side = max(1, LANES // places)
    base_shape = (max(1, places // LANES), octets // side, rows * SUB, LANES)
    kept = SUB * (-(-scalars // SUB))
    me = jnp.stack([lax.axis_index("gx"), lax.axis_index("gy")]).astype(I32)
    pos, put, lcol, acol = call(
        functools.partial(maps_body, dims),
        [
            ((listed, LANES), F32),
            ((ny * LANES, cells), BF),
            ((places, LANES), I32),
            ((places, LANES), I32),
        ],
        [me, inv, ot, box[1], box[2], leave_slots, arrive_slots],
        smem=(0,),
        scratch=[pltpu.VMEM((places, LANES), F32)],
    )

    def chemistry(f, a, token, out, more=()):
        return call(
            functools.partial(chem_body, devices, rows),
            [(listed_shape, F32, True), (out, F32)],
            [react_count, f, a, ot, rsel, w1, w2, w3, token, *more],
            smem=(0,),
            hbm=(2,),
            scratch=[listed_vmem, listed_vmem, pltpu.VMEM((rows, listed), F32)]
            + [dma((octets,)), dma((octets,))],
        )

    f = exchange(sent)
    change, source = chemistry(f, a, pos, (flat, LANES))
    home = exchange(source)
    q, token = call(
        functools.partial(middle_body, block, devices),
        [(state_shape, F32, True), ((1, LANES), F32)],
        [q, f, change, ot, rate, partner],
        hbm=(0, 2),
        scratch=[state_vmem, state_vmem, listed_vmem, per_block, per_block, per_listed],
    )
    sent, grid = call(
        functools.partial(again_body, dims),
        [((flat, LANES), F32), ((flat, LANES), F32)],
        [home, grid, arrival, inv, lab, token],
        scratch=[pltpu.VMEM((flat, LANES), F32)],
    )
    a, base, token = call(
        functools.partial(list_body, block),
        [(listed_shape, F32, True), (base_shape, F32), ((1, LANES), F32)],
        [q, rate, rsel, ot, lcol],
        hbm=(0,),
        scratch=[
            state_vmem,
            listed_vmem,
            per_block,
            per_listed,
        ],
    )
    f = exchange(sent)
    leaving, token = call(
        functools.partial(early_body, devices, rows, span, scalars, heads),
        [((places * span + flat, LANES), F32), ((1, LANES), F32)],
        [react_count, f, base, ot, rate, lcol, w1, w2, w3, grid, token],
        smem=(0,),
        scratch=[pltpu.VMEM(base_shape, F32)],
    )
    change, source = chemistry(f, a, token, (ny, kept, LANES), [pos])
    moved = exchange(leaving)
    state, token = call(
        functools.partial(settle_body, block, devices),
        [(state_shape, F32, True), ((1, LANES), F32)],
        [q, f, change, ot, rate],
        hbm=(0, 2),
        scratch=[state_vmem, state_vmem, listed_vmem, per_block, per_block, per_listed],
    )
    source = lax.all_to_all(source, "gy", split_axis=0, concat_axis=0, tiled=True)
    (grid,) = call(
        functools.partial(unpack_body, devices, own),
        [((scalars * quads, LANES), F32)],
        [source, moved, put],
    )
    grid_out = grid.reshape(grid_scalars.shape)
    steps = -(-scalars // per)
    (state,) = call(
        functools.partial(arrive_body, span, devices),
        [(state_shape, F32, True)],
        [state, moved, acol],
        hbm=(0,),
        scratch=[
            state_vmem,
            state_vmem,
            pltpu.VMEM((places, cells), BF),
            dma((steps,)),
            dma((steps,)),
        ],
    )
    return (grid_out, state)


def solution(mesh):
    placed = (
        P(None, "gx", "gy", None),
        P("gx", "gy", None),
        P(None, None, ("gx", "gy")),
        P("gx", "gy", None),
        P("gx", "gy", None),
        P(("gx", "gy")),
        P(None, ("gx", "gy")),
        P(),
        P(),
        P(),
        P(("gx", "gy"), None),
        P(("gx", "gy")),
        P(("gx", "gy"), None),
        P(("gx", "gy"), None),
    )

    return jax.shard_map(
        per_device,
        mesh=mesh,
        in_specs=placed,
        out_specs=(P(None, "gx", "gy", None), P(None, None, ("gx", "gy"))),
        check_vma=False,
    )
```

```python
import functools

import jax
import jax.numpy as jnp
from jax import lax
from jax.experimental import pallas as pl
from jax.experimental.pallas import tpu as pltpu
from jax.sharding import PartitionSpec as P


DIFFUSION = 0.1
PAIR_WEIGHT = 0.4
LANES = 128
SUB = 8
BF = jnp.bfloat16
F32 = jnp.float32
I32 = jnp.int32

NT = (((1,), (1,)), ((), ()))
NN = (((1,), (0,)), ((), ()))


def call(body, outs, ins, smem=(), hbm=(), scratch=(), limit=24):
    spaces = {**{i: pltpu.SMEM for i in smem}, **{i: pl.ANY for i in hbm}}
    ins = [pltpu.with_memory_space_constraint(x, pltpu.HBM) if i in hbm else x for i, x in enumerate(ins)]
    return pl.pallas_call(
        body,
        out_shape=[
            pltpu.HBM(o[0], o[1]) if len(o) > 2 else jax.ShapeDtypeStruct(o[0], o[1]) for o in outs
        ],
        in_specs=[
            pl.BlockSpec(memory_space=spaces.get(i, pltpu.VMEM)) for i in range(len(ins))
        ],
        out_specs=[
            pl.BlockSpec(memory_space=pl.ANY if len(o) > 2 else pltpu.VMEM) for o in outs
        ],
        scratch_shapes=list(scratch),
        compiler_params=pltpu.CompilerParams(vmem_limit_bytes=limit << 20),
    )(*ins)


class Stream:
    def __init__(self, src, dst, sem, size, dim=0):
        self.src, self.dst, self.sem, self.size, self.dim = src, dst, sem, size, dim
        self.count = -(-src.shape[dim] // size)

    def copy(self, i, size=None):
        at = (slice(None),) * self.dim + (pl.ds(i * self.size, size or self.size),)
        return pltpu.make_async_copy(self.src.at[at], self.dst.at[at], self.sem.at[i])

    def tail(self, i):
        return min(self.size, self.src.shape[self.dim] - i * self.size)

    def start_all(self):
        for i in range(self.count):
            self.copy(i, self.tail(i)).start()

    def wait_all(self, first=0):
        for i in range(first, self.count):
            self.copy(i, self.tail(i)).wait()


def dot(a, b, dims):
    return lax.dot_general(a, b, dims, preferred_element_type=F32)


def halves(x):
    high = x.astype(BF)
    return high, (x - high.astype(F32)).astype(BF)


def dot_split(x, onehot, dims):
    high, low = halves(x)
    y = dot(jnp.concatenate([high, low], axis=0), onehot, dims)
    return y[: x.shape[0]] + y[x.shape[0] :]


def load_filtered(f_ref, devices, rows, tiles):
    stride = f_ref.shape[0] // devices
    return jnp.concatenate(
        [
            jnp.concatenate(
                [
                    f_ref[pl.ds(i * tiles + t, devices, stride=stride), :]
                    for i in range(rows // devices)
                ],
                axis=0,
            )
            for t in range(tiles)
        ],
        axis=1,
    )


def divisor(n, most):
    return max(k for k in range(1, most + 1) if n % k == 0)


def mix(s0, block, p_ref, partner_ref, q_ref):
    _, particles, cells = p_ref.shape
    groups = particles // SUB
    for t in range(cells // LANES):
        lanes = pl.ds(t * LANES, LANES)
        rows, homes = [], []
        for j in range(groups):
            index = partner_ref[pl.ds(j * SUB, SUB), lanes]
            rows.append(index & (SUB - 1))
            homes.append(index >> 3)

        def step(i, carry):
            s = s0 + i
            x = [p_ref[s, pl.ds(k * SUB, SUB), lanes] for k in range(groups)]
            for j in range(groups):
                mate = jnp.take_along_axis(x[0], rows[j], axis=0)
                for k in range(1, groups):
                    other = jnp.take_along_axis(x[k], rows[j], axis=0)
                    mate = jnp.where(homes[j] == k, other, mate)
                q_ref[s, pl.ds(j * SUB, SUB), lanes] = x[j] + PAIR_WEIGHT * (mate - x[j])
            return carry

        lax.fori_loop(0, block, step, 0, unroll=True)


def put_scalar(ref, s, value):
    for o in range(ref.shape[1]):
        for t in range(ref.shape[0]):
            part = value[o * SUB : (o + 1) * SUB, t * LANES : (t + 1) * LANES]
            ref[t, o, pl.ds(s * SUB, SUB), :] = part


def get_scalar(ref, s):
    return jnp.concatenate(
        [
            jnp.concatenate(
                [ref[t, o, pl.ds(s * SUB, SUB), :] for t in range(ref.shape[0])], axis=1
            )
            for o in range(ref.shape[1])
        ],
        axis=0,
    )


def list_cells(s0, block, q_ref, onehot, keep, a_ref):
    _, particles, cells = q_ref.shape
    x = q_ref[pl.ds(s0, block)].reshape(block * particles, cells)
    y = dot_split(x, onehot, NT) * keep
    for i in range(block):
        put_scalar(a_ref, s0 + i, y[i * particles : (i + 1) * particles])


def list_body(
    block,
    q_hbm,
    rate_ref,
    rsel_ref,
    ot_ref,
    lcol_ref,
    a_hbm,
    base_ref,
    token_ref,
    q_ref,
    a_ref,
    in_sem,
    a_sem,
):
    scalars, particles, cells = q_ref.shape
    into = Stream(q_hbm, q_ref, in_sem, block)
    out_a = Stream(a_ref, a_hbm, a_sem, block * SUB, 2)
    into.start_all()
    token_ref[...] = rate_ref[:, :LANES]
    leaves = cell_onehot(lcol_ref, cells)
    places = lcol_ref.shape[0]
    side = max(1, LANES // places)
    keep = 1.0 - rate_ref[...]
    half = block * particles

    def step(b, carry):
        into.copy(b).wait()
        x = q_ref[pl.ds(b * block, block)].reshape(half, cells) * keep
        both = jnp.concatenate(halves(x), axis=0)
        y = dot(both, ot_ref[...], NT)
        y = y[:half] + y[half:]
        z = dot(both, leaves, NT)
        z = z[:half] + z[half:]
        for i in range(block):
            put_scalar(a_ref, b * block + i, y[i * particles : (i + 1) * particles])
            mine = z[i * particles : (i + 1) * particles]
            for o in range(base_ref.shape[1]):
                octets = [
                    mine[(o * side + u) * SUB : (o * side + u + 1) * SUB] for u in range(side)
                ]
                wide = jnp.concatenate(octets, axis=1)
                for t in range(base_ref.shape[0]):
                    at = pl.ds((b * block + i) * SUB, SUB)
                    base_ref[t, o, at, :] = wide[:, t * LANES : (t + 1) * LANES]
        out_a.copy(b).start()
        return carry

    lax.fori_loop(0, scalars // block, step, 0)
    clear_rest(scalars, base_ref)
    clear_rest(scalars, a_ref)
    for b in range(scalars // block, out_a.count):
        out_a.copy(b, out_a.tail(b)).start()
    out_a.wait_all()


def clear_rest(scalars, ref):
    rest = ref.shape[2] - scalars * SUB
    for t in range(ref.shape[0]):
        for o in range(ref.shape[1]):
            ref[t, o, pl.ds(scalars * SUB, rest), :] = jnp.zeros((rest, LANES), F32)


def open_body(
    block,
    p_hbm,
    partner_hbm,
    rate_hbm,
    list_hbm,
    q_hbm,
    a_hbm,
    ot_ref,
    rsel_ref,
    p_ref,
    q_ref,
    a_ref,
    partner_ref,
    rate_ref,
    list_ref,
    in_sem,
    out_sem,
    a_sem,
    few_sem,
):
    scalars, _, cells = p_ref.shape
    into, out = Stream(p_hbm, p_ref, in_sem, block), Stream(q_ref, q_hbm, out_sem, block)
    out_a = Stream(a_ref, a_hbm, a_sem, block * SUB, 2)
    few = [
        pltpu.make_async_copy(src, dst, few_sem.at[i])
        for i, (src, dst) in enumerate(
            [(list_hbm, list_ref), (rate_hbm, rate_ref), (partner_hbm, partner_ref)]
        )
    ]
    for c in few:
        c.start()
    into.start_all()
    for c in few:
        c.wait()
    column = jnp.broadcast_to(list_ref[...].astype(F32), (SUB, list_ref.shape[1])).T[:, :1]
    cell = lax.broadcasted_iota(I32, ot_ref.shape, 1).astype(F32)
    onehot = (column == cell).astype(F32)
    ot_ref[...] = onehot.astype(BF)
    rate = jnp.broadcast_to(rate_ref[...], (SUB, cells))
    rsel_ref[...] = dot_split(rate, onehot.astype(BF), NT)
    clear_rest(scalars, a_ref)

    def step(b, carry):
        into.copy(b).wait()
        mix(b * block, block, p_ref, partner_ref, q_ref)
        out.copy(b).start()
        list_cells(b * block, block, q_ref, ot_ref[...], 1.0 - rsel_ref[0:1, :], a_ref)
        out_a.copy(b).start()
        return carry

    whole = scalars // block
    for b in range(whole, out_a.count):
        out_a.copy(b, out_a.tail(b)).start()
    lax.fori_loop(0, whole, step, 0)
    out.wait_all()
    out_a.wait_all()


def settle_block(s0, block, q_ref, f_ref, r_ref, ot_ref, rate_ref, out_ref, devices):
    _, particles, cells = q_ref.shape
    tiles = cells // LANES
    rate = rate_ref[...]
    keep = 1.0 - rate
    r = jnp.concatenate([get_scalar(r_ref, s0 + i) for i in range(block)], axis=0)
    spread = dot(r.astype(BF), ot_ref[...], NN)
    for i in range(block):
        s = s0 + i
        at = lax.rem(s, devices) * (f_ref.shape[0] // devices) + lax.div(s, devices) * tiles
        f = jnp.concatenate([f_ref[pl.ds(at + t, 1), :] for t in range(tiles)], axis=1)
        out_ref[s0 + i] = (
            keep * q_ref[s0 + i] + rate * f + spread[i * particles : (i + 1) * particles]
        )


def middle_body(
    block,
    devices,
    q_hbm,
    f_ref,
    r_hbm,
    ot_ref,
    rate_ref,
    partner_ref,
    out_hbm,
    token_ref,
    q_ref,
    now_ref,
    r_ref,
    in_sem,
    out_sem,
    r_sem,
):
    scalars = q_ref.shape[0]
    into, out = Stream(q_hbm, q_ref, in_sem, block), Stream(q_ref, out_hbm, out_sem, block)
    changes = Stream(r_hbm, r_ref, r_sem, block * SUB, 2)
    for b in range(q_ref.shape[0] // block):
        changes.copy(b).start()
        into.copy(b).start()
    token_ref[...] = rate_ref[:, :LANES]

    def step(b, carry):
        changes.copy(b).wait()
        into.copy(b).wait()
        s0 = b * block
        settle_block(s0, block, q_ref, f_ref, r_ref, ot_ref, rate_ref, now_ref, devices)
        mix(s0, block, now_ref, partner_ref, q_ref)
        out.copy(b).start()
        return carry

    lax.fori_loop(0, scalars // block, step, 0)
    out.wait_all()


def half_silu(y):
    return (y + y * jnp.tanh(y)).astype(BF)


def chem_body(
    devices,
    rows,
    count_ref,
    f_ref,
    a_hbm,
    ot_ref,
    rsel_ref,
    w1_ref,
    w2_ref,
    w3_ref,
    token_ref,
    *refs,
):
    pos_refs, refs = refs[:-7], refs[-7:]
    r_hbm, s_ref, a_ref, r_ref, pull_ref, in_sem, out_sem = refs
    tiles = ot_ref.shape[1] // LANES
    listed = ot_ref.shape[0]
    particles = a_ref.shape[1] * SUB
    into, out = Stream(a_hbm, a_ref, in_sem, 1, 1), Stream(r_ref, r_hbm, out_sem, 1, 1)
    into.start_all()
    f = load_filtered(f_ref, devices, rows, tiles)
    pull_ref[...] = rsel_ref[0:1, :] * dot_split(f, ot_ref[...], NT)
    live = lax.broadcasted_iota(I32, (1, listed), 1) < count_ref[0]

    def first(g):
        parts = []
        for i in range(2):
            p = 2 * g + i
            at = pl.ds(p & (SUB - 1), rows, stride=SUB)
            for t in range(listed // LANES):
                pull = pull_ref[:, t * LANES : (t + 1) * LANES]
                parts.append((a_ref[t, p >> 3, at, :] + pull).astype(BF))
        return half_silu(dot(w1_ref[...], jnp.concatenate(parts, axis=1), NN))

    def second(one):
        return half_silu(dot(w2_ref[...], one, NN))

    def third(g, two, total):
        change = dot(w3_ref[...], two, NN).astype(BF).astype(F32)
        for i in range(2):
            r = jnp.where(live, change[:, i * listed : (i + 1) * listed], 0.0)
            p = 2 * g + i
            at = pl.ds(p & (SUB - 1), rows, stride=SUB)
            for t in range(listed // LANES):
                r_ref[t, p >> 3, at, :] = r[:, t * LANES : (t + 1) * LANES]
            total = total + r
        return total

    total = jnp.zeros((rows, listed), F32)
    groups, each = particles // 2, SUB // 2
    ones, twos = {}, {}
    for n in range(groups + 2):
        if n < groups:
            if n % each == 0:
                into.copy(n // each).wait()
            ones[n] = first(n)
        if 0 < n <= groups:
            twos[n - 1] = second(ones.pop(n - 1))
        if n > 1:
            total = third(n - 2, twos.pop(n - 2), total)
            if (n - 1) % each == 0 and n - 1 < groups:
                out.copy((n - 1) // each - 1).start()
    out.copy(particles // SUB - 1).start()
    source = total * (1.0 / particles)
    if pos_refs:
        boxes_source(source, *pos_refs, s_ref)
    else:
        source = dot_split(source, ot_ref[...], NN)
        stride = s_ref.shape[0] // devices
        for i in range(rows // devices):
            for t in range(tiles):
                part = source[i * devices : (i + 1) * devices, t * LANES : (t + 1) * LANES]
                s_ref[pl.ds(i * tiles + t, devices, stride=stride), :] = part
    out.wait_all()


def boxes_source(source, pos_ref, s_ref):
    listed = source.shape[1]
    boxes = s_ref.shape[0]
    put = lax.broadcasted_iota(I32, (listed, boxes * LANES), 1).astype(F32) == pos_ref[:, :1]
    sent = dot_split(source, put.astype(F32).astype(BF), NN)
    for b in range(boxes):
        s_ref[b] = sent[: s_ref.shape[1], b * LANES : (b + 1) * LANES]


def early_body(
    devices,
    rows,
    span,
    scalars,
    particles,
    count_ref,
    f_ref,
    base_ref,
    ot_ref,
    rate_ref,
    lcol_ref,
    w1_ref,
    w2_ref,
    w3_ref,
    token_ref,
    out_ref,
    end_ref,
    v_ref,
):
    listed, cells = ot_ref.shape
    tiles = cells // LANES
    places = lcol_ref.shape[0]
    side = max(1, LANES // places)
    wide = base_ref.shape[0]
    end_ref[...] = rate_ref[:, :LANES]
    f = load_filtered(f_ref, devices, rows, tiles)
    leaves = cell_onehot(lcol_ref, cells)
    rate = dot_split(jnp.broadcast_to(rate_ref[...], (SUB, cells)), leaves, NT)[:1]
    pull = rate * dot_split(f, leaves, NT)
    live = (lax.broadcasted_iota(I32, (SUB, listed), 1) < count_ref[0]).astype(F32).astype(BF)
    live = dot(dot(live, ot_ref[...], NN).astype(BF), leaves, NT)[:1]
    pull = jnp.concatenate([pull] * side, axis=1)
    live = jnp.concatenate([live] * side, axis=1) > 0.5
    count = 4 // wide

    todo = [(o, i) for o in range(particles // SUB // side) for i in range(0, SUB, count)]
    tile = [(u, t) for u in range(count) for t in range(wide)]
    ones, twos, fed = {}, {}, {}
    for n in range(len(todo) + 2):
        if n < len(todo):
            o, i = todo[n]
            fed[n] = jnp.concatenate(
                [
                    base_ref[t, o, pl.ds(i + u, rows, stride=SUB), :]
                    + pull[:, t * LANES : (t + 1) * LANES]
                    for u, t in tile
                ],
                axis=1,
            )
            ones[n] = half_silu(dot(w1_ref[...], fed[n].astype(BF), NN))
        if 0 < n <= len(todo):
            twos[n - 1] = half_silu(dot(w2_ref[...], ones[n - 1], NN))
        if n > 1:
            o, i = todo[n - 2]
            change = dot(w3_ref[...], twos[n - 2], NN).astype(BF).astype(F32)
            for c, (u, t) in enumerate(tile):
                cols = slice(c * LANES, (c + 1) * LANES)
                mask = live[:, t * LANES : (t + 1) * LANES]
                v_ref[t, o, pl.ds(i + u, rows, stride=SUB), :] = fed[n - 2][:, cols] + jnp.where(
                    mask, change[:, cols], 0.0
                )

    per = LANES // particles
    stride = out_ref.shape[0] // devices

    def scalar(s):
        parts = []
        for o in range(particles // SUB // side):
            at = pl.ds(s * SUB, SUB)
            row = jnp.concatenate([v_ref[t, o, at, :] for t in range(wide)], axis=1)
            parts += [row[:, u * places : (u + 1) * places] for u in range(side)]
        return jnp.concatenate(parts, axis=0)

    def part(b, count):
        value = jnp.concatenate([scalar(b * per + i) for i in range(count)], axis=0)
        if count < per:
            rest = jnp.zeros(((per - count) * particles, places), F32)
            value = jnp.concatenate([value, rest], axis=0)
        value = value.T
        for c in range(places // devices):
            at = pl.ds(c * span + b, devices, stride=stride)
            out_ref[at, :] = value[c * devices : (c + 1) * devices]

    def step(b, carry):
        part(b, per)
        return carry

    whole = scalars // per
    lax.fori_loop(0, whole, step, 0, unroll=2)
    zeros = jnp.zeros((devices, LANES), F32)
    for c in range(places // devices):
        for b in range(whole, span):
            out_ref[pl.ds(c * span + b, devices, stride=stride), :] = zeros
    if scalars > whole * per:
        part(whole, scalars - whole * per)


def columns(row_ref, devices, out_ref, turn_ref):
    places = row_ref.shape[1]
    count = places // devices
    column = jnp.broadcast_to(row_ref[...].astype(F32), (SUB, places)).T[:, :1]
    turn_ref[...] = jnp.broadcast_to(column, turn_ref.shape)
    for c in range(count):
        part = turn_ref[pl.ds(c, devices, stride=count), :]
        out_ref[c * devices : (c + 1) * devices] = part.astype(I32)


def maps_body(
    dims,
    me_ref,
    lab_ref,
    ot_ref,
    owner_ref,
    slot_ref,
    leave_ref,
    arrive_ref,
    pos_ref,
    put_ref,
    lcol_ref,
    acol_ref,
    inv_ref,
    turn_ref,
):
    nx, ny, _, bx, by = dims
    invert(dims, lab_ref, inv_ref)
    columns(leave_ref, nx * ny, lcol_ref, turn_ref)
    columns(arrive_ref, nx * ny, acol_ref, turn_ref)
    quads = bx * by
    turns = quads * ny
    _, cells = ot_ref.shape
    at = me_ref[0] * 2 * turns + me_ref[1]
    code = jnp.concatenate([inv_ref[pl.ds(at + k * ny, 1), :] for k in range(quads)], axis=1)
    box = lax.rem(code, ny).astype(F32)
    boxes = lax.broadcasted_iota(I32, (ny, cells), 0).astype(F32)
    mine = (jnp.broadcast_to(box, (ny, cells)) == boxes).astype(F32)
    before = lax.broadcasted_iota(I32, (cells, cells), 0) < lax.broadcasted_iota(
        I32, (cells, cells), 1
    )
    count = dot(mine.astype(BF), before.astype(F32).astype(BF), NN)
    rank = jnp.sum(mine * count, axis=0, keepdims=True)
    rest = jnp.zeros((SUB - 2, cells), F32)
    found = dot(ot_ref[...], jnp.concatenate([box, rank, rest], axis=0).astype(BF), NT)
    pos = found[:, :1] * LANES + found[:, 1:2]
    pos_ref[...] = jnp.broadcast_to(pos, pos_ref.shape)
    flat = lambda ref: jnp.concatenate([ref[j : j + 1, :] for j in range(quads)], axis=1)
    owner, slot = flat(owner_ref).astype(F32), flat(slot_ref).astype(F32)
    first = owner * cells
    key = first + slot
    column = jnp.broadcast_to(key, (SUB, cells)).T[:, :1]
    ahead = (column < key) & (column >= first)
    place = owner * LANES + jnp.sum(ahead.astype(F32), axis=0, keepdims=True)
    step = min(cells, put_ref.shape[0])
    for b in range(put_ref.shape[0] // step):
        row = lax.broadcasted_iota(I32, (step, cells), 0).astype(F32) + b * step
        put_ref[b * step : (b + 1) * step] = (row == place).astype(F32).astype(BF)


def unpack_body(devices, own, s_ref, arr_ref, put_ref, out_ref):
    boxes, _ = s_ref.shape[:2]
    cells = put_ref.shape[1]
    quads = cells // LANES
    scalars = out_ref.shape[0] // quads
    stride = arr_ref.shape[0] // devices
    got = jnp.concatenate([s_ref[b] for b in range(boxes)], axis=1)
    source = dot_split(got, put_ref[...], NN)
    for j in range(quads):
        for i in range(own):
            n = min(devices, scalars - i * devices)
            if n > 0:
                grid = arr_ref[pl.ds(stride - own * quads + i * quads + j, n, stride=stride), :]
                part = source[i * devices : i * devices + n, j * LANES : (j + 1) * LANES]
                out_ref[pl.ds(i * devices * quads + j, n, stride=quads), :] = grid + part


def cell_onehot(col_ref, cells):
    shape = (col_ref.shape[0], cells)
    return (col_ref[:, :1] == lax.broadcasted_iota(I32, shape, 1)).astype(F32).astype(BF)


def settle_body(
    block,
    devices,
    q_hbm,
    f_ref,
    r_hbm,
    ot_ref,
    rate_ref,
    out_hbm,
    token_ref,
    q_ref,
    out_ref,
    r_ref,
    in_sem,
    out_sem,
    r_sem,
):
    into, out = Stream(q_hbm, q_ref, in_sem, block), Stream(out_ref, out_hbm, out_sem, block)
    changes = Stream(r_hbm, r_ref, r_sem, block * SUB, 2)
    for b in range(q_ref.shape[0] // block):
        changes.copy(b).start()
        into.copy(b).start()
    token_ref[...] = rate_ref[:, :LANES]

    def step(b, carry):
        changes.copy(b).wait()
        into.copy(b).wait()
        settle_block(b * block, block, q_ref, f_ref, r_ref, ot_ref, rate_ref, out_ref, devices)
        out.copy(b).start()
        return carry

    lax.fori_loop(0, q_ref.shape[0] // block, step, 0)
    out.wait_all()


def arrive_body(
    span, devices, p_hbm, arr_ref, acol_ref, out_hbm, p_ref, out_ref, hit_ref, in_sem, out_sem
):
    scalars, particles, cells = p_ref.shape
    places = acol_ref.shape[0]
    per = LANES // particles
    into, out = Stream(p_hbm, p_ref, in_sem, per), Stream(out_ref, out_hbm, out_sem, per)
    into.start_all()
    hit = (acol_ref[:, :1] == lax.broadcasted_iota(I32, (places, cells), 1)).astype(F32)
    hit_ref[...] = hit.astype(BF)
    taken = jnp.sum(hit, axis=0, keepdims=True) > 0.5
    stride = arr_ref.shape[0] // devices
    count = places // devices

    def place(b, size):
        first = stride - count * span + b
        x = jnp.concatenate(
            [arr_ref[pl.ds(first + c * span, devices, stride=stride), :] for c in range(count)],
            axis=0,
        ).T
        y = dot_split(x, hit_ref[...], NN)
        into.copy(b, size).wait()
        for i in range(size):
            s = b * per + i
            out_ref[s] = jnp.where(taken, y[i * particles : (i + 1) * particles], p_ref[s])
        out.copy(b, size).start()

    def step(b, carry):
        place(b, per)
        return carry

    whole = scalars // per
    lax.fori_loop(0, whole, step, 0)
    if scalars > whole * per:
        place(whole, scalars - whole * per)
    out.wait_all()


def stencil(value, speed, bx, by, lanes_y):
    boxes = value[0].shape[0]
    row = lax.broadcasted_iota(I32, value[0].shape, 0) % lanes_y
    zero = jnp.zeros((lanes_y, LANES), F32)

    def x_low(v):
        return jnp.concatenate([zero, v[: boxes - lanes_y]], axis=0)

    def x_high(v):
        return jnp.concatenate([v[lanes_y:], zero], axis=0)

    def y_low(v):
        return jnp.where(row == 0, 0.0, pltpu.roll(v, 1, 0))

    def y_high(v):
        return jnp.where(row == lanes_y - 1, 0.0, pltpu.roll(v, boxes - 1, 0))

    out = []
    for i in range(bx):
        for j in range(by):
            c = value[i * by + j]
            up = value[(i - 1) * by + j] if i else x_low(value[(bx - 1) * by + j])
            down = value[(i + 1) * by + j] if i < bx - 1 else x_high(value[j])
            left = value[i * by + j - 1] if j else y_low(value[i * by + by - 1])
            right = value[i * by + j + 1] if j < by - 1 else y_high(value[i * by])
            beside = up + down + left + right + pltpu.roll(c, 1, 1) + pltpu.roll(c, LANES - 1, 1)
            out.append(c + DIFFUSION * (beside - 6.0 * c) - speed[i * by + j] * (c - up))
    return out


def route(src_ref, first_row, row_step, item_step, items, own, quads, lanes_y, rows, lanes):
    shape = (lanes_y, LANES)
    out = []
    for k in range(len(rows)):

        def step(y, acc):
            for j in range(items):
                hit = rows[k] == (j * lanes_y + y)
                at = first_row + y * row_step + j * item_step
                lines = [src_ref[pl.ds(at + s * quads, 1), :] for s in range(own)]
                acc = [
                    jnp.where(
                        hit,
                        jnp.take_along_axis(jnp.broadcast_to(v, shape), lanes[k], axis=1),
                        old,
                    )
                    for v, old in zip(lines, acc)
                ]
            return tuple(acc)

        zero = tuple(jnp.zeros(shape, F32) for _ in range(own))
        out.append(lax.fori_loop(0, lanes_y, step, zero, unroll=min(lanes_y, 8)))
    return [[out[k][s] for k in range(len(rows))] for s in range(own)]


def load_rows(ref, offset, stride, count):
    return ref[pl.ds(offset, count, stride=stride), :]


def pack_body(
    width,
    lanes_y,
    grid_hbm,
    owner_hbm,
    slot_hbm,
    speed_hbm,
    out_ref,
    grid_ref,
    owner_ref,
    slot_ref,
    speed_ref,
    sem,
):
    pairs = [
        (grid_hbm, grid_ref),
        (owner_hbm, owner_ref),
        (slot_hbm, slot_ref),
        (speed_hbm, speed_ref),
    ]
    copies = [pltpu.make_async_copy(a, b, sem.at[i]) for i, (a, b) in enumerate(pairs)]
    for c in copies:
        c.start()
    for c in copies:
        c.wait()
    quads = owner_ref.shape[0]
    stride = width + 2 * quads
    total = grid_ref.shape[0]
    slot = slot_ref[...]
    label = ((slot >> 7) * lanes_y + owner_ref[...]) * LANES + (slot & (LANES - 1))
    tail = jnp.concatenate([label.astype(F32), speed_ref[...]], axis=0)
    devices = out_ref.shape[0] // stride
    for d in range(devices):
        for i in range(width // quads):
            at = d * stride + i * quads
            src = (i * devices + d) * quads
            if src < total:
                out_ref[at : at + quads] = grid_ref[src : src + quads]
            else:
                out_ref[at : at + quads] = jnp.zeros((quads, LANES), F32)
        out_ref[d * stride + width : (d + 1) * stride] = tail


def weights_body(w1_ref, w2_ref, w3_ref, token_ref, a_ref, b_ref, c_ref):
    scalars, hidden = w1_ref.shape
    rest = jnp.zeros((a_ref.shape[1] - scalars, hidden), F32)
    a_ref[...] = jnp.concatenate([w1_ref[...].astype(F32) * 0.5, rest], axis=0).T.astype(BF)
    b_ref[...] = (w2_ref[...].astype(F32) * 0.5).astype(BF)
    c_ref[...] = jnp.concatenate([w3_ref[...].astype(F32), rest], axis=0).astype(BF)


def start_body(dims, arr_ref, token_ref, g_ref, f_ref, lab_ref, high_ref, low_ref):
    nx, ny, own, bx, by = dims
    quads = bx * by
    boxes = nx * ny
    width = own * quads
    stride = width + 2 * quads
    turns = quads * ny
    speed = [load_rows(arr_ref, width + quads + j, stride, boxes) for j in range(quads)]
    for s in range(own):
        value = [load_rows(arr_ref, s * quads + j, stride, boxes) for j in range(quads)]
        for j, v in enumerate(stencil(value, speed, bx, by, ny)):
            at = pl.ds(s * quads + j, boxes, stride=width)
            g_ref[at, :] = v
            high = v.astype(BF).astype(F32)
            high_ref[at, :] = high
            low_ref[at, :] = v - high
    for j in range(quads):
        lab_ref[pl.ds(j * boxes, boxes), :] = load_rows(arr_ref, width + j, stride, boxes).astype(
            I32
        )
    sub_of = lax.broadcasted_iota(I32, (turns, LANES), 0).astype(F32).astype(BF)
    sub_lane = lax.broadcasted_iota(I32, (LANES, LANES), 0).astype(F32).astype(BF)
    none = jnp.zeros((turns, LANES), BF)
    unit = jnp.ones((LANES, LANES), BF)

    def group(x, carry):
        def gather(y, acc):
            left, right = [], []
            for j in range(quads):
                line = lab_ref[pl.ds(j * boxes + x * ny + y, 1), :]
                hit = jnp.broadcast_to((line >> 7).astype(F32).astype(BF), (turns, LANES)) == sub_of
                parts = []
                for s in range(own):
                    at = pl.ds((x * ny + y) * width + s * quads + j, 1)
                    for ref in (high_ref, low_ref):
                        value = jnp.broadcast_to(ref[at, :].astype(BF), (turns, LANES))
                        parts.append(jnp.where(hit, value, none))
                left.append(jnp.concatenate(parts, axis=0))
                lane = jnp.broadcast_to((line & (LANES - 1)).astype(F32).astype(BF), (LANES, LANES))
                right.append(jnp.where(lane == sub_lane, unit, jnp.zeros_like(unit)))
            return acc + dot(jnp.concatenate(left, axis=1), jnp.concatenate(right, axis=1), NT)

        zero = jnp.zeros((2 * own * turns, LANES), F32)
        acc = lax.fori_loop(0, ny, gather, zero, unroll=min(ny, 8))
        for s in range(own):
            out = acc[2 * s * turns : (2 * s + 1) * turns] + acc[(2 * s + 1) * turns :][:turns]
            for k in range(quads):
                at = pl.ds(x * ny * width + s * quads + k, ny, stride=width)
                f_ref[at, :] = out[k * ny : (k + 1) * ny]
        return carry

    lax.fori_loop(0, nx, group, 0)


def invert(dims, lab_ref, inv_ref):
    nx, ny, _, bx, by = dims
    quads = bx * by
    boxes = nx * ny
    turns = quads * ny
    lane_of = lax.broadcasted_iota(I32, (turns, LANES), 1).astype(F32).astype(BF)
    sub_of = lax.broadcasted_iota(I32, (turns, LANES), 0).astype(F32).astype(BF)
    sub_lane = lax.broadcasted_iota(I32, (LANES, LANES), 0).astype(F32).astype(BF)
    none = jnp.zeros((turns, LANES), BF)
    unit = jnp.ones((LANES, LANES), BF)

    def group(x, carry):
        def gather(y, acc):
            left, right = [], []
            for j in range(quads):
                line = lab_ref[pl.ds(j * boxes + x * ny + y, 1), :]
                hit = jnp.broadcast_to((line >> 7).astype(F32).astype(BF), (turns, LANES)) == sub_of
                code = jnp.full((turns, LANES), j * ny + y).astype(F32).astype(BF)
                left.append(
                    jnp.concatenate([jnp.where(hit, code, none), jnp.where(hit, lane_of, none)], axis=0)
                )
                lane = jnp.broadcast_to((line & (LANES - 1)).astype(F32).astype(BF), (LANES, LANES))
                right.append(jnp.where(lane == sub_lane, unit, jnp.zeros_like(unit)))
            return acc + dot(
                jnp.concatenate(left, axis=1), jnp.concatenate(right, axis=1), NT
            )

        code = lax.fori_loop(0, ny, gather, jnp.zeros((2 * turns, LANES), F32), unroll=8)
        code = code.astype(I32)
        inv_ref[pl.ds(x * 2 * turns, 2 * turns), :] = code
        return carry

    lax.fori_loop(0, nx, group, 0)


def send_filtered(dims, g_ref, g_stride, g_first, inv_ref, f_ref):
    nx, ny, own, bx, by = dims
    quads = bx * by
    turns = quads * ny
    f_stride = f_ref.shape[0] // (nx * ny)

    def group(x, carry):
        base = x * 2 * turns
        rows = [inv_ref[pl.ds(base + k * ny, ny), :] for k in range(quads)]
        lanes = [inv_ref[pl.ds(base + turns + k * ny, ny), :] for k in range(quads)]
        first = x * ny * g_stride + g_first
        out = route(g_ref, first, g_stride, 1, quads, own, quads, ny, rows, lanes)
        for s in range(own):
            for k in range(quads):
                at = pl.ds(x * ny * f_stride + s * quads + k, ny, stride=f_stride)
                f_ref[at, :] = out[s][k]
        return carry

    lax.fori_loop(0, nx, group, 0)


def add_source(dims, s_ref, g_ref, lab_ref, out_ref):
    nx, ny, own, bx, by = dims
    quads = bx * by
    boxes = nx * ny
    width = own * quads
    stride = s_ref.shape[0] // boxes

    def group(x, carry):
        labels = [lab_ref[pl.ds(j * boxes + x * ny, ny), :] for j in range(quads)]
        rows = [v >> 7 for v in labels]
        lanes = [v & (LANES - 1) for v in labels]
        out = route(s_ref, x * ny * stride, stride, 1, quads, own, quads, ny, rows, lanes)
        for s in range(own):
            for k in range(quads):
                at = pl.ds(x * ny * width + s * quads + k, ny, stride=width)
                out_ref[at, :] = g_ref[at, :] + out[s][k]
        return carry

    lax.fori_loop(0, nx, group, 0)


def again_body(dims, s_ref, g_ref, arr_ref, inv_ref, lab_ref, token_ref, f_ref, mid_ref):
    nx, ny, own, bx, by = dims
    quads = bx * by
    boxes = nx * ny
    width = own * quads
    stride = width + 2 * quads
    add_source(dims, s_ref, g_ref, lab_ref, mid_ref)
    speed = [load_rows(arr_ref, width + quads + j, stride, boxes) for j in range(quads)]
    for s in range(own):
        value = [load_rows(mid_ref, s * quads + j, width, boxes) for j in range(quads)]
        for j, v in enumerate(stencil(value, speed, bx, by, ny)):
            f_ref[pl.ds(width + s * quads + j, boxes, stride=2 * width), :] = v
    send_filtered(dims, f_ref, 2 * width, width, inv_ref, f_ref)


def per_device(
    grid_scalars,
    axial_speed,
    particles,
    cell_owner,
    cell_slot,
    mix_rate,
    partner,
    chem_input,
    chem_hidden,
    chem_output,
    react_slots,
    react_count,
    leave_slots,
    arrive_slots,
):
    both = ("gx", "gy")
    nx, ny = lax.axis_size("gx"), lax.axis_size("gy")
    devices = nx * ny
    scalars, bx, by, nz = grid_scalars.shape
    heads, cells = partner.shape
    listed = react_slots.shape[1]
    hidden = chem_hidden.shape[0]
    quads = bx * by
    own = -(-scalars // devices)
    rows = devices * own
    width = own * quads
    tiles = cells // LANES
    assert nz == LANES and tiles == quads and heads % SUB == 0 and LANES % heads == 0
    dims = (nx, ny, own, bx, by)
    flat = devices * width

    box = [
        grid_scalars.reshape(-1, LANES),
        cell_owner.reshape(quads, LANES),
        cell_slot.reshape(quads, LANES),
        axial_speed.reshape(quads, LANES),
    ]
    (first,) = call(
        functools.partial(pack_body, width, ny),
        [((devices * (width + 2 * quads), LANES), F32)],
        box,
        hbm=(0, 1, 2, 3),
        scratch=[pltpu.VMEM(x.shape, x.dtype) for x in box] + [pltpu.SemaphoreType.DMA((4,))],
    )

    def exchange(x):
        count = x.shape[0] // devices
        tile = SUB if count % SUB == 0 else SUB // 2
        x = x.reshape(devices, count // tile, tile, LANES)
        return lax.all_to_all(x, both, split_axis=0, concat_axis=0, tiled=True).reshape(-1, LANES)

    arrival = exchange(first)

    rate = mix_rate.reshape(1, cells)
    state_shape = (scalars, heads, cells)
    listed_shape = (listed // LANES, heads // SUB, rows * SUB, LANES)
    block = divisor(scalars, 6)
    octets = heads // SUB
    state_vmem = pltpu.VMEM(state_shape, F32)
    listed_vmem = pltpu.VMEM(listed_shape, F32)
    dma = pltpu.SemaphoreType.DMA
    per_block = dma((scalars // block,))
    per_listed = dma((-(-rows // block),))
    q, a, ot, rsel = call(
        functools.partial(open_body, block),
        [
            (state_shape, F32, True),
            (listed_shape, F32, True),
            ((listed, cells), BF),
            ((SUB, listed), F32),
        ],
        [particles, partner, rate, react_slots],
        hbm=(0, 1, 2, 3),
        scratch=[
            state_vmem,
            state_vmem,
            listed_vmem,
            pltpu.VMEM(partner.shape, I32),
            pltpu.VMEM(rate.shape, F32),
            pltpu.VMEM(react_slots.shape, I32),
            per_block,
            per_block,
            per_listed,
            dma((3,)),
        ],
    )
    grid, sent, lab = call(
        functools.partial(start_body, dims),
        [((flat, LANES), F32), ((flat, LANES), F32), ((quads * devices, LANES), I32)],
        [arrival, rsel],
        scratch=[pltpu.VMEM((flat, LANES), F32)] * 2,
    )

    w1, w2, w3 = call(
        weights_body,
        [((hidden, rows), BF), ((hidden, hidden), BF), ((rows, hidden), BF)],
        [chem_input.T, chem_hidden, chem_output, lab],
    )

    per = LANES // heads
    span = 2 * (-(-scalars // (per * 2)))
    places = leave_slots.shape[1]
    side = max(1, LANES // places)
    base_shape = (max(1, places // LANES), octets // side, rows * SUB, LANES)
    kept = SUB * (-(-scalars // SUB))
    me = jnp.stack([lax.axis_index("gx"), lax.axis_index("gy")]).astype(I32)
    pos, put, lcol, acol, inv = call(
        functools.partial(maps_body, dims),
        [
            ((listed, LANES), F32),
            ((ny * LANES, cells), BF),
            ((places, LANES), I32),
            ((places, LANES), I32),
            ((nx * 2 * quads * ny, LANES), I32),
        ],
        [me, lab, ot, box[1], box[2], leave_slots, arrive_slots],
        smem=(0,),
        scratch=[pltpu.VMEM((places, LANES), F32)],
    )

    def chemistry(f, a, token, out, more=()):
        return call(
            functools.partial(chem_body, devices, rows),
            [(listed_shape, F32, True), (out, F32)],
            [react_count, f, a, ot, rsel, w1, w2, w3, token, *more],
            smem=(0,),
            hbm=(2,),
            scratch=[listed_vmem, listed_vmem, pltpu.VMEM((rows, listed), F32)]
            + [dma((octets,)), dma((octets,))],
        )

    f = exchange(sent)
    change, source = chemistry(f, a, pos, (flat, LANES))
    home = exchange(source)
    q, token = call(
        functools.partial(middle_body, block, devices),
        [(state_shape, F32, True), ((1, LANES), F32)],
        [q, f, change, ot, rate, partner],
        hbm=(0, 2),
        scratch=[state_vmem, state_vmem, listed_vmem, per_block, per_block, per_listed],
    )
    (sent,) = call(
        functools.partial(again_body, dims),
        [((2 * flat, LANES), F32)],
        [home, grid, arrival, inv, lab, token],
        scratch=[pltpu.VMEM((flat, LANES), F32)],
    )
    a, base, token = call(
        functools.partial(list_body, block),
        [(listed_shape, F32, True), (base_shape, F32), ((1, LANES), F32)],
        [q, rate, rsel, ot, lcol],
        hbm=(0,),
        scratch=[
            state_vmem,
            listed_vmem,
            per_block,
            per_listed,
        ],
    )
    f = exchange(sent)
    leaving, token = call(
        functools.partial(early_body, devices, rows, span, scalars, heads),
        [((places * span, LANES), F32), ((1, LANES), F32)],
        [react_count, f, base, ot, rate, lcol, w1, w2, w3, token],
        smem=(0,),
        scratch=[pltpu.VMEM(base_shape, F32)],
    )
    change, source = chemistry(f, a, token, (ny, kept, LANES), [pos])
    moved = exchange(leaving)
    state, token = call(
        functools.partial(settle_body, block, devices),
        [(state_shape, F32, True), ((1, LANES), F32)],
        [q, f, change, ot, rate],
        hbm=(0, 2),
        scratch=[state_vmem, state_vmem, listed_vmem, per_block, per_block, per_listed],
    )
    source = lax.all_to_all(source, "gy", split_axis=0, concat_axis=0, tiled=True)
    (grid,) = call(
        functools.partial(unpack_body, devices, own),
        [((scalars * quads, LANES), F32)],
        [source, f, put],
    )
    grid_out = grid.reshape(grid_scalars.shape)
    steps = -(-scalars // per)
    (state,) = call(
        functools.partial(arrive_body, span, devices),
        [(state_shape, F32, True)],
        [state, moved, acol],
        hbm=(0,),
        scratch=[
            state_vmem,
            state_vmem,
            pltpu.VMEM((places, cells), BF),
            dma((steps,)),
            dma((steps,)),
        ],
    )
    return (grid_out, state)


def solution(mesh):
    placed = (
        P(None, "gx", "gy", None),
        P("gx", "gy", None),
        P(None, None, ("gx", "gy")),
        P("gx", "gy", None),
        P("gx", "gy", None),
        P(("gx", "gy")),
        P(None, ("gx", "gy")),
        P(),
        P(),
        P(),
        P(("gx", "gy"), None),
        P(("gx", "gy")),
        P(("gx", "gy"), None),
        P(("gx", "gy"), None),
    )

    return jax.shard_map(
        per_device,
        mesh=mesh,
        in_specs=placed,
        out_specs=(P(None, "gx", "gy", None), P(None, None, ("gx", "gy"))),
        check_vma=False,
    )
```

```python
import functools

import jax
import jax.numpy as jnp
from jax import lax
from jax.experimental import pallas as pl
from jax.experimental.pallas import tpu as pltpu
from jax.sharding import PartitionSpec as P


DIFFUSION = 0.1
PAIR_WEIGHT = 0.4
LANES = 128
SUB = 8
BF = jnp.bfloat16
F32 = jnp.float32
I32 = jnp.int32

NT = (((1,), (1,)), ((), ()))
NN = (((1,), (0,)), ((), ()))


def call(body, outs, ins, smem=(), hbm=(), scratch=(), limit=24):
    spaces = {**{i: pltpu.SMEM for i in smem}, **{i: pl.ANY for i in hbm}}
    ins = [pltpu.with_memory_space_constraint(x, pltpu.HBM) if i in hbm else x for i, x in enumerate(ins)]
    return pl.pallas_call(
        body,
        out_shape=[
            pltpu.HBM(o[0], o[1]) if len(o) > 2 else jax.ShapeDtypeStruct(o[0], o[1]) for o in outs
        ],
        in_specs=[
            pl.BlockSpec(memory_space=spaces.get(i, pltpu.VMEM)) for i in range(len(ins))
        ],
        out_specs=[
            pl.BlockSpec(memory_space=pl.ANY if len(o) > 2 else pltpu.VMEM) for o in outs
        ],
        scratch_shapes=list(scratch),
        compiler_params=pltpu.CompilerParams(vmem_limit_bytes=limit << 20),
    )(*ins)


class Stream:
    def __init__(self, src, dst, sem, size, dim=0):
        self.src, self.dst, self.sem, self.size, self.dim = src, dst, sem, size, dim
        self.count = -(-src.shape[dim] // size)

    def copy(self, i, size=None):
        at = (slice(None),) * self.dim + (pl.ds(i * self.size, size or self.size),)
        return pltpu.make_async_copy(self.src.at[at], self.dst.at[at], self.sem.at[i])

    def tail(self, i):
        return min(self.size, self.src.shape[self.dim] - i * self.size)

    def start_all(self):
        for i in range(self.count):
            self.copy(i, self.tail(i)).start()

    def wait_all(self, first=0):
        for i in range(first, self.count):
            self.copy(i, self.tail(i)).wait()


def dot(a, b, dims):
    return lax.dot_general(a, b, dims, preferred_element_type=F32)


def halves(x):
    high = x.astype(BF)
    return high, (x - high.astype(F32)).astype(BF)


def dot_split(x, onehot, dims):
    high, low = halves(x)
    y = dot(jnp.concatenate([high, low], axis=0), onehot, dims)
    return y[: x.shape[0]] + y[x.shape[0] :]


def load_filtered(f_ref, devices, rows, tiles):
    stride = f_ref.shape[0] // devices
    return jnp.concatenate(
        [
            jnp.concatenate(
                [
                    f_ref[pl.ds(i * tiles + t, devices, stride=stride), :]
                    for i in range(rows // devices)
                ],
                axis=0,
            )
            for t in range(tiles)
        ],
        axis=1,
    )


def divisor(n, most):
    return max(k for k in range(1, most + 1) if n % k == 0)


def mix(s0, block, p_ref, partner_ref, q_ref):
    _, particles, cells = p_ref.shape
    groups = particles // SUB
    for t in range(cells // LANES):
        lanes = pl.ds(t * LANES, LANES)
        rows, homes = [], []
        for j in range(groups):
            index = partner_ref[pl.ds(j * SUB, SUB), lanes]
            rows.append(index & (SUB - 1))
            homes.append(index >> 3)

        def step(i, carry):
            s = s0 + i
            x = [p_ref[s, pl.ds(k * SUB, SUB), lanes] for k in range(groups)]
            for j in range(groups):
                mate = jnp.take_along_axis(x[0], rows[j], axis=0)
                for k in range(1, groups):
                    other = jnp.take_along_axis(x[k], rows[j], axis=0)
                    mate = jnp.where(homes[j] == k, other, mate)
                q_ref[s, pl.ds(j * SUB, SUB), lanes] = x[j] + PAIR_WEIGHT * (mate - x[j])
            return carry

        lax.fori_loop(0, block, step, 0, unroll=True)


def put_scalar(ref, s, value):
    for o in range(ref.shape[1]):
        for t in range(ref.shape[0]):
            part = value[o * SUB : (o + 1) * SUB, t * LANES : (t + 1) * LANES]
            ref[t, o, pl.ds(s * SUB, SUB), :] = part


def get_scalar(ref, s):
    return jnp.concatenate(
        [
            jnp.concatenate(
                [ref[t, o, pl.ds(s * SUB, SUB), :] for t in range(ref.shape[0])], axis=1
            )
            for o in range(ref.shape[1])
        ],
        axis=0,
    )


def list_cells(s0, block, q_ref, onehot, keep, a_ref):
    _, particles, cells = q_ref.shape
    x = q_ref[pl.ds(s0, block)].reshape(block * particles, cells)
    y = dot_split(x, onehot, NT) * keep
    for i in range(block):
        put_scalar(a_ref, s0 + i, y[i * particles : (i + 1) * particles])


def list_body(
    block,
    q_hbm,
    rate_ref,
    rsel_ref,
    ot_ref,
    lcol_ref,
    a_hbm,
    base_ref,
    token_ref,
    q_ref,
    a_ref,
    in_sem,
    a_sem,
):
    scalars, particles, cells = q_ref.shape
    into = Stream(q_hbm, q_ref, in_sem, block)
    out_a = Stream(a_ref, a_hbm, a_sem, block * SUB, 2)
    into.start_all()
    token_ref[...] = rate_ref[:, :LANES]
    leaves = cell_onehot(lcol_ref, cells)
    places = lcol_ref.shape[0]
    side = max(1, LANES // places)
    keep = 1.0 - rate_ref[...]
    half = block * particles

    def step(b, carry):
        into.copy(b).wait()
        x = q_ref[pl.ds(b * block, block)].reshape(half, cells) * keep
        both = jnp.concatenate(halves(x), axis=0)
        y = dot(both, ot_ref[...], NT)
        y = y[:half] + y[half:]
        z = dot(both, leaves, NT)
        z = z[:half] + z[half:]
        for i in range(block):
            put_scalar(a_ref, b * block + i, y[i * particles : (i + 1) * particles])
            mine = z[i * particles : (i + 1) * particles]
            for o in range(base_ref.shape[1]):
                octets = [
                    mine[(o * side + u) * SUB : (o * side + u + 1) * SUB] for u in range(side)
                ]
                wide = jnp.concatenate(octets, axis=1)
                for t in range(base_ref.shape[0]):
                    at = pl.ds((b * block + i) * SUB, SUB)
                    base_ref[t, o, at, :] = wide[:, t * LANES : (t + 1) * LANES]
        out_a.copy(b).start()
        return carry

    lax.fori_loop(0, scalars // block, step, 0)
    clear_rest(scalars, base_ref)
    clear_rest(scalars, a_ref)
    for b in range(scalars // block, out_a.count):
        out_a.copy(b, out_a.tail(b)).start()
    out_a.wait_all()


def clear_rest(scalars, ref):
    rest = ref.shape[2] - scalars * SUB
    for t in range(ref.shape[0]):
        for o in range(ref.shape[1]):
            ref[t, o, pl.ds(scalars * SUB, rest), :] = jnp.zeros((rest, LANES), F32)


def open_body(
    block,
    p_hbm,
    partner_hbm,
    rate_hbm,
    list_hbm,
    q_hbm,
    a_hbm,
    ot_ref,
    rsel_ref,
    p_ref,
    q_ref,
    a_ref,
    partner_ref,
    rate_ref,
    list_ref,
    in_sem,
    out_sem,
    a_sem,
    few_sem,
):
    scalars, _, cells = p_ref.shape
    into, out = Stream(p_hbm, p_ref, in_sem, block), Stream(q_ref, q_hbm, out_sem, block)
    out_a = Stream(a_ref, a_hbm, a_sem, block * SUB, 2)
    few = [
        pltpu.make_async_copy(src, dst, few_sem.at[i])
        for i, (src, dst) in enumerate(
            [(list_hbm, list_ref), (rate_hbm, rate_ref), (partner_hbm, partner_ref)]
        )
    ]
    for c in few:
        c.start()
    into.start_all()
    for c in few:
        c.wait()
    column = jnp.broadcast_to(list_ref[...].astype(F32), (SUB, list_ref.shape[1])).T[:, :1]
    cell = lax.broadcasted_iota(I32, ot_ref.shape, 1).astype(F32)
    onehot = (column == cell).astype(F32)
    ot_ref[...] = onehot.astype(BF)
    rate = jnp.broadcast_to(rate_ref[...], (SUB, cells))
    rsel_ref[...] = dot_split(rate, onehot.astype(BF), NT)
    clear_rest(scalars, a_ref)

    def step(b, carry):
        into.copy(b).wait()
        mix(b * block, block, p_ref, partner_ref, q_ref)
        out.copy(b).start()
        list_cells(b * block, block, q_ref, ot_ref[...], 1.0 - rsel_ref[0:1, :], a_ref)
        out_a.copy(b).start()
        return carry

    whole = scalars // block
    for b in range(whole, out_a.count):
        out_a.copy(b, out_a.tail(b)).start()
    lax.fori_loop(0, whole, step, 0)
    out.wait_all()
    out_a.wait_all()


def settle_block(s0, block, q_ref, f_ref, r_ref, ot_ref, rate_ref, out_ref, devices):
    _, particles, cells = q_ref.shape
    tiles = cells // LANES
    rate = rate_ref[...]
    keep = 1.0 - rate
    r = jnp.concatenate([get_scalar(r_ref, s0 + i) for i in range(block)], axis=0)
    spread = dot(r.astype(BF), ot_ref[...], NN)
    for i in range(block):
        s = s0 + i
        at = lax.rem(s, devices) * (f_ref.shape[0] // devices) + lax.div(s, devices) * tiles
        f = jnp.concatenate([f_ref[pl.ds(at + t, 1), :] for t in range(tiles)], axis=1)
        out_ref[s0 + i] = (
            keep * q_ref[s0 + i] + rate * f + spread[i * particles : (i + 1) * particles]
        )


def middle_body(
    block,
    devices,
    q_hbm,
    f_ref,
    r_hbm,
    ot_ref,
    rate_ref,
    partner_ref,
    out_hbm,
    token_ref,
    q_ref,
    now_ref,
    r_ref,
    in_sem,
    out_sem,
    r_sem,
):
    scalars = q_ref.shape[0]
    into, out = Stream(q_hbm, q_ref, in_sem, block), Stream(q_ref, out_hbm, out_sem, block)
    changes = Stream(r_hbm, r_ref, r_sem, block * SUB, 2)
    for b in range(q_ref.shape[0] // block):
        changes.copy(b).start()
        into.copy(b).start()
    token_ref[...] = rate_ref[:, :LANES]

    def step(b, carry):
        changes.copy(b).wait()
        into.copy(b).wait()
        s0 = b * block
        settle_block(s0, block, q_ref, f_ref, r_ref, ot_ref, rate_ref, now_ref, devices)
        mix(s0, block, now_ref, partner_ref, q_ref)
        out.copy(b).start()
        return carry

    lax.fori_loop(0, scalars // block, step, 0)
    out.wait_all()


def half_silu(y):
    return (y + y * jnp.tanh(y)).astype(BF)


def chem_body(
    devices,
    rows,
    count_ref,
    f_ref,
    a_hbm,
    ot_ref,
    rsel_ref,
    w1_ref,
    w2_ref,
    w3_ref,
    token_ref,
    *refs,
):
    pos_refs, refs = refs[:-7], refs[-7:]
    r_hbm, s_ref, a_ref, r_ref, pull_ref, in_sem, out_sem = refs
    tiles = ot_ref.shape[1] // LANES
    listed = ot_ref.shape[0]
    particles = a_ref.shape[1] * SUB
    into, out = Stream(a_hbm, a_ref, in_sem, 1, 1), Stream(r_ref, r_hbm, out_sem, 1, 1)
    into.start_all()
    f = load_filtered(f_ref, devices, rows, tiles)
    pull_ref[...] = rsel_ref[0:1, :] * dot_split(f, ot_ref[...], NT)
    live = lax.broadcasted_iota(I32, (1, listed), 1) < count_ref[0]

    def first(g):
        parts = []
        for i in range(2):
            p = 2 * g + i
            at = pl.ds(p & (SUB - 1), rows, stride=SUB)
            for t in range(listed // LANES):
                pull = pull_ref[:, t * LANES : (t + 1) * LANES]
                parts.append((a_ref[t, p >> 3, at, :] + pull).astype(BF))
        return half_silu(dot(w1_ref[...], jnp.concatenate(parts, axis=1), NN))

    def second(one):
        return half_silu(dot(w2_ref[...], one, NN))

    def third(g, two, total):
        change = dot(w3_ref[...], two, NN).astype(BF).astype(F32)
        for i in range(2):
            r = jnp.where(live, change[:, i * listed : (i + 1) * listed], 0.0)
            p = 2 * g + i
            at = pl.ds(p & (SUB - 1), rows, stride=SUB)
            for t in range(listed // LANES):
                r_ref[t, p >> 3, at, :] = r[:, t * LANES : (t + 1) * LANES]
            total = total + r
        return total

    total = jnp.zeros((rows, listed), F32)
    groups, each = particles // 2, SUB // 2
    ones, twos = {}, {}
    for n in range(groups + 2):
        if n < groups:
            if n % each == 0:
                into.copy(n // each).wait()
            ones[n] = first(n)
        if 0 < n <= groups:
            twos[n - 1] = second(ones.pop(n - 1))
        if n > 1:
            total = third(n - 2, twos.pop(n - 2), total)
            if (n - 1) % each == 0 and n - 1 < groups:
                out.copy((n - 1) // each - 1).start()
    out.copy(particles // SUB - 1).start()
    source = total * (1.0 / particles)
    if pos_refs:
        boxes_source(source, *pos_refs, s_ref)
    else:
        source = dot_split(source, ot_ref[...], NN)
        stride = s_ref.shape[0] // devices
        for i in range(rows // devices):
            for t in range(tiles):
                part = source[i * devices : (i + 1) * devices, t * LANES : (t + 1) * LANES]
                s_ref[pl.ds(i * tiles + t, devices, stride=stride), :] = part
    out.wait_all()


def boxes_source(source, pos_ref, s_ref):
    listed = source.shape[1]
    boxes = s_ref.shape[0]
    put = lax.broadcasted_iota(I32, (listed, boxes * LANES), 1).astype(F32) == pos_ref[:, :1]
    sent = dot_split(source, put.astype(F32).astype(BF), NN)
    for b in range(boxes):
        s_ref[b] = sent[: s_ref.shape[1], b * LANES : (b + 1) * LANES]


def early_body(
    devices,
    rows,
    span,
    scalars,
    particles,
    count_ref,
    f_ref,
    base_ref,
    ot_ref,
    rate_ref,
    lcol_ref,
    w1_ref,
    w2_ref,
    w3_ref,
    token_ref,
    out_ref,
    end_ref,
    v_ref,
):
    listed, cells = ot_ref.shape
    tiles = cells // LANES
    places = lcol_ref.shape[0]
    side = max(1, LANES // places)
    wide = base_ref.shape[0]
    end_ref[...] = rate_ref[:, :LANES]
    f = load_filtered(f_ref, devices, rows, tiles)
    leaves = cell_onehot(lcol_ref, cells)
    rate = dot_split(jnp.broadcast_to(rate_ref[...], (SUB, cells)), leaves, NT)[:1]
    pull = rate * dot_split(f, leaves, NT)
    live = (lax.broadcasted_iota(I32, (SUB, listed), 1) < count_ref[0]).astype(F32).astype(BF)
    live = dot(dot(live, ot_ref[...], NN).astype(BF), leaves, NT)[:1]
    pull = jnp.concatenate([pull] * side, axis=1)
    live = jnp.concatenate([live] * side, axis=1) > 0.5
    count = 4 // wide

    todo = [(o, i) for o in range(particles // SUB // side) for i in range(0, SUB, count)]
    tile = [(u, t) for u in range(count) for t in range(wide)]
    ones, twos, fed = {}, {}, {}
    for n in range(len(todo) + 2):
        if n < len(todo):
            o, i = todo[n]
            fed[n] = jnp.concatenate(
                [
                    base_ref[t, o, pl.ds(i + u, rows, stride=SUB), :]
                    + pull[:, t * LANES : (t + 1) * LANES]
                    for u, t in tile
                ],
                axis=1,
            )
            ones[n] = half_silu(dot(w1_ref[...], fed[n].astype(BF), NN))
        if 0 < n <= len(todo):
            twos[n - 1] = half_silu(dot(w2_ref[...], ones[n - 1], NN))
        if n > 1:
            o, i = todo[n - 2]
            change = dot(w3_ref[...], twos[n - 2], NN).astype(BF).astype(F32)
            for c, (u, t) in enumerate(tile):
                cols = slice(c * LANES, (c + 1) * LANES)
                mask = live[:, t * LANES : (t + 1) * LANES]
                v_ref[t, o, pl.ds(i + u, rows, stride=SUB), :] = fed[n - 2][:, cols] + jnp.where(
                    mask, change[:, cols], 0.0
                )

    per = LANES // particles
    stride = out_ref.shape[0] // devices

    def scalar(s):
        parts = []
        for o in range(particles // SUB // side):
            at = pl.ds(s * SUB, SUB)
            row = jnp.concatenate([v_ref[t, o, at, :] for t in range(wide)], axis=1)
            parts += [row[:, u * places : (u + 1) * places] for u in range(side)]
        return jnp.concatenate(parts, axis=0)

    def part(b, count):
        value = jnp.concatenate([scalar(b * per + i) for i in range(count)], axis=0)
        if count < per:
            rest = jnp.zeros(((per - count) * particles, places), F32)
            value = jnp.concatenate([value, rest], axis=0)
        value = value.T
        for c in range(places // devices):
            at = pl.ds(c * span + b, devices, stride=stride)
            out_ref[at, :] = value[c * devices : (c + 1) * devices]

    def step(b, carry):
        part(b, per)
        return carry

    whole = scalars // per
    lax.fori_loop(0, whole, step, 0, unroll=True)
    zeros = jnp.zeros((devices, LANES), F32)
    for c in range(places // devices):
        for b in range(whole, span):
            out_ref[pl.ds(c * span + b, devices, stride=stride), :] = zeros
    if scalars > whole * per:
        part(whole, scalars - whole * per)


def columns(row_ref, devices, out_ref, turn_ref):
    places = row_ref.shape[1]
    count = places // devices
    column = jnp.broadcast_to(row_ref[...].astype(F32), (SUB, places)).T[:, :1]
    turn_ref[...] = jnp.broadcast_to(column, turn_ref.shape)
    for c in range(count):
        part = turn_ref[pl.ds(c, devices, stride=count), :]
        out_ref[c * devices : (c + 1) * devices] = part.astype(I32)


def maps_body(
    dims,
    me_ref,
    lab_ref,
    ot_ref,
    owner_ref,
    slot_ref,
    leave_ref,
    arrive_ref,
    pos_ref,
    put_ref,
    lcol_ref,
    acol_ref,
    inv_ref,
    turn_ref,
):
    nx, ny, _, bx, by = dims
    invert(dims, lab_ref, inv_ref)
    columns(leave_ref, nx * ny, lcol_ref, turn_ref)
    columns(arrive_ref, nx * ny, acol_ref, turn_ref)
    quads = bx * by
    turns = quads * ny
    _, cells = ot_ref.shape
    at = me_ref[0] * 2 * turns + me_ref[1]
    code = jnp.concatenate([inv_ref[pl.ds(at + k * ny, 1), :] for k in range(quads)], axis=1)
    box = lax.rem(code, ny).astype(F32)
    boxes = lax.broadcasted_iota(I32, (ny, cells), 0).astype(F32)
    mine = (jnp.broadcast_to(box, (ny, cells)) == boxes).astype(F32)
    before = lax.broadcasted_iota(I32, (cells, cells), 0) < lax.broadcasted_iota(
        I32, (cells, cells), 1
    )
    count = dot(mine.astype(BF), before.astype(F32).astype(BF), NN)
    rank = jnp.sum(mine * count, axis=0, keepdims=True)
    rest = jnp.zeros((SUB - 2, cells), F32)
    found = dot(ot_ref[...], jnp.concatenate([box, rank, rest], axis=0).astype(BF), NT)
    pos = found[:, :1] * LANES + found[:, 1:2]
    pos_ref[...] = jnp.broadcast_to(pos, pos_ref.shape)
    flat = lambda ref: jnp.concatenate([ref[j : j + 1, :] for j in range(quads)], axis=1)
    owner, slot = flat(owner_ref).astype(F32), flat(slot_ref).astype(F32)
    first = owner * cells
    key = first + slot
    column = jnp.broadcast_to(key, (SUB, cells)).T[:, :1]
    ahead = (column < key) & (column >= first)
    place = owner * LANES + jnp.sum(ahead.astype(F32), axis=0, keepdims=True)
    step = min(cells, put_ref.shape[0])
    for b in range(put_ref.shape[0] // step):
        row = lax.broadcasted_iota(I32, (step, cells), 0).astype(F32) + b * step
        put_ref[b * step : (b + 1) * step] = (row == place).astype(F32).astype(BF)


def unpack_body(devices, own, s_ref, arr_ref, put_ref, out_ref):
    boxes, _ = s_ref.shape[:2]
    cells = put_ref.shape[1]
    quads = cells // LANES
    scalars = out_ref.shape[0] // quads
    stride = arr_ref.shape[0] // devices
    got = jnp.concatenate([s_ref[b] for b in range(boxes)], axis=1)
    source = dot_split(got, put_ref[...], NN)
    for j in range(quads):
        for i in range(own):
            n = min(devices, scalars - i * devices)
            if n > 0:
                grid = arr_ref[pl.ds(stride - own * quads + i * quads + j, n, stride=stride), :]
                part = source[i * devices : i * devices + n, j * LANES : (j + 1) * LANES]
                out_ref[pl.ds(i * devices * quads + j, n, stride=quads), :] = grid + part


def cell_onehot(col_ref, cells):
    shape = (col_ref.shape[0], cells)
    return (col_ref[:, :1] == lax.broadcasted_iota(I32, shape, 1)).astype(F32).astype(BF)


def settle_body(
    block,
    devices,
    q_hbm,
    f_ref,
    r_hbm,
    ot_ref,
    rate_ref,
    out_hbm,
    token_ref,
    q_ref,
    out_ref,
    r_ref,
    in_sem,
    out_sem,
    r_sem,
):
    into, out = Stream(q_hbm, q_ref, in_sem, block), Stream(out_ref, out_hbm, out_sem, block)
    changes = Stream(r_hbm, r_ref, r_sem, block * SUB, 2)
    for b in range(q_ref.shape[0] // block):
        changes.copy(b).start()
        into.copy(b).start()
    token_ref[...] = rate_ref[:, :LANES]

    def step(b, carry):
        changes.copy(b).wait()
        into.copy(b).wait()
        settle_block(b * block, block, q_ref, f_ref, r_ref, ot_ref, rate_ref, out_ref, devices)
        out.copy(b).start()
        return carry

    lax.fori_loop(0, q_ref.shape[0] // block, step, 0)
    out.wait_all()


def arrive_body(
    span, devices, p_hbm, arr_ref, acol_ref, out_hbm, p_ref, out_ref, hit_ref, in_sem, out_sem
):
    scalars, particles, cells = p_ref.shape
    places = acol_ref.shape[0]
    per = LANES // particles
    into, out = Stream(p_hbm, p_ref, in_sem, per), Stream(out_ref, out_hbm, out_sem, per)
    into.start_all()
    hit = (acol_ref[:, :1] == lax.broadcasted_iota(I32, (places, cells), 1)).astype(F32)
    hit_ref[...] = hit.astype(BF)
    taken = jnp.sum(hit, axis=0, keepdims=True) > 0.5
    stride = arr_ref.shape[0] // devices
    count = places // devices

    def place(b, size):
        first = stride - count * span + b
        x = jnp.concatenate(
            [arr_ref[pl.ds(first + c * span, devices, stride=stride), :] for c in range(count)],
            axis=0,
        ).T
        y = dot_split(x, hit_ref[...], NN)
        into.copy(b, size).wait()
        for i in range(size):
            s = b * per + i
            out_ref[s] = jnp.where(taken, y[i * particles : (i + 1) * particles], p_ref[s])
        out.copy(b, size).start()

    def step(b, carry):
        place(b, per)
        return carry

    whole = scalars // per
    lax.fori_loop(0, whole, step, 0)
    if scalars > whole * per:
        place(whole, scalars - whole * per)
    out.wait_all()


def stencil(value, speed, bx, by, lanes_y):
    boxes = value[0].shape[0]
    row = lax.broadcasted_iota(I32, value[0].shape, 0) % lanes_y
    zero = jnp.zeros((lanes_y, LANES), F32)

    def x_low(v):
        return jnp.concatenate([zero, v[: boxes - lanes_y]], axis=0)

    def x_high(v):
        return jnp.concatenate([v[lanes_y:], zero], axis=0)

    def y_low(v):
        return jnp.where(row == 0, 0.0, pltpu.roll(v, 1, 0))

    def y_high(v):
        return jnp.where(row == lanes_y - 1, 0.0, pltpu.roll(v, boxes - 1, 0))

    out = []
    for i in range(bx):
        for j in range(by):
            c = value[i * by + j]
            up = value[(i - 1) * by + j] if i else x_low(value[(bx - 1) * by + j])
            down = value[(i + 1) * by + j] if i < bx - 1 else x_high(value[j])
            left = value[i * by + j - 1] if j else y_low(value[i * by + by - 1])
            right = value[i * by + j + 1] if j < by - 1 else y_high(value[i * by])
            beside = up + down + left + right + pltpu.roll(c, 1, 1) + pltpu.roll(c, LANES - 1, 1)
            out.append(c + DIFFUSION * (beside - 6.0 * c) - speed[i * by + j] * (c - up))
    return out


def route(src_ref, first_row, row_step, item_step, items, own, quads, lanes_y, rows, lanes):
    shape = (lanes_y, LANES)
    out = []
    for k in range(len(rows)):

        def step(y, acc):
            for j in range(items):
                hit = rows[k] == (j * lanes_y + y)
                at = first_row + y * row_step + j * item_step
                lines = [src_ref[pl.ds(at + s * quads, 1), :] for s in range(own)]
                acc = [
                    jnp.where(
                        hit,
                        jnp.take_along_axis(jnp.broadcast_to(v, shape), lanes[k], axis=1),
                        old,
                    )
                    for v, old in zip(lines, acc)
                ]
            return tuple(acc)

        zero = tuple(jnp.zeros(shape, F32) for _ in range(own))
        out.append(lax.fori_loop(0, lanes_y, step, zero, unroll=min(lanes_y, 8)))
    return [[out[k][s] for k in range(len(rows))] for s in range(own)]


def load_rows(ref, offset, stride, count):
    return ref[pl.ds(offset, count, stride=stride), :]


def pack_body(
    width,
    lanes_y,
    grid_hbm,
    owner_hbm,
    slot_hbm,
    speed_hbm,
    out_ref,
    grid_ref,
    owner_ref,
    slot_ref,
    speed_ref,
    sem,
):
    pairs = [
        (grid_hbm, grid_ref),
        (owner_hbm, owner_ref),
        (slot_hbm, slot_ref),
        (speed_hbm, speed_ref),
    ]
    copies = [pltpu.make_async_copy(a, b, sem.at[i]) for i, (a, b) in enumerate(pairs)]
    for c in copies:
        c.start()
    for c in copies:
        c.wait()
    quads = owner_ref.shape[0]
    stride = width + 2 * quads
    total = grid_ref.shape[0]
    slot = slot_ref[...]
    label = ((slot >> 7) * lanes_y + owner_ref[...]) * LANES + (slot & (LANES - 1))
    tail = jnp.concatenate([label.astype(F32), speed_ref[...]], axis=0)
    devices = out_ref.shape[0] // stride
    for d in range(devices):
        for i in range(width // quads):
            at = d * stride + i * quads
            src = (i * devices + d) * quads
            if src < total:
                out_ref[at : at + quads] = grid_ref[src : src + quads]
            else:
                out_ref[at : at + quads] = jnp.zeros((quads, LANES), F32)
        out_ref[d * stride + width : (d + 1) * stride] = tail


def weights_body(w1_ref, w2_ref, w3_ref, token_ref, a_ref, b_ref, c_ref):
    scalars, hidden = w1_ref.shape
    rest = jnp.zeros((a_ref.shape[1] - scalars, hidden), F32)
    a_ref[...] = jnp.concatenate([w1_ref[...].astype(F32) * 0.5, rest], axis=0).T.astype(BF)
    b_ref[...] = (w2_ref[...].astype(F32) * 0.5).astype(BF)
    c_ref[...] = jnp.concatenate([w3_ref[...].astype(F32), rest], axis=0).astype(BF)


def start_body(dims, arr_ref, token_ref, g_ref, f_ref, lab_ref, high_ref, low_ref):
    nx, ny, own, bx, by = dims
    quads = bx * by
    boxes = nx * ny
    width = own * quads
    stride = width + 2 * quads
    turns = quads * ny
    speed = [load_rows(arr_ref, width + quads + j, stride, boxes) for j in range(quads)]
    for s in range(own):
        value = [load_rows(arr_ref, s * quads + j, stride, boxes) for j in range(quads)]
        for j, v in enumerate(stencil(value, speed, bx, by, ny)):
            at = pl.ds(s * quads + j, boxes, stride=width)
            g_ref[at, :] = v
            high = v.astype(BF).astype(F32)
            high_ref[at, :] = high
            low_ref[at, :] = v - high
    for j in range(quads):
        lab_ref[pl.ds(j * boxes, boxes), :] = load_rows(arr_ref, width + j, stride, boxes).astype(
            I32
        )
    sub_of = lax.broadcasted_iota(I32, (turns, LANES), 0).astype(F32).astype(BF)
    sub_lane = lax.broadcasted_iota(I32, (LANES, LANES), 0).astype(F32).astype(BF)
    none = jnp.zeros((turns, LANES), BF)
    unit = jnp.ones((LANES, LANES), BF)

    def group(x, carry):
        def gather(y, acc):
            left, right = [], []
            for j in range(quads):
                line = lab_ref[pl.ds(j * boxes + x * ny + y, 1), :]
                hit = jnp.broadcast_to((line >> 7).astype(F32).astype(BF), (turns, LANES)) == sub_of
                parts = []
                for s in range(own):
                    at = pl.ds((x * ny + y) * width + s * quads + j, 1)
                    for ref in (high_ref, low_ref):
                        value = jnp.broadcast_to(ref[at, :].astype(BF), (turns, LANES))
                        parts.append(jnp.where(hit, value, none))
                left.append(jnp.concatenate(parts, axis=0))
                lane = jnp.broadcast_to((line & (LANES - 1)).astype(F32).astype(BF), (LANES, LANES))
                right.append(jnp.where(lane == sub_lane, unit, jnp.zeros_like(unit)))
            return acc + dot(jnp.concatenate(left, axis=1), jnp.concatenate(right, axis=1), NT)

        zero = jnp.zeros((2 * own * turns, LANES), F32)
        acc = lax.fori_loop(0, ny, gather, zero, unroll=min(ny, 8))
        for s in range(own):
            out = acc[2 * s * turns : (2 * s + 1) * turns] + acc[(2 * s + 1) * turns :][:turns]
            for k in range(quads):
                at = pl.ds(x * ny * width + s * quads + k, ny, stride=width)
                f_ref[at, :] = out[k * ny : (k + 1) * ny]
        return carry

    lax.fori_loop(0, nx, group, 0)


def invert(dims, lab_ref, inv_ref):
    nx, ny, _, bx, by = dims
    quads = bx * by
    boxes = nx * ny
    turns = quads * ny
    lane_of = lax.broadcasted_iota(I32, (turns, LANES), 1).astype(F32).astype(BF)
    sub_of = lax.broadcasted_iota(I32, (turns, LANES), 0).astype(F32).astype(BF)
    sub_lane = lax.broadcasted_iota(I32, (LANES, LANES), 0).astype(F32).astype(BF)
    none = jnp.zeros((turns, LANES), BF)
    unit = jnp.ones((LANES, LANES), BF)

    def group(x, carry):
        def gather(y, acc):
            left, right = [], []
            for j in range(quads):
                line = lab_ref[pl.ds(j * boxes + x * ny + y, 1), :]
                hit = jnp.broadcast_to((line >> 7).astype(F32).astype(BF), (turns, LANES)) == sub_of
                code = jnp.full((turns, LANES), j * ny + y).astype(F32).astype(BF)
                left.append(
                    jnp.concatenate([jnp.where(hit, code, none), jnp.where(hit, lane_of, none)], axis=0)
                )
                lane = jnp.broadcast_to((line & (LANES - 1)).astype(F32).astype(BF), (LANES, LANES))
                right.append(jnp.where(lane == sub_lane, unit, jnp.zeros_like(unit)))
            return acc + dot(
                jnp.concatenate(left, axis=1), jnp.concatenate(right, axis=1), NT
            )

        code = lax.fori_loop(0, ny, gather, jnp.zeros((2 * turns, LANES), F32), unroll=8)
        code = code.astype(I32)
        inv_ref[pl.ds(x * 2 * turns, 2 * turns), :] = code
        return carry

    lax.fori_loop(0, nx, group, 0)


def scatter(parts_refs, first_row, row_step, quads, own, lanes_y, target):
    turns = quads * lanes_y
    sub_of = lax.broadcasted_iota(I32, (turns, LANES), 0).astype(F32).astype(BF)
    sub_lane = lax.broadcasted_iota(I32, (LANES, LANES), 0).astype(F32).astype(BF)
    none = jnp.zeros((turns, LANES), BF)
    unit = jnp.ones((LANES, LANES), BF)

    def step(y, acc):
        left, right = [], []
        for j in range(quads):
            row, lane = target(j, y)
            hit = jnp.broadcast_to(row.astype(F32).astype(BF), (turns, LANES)) == sub_of
            parts = []
            for s in range(own):
                at = pl.ds(first_row + y * row_step + s * quads + j, 1)
                for ref in parts_refs:
                    value = jnp.broadcast_to(ref[at, :].astype(BF), (turns, LANES))
                    parts.append(jnp.where(hit, value, none))
            left.append(jnp.concatenate(parts, axis=0))
            lane = jnp.broadcast_to(lane.astype(F32).astype(BF), (LANES, LANES))
            right.append(jnp.where(lane == sub_lane, unit, jnp.zeros_like(unit)))
        return acc + dot(jnp.concatenate(left, axis=1), jnp.concatenate(right, axis=1), NT)

    zero = jnp.zeros((2 * own * turns, LANES), F32)
    acc = lax.fori_loop(0, lanes_y, step, zero, unroll=min(lanes_y, 8))
    parts = [acc[i * turns : (i + 1) * turns] for i in range(2 * own)]
    return [parts[2 * s] + parts[2 * s + 1] for s in range(own)]


def both_ways(dims, src_ref, high_ref, low_ref, pull, push, store):
    nx, ny, own, bx, by = dims
    quads = bx * by
    width = own * quads
    high = src_ref[...].astype(BF).astype(F32)
    high_ref[...] = high
    low_ref[...] = src_ref[...] - high

    def routed(x):
        rows, lanes = pull(x)
        return route(src_ref, x * ny * width, width, 1, quads, own, quads, ny, rows, lanes)

    def pair(i, carry):
        x, z = 2 * i, 2 * i + 1
        out = routed(x)
        other = scatter((high_ref, low_ref), z * ny * width, width, quads, own, ny, push(z))
        for s in range(own):
            for k in range(quads):
                store(pl.ds(x * ny * width + s * quads + k, ny, stride=width), out[s][k])
                at = pl.ds(z * ny * width + s * quads + k, ny, stride=width)
                store(at, other[s][k * ny : (k + 1) * ny])
        return carry

    lax.fori_loop(0, nx // 2, pair, 0)
    for x in range(nx // 2 * 2, nx):
        out = routed(x)
        for s in range(own):
            for k in range(quads):
                store(pl.ds(x * ny * width + s * quads + k, ny, stride=width), out[s][k])


def again_body(
    dims,
    s_ref,
    g_ref,
    arr_ref,
    inv_ref,
    lab_ref,
    token_ref,
    f_ref,
    mid_ref,
    out_ref,
    high_ref,
    low_ref,
):
    nx, ny, own, bx, by = dims
    quads = bx * by
    boxes = nx * ny
    width = own * quads
    stride = width + 2 * quads
    turns = quads * ny

    def by_label(x):
        labels = [lab_ref[pl.ds(j * boxes + x * ny, ny), :] for j in range(quads)]
        return [v >> 7 for v in labels], [v & (LANES - 1) for v in labels]

    def by_inverse(x):
        base = x * 2 * turns
        rows = [inv_ref[pl.ds(base + k * ny, ny), :] for k in range(quads)]
        return rows, [inv_ref[pl.ds(base + turns + k * ny, ny), :] for k in range(quads)]

    def to_label(x):
        def target(j, y):
            line = lab_ref[pl.ds(j * boxes + x * ny + y, 1), :]
            return line >> 7, line & (LANES - 1)

        return target

    def to_inverse(x):
        def target(k, y):
            at = x * 2 * turns + k * ny + y
            return inv_ref[pl.ds(at, 1), :], inv_ref[pl.ds(at + turns, 1), :]

        return target

    def add(at, value):
        mid_ref[at, :] = g_ref[at, :] + value

    both_ways(dims, s_ref, high_ref, low_ref, by_label, to_inverse, add)
    speed = [load_rows(arr_ref, width + quads + j, stride, boxes) for j in range(quads)]
    for s in range(own):
        value = [load_rows(mid_ref, s * quads + j, width, boxes) for j in range(quads)]
        for j, v in enumerate(stencil(value, speed, bx, by, ny)):
            out_ref[pl.ds(s * quads + j, boxes, stride=width), :] = v


    def keep(at, value):
        mid_ref[at, :] = value

    both_ways(dims, out_ref, high_ref, low_ref, by_inverse, to_label, keep)
    for d in range(boxes):
        f_ref[2 * d * width : (2 * d + 1) * width] = mid_ref[d * width : (d + 1) * width]
        f_ref[(2 * d + 1) * width : (2 * d + 2) * width] = out_ref[d * width : (d + 1) * width]


def per_device(
    grid_scalars,
    axial_speed,
    particles,
    cell_owner,
    cell_slot,
    mix_rate,
    partner,
    chem_input,
    chem_hidden,
    chem_output,
    react_slots,
    react_count,
    leave_slots,
    arrive_slots,
):
    both = ("gx", "gy")
    nx, ny = lax.axis_size("gx"), lax.axis_size("gy")
    devices = nx * ny
    scalars, bx, by, nz = grid_scalars.shape
    heads, cells = partner.shape
    listed = react_slots.shape[1]
    hidden = chem_hidden.shape[0]
    quads = bx * by
    own = -(-scalars // devices)
    rows = devices * own
    width = own * quads
    tiles = cells // LANES
    assert nz == LANES and tiles == quads and heads % SUB == 0 and LANES % heads == 0
    dims = (nx, ny, own, bx, by)
    flat = devices * width

    box = [
        grid_scalars.reshape(-1, LANES),
        cell_owner.reshape(quads, LANES),
        cell_slot.reshape(quads, LANES),
        axial_speed.reshape(quads, LANES),
    ]
    (first,) = call(
        functools.partial(pack_body, width, ny),
        [((devices * (width + 2 * quads), LANES), F32)],
        box,
        hbm=(0, 1, 2, 3),
        scratch=[pltpu.VMEM(x.shape, x.dtype) for x in box] + [pltpu.SemaphoreType.DMA((4,))],
    )

    def exchange(x):
        count = x.shape[0] // devices
        tile = SUB if count % SUB == 0 else SUB // 2
        x = x.reshape(devices, count // tile, tile, LANES)
        return lax.all_to_all(x, both, split_axis=0, concat_axis=0, tiled=True).reshape(-1, LANES)

    arrival = exchange(first)

    rate = mix_rate.reshape(1, cells)
    state_shape = (scalars, heads, cells)
    listed_shape = (listed // LANES, heads // SUB, rows * SUB, LANES)
    block = divisor(scalars, 6)
    octets = heads // SUB
    state_vmem = pltpu.VMEM(state_shape, F32)
    listed_vmem = pltpu.VMEM(listed_shape, F32)
    dma = pltpu.SemaphoreType.DMA
    per_block = dma((scalars // block,))
    per_listed = dma((-(-rows // block),))
    q, a, ot, rsel = call(
        functools.partial(open_body, block),
        [
            (state_shape, F32, True),
            (listed_shape, F32, True),
            ((listed, cells), BF),
            ((SUB, listed), F32),
        ],
        [particles, partner, rate, react_slots],
        hbm=(0, 1, 2, 3),
        scratch=[
            state_vmem,
            state_vmem,
            listed_vmem,
            pltpu.VMEM(partner.shape, I32),
            pltpu.VMEM(rate.shape, F32),
            pltpu.VMEM(react_slots.shape, I32),
            per_block,
            per_block,
            per_listed,
            dma((3,)),
        ],
    )
    grid, sent, lab = call(
        functools.partial(start_body, dims),
        [((flat, LANES), F32), ((flat, LANES), F32), ((quads * devices, LANES), I32)],
        [arrival, rsel],
        scratch=[pltpu.VMEM((flat, LANES), F32)] * 2,
    )

    w1, w2, w3 = call(
        weights_body,
        [((hidden, rows), BF), ((hidden, hidden), BF), ((rows, hidden), BF)],
        [chem_input.T, chem_hidden, chem_output, lab],
    )

    per = LANES // heads
    span = 2 * (-(-scalars // (per * 2)))
    places = leave_slots.shape[1]
    side = max(1, LANES // places)
    base_shape = (max(1, places // LANES), octets // side, rows * SUB, LANES)
    kept = SUB * (-(-scalars // SUB))
    me = jnp.stack([lax.axis_index("gx"), lax.axis_index("gy")]).astype(I32)
    pos, put, lcol, acol, inv = call(
        functools.partial(maps_body, dims),
        [
            ((listed, LANES), F32),
            ((ny * LANES, cells), BF),
            ((places, LANES), I32),
            ((places, LANES), I32),
            ((nx * 2 * quads * ny, LANES), I32),
        ],
        [me, lab, ot, box[1], box[2], leave_slots, arrive_slots],
        smem=(0,),
        scratch=[pltpu.VMEM((places, LANES), F32)],
    )

    def chemistry(f, a, token, out, more=()):
        return call(
            functools.partial(chem_body, devices, rows),
            [(listed_shape, F32, True), (out, F32)],
            [react_count, f, a, ot, rsel, w1, w2, w3, token, *more],
            smem=(0,),
            hbm=(2,),
            scratch=[listed_vmem, listed_vmem, pltpu.VMEM((rows, listed), F32)]
            + [dma((octets,)), dma((octets,))],
        )

    f = exchange(sent)
    change, source = chemistry(f, a, pos, (flat, LANES))
    home = exchange(source)
    q, token = call(
        functools.partial(middle_body, block, devices),
        [(state_shape, F32, True), ((1, LANES), F32)],
        [q, f, change, ot, rate, partner],
        hbm=(0, 2),
        scratch=[state_vmem, state_vmem, listed_vmem, per_block, per_block, per_listed],
    )
    (sent,) = call(
        functools.partial(again_body, dims),
        [((2 * flat, LANES), F32)],
        [home, grid, arrival, inv, lab, token],
        scratch=[pltpu.VMEM((flat, LANES), F32)] * 4,
    )
    a, base, token = call(
        functools.partial(list_body, block),
        [(listed_shape, F32, True), (base_shape, F32), ((1, LANES), F32)],
        [q, rate, rsel, ot, lcol],
        hbm=(0,),
        scratch=[
            state_vmem,
            listed_vmem,
            per_block,
            per_listed,
        ],
    )
    f = exchange(sent)
    leaving, token = call(
        functools.partial(early_body, devices, rows, span, scalars, heads),
        [((places * span, LANES), F32), ((1, LANES), F32)],
        [react_count, f, base, ot, rate, lcol, w1, w2, w3, token],
        smem=(0,),
        scratch=[pltpu.VMEM(base_shape, F32)],
    )
    change, source = chemistry(f, a, token, (ny, kept, LANES), [pos])
    moved = exchange(leaving)
    state, token = call(
        functools.partial(settle_body, block, devices),
        [(state_shape, F32, True), ((1, LANES), F32)],
        [q, f, change, ot, rate],
        hbm=(0, 2),
        scratch=[state_vmem, state_vmem, listed_vmem, per_block, per_block, per_listed],
    )
    source = lax.all_to_all(source, "gy", split_axis=0, concat_axis=0, tiled=True)
    (grid,) = call(
        functools.partial(unpack_body, devices, own),
        [((scalars * quads, LANES), F32)],
        [source, f, put],
    )
    grid_out = grid.reshape(grid_scalars.shape)
    steps = -(-scalars // per)
    (state,) = call(
        functools.partial(arrive_body, span, devices),
        [(state_shape, F32, True)],
        [state, moved, acol],
        hbm=(0,),
        scratch=[
            state_vmem,
            state_vmem,
            pltpu.VMEM((places, cells), BF),
            dma((steps,)),
            dma((steps,)),
        ],
    )
    return (grid_out, state)


def solution(mesh):
    placed = (
        P(None, "gx", "gy", None),
        P("gx", "gy", None),
        P(None, None, ("gx", "gy")),
        P("gx", "gy", None),
        P("gx", "gy", None),
        P(("gx", "gy")),
        P(None, ("gx", "gy")),
        P(),
        P(),
        P(),
        P(("gx", "gy"), None),
        P(("gx", "gy")),
        P(("gx", "gy"), None),
        P(("gx", "gy"), None),
    )

    return jax.shard_map(
        per_device,
        mesh=mesh,
        in_specs=placed,
        out_specs=(P(None, "gx", "gy", None), P(None, None, ("gx", "gy"))),
        check_vma=False,
    )
```
